32 devices in a mesh: dp: 8 (over y, x, core), tensor: 4 (over z).
Axes of the slice: x: 2, y: 2, z: 4, core: 2. Of those that a mesh axis runs over, the one named last changes fastest.
Arguments:
- tokens: bfloat16 [16384, 768], P(('dp', 'tensor')), may hold values from -6 to 6
- cotangent: bfloat16 [16384, 768], P(('dp', 'tensor')), may hold values from -6 to 6
- deal: int32 [16384], P(('dp', 'tensor')), may hold values from 0 to 7, as said below
- lengths: int32 [8, 8], P('dp'), may hold values from 1 to 1024, 2048 in all within a row
- routes: int32 [16384, 2], P('dp'), may hold values from 0 to 11, all different within a row; in each aligned block of 2048 rows (0 to 2047, 2048 to 4095, ...) at most 512 rows name the same one
- gate_residual: float32 [16384, 12], P(('dp', 'tensor')), may hold values from -4 to 4
- w_qkv: bfloat16 [768, 3, 768], P('dp', None, 'tensor'), may hold values from -0.21875 to 0.21875
- w_out: bfloat16 [768, 768], P('dp', 'tensor'), may hold values from -1.25 to 1.25
- w_gate_up: bfloat16 [768, 8, 2, 2048], P('dp', None, None, 'tensor'), may hold values from -0.21875 to 0.21875
- w_down: bfloat16 [768, 8, 2048], P('dp', None, 'tensor'), may hold values from -0.25 to 0.25
- norm_gain_attn: float32 [768], replicated, may hold values from 0.1 to 1.9
- norm_gain_moe: float32 [768], replicated, may hold values from 0.1 to 1.9
- w_router: float32 [768, 12], replicated, may hold values from -0.15625 to 0.15625
- w_const: float32 [2, 768, 2], replicated, may hold values from -0.21875 to 0.21875
- v_const: float32 [2, 768], replicated, may hold values from -5 to 5
Outputs:
- output: bfloat16 [16384, 768], P(('dp', 'tensor'))
- grad_tokens: bfloat16 [16384, 768], P(('dp', 'tensor'))
- grad_residual: float32 [16384, 12], P(('dp', 'tensor'))
- grad_qkv: float32 [768, 3, 768], P('dp', None, 'tensor')
- grad_out: float32 [768, 768], P('dp', 'tensor')
- grad_gate_up: float32 [768, 8, 2, 2048], P('dp', None, None, 'tensor')
- grad_down: float32 [768, 8, 2048], P('dp', None, 'tensor')
- grad_gain_attn: float32 [768], replicated
- grad_gain_moe: float32 [768], replicated
- grad_router: float32 [768, 12], replicated
- grad_const: float32 [2, 768, 2], replicated
- grad_vconst: float32 [2, 768], replicated
The draws below stay inside these ranges and needn't reach their ends.
Inputs may be any that keep to these rules, and one draw needn't show every extreme that they name: `deal`: every device deals exactly 64 of its tokens to each index of dp. Each row of a group's lengths sums to 2048; its largest is 1024. `routes`: A row names two different experts: 0 to 7 feed-forward, 8 zero, 9 copy, 10 and 11 constant. In the 2048 rows of one token group no expert is named by more than 512 rows, a bound that some block reaches.
All inputs are finite; a program needn't handle non-finite values.
Results may differ from the reference program's by a relative error of at most 0.02.
Values may be sent and summed in bfloat16 or wider, within the bound.
A program may use at most 256 MiB of HBM per device.

```python
import math
import jax
import jax.numpy as jnp
import numpy as np
from jax import lax

D = 768
HEADS = 12
HEAD_DIM = 64
FF = 2048
EXPERTS = 8
ALL_EXPERTS = 12
TOK_DEV = 512
NSEQ = 8
GRP = 2048
TOKENS = 16384
LONGEST = 1024
CAP = 512
SHARE = 64
N_DP = 8
N_TENSOR = 4


def draw_deal(key, part):
    device_count = TOKENS // TOK_DEV
    base_rows = jnp.arange(TOK_DEV, dtype=jnp.int32) // SHARE
    key_list = jax.random.split(key, device_count)
    shuffled = jax.vmap(lambda single: jax.random.permutation(single, base_rows))(key_list)
    return shuffled.reshape(-1).astype(jnp.int32)


def block_levels(own_key, dims, pieces, least, top_value):
    def one(dim, shards_of):
        heights = jax.random.uniform(jax.random.fold_in(jax.random.fold_in(own_key, 6), dim), (shards_of,), jnp.float32, least / len(pieces), top_value / len(pieces))
        return jnp.repeat(jnp.exp(heights), dims[dim] // shards_of).reshape((-1,) + (1,) * (len(dims) - dim - 1))

    loudness = one(*pieces[0])
    for cut in pieces[1:]:
        loudness = loudness * one(*cut)
    return loudness


def length_profile(number_of, total, reach, skew):
    weights = [(1 << 20) // math.isqrt(grade ** skew) + 1 for grade in range(2, number_of + 1)]
    spare, given = total - reach - (number_of - 1), [1] * (number_of - 1)
    while spare > 0:
        movable = [i for i in range(number_of - 1) if given[i] < reach]
        mass, remaining = sum([weights[i] for i in movable]), spare
        for i in movable:
            extra = min(reach - given[i], max(1, remaining * weights[i] // mass), spare)
            given[i] = given[i] + extra
            spare = spare - extra
    return np.array([reach] + given)


def ragged_sizes(own_key, number_of, total, limit, slope):
    if number_of == 2:
        one = jax.random.randint(own_key, (), max(1, total - limit), min(limit, total - 1) + 1)
        return jnp.stack([one, total - one])
    tallies = jnp.asarray(length_profile(number_of, total, limit, slope), jnp.int32)
    twos = (number_of - 1) // 2
    donor, receiver = tallies[1:1 + 2 * twos:2], tallies[2:2 + 2 * twos:2]
    room = jnp.minimum(donor - 1, limit - receiver)
    moved = jax.random.randint(jax.random.fold_in(own_key, 1), (twos,), 0, 1 << 20) % (room + 1)
    tallies = tallies.at[1:1 + 2 * twos:2].set(donor - moved).at[2:2 + 2 * twos:2].set(receiver + moved)
    return tallies[jax.random.permutation(jax.random.fold_in(own_key, 2), number_of)]


def shared_out(key, own, number, rows, amount, top, bound, skew):
    ranking = jax.random.permutation(key, amount)
    heavy_load, usual = load_shares(amount, rows * top, bound, skew, True), load_shares(amount, rows * top, bound, skew, False)
    places = jnp.arange(amount)

    def named(sizes, rotation):
        used = int((sizes > 0).sum())
        fixed = max(1, used // 4)
        passed = fixed + (places - fixed + rotation * (used - fixed)) % max(1, amount - fixed)
        return jnp.zeros((amount,), jnp.int32).at[ranking[jnp.where(places < fixed, places, passed)]].set(jnp.asarray(sizes, jnp.int32))

    sizes = jnp.where(number % 4 == 0, named(heavy_load, number // 4), named(usual, number - number // 4 - 1))
    mixed = jax.random.permutation(jax.random.fold_in(own, 3), amount)
    donor, receiver = mixed[0:amount // 2 * 2:2], mixed[1:amount // 2 * 2:2]
    room = jnp.minimum(sizes[donor] - 1, bound - sizes[receiver]) // 2
    room = jnp.where((donor == ranking[0]) | (receiver == ranking[0]) | (sizes[receiver] == 0), 0, jnp.maximum(room, 0))
    passed = jax.random.randint(jax.random.fold_in(own, 4), (amount // 2,), 0, 1 << 20) % (room + 1)
    sizes = sizes.at[donor].add(-passed).at[receiver].add(passed)
    members = jnp.searchsorted(jnp.cumsum(sizes), jnp.arange(rows * top), side="right").astype(jnp.int32)
    grid = members.reshape(top, rows).T
    grid = grid[jax.random.permutation(jax.random.fold_in(own, 1), rows)]
    rotation = jax.random.randint(jax.random.fold_in(own, 2), (rows, 1), 0, top)
    return jnp.take_along_axis(grid, (jnp.arange(top)[None, :] + rotation) % top, axis=1)


def load_shares(count, total, limit, slope, full):
    weights = [(1 << 20) // math.isqrt(rank ** slope) + 1 for rank in range(1, count + 1)]
    largest = limit if full else min(limit, max(-(-total // count), total * weights[0] // sum(weights)))
    least = 1 if total - largest >= count - 1 else 0
    holding, rest = [largest] + [least] * (count - 1), total - largest - least * (count - 1)
    while rest > 0:
        free = [i for i in range(1, count) if holding[i] < largest] or [i for i in range(1, count) if holding[i] < limit]
        whole, budget = sum([weights[i] for i in free]), rest
        for i in free:
            extra = min(limit - holding[i], max(1, budget * weights[i] // whole), rest)
            holding[i] = holding[i] + extra
            rest = rest - extra
    return np.array(holding)


def noise(stream_key, shape, scale, bound, pieces=(), held_as=jnp.bfloat16):
    drawn = jax.random.normal(stream_key, shape, jnp.float32) * scale
    if len(pieces) > 0:
        drawn = block_levels(stream_key, shape, pieces, -0.22, 0.18) * drawn
    return jnp.clip(drawn, min=-bound, max=bound).astype(held_as)


def setup_inputs(seed: int = 0) -> dict:
    key_of = jax.random.split(jax.random.key(seed), 16)
    tokens = noise(key_of[0], (TOKENS, D), 1.0, 6.0, ((0, 32),))
    cotangent = noise(key_of[1], (TOKENS, D), 1.0, 6.0, ((0, 32),))
    deal = draw_deal(jax.random.fold_in(key_of[15], 71), 0)
    lengths = jax.vmap(lambda own: ragged_sizes(own, NSEQ, GRP, LONGEST, 2))(jax.random.split(key_of[3], N_DP)).reshape((N_DP, NSEQ)).astype(jnp.int32)
    routes_keys = jax.random.split(jax.random.fold_in(key_of[4], 1), TOKENS // GRP)
    routes_turns = jax.random.permutation(jax.random.fold_in(key_of[4], 3), TOKENS // GRP)
    routes = jax.vmap(lambda own, number: shared_out(jax.random.fold_in(key_of[4], 2), own, number, GRP, ALL_EXPERTS, 2, CAP, 1))(routes_keys, routes_turns).reshape((TOKENS, 2))
    gate_residual = noise(key_of[5], (TOKENS, ALL_EXPERTS), 0.5, 4.0, ((0, 32),), jnp.float32)
    w_qkv = noise(key_of[6], (D, 3, D), D ** -0.5, 0.21875, ((0, 8), (2, 4)))
    w_out = noise(key_of[7], (D, D), (D // 32) ** -0.5, 1.25, ((0, 8), (1, 4)))
    w_gate_up = noise(key_of[8], (D, EXPERTS, 2, FF), D ** -0.5, 0.21875, ((0, 8), (3, 4)))
    w_down = noise(key_of[9], (D, EXPERTS, FF), (FF // 4) ** -0.5, 0.25, ((0, 8), (2, 4)))
    norm_gain_attn = jnp.clip(1.0 + 0.18 * jax.random.normal(key_of[10], (D,), jnp.float32), 0.1, 1.9)
    norm_gain_moe = jnp.clip(1.0 + 0.18 * jax.random.normal(key_of[11], (D,), jnp.float32), 0.1, 1.9)
    w_router = noise(key_of[12], (D, ALL_EXPERTS), (2 * D) ** -0.5, 0.15625, (), jnp.float32)
    w_const = noise(key_of[13], (2, D, 2), D ** -0.5, 0.21875, (), jnp.float32)
    v_const = noise(key_of[14], (2, D), 1.0, 5.0, (), jnp.float32)
    return dict(tokens=tokens, cotangent=cotangent, deal=deal, lengths=lengths, routes=routes, gate_residual=gate_residual, w_qkv=w_qkv, w_out=w_out, w_gate_up=w_gate_up, w_down=w_down, norm_gain_attn=norm_gain_attn, norm_gain_moe=norm_gain_moe, w_router=w_router, w_const=w_const, v_const=v_const)


PRECISE = lax.Precision.HIGHEST
EPSILON = 1e-06
MASKED_SCORE = -1e+30

@jax.custom_vjp
def low(v):
    return lax.optimization_barrier(v.astype(jnp.bfloat16)).astype(jnp.float32)

@jax.custom_vjp
def low_back(v):
    return v

def low_keep(v):
    return (low(v), None)

def low_pass(kept, grad):
    return (grad,)

def back_keep(v):
    return (v, None)

def back_low(kept, grad):
    return (low(grad),)
low.defvjp(low_keep, low_pass)
low_back.defvjp(back_keep, back_low)

def rms_norm(values, gain):
    return values * lax.rsqrt(lax.optimization_barrier(jnp.mean(values * values, axis=-1, keepdims=True)) + EPSILON) * gain

def rotate(values, cosine, sine):
    half_dim = values.shape[-1] // 2
    turned = jnp.concatenate([-values[..., half_dim:], values[..., :half_dim]], axis=-1)
    return values * cosine + turned * sine

def positions(seq_lengths, total_rows):
    finish = jnp.cumsum(seq_lengths.astype(jnp.int32)).astype(jnp.int32)
    row_ids = jnp.arange(total_rows, dtype=jnp.int32)
    segment = lax.optimization_barrier(jnp.sum((row_ids[:, None] >= finish[None, :]).astype(jnp.int32), axis=1)).astype(jnp.int32)
    begins = finish - seq_lengths.astype(jnp.int32)
    select = segment[:, None] == jnp.arange(seq_lengths.shape[0], dtype=jnp.int32)[None, :]
    opening = lax.optimization_barrier(jnp.sum(jnp.where(select, begins[None, :], 0), axis=1)).astype(jnp.int32)
    return (segment, row_ids - opening)

def rope_tables(place):
    half_dim = HEAD_DIM // 2
    rates = jnp.exp(jnp.arange(half_dim, dtype=jnp.float32) * (-2.0 * math.log(10000.0) / HEAD_DIM))
    angles = place.astype(jnp.float32)[:, None] * rates[None, :]
    cosine = jnp.concatenate([jnp.cos(angles), jnp.cos(angles)], axis=-1)[:, None, :]
    sine = jnp.concatenate([jnp.sin(angles), jnp.sin(angles)], axis=-1)[:, None, :]
    return (cosine, sine)

def expert_tables(route, expert_count, capacity):
    flat_ids = route.reshape(-1).astype(jnp.int32)
    entries = flat_ids.shape[0]
    hit_table = (flat_ids[:, None] == jnp.arange(expert_count, dtype=jnp.int32)[None, :]).astype(jnp.int32)
    rank_in = jnp.cumsum(hit_table, axis=0) - 1
    slot_in = lax.optimization_barrier(jnp.sum(hit_table * rank_in, axis=1))
    routed = lax.optimization_barrier(jnp.sum(hit_table, axis=1)) > 0
    entry_slot = jnp.where(routed, flat_ids * capacity + slot_in, expert_count * capacity).astype(jnp.int32)
    slot_owner = jnp.zeros((expert_count * capacity + 1,), jnp.int32).at[entry_slot].set(jnp.arange(entries, dtype=jnp.int32))[:-1]
    filled = jnp.zeros((expert_count * capacity + 1,), jnp.float32).at[entry_slot].set(1.0)[:-1]
    return (entry_slot, slot_owner, filled)

def router(normed, residual, router_weight, route):
    logits = jnp.dot(normed, router_weight, precision=PRECISE) + residual
    choose = route[:, :, None] == jnp.arange(router_weight.shape[1], dtype=jnp.int32)[None, None, :]
    picked = lax.optimization_barrier(jnp.sum(jnp.where(choose, logits[:, None, :], 0.0), axis=-1))
    return jax.nn.softmax(picked, axis=-1)

def local_experts(normed, gates, route, const_weight, const_vector):
    mixing = jax.nn.softmax(jnp.einsum('nd,cdj->ncj', normed, const_weight, precision=PRECISE), axis=-1)
    constant = mixing[:, :, 0:1] * normed[:, None, :] + mixing[:, :, 1:2] * const_vector[None, :, :]
    copy_weight = lax.optimization_barrier(jnp.sum(jnp.where(route == EXPERTS + 1, gates, 0.0), axis=1))
    const_first = lax.optimization_barrier(jnp.sum(jnp.where(route == EXPERTS + 2, gates, 0.0), axis=1))
    const_second = lax.optimization_barrier(jnp.sum(jnp.where(route == EXPERTS + 3, gates, 0.0), axis=1))
    return copy_weight[:, None] * normed + const_first[:, None] * constant[:, 0] + const_second[:, None] * constant[:, 1]

def group_forward(x_group, seq_lengths, route, residual, wqkv, wout, wgu, wdown, gain_attn, gain_moe, router_weight, const_weight, const_vector):
    normed = low(rms_norm(x_group, gain_attn))
    qkv = low_back(jnp.einsum('nd,dcm->ncm', normed, wqkv, precision=PRECISE))
    segment, place = positions(seq_lengths, GRP)
    cosine, sine = rope_tables(place)
    split = qkv.reshape(GRP, 3, HEADS, HEAD_DIM)
    query = low(rotate(split[:, 0], cosine, sine))
    keys = low(rotate(split[:, 1], cosine, sine))
    values = low(split[:, 2])
    block = min(512, GRP)
    row_ids = jnp.arange(GRP, dtype=jnp.int32)
    scale = HEAD_DIM ** (-0.5)

    def attend(start):
        query_rows = lax.dynamic_slice_in_dim(query, start, block, 0)
        seg_rows = lax.dynamic_slice_in_dim(segment, start, block, 0)
        row_here = start + jnp.arange(block, dtype=jnp.int32)
        score = low_back(jnp.einsum('qhd,khd->hqk', query_rows, keys, precision=PRECISE) * scale)
        allowed = (seg_rows[:, None] == segment[None, :]) & (row_ids[None, :] <= row_here[:, None])
        score = jnp.where(allowed[None], score, MASKED_SCORE)
        weight = low(jax.nn.softmax(score, axis=-1))
        return jnp.einsum('hqk,khd->qhd', weight, values, precision=PRECISE)
    starts = jnp.arange(GRP // block, dtype=jnp.int32) * block
    mixed = lax.map(jax.checkpoint(attend), starts)
    mixed = low_back(low(mixed.reshape(GRP, D)))
    attended = low_back(jnp.einsum('nm,dm->nd', mixed, wout, precision=PRECISE))
    x_mid = x_group + attended
    normed_moe = low(rms_norm(x_mid, gain_moe))
    gates = low(router(normed_moe, residual, router_weight, route))
    entry_slot, slot_owner, filled = expert_tables(route, EXPERTS, CAP)
    inputs = normed_moe[slot_owner // 2].reshape(EXPERTS, CAP, D)
    projected = low_back(jnp.einsum('ecd,dejf->ecjf', inputs, wgu, precision=PRECISE))
    activated = low(jax.nn.silu(projected[:, :, 0]) * projected[:, :, 1])
    produced = low_back(jnp.einsum('ecf,def->ecd', activated, wdown, precision=PRECISE))
    table = jnp.concatenate([produced.reshape(EXPERTS * CAP, D), jnp.zeros((1, D), jnp.float32)], axis=0)
    routed = lax.optimization_barrier(jnp.sum((table[entry_slot] * gates.reshape(-1, 1)).reshape(GRP, 2, D), axis=1))
    local = local_experts(normed_moe, gates, route, const_weight, const_vector)
    return x_mid + routed + local

def balanced_index(deal):
    device_count = TOKENS // TOK_DEV
    deal_rows = deal.reshape(device_count, TOK_DEV).astype(jnp.int32)
    local_ids = jnp.arange(TOK_DEV, dtype=jnp.int32)
    order = jnp.argsort(deal_rows * TOK_DEV + local_ids[None, :], axis=1).astype(jnp.int32)
    target = jnp.take_along_axis(deal_rows, order, axis=1)
    device_ids = jnp.arange(device_count, dtype=jnp.int32)[:, None]
    source_dp = device_ids // N_TENSOR
    tensor_pos = device_ids % N_TENSOR
    slot_here = source_dp * SHARE + local_ids[None, :] - target * SHARE
    placed = ((target * N_TENSOR + tensor_pos) * TOK_DEV + slot_here).reshape(-1).astype(jnp.int32)
    source = (device_ids * TOK_DEV + order).reshape(-1).astype(jnp.int32)
    return jnp.zeros((TOKENS,), jnp.int32).at[placed].set(source)

def reference(tokens, cotangent, deal, lengths, routes, gate_residual, w_qkv, w_out, w_gate_up, w_down, norm_gain_attn, norm_gain_moe, w_router, w_const, v_const):
    gather_index = balanced_index(deal)
    order_back = jnp.zeros((TOKENS,), jnp.int32).at[gather_index].set(jnp.arange(TOKENS, dtype=jnp.int32))
    x_bal = tokens.astype(jnp.float32)[gather_index]
    g_bal = cotangent.astype(jnp.float32)[gather_index]
    route_groups = routes.reshape(N_DP, GRP, 2).astype(jnp.int32)

    def forward(x_all, residual_all, wqkv, wout, wgu, wdown, gain_attn, gain_moe, router_weight, const_weight, const_vector):

        def one_group(item):
            x_group, seq_lengths, route, residual = item
            return group_forward(x_group, seq_lengths, route, residual, wqkv, wout, wgu, wdown, gain_attn, gain_moe, router_weight, const_weight, const_vector)
        result = lax.map(jax.checkpoint(one_group), (x_all.reshape(N_DP, GRP, D), lengths, route_groups, residual_all.reshape(N_DP, GRP, ALL_EXPERTS)))
        return result.reshape(TOKENS, D)
    result, pullback = jax.vjp(forward, x_bal, gate_residual, w_qkv.astype(jnp.float32), w_out.astype(jnp.float32), w_gate_up.astype(jnp.float32), w_down.astype(jnp.float32), norm_gain_attn, norm_gain_moe, w_router, w_const, v_const)
    grads = pullback(g_bal)
    output = result.astype(jnp.bfloat16)[order_back]
    grad_tokens = grads[0].astype(jnp.bfloat16)[order_back]
    return (output, grad_tokens, grads[1], grads[2], grads[3], grads[4], grads[5], grads[6], grads[7], grads[8], grads[9], grads[10])
```

```python
import functools
import math

import jax
import jax.numpy as jnp
from jax import lax
from jax.experimental import pallas as pl
from jax.experimental.pallas import tpu as pltpu
from jax.sharding import PartitionSpec as P

D = 768
HEAD_DIM = 64
HEADS = 12
EXPERTS = 8
LONGEST = 1024
EPSILON = 1e-6
MASKED = -1e30
F32, BF16, I32 = jnp.float32, jnp.bfloat16, jnp.int32
NN = (((1,), (0,)), ((), ()))
NT = (((1,), (1,)), ((), ()))
TN = (((0,), (0,)), ((), ()))
SCORE_SCALE = HEAD_DIM**-0.5
LOG2E = 1.4426950408889634
TILE = 160
ROWS = 256
SPARE = 16
VMEM_CAP = 66_000_000


def mm(a, b, dims):
    return lax.dot_general(a, b, dims, preferred_element_type=F32)


def iota(shape, axis):
    return lax.broadcasted_iota(I32, shape, axis)


def pick(cond):
    return jnp.where(cond, 1.0, 0.0).astype(BF16)


def split2(v):
    high = v.astype(BF16)
    return high, (v - high.astype(F32)).astype(BF16)


def split3(v):
    high = v.astype(BF16)
    rest = v - high.astype(F32)
    mid = rest.astype(BF16)
    return high, mid, (rest - mid.astype(F32)).astype(BF16)


def vmem():
    return pl.BlockSpec(memory_space=pltpu.VMEM)


def smem():
    return pl.BlockSpec(memory_space=pltpu.SMEM)


def call(body, name, outs, operands, scalars=0, scratch=()):
    return pl.pallas_call(
        body,
        name=name,
        out_shape=[jax.ShapeDtypeStruct(*o) for o in outs],
        in_specs=[smem()] * scalars + [vmem()] * (len(operands) - scalars),
        out_specs=[vmem()] * len(outs),
        scratch_shapes=list(scratch),
        compiler_params=pltpu.CompilerParams(vmem_limit_bytes=VMEM_CAP),
    )(*operands)


def deal_body(n_dp, t_ref, deal_ref, tok_ref, cot_ref, routes_ref, xs_ref, gs_ref, pos_ref, slot_ref, cnt_ref):
    rows = tok_ref.shape[0]
    first, second = iota((rows, rows), 0), iota((rows, rows), 1)
    before = pick(first < second)
    deal = deal_ref[...]
    hit = iota((n_dp, rows), 0) == deal
    rank = mm(pick(hit), before, NN)
    rank = jnp.sum(jnp.where(hit, rank, 0.0), axis=0, keepdims=True).astype(I32)
    pos = deal * (rows // n_dp) + rank
    pos_ref[...] = pos
    place = pick(first == pos)
    xs_ref[...] = mm(place, tok_ref[...], NN).astype(BF16)
    gs_ref[...] = mm(place, cot_ref[...], NN).astype(BF16)
    expert = iota((EXPERTS, rows), 0)
    for j in range(routes_ref.shape[0]):
        route = routes_ref[t_ref[0] ^ j]
        named = (expert == route[0:1]) | (expert == route[1:2])
        ahead = mm(pick(named), before, NN).astype(I32)
        slot_ref[j] = jnp.where(named, ahead, -1)
        total = jnp.sum(jnp.where(named, 1.0, 0.0), axis=1, keepdims=True).astype(I32)
        cnt_ref[j] = jnp.broadcast_to(total, (EXPERTS, 128))


def restore_body(pos_ref, a_ref, b_ref, oa_ref, ob_ref):
    rows = a_ref.shape[0]
    place = pick(iota((rows, rows), 0) == pos_ref[...])
    oa_ref[...] = mm(place, a_ref[...], TN).astype(BF16)
    ob_ref[...] = mm(place, b_ref[...], TN).astype(BF16)


def turn(u):
    low = (iota((1, u.shape[1]), 1) % HEAD_DIM) < HEAD_DIM // 2
    half = HEAD_DIM // 2
    return jnp.where(low, pltpu.roll(u, u.shape[1] - half, 1), pltpu.roll(u, half, 1))


def wide(table):
    return jnp.concatenate([table] * (D // 128), axis=1)


def key_bias(start, block, first_row, base):
    window = LONGEST + block
    key = iota((window, block), 0) + first_row
    row = iota((1, block), 1) + (base + first_row)
    return jnp.where((key >= start) & (key <= row), 0.0, MASKED)


def attention_body(x0_ref, x1_ref, x2_ref, w_ref, gain_ref, cos_ref, sin_ref, start_ref,
                   h_ref, q_ref, k_ref, v_ref, o_ref, lse_ref, bias_ref):
    rows = x0_ref.shape[0]
    step = 256
    gain = gain_ref[...]
    for c, x_ref in enumerate((x2_ref, x1_ref, x0_ref)):
        def project(i, _, c=c, x_ref=x_ref):
            at = pl.multiple_of(i * step, step)
            x = x_ref[pl.ds(at, step), :].astype(F32)
            h = x * lax.rsqrt(jnp.mean(x * x, axis=1, keepdims=True) + EPSILON) * gain
            h = h.astype(BF16)
            to = pl.ds(pl.multiple_of(c * rows + i * step, step), step)
            h_ref[to, :] = h
            cos, sin = wide(cos_ref[to, :]), wide(sin_ref[to, :])
            k = mm(h, w_ref[:, D : 2 * D], NN)
            k_ref[to, :] = (k * cos + turn(k) * sin).astype(BF16)
            v_ref[to, :] = mm(h, w_ref[:, 2 * D : 3 * D], NN).astype(BF16)
            if c == 2:
                q = mm(h, w_ref[:, 0:D], NN)
                q_ref[pl.ds(at, step), :] = (q * cos + turn(q) * sin).astype(BF16)
            return 0

        lax.fori_loop(0, rows // step, project, 0)

    block = step
    window = LONGEST + block
    lane = iota((1, 128), 1) // HEAD_DIM
    for rb in range(rows // block):
        first = rb * block
        bias_ref[...] = key_bias(start_ref[:, first : first + block], block, first, LONGEST)

        def pair(i, _, first=first):
            lanes = pl.ds(pl.multiple_of(i * 128, 128), 128)
            k = k_ref[first : first + window, lanes]
            vt = v_ref[first : first + window, lanes].T
            q = q_ref[first : first + block, lanes]
            parts = []
            for half in range(2):
                qm = jnp.where(lane == half, q, jnp.zeros_like(q))
                s = mm(k, qm, NT) * (SCORE_SCALE * LOG2E) + bias_ref[...]
                top = jnp.max(s, axis=0, keepdims=True)
                p = jnp.exp2(s - top)
                total = jnp.sum(p, axis=0, keepdims=True)
                out = mm(vt[half * HEAD_DIM : (half + 1) * HEAD_DIM], p.astype(BF16), NN)
                parts.append(out * (1.0 / total))
                lse_ref[pl.ds(i * 2 + half, 1), first : first + block] = top + jnp.log2(total)
            o_ref[first : first + block, lanes] = jnp.concatenate(parts, axis=0).T.astype(BF16)
            return 0

        lax.fori_loop(0, HEADS // 2, pair, 0)


def attention_back_body(q_ref, k_ref, v_ref, do_ref, lse_ref, delta_ref, start_ref, cos_ref, sin_ref, w_ref,
                        dq_ref, dk_ref, dv_ref, d0_ref, d1_ref, d2_ref, bias_ref, dkf_ref, dvf_ref, dqf_ref):
    rows = q_ref.shape[0]
    block = 256
    window = LONGEST + block
    lane = iota((1, 128), 1) // HEAD_DIM
    for rb in range(rows // block):
        first = rb * block
        bias_ref[...] = key_bias(start_ref[:, first : first + block], block, first, LONGEST)

        def pair(i, _, first=first):
            lanes = pl.ds(pl.multiple_of(i * 128, 128), 128)
            k = k_ref[first : first + window, lanes]
            v = v_ref[first : first + window, lanes]
            kt = k.T
            q = q_ref[first : first + block, lanes]
            do = do_ref[first : first + block, lanes]
            dk = jnp.zeros((window, 128), F32)
            dv = jnp.zeros((window, 128), F32)
            parts = []
            for half in range(2):
                qm = jnp.where(lane == half, q, jnp.zeros_like(q))
                dom = jnp.where(lane == half, do, jnp.zeros_like(do))
                head = pl.ds(i * 2 + half, 1)
                s = mm(k, qm, NT) * (SCORE_SCALE * LOG2E) + bias_ref[...]
                p = jnp.exp2(s - lse_ref[head, first : first + block])
                dp = mm(v, dom, NT)
                ds = (p * (dp - delta_ref[head, first : first + block])).astype(BF16)
                dv = dv + mm(p.astype(BF16), dom, NN)
                dk = dk + mm(ds, qm, NN)
                parts.append(mm(kt[half * HEAD_DIM : (half + 1) * HEAD_DIM], ds, NN))
            dqf_ref[first : first + block, lanes] = jnp.concatenate(parts, axis=0).T
            if first == 0:
                dkf_ref[0:window, lanes] = dk
                dvf_ref[0:window, lanes] = dv
            else:
                old = window - block
                dkf_ref[first : first + old, lanes] += dk[0:old]
                dvf_ref[first : first + old, lanes] += dv[0:old]
                dkf_ref[first + old : first + window, lanes] = dk[old:]
                dvf_ref[first + old : first + window, lanes] = dv[old:]
            return 0

        lax.fori_loop(0, HEADS // 2, pair, 0)

    for c, out_ref in enumerate((d2_ref, d1_ref, d0_ref)):
        def finish(i, _, c=c, out_ref=out_ref):
            at = pl.ds(pl.multiple_of(i * block, block), block)
            to = pl.ds(pl.multiple_of(c * rows + i * block, block), block)
            cos, sin = wide(cos_ref[to, :]), wide(sin_ref[to, :])
            dk = dkf_ref[to, :] * SCORE_SCALE
            dk = (dk * cos - turn(dk) * sin).astype(BF16)
            dv = dvf_ref[to, :].astype(BF16)
            dk_ref[to, :] = dk
            dv_ref[to, :] = dv
            total = mm(dk, w_ref[:, D : 2 * D], NT) + mm(dv, w_ref[:, 2 * D : 3 * D], NT)
            if c == 2:
                dq = dqf_ref[at, :] * SCORE_SCALE
                dq = (dq * cos - turn(dq) * sin).astype(BF16)
                dq_ref[at, :] = dq
                total = total + mm(dq, w_ref[:, 0:D], NT)
            out_ref[at, :] = total.astype(out_ref.dtype)
            return 0

        lax.fori_loop(0, rows // block, finish, 0)


def attention_grads_body(x0_ref, x1_ref, x2_ref, h_ref, dq_ref, dk_ref, dv_ref, da_ref, o_ref, d0_ref, d1_ref, d2_ref,
                         gw_ref, gain_ref):
    rows = x0_ref.shape[0]
    h = h_ref[...]
    for c in range(D // 256):
        cols = slice(c * 256, (c + 1) * 256)
        gw_ref[:, c * 256 : c * 256 + 256] = mm(h[2 * rows :], dq_ref[:, cols], TN).astype(BF16)
        gw_ref[:, D + c * 256 : D + c * 256 + 256] = mm(h, dk_ref[:, cols], TN).astype(BF16)
        gw_ref[:, 2 * D + c * 256 : 2 * D + c * 256 + 256] = mm(h, dv_ref[:, cols], TN).astype(BF16)
        gw_ref[:, 3 * D + c * 256 : 3 * D + c * 256 + 256] = mm(da_ref[...], o_ref[:, cols], TN).astype(BF16)
    total = jnp.zeros((1, D), F32)
    for x_ref, d_ref in ((x0_ref, d0_ref), (x1_ref, d1_ref), (x2_ref, d2_ref)):
        x = x_ref[...].astype(F32)
        r = lax.rsqrt(jnp.mean(x * x, axis=1, keepdims=True) + EPSILON)
        total = total + jnp.sum(d_ref[...].astype(F32) * x * r, axis=0, keepdims=True)
    gain_ref[...] = jnp.broadcast_to(total, (8, D))


def router_body(t_ref, o_ref, w_ref, x_ref, gain_ref, res_ref, wrc_ref, routes_ref, x1_ref, hp_ref, gt_ref):
    rows = o_ref.shape[0]
    x1 = x_ref[...].astype(F32) + mm(o_ref[...], w_ref[:, 3 * D : 4 * D], NT)
    x1_ref[...] = x1
    h = x1 * lax.rsqrt(jnp.mean(x1 * x1, axis=1, keepdims=True) + EPSILON) * gain_ref[...]
    h = h.astype(BF16)
    hp_ref[0:rows, :] = h
    high, mid, low = split3(wrc_ref[...])
    z = mm(low, h, NT) + mm(mid, h, NT) + mm(high, h, NT) + res_ref[...]
    route = routes_ref[t_ref[0]]
    expert = iota(z.shape, 0)
    named0, named1 = expert == route[0:1], expert == route[1:2]
    c0 = jnp.sum(jnp.where(named0, z, 0.0), axis=0, keepdims=True)
    c1 = jnp.sum(jnp.where(named1, z, 0.0), axis=0, keepdims=True)
    top = jnp.maximum(c0, c1)
    e0, e1 = jnp.exp(c0 - top), jnp.exp(c1 - top)
    g0, g1 = e0 / (e0 + e1), e1 / (e0 + e1)
    table = [g0, g1]
    for j in range(2):
        l0, l1 = z[12 + 2 * j : 13 + 2 * j], z[13 + 2 * j : 14 + 2 * j]
        top = jnp.maximum(l0, l1)
        m0, m1 = jnp.exp(l0 - top), jnp.exp(l1 - top)
        table += [m0 / (m0 + m1), m1 / (m0 + m1)]
    gt_ref[...] = jnp.concatenate(table + [jnp.zeros((2, rows), F32)], axis=0)
    gates = jnp.where(named0, g0, jnp.where(named1, g1, 0.0))
    gates = jnp.where(expert < EXPERTS, gates, 0.0)
    hp_ref[rows : rows + SPARE, :] = jnp.concatenate([gates, jnp.zeros((SPARE, D - rows), F32)], axis=1).astype(BF16)


def local_body(t_ref, x1_ref, hp_ref, g_ref, gt_ref, routes_ref, v_ref, xl_ref, dhl_ref, sm_ref, gv_ref):
    rows = x1_ref.shape[0]
    h, g = hp_ref[0:rows, :], g_ref[...]
    hf, gf = h.astype(F32), g.astype(F32)
    route = routes_ref[t_ref[0]]
    low0 = gt_ref[0:1].astype(BF16).astype(F32)
    low1 = gt_ref[1:2].astype(BF16).astype(F32)

    def weight(e):
        return jnp.where(route[0:1] == e, low0, 0.0) + jnp.where(route[1:2] == e, low1, 0.0)

    copy, first, second = weight(EXPERTS + 1), weight(EXPERTS + 2), weight(EXPERTS + 3)
    m00, m01, m10, m11 = gt_ref[2:3], gt_ref[3:4], gt_ref[4:5], gt_ref[5:6]
    a = copy + first * m00 + second * m10
    b0, b1 = first * m01, second * m11
    table = jnp.concatenate([a, b0, b1, jnp.zeros((125, rows), F32)], axis=0).T
    ac, b0c, b1c = table[:, 0:1], table[:, 1:2], table[:, 2:3]
    v = v_ref[...]
    xl_ref[...] = x1_ref[...] + ac * hf + b0c * v[0:1] + b1c * v[1:2]
    dhl_ref[...] = ac * gf
    ones = jnp.ones((8, D), BF16)
    high, low = split2(hf * gf)
    gh = (mm(ones, high, NT) + mm(ones, low, NT))[0:1]
    vh, vm, vl = split3(v)
    gvs = mm(vl, g, NT) + mm(vm, g, NT) + mm(vh, g, NT)
    gv0, gv1 = gvs[0:1], gvs[1:2]
    zero = jnp.zeros((9, rows), F32)
    dl0 = first * m00 * m01 * (gh - gv0)
    dl1 = second * m10 * m11 * (gh - gv1)
    sm_ref[...] = jnp.concatenate(
        [zero, gh, m00 * gh + m01 * gv0, m10 * gh + m11 * gv1, dl0, -dl0, dl1, -dl1], axis=0
    )
    bh, bm, bl = split3(jnp.concatenate([b0, b1, jnp.zeros((6, rows), F32)], axis=0))
    gv_ref[...] = mm(bl, g, NN) + mm(bm, g, NN) + mm(bh, g, NN)


def middle_back_body(t_ref, c0_ref, c1_ref, c2_ref, c3_ref, dhl_ref, gt_ref, sm_ref, routes_ref, wrc_ref, x1_ref, gain_ref, g_ref,
                     hp_ref, w_ref, o_ref, gv_ref, dx_ref, da_ref, do_ref, delta_ref, dres_ref, small_ref):
    rows = x1_ref.shape[0]
    chunks = (c0_ref, c1_ref, c2_ref, c3_ref)
    dgf = jnp.zeros((SPARE, rows), F32)
    dh = dhl_ref[...]
    for c in chunks:
        dgf = dgf + c[rows : rows + SPARE, 0:rows].astype(F32)
        dh = dh + c[0:rows, :].astype(F32)
    dgate = jnp.concatenate([dgf[0:EXPERTS] + dgf[EXPERTS:], sm_ref[EXPERTS:SPARE]], axis=0)
    route = routes_ref[t_ref[0]]
    expert = iota((SPARE, rows), 0)
    named0, named1 = expert == route[0:1], expert == route[1:2]
    g0, g1 = gt_ref[0:1], gt_ref[1:2]
    d0 = jnp.sum(jnp.where(named0, dgate, 0.0), axis=0, keepdims=True)
    d1 = jnp.sum(jnp.where(named1, dgate, 0.0), axis=0, keepdims=True)
    inner = g0 * d0 + g1 * d1
    dz = jnp.where(named0, g0 * (d0 - inner), jnp.where(named1, g1 * (d1 - inner), 0.0))
    dres_ref[...] = dz
    dz = jnp.where(expert < 12, dz, sm_ref[...])
    zh, zm, zl = split3(dz)
    wh, wm, wl = split3(wrc_ref[...])
    dh = dh + (mm(zh, wl, TN) + mm(zl, wh, TN) + mm(zm, wm, TN) + mm(zh, wm, TN) + mm(zm, wh, TN) + mm(zh, wh, TN))
    h = hp_ref[0:rows, :]
    small_ref[0:SPARE, :] = mm(zl, h, NN) + mm(zm, h, NN) + mm(zh, h, NN)
    x1 = x1_ref[...]
    r = lax.rsqrt(jnp.mean(x1 * x1, axis=1, keepdims=True) + EPSILON)
    xr = x1 * r
    grad_gain = jnp.sum(dh * xr, axis=0, keepdims=True)
    gv = gv_ref[...]
    small_ref[SPARE : SPARE + 8, :] = jnp.concatenate([gv[0:2], grad_gain, gv[3:8]], axis=0)
    scaled = dh * gain_ref[...]
    dx = g_ref[...].astype(F32) + r * (scaled - xr * jnp.mean(xr * scaled, axis=1, keepdims=True))
    dx_ref[...] = dx
    da = dx.astype(BF16)
    da_ref[...] = da
    do = mm(da, w_ref[:, 3 * D : 4 * D], NN).astype(BF16)
    do_ref[...] = do
    high, low = split2(do.astype(F32) * o_ref[...].astype(F32))
    heads = pick(iota((SPARE, D), 1) // HEAD_DIM == iota((SPARE, D), 0))
    delta_ref[...] = mm(heads, high, NT) + mm(heads, low, NT)


def final_back_body(x_ref, d0_ref, r1_ref, r2_ref, dx_ref, gain_ref, out_ref):
    x = x_ref[...].astype(F32)
    dh = d0_ref[...] + r1_ref[...].astype(F32) + r2_ref[...].astype(F32)
    r = lax.rsqrt(jnp.mean(x * x, axis=1, keepdims=True) + EPSILON)
    xr = x * r
    scaled = dh * gain_ref[...]
    out_ref[...] = (dx_ref[...] + r * (scaled - xr * jnp.mean(xr * scaled, axis=1, keepdims=True))).astype(BF16)


def experts_body(ff, chunks, cnt_ref, *refs):
    h_refs, g_refs = refs[:chunks], refs[chunks : 2 * chunks]
    slot_ref, w_ref = refs[2 * chunks : 2 * chunks + 2]
    o_refs, d_refs = refs[2 * chunks + 2 : 3 * chunks + 2], refs[3 * chunks + 2 : 4 * chunks + 2]
    gw_ref, xbuf, gbuf, cbuf, onehot, fbuf, dbuf, gacc, gates, dgrow, off_ref, base_ref, nt_ref = refs[4 * chunks + 2 :]
    rows = slot_ref.shape[2]
    e = pl.program_id(0)

    def match(j, expert, tile):
        slots = slot_ref[j, pl.ds(expert, 1), :]
        return (iota((TILE, rows), 0) + tile * TILE) == slots

    def store_rows(at, count, hit, x, gs, gate_row):
        to = pl.ds(pl.multiple_of(at, 16), TILE)
        keep = iota((TILE, 1), 0) < count
        col = jnp.sum(jnp.where(hit, gate_row, 0.0), axis=1, keepdims=True)
        xbuf[to, :] = jnp.where(keep, x, xbuf[to, :].astype(F32)).astype(BF16)
        gbuf[to, :] = jnp.where(keep, gs, gbuf[to, :].astype(F32)).astype(BF16)
        cbuf[to, :] = jnp.where(keep, jnp.broadcast_to(col, (TILE, 128)), cbuf[to, :])

    def round16(n):
        return ((n + 15) // 16) * 16

    @pl.when(e == 0)
    def _gather():
        at = jnp.int32(0)
        for ex in range(EXPERTS):
            base_ref[ex] = at
            here = at
            for j in range(chunks):
                off_ref[j * EXPERTS + ex] = here
                here = here + round16(cnt_ref[j * EXPERTS + ex])
            tiles = (here - at + (ROWS - 1)) // ROWS
            nt_ref[ex] = tiles
            tail = pl.ds(pl.multiple_of(here, 16), ROWS)
            xbuf[tail, :] = jnp.zeros((ROWS, D), BF16)
            gbuf[tail, :] = jnp.zeros((ROWS, D), BF16)
            cbuf[tail, :] = jnp.zeros((ROWS, 128), F32)
            at = at + tiles * ROWS
        for j in range(chunks):
            gates[...] = h_refs[j][rows : rows + SPARE, 0:rows].astype(F32)

            def two(i, _, j=j):
                hits = [match(j, 2 * i + half, 0) for half in range(2)]
                sel = jnp.concatenate([pick(hit) for hit in hits], axis=0)
                x = mm(sel, h_refs[j][0:rows, :], NN)
                gs = mm(sel, g_refs[j][...], NN)
                for half in range(2):
                    ex = 2 * i + half
                    count = round16(jnp.minimum(cnt_ref[j * EXPERTS + ex], TILE))
                    part = slice(half * TILE, (half + 1) * TILE)
                    store_rows(off_ref[j * EXPERTS + ex], count, hits[half], x[part], gs[part], gates[pl.ds(ex, 1), :])
                return 0

            lax.fori_loop(0, EXPERTS // 2, two, 0)

            def rare(ex, _, j=j):
                def more(tile, _):
                    hit = match(j, ex, tile)
                    sel = pick(hit)
                    count = round16(jnp.minimum(cnt_ref[j * EXPERTS + ex] - tile * TILE, TILE))
                    store_rows(
                        off_ref[j * EXPERTS + ex] + tile * TILE,
                        count,
                        hit,
                        mm(sel, h_refs[j][0:rows, :], NN),
                        mm(sel, g_refs[j][...], NN),
                        gates[pl.ds(ex, 1), :],
                    )
                    return 0

                return lax.fori_loop(1, (cnt_ref[j * EXPERTS + ex] + (TILE - 1)) // TILE, more, 0)

            lax.fori_loop(0, EXPERTS, rare, 0)

    gacc[...] = jnp.zeros_like(gacc)

    def tile_step(m, _):
        at = pl.ds(pl.multiple_of(base_ref[e] + m * ROWS, 16), ROWS)
        x = xbuf[at, :]
        gs = gbuf[at, :].astype(F32)
        gate = wide(cbuf[at, :])
        u = mm(x, w_ref[:, 0:ff], NN)
        up = mm(x, w_ref[:, ff : 2 * ff], NN)
        sig = jax.nn.sigmoid(u)
        silu = u * sig
        act = (silu * up).astype(BF16)
        f = mm(act, w_ref[:, 2 * ff : 3 * ff], NT)
        cbuf[at, :] = jnp.broadcast_to(jnp.sum(gs * f, axis=1, keepdims=True), (ROWS, 128))
        gbuf[at, :] = (f * gate).astype(BF16)
        df = (gs * gate).astype(BF16)
        dact = mm(df, w_ref[:, 2 * ff : 3 * ff], NN)
        dup = (dact * silu).astype(BF16)
        du = (dact * up * sig * (1.0 + u * (1.0 - sig))).astype(BF16)
        xbuf[at, :] = (mm(du, w_ref[:, 0:ff], NT) + mm(dup, w_ref[:, ff : 2 * ff], NT)).astype(BF16)
        gacc[:, 0:ff] += mm(x, du, TN)
        gacc[:, ff : 2 * ff] += mm(x, dup, TN)
        gacc[:, 2 * ff : 3 * ff] += mm(df, act, TN)
        return 0

    lax.fori_loop(0, nt_ref[e], tile_step, 0)
    gw_ref[...] = gacc[...].astype(BF16)

    @pl.when(e == EXPERTS - 1)
    def _scatter():
        for j in range(chunks):
            def take(ex, _, j=j):
                at = pl.ds(pl.multiple_of(off_ref[j * EXPERTS + ex], 16), TILE)
                to = pl.ds(pl.multiple_of(ex * TILE, 16), TILE)
                hit = match(j, ex, 0)
                onehot[to, :] = pick(hit)
                fbuf[to, :] = gbuf[at, :]
                dbuf[to, :] = xbuf[at, :]
                col = jnp.concatenate([cbuf[at, :]] * (rows // 128), axis=1)
                dgrow[pl.ds(ex, 1), :] = jnp.sum(jnp.where(hit, col, 0.0), axis=0, keepdims=True)
                return 0

            lax.fori_loop(0, EXPERTS, take, 0)
            gacc[0:rows, 0:D] = mm(onehot[...], fbuf[...], TN)
            gacc[0:rows, D : 2 * D] = mm(onehot[...], dbuf[...], TN)

            def rare(ex, _, j=j):
                def more(tile, _):
                    at = pl.ds(pl.multiple_of(off_ref[j * EXPERTS + ex] + tile * TILE, 16), TILE)
                    hit = match(j, ex, tile)
                    sel = pick(hit)
                    gacc[0:rows, 0:D] += mm(sel, gbuf[at, :], TN)
                    gacc[0:rows, D : 2 * D] += mm(sel, xbuf[at, :], TN)
                    col = jnp.concatenate([cbuf[at, :]] * (rows // 128), axis=1)
                    dgrow[pl.ds(ex, 1), :] += jnp.sum(jnp.where(hit, col, 0.0), axis=0, keepdims=True)
                    return 0

                return lax.fori_loop(1, (cnt_ref[j * EXPERTS + ex] + (TILE - 1)) // TILE, more, 0)

            lax.fori_loop(0, EXPERTS, rare, 0)
            o_refs[j][...] = gacc[0:rows, 0:D].astype(BF16)
            d_refs[j][0:rows, :] = gacc[0:rows, D : 2 * D].astype(BF16)
            total = dgrow[...]
            high = total.astype(BF16).astype(F32)
            both = jnp.concatenate([high, total - high], axis=0)
            d_refs[j][rows : rows + SPARE, :] = jnp.concatenate(
                [both, jnp.zeros((SPARE, D - rows), F32)], axis=1
            ).astype(BF16)


def experts_call(counts, hs, gs, slots, weights, ff):
    chunks, rows = len(hs), slots.shape[2]
    width = 3 * ff
    most = (rows + 15 * chunks + ROWS - 1) // ROWS * ROWS * EXPERTS + ROWS
    whole = lambda shape: pl.BlockSpec(shape, lambda e: (0,) * len(shape), pipeline_mode=pl.Buffered(1))
    packed = (rows + SPARE, D)
    return pl.pallas_call(
        functools.partial(experts_body, ff, chunks),
        name="experts",
        grid=(EXPERTS,),
        in_specs=[smem()]
        + [whole(packed)] * chunks
        + [whole((rows, D))] * chunks
        + [whole(slots.shape), pl.BlockSpec((D, width), lambda e: (0, e))],
        out_specs=[whole((rows, D))] * chunks + [whole(packed)] * chunks + [pl.BlockSpec((D, width), lambda e: (0, e))],
        out_shape=[jax.ShapeDtypeStruct((rows, D), BF16)] * chunks
        + [jax.ShapeDtypeStruct(packed, BF16)] * chunks
        + [jax.ShapeDtypeStruct((D, EXPERTS * width), BF16)],
        scratch_shapes=[
            pltpu.VMEM((most, D), BF16),
            pltpu.VMEM((most, D), BF16),
            pltpu.VMEM((most, 128), F32),
            pltpu.VMEM((EXPERTS * TILE, rows), BF16),
            pltpu.VMEM((EXPERTS * TILE, D), BF16),
            pltpu.VMEM((EXPERTS * TILE, D), BF16),
            pltpu.VMEM((D, width), F32),
            pltpu.VMEM((SPARE, rows), F32),
            pltpu.VMEM((EXPERTS, rows), F32),
            pltpu.SMEM((chunks * EXPERTS,), I32),
            pltpu.SMEM((EXPERTS,), I32),
            pltpu.SMEM((EXPERTS,), I32),
        ],
        compiler_params=pltpu.CompilerParams(
            dimension_semantics=("arbitrary",), vmem_limit_bytes=VMEM_CAP
        ),
    )(counts, *hs, *gs, slots, weights)


def rope_tables(lengths, first, count):
    finish = jnp.sum(jnp.where(jnp.arange(lengths.shape[0])[:, None] <= jnp.arange(lengths.shape[0])[None, :], lengths[:, None], 0), axis=0)
    begins = finish - lengths
    rows = first + jnp.arange(count, dtype=I32)
    opening = jnp.max(jnp.where(begins[None, :] <= rows[:, None], begins[None, :], 0), axis=1)
    place = rows - opening
    half = HEAD_DIM // 2
    rates = jnp.exp(jnp.arange(half, dtype=F32) * (-2.0 * math.log(10000.0) / HEAD_DIM))
    angles = place.astype(F32)[:, None] * rates[None, :]
    cos, sin = jnp.cos(angles), jnp.sin(angles)
    return place, jnp.concatenate([cos] * 4, axis=1), jnp.concatenate([-sin, sin] * 2, axis=1)


def body(tokens, cotangent, deal, lengths, routes, gate_residual, w_qkv, w_out, w_gate_up, w_down,
         norm_gain_attn, norm_gain_moe, w_router, w_const, v_const):
    rows = tokens.shape[0]
    n_dp, n_t = lax.axis_size("dp"), lax.axis_size("tensor")
    t = lax.axis_index("tensor")
    t_arr = jnp.reshape(t, (1,)).astype(I32)
    ff = w_down.shape[2]
    d_here = w_qkv.shape[0]

    def swap(v, j):
        return lax.ppermute(v, "tensor", [(i, i ^ j) for i in range(n_t)])

    def shift(v, by):
        return lax.ppermute(v, "tensor", [(i, i + by) for i in range(n_t) if 0 <= i + by < n_t])

    attn_shard = jnp.concatenate([w_qkv, w_out[:, None, :]], axis=1)
    attn_shard = lax.all_gather(attn_shard, "tensor", axis=2, tiled=True).reshape(d_here, 4 * D)
    w_attn = lax.all_gather(attn_shard, "dp", axis=0, tiled=True)
    ff_shard = jnp.concatenate([w_gate_up.reshape(d_here, EXPERTS, 2 * ff), w_down], axis=2)
    w_ff = lax.all_gather(ff_shard.reshape(d_here, EXPERTS * 3 * ff), "dp", axis=0, tiled=True)

    routes_t = routes.reshape(n_t, rows, 2).transpose(0, 2, 1)
    xs, gs, pos, slots, counts = call(
        functools.partial(deal_body, n_dp),
        "deal",
        [((rows, D), BF16), ((rows, D), BF16), ((1, rows), I32), ((n_t, EXPERTS, rows), I32), ((n_t, EXPERTS, 128), I32)],
        [t_arr, deal.reshape(1, rows), tokens, cotangent, routes_t],
        1,
    )
    counts = counts[:, :, 0].reshape(n_t * EXPERTS)
    x0 = lax.all_to_all(xs, "dp", split_axis=0, concat_axis=0, tiled=True)
    g0 = lax.all_to_all(gs, "dp", split_axis=0, concat_axis=0, tiled=True)
    x1, x2 = shift(x0, 1), shift(x0, 2)
    g_chunks = [g0] + [swap(g0, j) for j in range(1, n_t)]

    place, cos, sin = rope_tables(lengths[0], (t - 2) * rows, 3 * rows)
    start = (LONGEST + jnp.arange(rows, dtype=I32) - place[2 * rows :]).reshape(1, rows)
    gain_attn, gain_moe = norm_gain_attn.reshape(1, D), norm_gain_moe.reshape(1, D)
    window = LONGEST + 256
    ext = (3 * rows, D)
    h, q, k, v, o, lse = call(
        attention_body,
        "attention",
        [(ext, BF16), ((rows, D), BF16), (ext, BF16), (ext, BF16), ((rows, D), BF16), ((SPARE, rows), F32)],
        [x0, x1, x2, w_attn, gain_attn, cos, sin, start],
        scratch=[pltpu.VMEM((window, 256), F32)],
    )

    res_t = jnp.concatenate([gate_residual.T, jnp.zeros((4, rows), F32)], axis=0)
    wrc = jnp.concatenate([w_router.T, w_const.transpose(0, 2, 1).reshape(4, D)], axis=0)
    v8 = jnp.concatenate([v_const, jnp.zeros((6, D), F32)], axis=0)
    xm, hp, gt = call(
        router_body,
        "router",
        [((rows, D), F32), ((rows + SPARE, D), BF16), ((8, rows), F32)],
        [t_arr, o, w_attn, x0, gain_moe, res_t, wrc, routes_t],
        1,
    )
    h_chunks = [hp] + [swap(hp, j) for j in range(1, n_t)]
    xl, dhl, sm, gv = call(
        local_body,
        "local_experts",
        [((rows, D), F32), ((rows, D), F32), ((SPARE, rows), F32), ((8, D), F32)],
        [t_arr, xm, hp, g0, gt, routes_t, v8],
        1,
    )

    made = experts_call(counts, h_chunks, g_chunks, slots, w_ff, ff)
    out_parts, back_parts, gw_ff = made[:n_t], made[n_t : 2 * n_t], made[2 * n_t]
    back_chunks = [back_parts[0]] + [swap(back_parts[j], j) for j in range(1, n_t)]
    out_chunks = [out_parts[0]] + [swap(out_parts[j], j) for j in range(1, n_t)]
    ff_sum = lax.psum_scatter(gw_ff, "dp", scatter_dimension=0, tiled=True)

    dx, da, do, delta, dres, small = call(
        middle_back_body,
        "middle_back",
        [((rows, D), F32), ((rows, D), BF16), ((rows, D), BF16), ((SPARE, rows), F32), ((SPARE, rows), F32), ((SPARE + 8, D), F32)],
        [t_arr, *back_chunks, dhl, gt, sm, routes_t, wrc, xm, gain_moe, g0, hp, w_attn, o, gv],
        1,
    )
    small_all = jnp.sum(lax.all_gather(small, ("dp", "tensor"), axis=0, tiled=False), axis=0)

    dq, dk, dv, d0, d1, d2 = call(
        attention_back_body,
        "attention_back",
        [((rows, D), BF16), (ext, BF16), (ext, BF16), ((rows, D), F32), ((rows, D), BF16), ((rows, D), BF16)],
        [q, k, v, do, lse, delta, start, cos, sin, w_attn],
        scratch=[pltpu.VMEM((window, 256), F32), pltpu.VMEM(ext, F32), pltpu.VMEM(ext, F32), pltpu.VMEM((rows, D), F32)],
    )
    r1, r2 = shift(d1, -1), shift(d2, -2)
    gw_attn, gain_part = call(
        attention_grads_body,
        "attention_grads",
        [((D, 4 * D), BF16), ((8, D), F32)],
        [x0, x1, x2, h, dq, dk, dv, da, o, d0, d1, d2],
    )
    gain_all = jnp.sum(lax.all_gather(gain_part[0:1], ("dp", "tensor"), axis=0, tiled=True), axis=0)
    (d_start,) = call(final_back_body, "final_back", [((rows, D), BF16)], [x0, d0, r1, r2, dx, gain_attn])
    result = xl
    for part in out_chunks:
        result = result + part.astype(F32)
    result = result.astype(BF16)
    back_out = lax.all_to_all(result, "dp", split_axis=0, concat_axis=0, tiled=True)
    back_grad = lax.all_to_all(d_start, "dp", split_axis=0, concat_axis=0, tiled=True)
    output, grad_tokens = call(restore_body, "restore", [((rows, D), BF16)] * 2, [pos, back_out, back_grad])

    attn_sum = lax.psum_scatter(gw_attn, "dp", scatter_dimension=0, tiled=True).reshape(d_here, 4, n_t, D // n_t)

    def share(j):
        return lax.dynamic_index_in_dim(attn_sum, t ^ j, 2, keepdims=False)

    attn_own = share(0).astype(F32)
    for j in range(1, n_t):
        attn_own = attn_own + swap(share(j), j).astype(F32)
    ff_own = ff_sum.reshape(d_here, EXPERTS, 3 * ff).astype(F32)
    return (
        output,
        grad_tokens,
        dres[0:12].T,
        attn_own[:, 0:3],
        attn_own[:, 3],
        ff_own[:, :, 0 : 2 * ff].reshape(d_here, EXPERTS, 2, ff),
        ff_own[:, :, 2 * ff :],
        gain_all,
        small_all[SPARE + 2],
        small_all[0:12].T,
        small_all[12:16].reshape(2, 2, D).transpose(0, 2, 1),
        small_all[SPARE : SPARE + 2],
    )


def solution(mesh):
    both, every = P(("dp", "tensor"), None), P()
    weights = (P("dp", None, "tensor"), P("dp", "tensor"), P("dp", None, None, "tensor"), P("dp", None, "tensor"))
    return jax.shard_map(
        body,
        mesh=mesh,
        in_specs=(both, both, P(("dp", "tensor")), P("dp", None), P("dp", None), both, *weights) + (every,) * 5,
        out_specs=(both, both, both, *weights) + (every,) * 5,
        check_vma=False,
    )
```

```python
import functools
import math

import jax
import jax.numpy as jnp
from jax import lax
from jax.experimental import pallas as pl
from jax.experimental.pallas import tpu as pltpu
from jax.sharding import PartitionSpec as P

D = 768
HEAD_DIM = 64
HEADS = 12
EXPERTS = 8
LONGEST = 1024
EPSILON = 1e-6
MASKED = -1e30
F32, BF16, I32 = jnp.float32, jnp.bfloat16, jnp.int32
NN = (((1,), (0,)), ((), ()))
NT = (((1,), (1,)), ((), ()))
TN = (((0,), (0,)), ((), ()))
SCORE_SCALE = HEAD_DIM**-0.5
LOG2E = 1.4426950408889634
TILE = 160
ROWS = 256
SPARE = 16
VMEM_CAP = 66_000_000


def mm(a, b, dims):
    return lax.dot_general(a, b, dims, preferred_element_type=F32)


def iota(shape, axis):
    return lax.broadcasted_iota(I32, shape, axis)


def pick(cond):
    return jnp.where(cond, 1.0, 0.0).astype(BF16)


def split2(v):
    high = v.astype(BF16)
    return high, (v - high.astype(F32)).astype(BF16)


def split3(v):
    high = v.astype(BF16)
    rest = v - high.astype(F32)
    mid = rest.astype(BF16)
    return high, mid, (rest - mid.astype(F32)).astype(BF16)


def vmem():
    return pl.BlockSpec(memory_space=pltpu.VMEM)


def smem():
    return pl.BlockSpec(memory_space=pltpu.SMEM)


def call(body, name, outs, operands, scalars=0, scratch=(), meet=None):
    return pl.pallas_call(
        body,
        name=name,
        out_shape=[jax.ShapeDtypeStruct(*o) for o in outs],
        in_specs=[smem()] * scalars + [vmem()] * (len(operands) - scalars),
        out_specs=[vmem()] * len(outs),
        scratch_shapes=list(scratch),
        compiler_params=pltpu.CompilerParams(
            vmem_limit_bytes=VMEM_CAP, collective_id=meet, has_side_effects=meet is not None
        ),
    )(*operands)


def deal_body(n_dp, deal_ref, tok_ref, cot_ref, routes_ref, xs_ref, gs_ref, pos_ref, slot_ref, cnt_ref):
    rows = tok_ref.shape[0]
    first, second = iota((rows, rows), 0), iota((rows, rows), 1)
    before = pick(first < second)
    deal = deal_ref[...]
    hit = iota((n_dp, rows), 0) == deal
    rank = mm(pick(hit), before, NN)
    rank = jnp.sum(jnp.where(hit, rank, 0.0), axis=0, keepdims=True).astype(I32)
    pos = deal * (rows // n_dp) + rank
    pos_ref[...] = pos
    place = pick(first == pos)
    xs_ref[...] = mm(place, tok_ref[...], NN).astype(BF16)
    gs_ref[...] = mm(place, cot_ref[...], NN).astype(BF16)
    expert = iota((EXPERTS, rows), 0)
    for j in range(routes_ref.shape[0]):
        route = routes_ref[j]
        named = (expert == route[0:1]) | (expert == route[1:2])
        ahead = mm(pick(named), before, NN).astype(I32)
        slot_ref[j] = jnp.where(named, ahead, -1)
        total = jnp.sum(jnp.where(named, 1.0, 0.0), axis=1, keepdims=True).astype(I32)
        cnt_ref[j] = jnp.broadcast_to(total, (EXPERTS, 128))


def restore_body(pos_ref, a_ref, b_ref, oa_ref, ob_ref):
    rows = a_ref.shape[0]
    place = pick(iota((rows, rows), 0) == pos_ref[...])
    oa_ref[...] = mm(place, a_ref[...], TN).astype(BF16)
    ob_ref[...] = mm(place, b_ref[...], TN).astype(BF16)


class Line:
    def __init__(self, size):
        self.size = size
        self.place = lax.axis_index("tensor")
        self.sent = {k: [] for k in range(size)}

    def each(self, body):
        for k in range(self.size):
            pl.when(self.place == k)(functools.partial(body, k))

    def enter(self):
        sem = pltpu.get_barrier_semaphore()

        def greet(k):
            near = [n for n in (k - 1, k + 1) if 0 <= n < self.size]
            for n in near:
                pl.semaphore_signal(sem, 1, device_id={"tensor": self.place + (n - k)}, device_id_type=pl.DeviceIdType.MESH)
            pl.semaphore_wait(sem, len(near))

        self.each(greet)

    def copy(self, hop, src, dst, sems):
        return pltpu.make_async_remote_copy(
            src_ref=src,
            dst_ref=dst,
            send_sem=sems[0],
            recv_sem=sems[1],
            device_id={"tensor": self.place + hop},
            device_id_type=pl.DeviceIdType.MESH,
        )

    def send(self, k, to, refs):
        self.copy(to - k, *refs()).start()
        self.sent[k].append((to - k, refs))

    def arrived(self, k, dst, sems):
        self.copy((k ^ 1) - k, dst, dst, sems).wait_recv()

    def leave(self):
        def drain(k):
            for hop, refs in self.sent[k]:
                self.copy(hop, *refs()).wait_send()

        self.each(drain)


def sum_events(size, k):
    events = []
    for dest in range(size):
        if dest >= k and dest > 0:
            events.append((0 if k == 0 else size - 1 - dest + k, 1, dest))
        if dest <= k and dest < size - 1:
            events.append((0 if k == size - 1 else dest + size - 1 - k, -1, dest))
    drop = [(t, w, d) for t, w, d in events if (k == 0 and w == 1 and d == 0) or (k == size - 1 and w == -1 and d == k)]
    return sorted(ev for ev in events if ev not in drop)


def turn(u):
    low = (iota((1, u.shape[1]), 1) % HEAD_DIM) < HEAD_DIM // 2
    half = HEAD_DIM // 2
    return jnp.where(low, pltpu.roll(u, u.shape[1] - half, 1), pltpu.roll(u, half, 1))


def wide(table):
    return jnp.concatenate([table] * (D // 128), axis=1)


def key_bias(start, block, first_row, base):
    window = LONGEST + block
    key = iota((window, block), 0) + first_row
    row = iota((1, block), 1) + (base + first_row)
    return jnp.where((key >= start) & (key <= row), 0.0, MASKED)


def router_part(route, o_ref, w_ref, x_ref, gain_ref, res_ref, wrc_ref, x1_ref, hp_ref, gt_ref):
    rows = o_ref.shape[0]
    x1 = x_ref[...].astype(F32) + mm(o_ref[...], w_ref[:, 3 * D : 4 * D], NT)
    x1_ref[...] = x1
    h = x1 * lax.rsqrt(jnp.mean(x1 * x1, axis=1, keepdims=True) + EPSILON) * gain_ref[...]
    h = h.astype(BF16)
    hp_ref[0:rows, :] = h
    high, mid, low = split3(wrc_ref[...])
    z = mm(low, h, NT) + mm(mid, h, NT) + mm(high, h, NT) + res_ref[...]
    expert = iota(z.shape, 0)
    named0, named1 = expert == route[0:1], expert == route[1:2]
    c0 = jnp.sum(jnp.where(named0, z, 0.0), axis=0, keepdims=True)
    c1 = jnp.sum(jnp.where(named1, z, 0.0), axis=0, keepdims=True)
    top = jnp.maximum(c0, c1)
    e0, e1 = jnp.exp(c0 - top), jnp.exp(c1 - top)
    g0, g1 = e0 / (e0 + e1), e1 / (e0 + e1)
    table = [g0, g1]
    for j in range(2):
        l0, l1 = z[12 + 2 * j : 13 + 2 * j], z[13 + 2 * j : 14 + 2 * j]
        top = jnp.maximum(l0, l1)
        m0, m1 = jnp.exp(l0 - top), jnp.exp(l1 - top)
        table += [m0 / (m0 + m1), m1 / (m0 + m1)]
    gt_ref[...] = jnp.concatenate(table + [jnp.zeros((2, rows), F32)], axis=0)
    gates = jnp.where(named0, g0, jnp.where(named1, g1, 0.0))
    gates = jnp.where(expert < EXPERTS, gates, 0.0)
    hp_ref[rows : rows + SPARE, :] = jnp.concatenate([gates, jnp.zeros((SPARE, D - rows), F32)], axis=1).astype(BF16)


def local_part(route, x1_ref, hp_ref, g_ref, gt_ref, v_ref, xl_ref, dhl_ref, sm_ref, gv_ref):
    rows = x1_ref.shape[0]
    h, g = hp_ref[0:rows, :], g_ref[...]
    hf, gf = h.astype(F32), g.astype(F32)
    low0 = gt_ref[0:1].astype(BF16).astype(F32)
    low1 = gt_ref[1:2].astype(BF16).astype(F32)

    def weight(e):
        return jnp.where(route[0:1] == e, low0, 0.0) + jnp.where(route[1:2] == e, low1, 0.0)

    copy, first, second = weight(EXPERTS + 1), weight(EXPERTS + 2), weight(EXPERTS + 3)
    m00, m01, m10, m11 = gt_ref[2:3], gt_ref[3:4], gt_ref[4:5], gt_ref[5:6]
    a = copy + first * m00 + second * m10
    b0, b1 = first * m01, second * m11
    table = jnp.concatenate([a, b0, b1, jnp.zeros((125, rows), F32)], axis=0).T
    ac, b0c, b1c = table[:, 0:1], table[:, 1:2], table[:, 2:3]
    v = v_ref[...]
    xl_ref[...] = x1_ref[...] + ac * hf + b0c * v[0:1] + b1c * v[1:2]
    dhl_ref[...] = ac * gf
    ones = jnp.ones((8, D), BF16)
    high, low = split2(hf * gf)
    gh = (mm(ones, high, NT) + mm(ones, low, NT))[0:1]
    vh, vm, vl = split3(v)
    gvs = mm(vl, g, NT) + mm(vm, g, NT) + mm(vh, g, NT)
    gv0, gv1 = gvs[0:1], gvs[1:2]
    zero = jnp.zeros((9, rows), F32)
    dl0 = first * m00 * m01 * (gh - gv0)
    dl1 = second * m10 * m11 * (gh - gv1)
    sm_ref[...] = jnp.concatenate(
        [zero, gh, m00 * gh + m01 * gv0, m10 * gh + m11 * gv1, dl0, -dl0, dl1, -dl1], axis=0
    )
    bh, bm, bl = split3(jnp.concatenate([b0, b1, jnp.zeros((6, rows), F32)], axis=0))
    gv_ref[...] = mm(bl, g, NN) + mm(bm, g, NN) + mm(bh, g, NN)


def forward_body(size, x0_ref, g0_ref, w_ref, gain_ref, gain2_ref, cos_ref, sin_ref, start_ref, res_ref, wrc_ref, routes_ref, v8_ref,
                 x1_ref, x2_ref, h_ref, q_ref, k_ref, v_ref, o_ref, lse_ref, xm_ref, hp_ref, gall_ref, gt_ref, xl_ref,
                 dhl_ref, sm_ref, gv_ref,
                 bias_ref, sx, rx, sgu, rgu, sgd, rgd, shu, rhu, shd, rhd):
    rows = x0_ref.shape[0]
    step = 256
    line = Line(size)
    t = line.place
    last = size - 1
    line.enter()

    def begin(k):
        if k < last:
            line.send(k, k + 1, lambda: (x0_ref, x1_ref, (sx.at[0], rx.at[0])))
        if k > 0:
            line.send(k, k - 1, lambda: (g0_ref, gall_ref.at[k], (sgd.at[0], rgd.at[0])))

    line.each(begin)
    gain = gain_ref[...]

    def project_chunk(c, x_ref):
        def project(i, _):
            at = pl.multiple_of(i * step, step)
            x = x_ref[pl.ds(at, step), :].astype(F32)
            h = x * lax.rsqrt(jnp.mean(x * x, axis=1, keepdims=True) + EPSILON) * gain
            h = h.astype(BF16)
            to = pl.ds(pl.multiple_of(c * rows + i * step, step), step)
            h_ref[to, :] = h
            cos, sin = wide(cos_ref[to, :]), wide(sin_ref[to, :])
            k = mm(h, w_ref[:, D : 2 * D], NN)
            k_ref[to, :] = (k * cos + turn(k) * sin).astype(BF16)
            v_ref[to, :] = mm(h, w_ref[:, 2 * D : 3 * D], NN).astype(BF16)
            if c == 2:
                q = mm(h, w_ref[:, 0:D], NN)
                q_ref[pl.ds(at, step), :] = (q * cos + turn(q) * sin).astype(BF16)
            return 0

        lax.fori_loop(0, rows // step, project, 0)

    project_chunk(2, x0_ref)
    gall_ref[t] = g0_ref[...]

    def second(k):
        if k > 0:
            line.arrived(k, x1_ref, (sx.at[0], rx.at[0]))
        else:
            x1_ref[...] = jnp.zeros_like(x1_ref)
        if 0 < k < last:
            line.send(k, k + 1, lambda: (x1_ref, x2_ref, (sx.at[1], rx.at[1])))
        if k < last:
            line.send(k, k + 1, lambda: (g0_ref, gall_ref.at[k], (sgu.at[0], rgu.at[0])))
            line.arrived(k, gall_ref.at[k + 1], (sgd.at[0], rgd.at[0]))
            if k > 0:
                line.send(k, k - 1, lambda: (gall_ref.at[k + 1], gall_ref.at[k + 1], (sgd.at[1], rgd.at[1])))

    line.each(second)
    project_chunk(1, x1_ref)

    def third(k):
        if k > 1:
            line.arrived(k, x2_ref, (sx.at[1], rx.at[1]))
        else:
            x2_ref[...] = jnp.zeros_like(x2_ref)
        if k + 2 <= last:
            line.arrived(k, gall_ref.at[k + 2], (sgd.at[1], rgd.at[1]))
            if k > 0:
                line.send(k, k - 1, lambda: (gall_ref.at[k + 2], gall_ref.at[k + 2], (sgd.at[2], rgd.at[2])))

    line.each(third)
    project_chunk(0, x2_ref)

    block = step
    window = LONGEST + block
    lane = iota((1, 128), 1) // HEAD_DIM
    for rb in range(rows // block):
        first = rb * block
        bias_ref[...] = key_bias(start_ref[:, first : first + block], block, first, LONGEST)

        def pair(i, _, first=first):
            lanes = pl.ds(pl.multiple_of(i * 128, 128), 128)
            k = k_ref[first : first + window, lanes]
            vt = v_ref[first : first + window, lanes].T
            q = q_ref[first : first + block, lanes]
            parts = []
            for half in range(2):
                qm = jnp.where(lane == half, q, jnp.zeros_like(q))
                s = mm(k, qm, NT) * (SCORE_SCALE * LOG2E) + bias_ref[...]
                top = jnp.max(s, axis=0, keepdims=True)
                p = jnp.exp2(s - top)
                total = jnp.sum(p, axis=0, keepdims=True)
                out = mm(vt[half * HEAD_DIM : (half + 1) * HEAD_DIM], p.astype(BF16), NN)
                parts.append(out * (1.0 / total))
                lse_ref[pl.ds(i * 2 + half, 1), first : first + block] = top + jnp.log2(total)
            o_ref[first : first + block, lanes] = jnp.concatenate(parts, axis=0).T.astype(BF16)
            return 0

        lax.fori_loop(0, HEADS // 2, pair, 0)
        if rb == 0:
            def fourth(k):
                if k > 0:
                    line.arrived(k, gall_ref.at[k - 1], (sgu.at[0], rgu.at[0]))
                    if k < last:
                        line.send(k, k + 1, lambda: (gall_ref.at[k - 1], gall_ref.at[k - 1], (sgu.at[1], rgu.at[1])))

            line.each(fourth)

    route = routes_ref[t]
    router_part(route, o_ref, w_ref, x0_ref, gain2_ref, res_ref, wrc_ref, xm_ref, hp_ref.at[t], gt_ref)

    def fifth(k):
        if k < last:
            line.send(k, k + 1, lambda: (hp_ref.at[k], hp_ref.at[k], (shu.at[0], rhu.at[0])))
        if k > 0:
            line.send(k, k - 1, lambda: (hp_ref.at[k], hp_ref.at[k], (shd.at[0], rhd.at[0])))
        if k > 1:
            line.arrived(k, gall_ref.at[k - 2], (sgu.at[1], rgu.at[1]))
            if k < last:
                line.send(k, k + 1, lambda: (gall_ref.at[k - 2], gall_ref.at[k - 2], (sgu.at[2], rgu.at[2])))

    line.each(fifth)
    local_part(route, xm_ref, hp_ref.at[t], g0_ref, gt_ref, v8_ref, xl_ref, dhl_ref, sm_ref, gv_ref)

    def sixth(k):
        for hop in range(2):
            up, down = k - 1 - hop, k + 1 + hop
            if up >= 0:
                line.arrived(k, hp_ref.at[up], (shu.at[hop], rhu.at[hop]))
                if k < last:
                    line.send(k, k + 1, lambda up=up, hop=hop: (hp_ref.at[up], hp_ref.at[up], (shu.at[hop + 1], rhu.at[hop + 1])))
            if down <= last:
                line.arrived(k, hp_ref.at[down], (shd.at[hop], rhd.at[hop]))
                if k > 0:
                    line.send(k, k - 1, lambda down=down, hop=hop: (hp_ref.at[down], hp_ref.at[down], (shd.at[hop + 1], rhd.at[hop + 1])))
        if k == last:
            line.arrived(k, hp_ref.at[0], (shu.at[2], rhu.at[2]))
            line.arrived(k, gall_ref.at[0], (sgu.at[2], rgu.at[2]))
        if k == 0:
            line.arrived(k, hp_ref.at[last], (shd.at[2], rhd.at[2]))
            line.arrived(k, gall_ref.at[last], (sgd.at[2], rgd.at[2]))

    line.each(sixth)
    line.leave()


def middle_part(route, dh_ref, gt_ref, sm_ref, wrc_ref, x1_ref, gain_ref, g_ref, h2_ref, w_ref, o_ref, gv_ref,
                dx_ref, da_ref, do_ref, delta_ref, dres_ref, small_ref):
    rows = x1_ref.shape[0]
    dgf = dh_ref[rows : rows + SPARE, 0:rows]
    dh = dh_ref[0:rows, :]
    dgate = jnp.concatenate([dgf[0:EXPERTS] + dgf[EXPERTS:], sm_ref[EXPERTS:SPARE]], axis=0)
    expert = iota((SPARE, rows), 0)
    named0, named1 = expert == route[0:1], expert == route[1:2]
    g0, g1 = gt_ref[0:1], gt_ref[1:2]
    d0 = jnp.sum(jnp.where(named0, dgate, 0.0), axis=0, keepdims=True)
    d1 = jnp.sum(jnp.where(named1, dgate, 0.0), axis=0, keepdims=True)
    inner = g0 * d0 + g1 * d1
    dz = jnp.where(named0, g0 * (d0 - inner), jnp.where(named1, g1 * (d1 - inner), 0.0))
    dres_ref[...] = dz
    dz = jnp.where(expert < 12, dz, sm_ref[...])
    zh, zm, zl = split3(dz)
    wh, wm, wl = split3(wrc_ref[...])
    dh = dh + (mm(zh, wl, TN) + mm(zl, wh, TN) + mm(zm, wm, TN) + mm(zh, wm, TN) + mm(zm, wh, TN) + mm(zh, wh, TN))
    h = h2_ref[...]
    small_ref[0:SPARE, :] = mm(zl, h, NN) + mm(zm, h, NN) + mm(zh, h, NN)
    x1 = x1_ref[...]
    r = lax.rsqrt(jnp.mean(x1 * x1, axis=1, keepdims=True) + EPSILON)
    xr = x1 * r
    grad_gain = jnp.sum(dh * xr, axis=0, keepdims=True)
    gv = gv_ref[...]
    small_ref[SPARE : SPARE + 8, :] = jnp.concatenate([gv[0:2], grad_gain, gv[3:8]], axis=0)
    scaled = dh * gain_ref[...]
    dx = g_ref[...].astype(F32) + r * (scaled - xr * jnp.mean(xr * scaled, axis=1, keepdims=True))
    dx_ref[...] = dx
    da = dx.astype(BF16)
    da_ref[...] = da
    do = mm(da, w_ref[:, 3 * D : 4 * D], NN).astype(BF16)
    do_ref[...] = do
    high, low = split2(do.astype(F32) * o_ref[...].astype(F32))
    heads = pick(iota((SPARE, D), 1) // HEAD_DIM == iota((SPARE, D), 0))
    delta_ref[...] = mm(heads, high, NT) + mm(heads, low, NT)


def backward_body(size, back_ref, out_ref, dhl_ref, gt_ref, sm_ref, routes_ref, wrc_ref, xm_ref, gain_ref, g_ref, h2_ref, w_ref,
                  o_ref, gv_ref, q_ref, k_ref, v_ref, lse_ref, start_ref, cos_ref, sin_ref, xl_ref,
                  dx_ref, da_ref, dres_ref, small_ref, dq_ref, dk_ref, dv_ref, y_ref,
                  bias_ref, dkf_ref, dvf_ref, dh_ref, do_ref, delta_ref, bu_ref, bd_ref, fu_ref, fd_ref,
                  sbu, rbu, sbd, rbd, sfu, rfu, sfd, rfd):
    rows = xm_ref.shape[0]
    packed = rows + SPARE
    cut = 272
    pieces = (slice(0, cut), slice(cut, packed))
    line = Line(size)
    t = line.place
    last = size - 1
    line.enter()

    def handle(k, way, dest, part, index, mine_ref, up_ref, down_ref, ups, downs):
        slot = dest - 1 if way == 1 else dest
        first = k == (0 if way == 1 else last)
        mine = mine_ref.at[dest, part]

        def refs():
            held = (up_ref if way == 1 else down_ref).at[slot, part]
            sems = tuple(s.at[slot, index] for s in (ups if way == 1 else downs))
            return mine_ref.at[dest, part] if first else held, held, sems

        _, held, sems = refs()
        if not first:
            line.arrived(k, held, sems)
        if dest != k:
            if not first:
                held[...] = (held[...].astype(F32) + mine[...].astype(F32)).astype(BF16)
            line.send(k, k + way, refs)

    def sum_back(k):
        for _, way, dest in sum_events(size, k):
            for index, part in enumerate(pieces):
                handle(k, way, dest, part, index, back_ref, bu_ref, bd_ref, (sbu, rbu), (sbd, rbd))

    def sum_out(k, now):
        for time, way, dest in sum_events(size, k):
            if time == now:
                handle(k, way, dest, slice(0, rows), 0, out_ref, fu_ref, fd_ref, (sfu, rfu), (sfd, rfd))

    line.each(sum_back)
    line.each(lambda k: sum_out(k, 0))
    dh_ref[...] = back_ref[t].astype(F32)

    @pl.when(t > 0)
    def _():
        dh_ref[...] += bu_ref[t - 1].astype(F32)

    @pl.when(t < last)
    def _():
        dh_ref[...] += bd_ref[t].astype(F32)

    dh_ref[0:rows, :] += dhl_ref[...]
    middle_part(routes_ref[t], dh_ref, gt_ref, sm_ref, wrc_ref, xm_ref, gain_ref, g_ref, h2_ref, w_ref, o_ref, gv_ref,
                dx_ref, da_ref, do_ref, delta_ref, dres_ref, small_ref)
    line.each(lambda k: sum_out(k, 1))

    block = 256
    window = LONGEST + block
    lane = iota((1, 128), 1) // HEAD_DIM
    for rb in range(rows // block):
        first = rb * block
        bias_ref[rb] = key_bias(start_ref[:, first : first + block], block, first, LONGEST)

    def pair(i, _):
        lanes = pl.ds(pl.multiple_of(i * 128, 128), 128)
        for rb in range(rows // block):
            first = rb * block
            k = k_ref[first : first + window, lanes]
            v = v_ref[first : first + window, lanes]
            kt = k.T
            q = q_ref[first : first + block, lanes]
            do = do_ref[first : first + block, lanes]
            dk = jnp.zeros((window, 128), F32)
            dv = jnp.zeros((window, 128), F32)
            parts = []
            for half in range(2):
                qm = jnp.where(lane == half, q, jnp.zeros_like(q))
                dom = jnp.where(lane == half, do, jnp.zeros_like(do))
                head = pl.ds(i * 2 + half, 1)
                s = mm(k, qm, NT) * (SCORE_SCALE * LOG2E) + bias_ref[rb]
                p = jnp.exp2(s - lse_ref[head, first : first + block])
                dp = mm(v, dom, NT)
                ds = (p * (dp - delta_ref[head, first : first + block])).astype(BF16)
                dv = dv + mm(p.astype(BF16), dom, NN)
                dk = dk + mm(ds, qm, NN)
                parts.append(mm(kt[half * HEAD_DIM : (half + 1) * HEAD_DIM], ds, NN))
            dq = jnp.concatenate(parts, axis=0).T * SCORE_SCALE
            at = slice(2 * rows + first, 2 * rows + first + block)
            dq_ref[first : first + block, lanes] = (dq * cos_ref[at, :] - turn(dq) * sin_ref[at, :]).astype(BF16)
            if first == 0:
                dkf_ref[0:window, :] = dk
                dvf_ref[0:window, :] = dv
            else:
                old = window - block
                dkf_ref[first : first + old, :] += dk[0:old]
                dvf_ref[first : first + old, :] += dv[0:old]
                dkf_ref[first + old : first + window, :] = dk[old:]
                dvf_ref[first + old : first + window, :] = dv[old:]
        dk = dkf_ref[...] * SCORE_SCALE
        dk_ref[:, lanes] = (dk * cos_ref[...] - turn(dk) * sin_ref[...]).astype(BF16)
        dv_ref[:, lanes] = dvf_ref[...].astype(BF16)
        return 0

    lax.fori_loop(0, HEADS // 4, pair, 0)
    line.each(lambda k: sum_out(k, 2))
    lax.fori_loop(HEADS // 4, HEADS // 2, pair, 0)
    line.each(lambda k: sum_out(k, 3))
    xl_ref[...] += out_ref[t].astype(F32)

    @pl.when(t > 0)
    def _():
        xl_ref[...] += fu_ref[t - 1].astype(F32)

    @pl.when(t < last)
    def _():
        xl_ref[...] += fd_ref[t].astype(F32)

    y_ref[...] = xl_ref[...].astype(BF16)
    line.leave()


def grads_body(size, x0_ref, x1_ref, x2_ref, h_ref, dq_ref, dk_ref, dv_ref, da_ref, o_ref, w_ref, dx_ref, gain_ref,
               gw_ref, gpart_ref, out_ref, d0_ref, d1_ref, d2_ref, ra_ref, rb_ref, sems_s, sems_r):
    rows = x0_ref.shape[0]
    line = Line(size)
    last = size - 1
    block = 256
    line.enter()

    def hidden(c, d_ref):
        def one(i, _):
            at = pl.ds(pl.multiple_of(i * block, block), block)
            to = pl.ds(pl.multiple_of(c * rows + i * block, block), block)
            total = mm(dk_ref[to, :], w_ref[:, D : 2 * D], NT) + mm(dv_ref[to, :], w_ref[:, 2 * D : 3 * D], NT)
            if c == 2:
                total = total + mm(dq_ref[at, :], w_ref[:, 0:D], NT)
            d_ref[at, :] = total.astype(d_ref.dtype)
            return 0

        lax.fori_loop(0, rows // block, one, 0)

    def gain_of(x_ref, d_ref):
        x = x_ref[...].astype(F32)
        r = lax.rsqrt(jnp.mean(x * x, axis=1, keepdims=True) + EPSILON)
        return jnp.sum(d_ref[...].astype(F32) * x * r, axis=0, keepdims=True)

    hidden(0, d2_ref)

    def first(k):
        if k > 1:
            line.send(k, k - 1, lambda: (d2_ref, ra_ref, (sems_s.at[0], sems_r.at[0])))

    line.each(first)
    hidden(1, d1_ref)
    gain = gain_of(x2_ref, d2_ref) + gain_of(x1_ref, d1_ref)
    h = h_ref[...]

    def weight(column, left, right_ref):
        for c in range(D // 256):
            cols = slice(c * 256, (c + 1) * 256)
            gw_ref[:, column * D + c * 256 : column * D + c * 256 + 256] = mm(left, right_ref[:, cols], TN).astype(BF16)

    weight(1, h, dk_ref)

    def second(k):
        if 0 < k < last:
            line.arrived(k, ra_ref, (sems_s.at[0], sems_r.at[0]))
            d1_ref[...] = (d1_ref[...].astype(F32) + ra_ref[...].astype(F32)).astype(BF16)
        if k > 0:
            line.send(k, k - 1, lambda: (d1_ref, rb_ref, (sems_s.at[1], sems_r.at[1])))

    line.each(second)
    hidden(2, d0_ref)
    gpart_ref[...] = jnp.broadcast_to(gain + gain_of(x0_ref, d0_ref), (8, D))
    weight(2, h, dv_ref)
    weight(0, h[2 * rows :], dq_ref)
    weight(3, da_ref[...], o_ref)

    def third(k):
        if k < last:
            line.arrived(k, rb_ref, (sems_s.at[1], sems_r.at[1]))
            d0_ref[...] += rb_ref[...].astype(F32)

    line.each(third)
    x = x0_ref[...].astype(F32)
    r = lax.rsqrt(jnp.mean(x * x, axis=1, keepdims=True) + EPSILON)
    xr = x * r
    scaled = d0_ref[...] * gain_ref[...]
    out_ref[...] = (dx_ref[...] + r * (scaled - xr * jnp.mean(xr * scaled, axis=1, keepdims=True))).astype(BF16)
    line.leave()


def experts_body(ff, chunks, cnt_ref, h_refs, g_refs, slot_ref, w_ref, o_refs, d_refs, gw_ref,
                 xbuf, gbuf, cbuf, onehot, fbuf, dbuf, gacc, gates, dgrow, off_ref, base_ref, nt_ref):
    rows = slot_ref.shape[2]
    e = pl.program_id(0)

    def match(j, expert, tile):
        slots = slot_ref[j, pl.ds(expert, 1), :]
        return (iota((TILE, rows), 0) + tile * TILE) == slots

    def store_rows(at, count, hit, x, gs, gate_row):
        to = pl.ds(pl.multiple_of(at, 16), TILE)
        keep = iota((TILE, 1), 0) < count
        col = jnp.sum(jnp.where(hit, gate_row, 0.0), axis=1, keepdims=True)
        xbuf[to, :] = jnp.where(keep, x, xbuf[to, :].astype(F32)).astype(BF16)
        gbuf[to, :] = jnp.where(keep, gs, gbuf[to, :].astype(F32)).astype(BF16)
        cbuf[to, :] = jnp.where(keep, jnp.broadcast_to(col, (TILE, 128)), cbuf[to, :])

    def round16(n):
        return ((n + 15) // 16) * 16

    @pl.when(e == 0)
    def _gather():
        at = jnp.int32(0)
        for ex in range(EXPERTS):
            base_ref[ex] = at
            here = at
            for j in range(chunks):
                off_ref[j * EXPERTS + ex] = here
                here = here + round16(cnt_ref[j * EXPERTS + ex])
            tiles = (here - at + (ROWS - 1)) // ROWS
            nt_ref[ex] = tiles
            tail = pl.ds(pl.multiple_of(here, 16), ROWS)
            xbuf[tail, :] = jnp.zeros((ROWS, D), BF16)
            gbuf[tail, :] = jnp.zeros((ROWS, D), BF16)
            cbuf[tail, :] = jnp.zeros((ROWS, 128), F32)
            at = at + tiles * ROWS
        for j in range(chunks):
            gates[...] = h_refs[j, rows : rows + SPARE, 0:rows].astype(F32)

            def two(i, _, j=j):
                hits = [match(j, 2 * i + half, 0) for half in range(2)]
                sel = jnp.concatenate([pick(hit) for hit in hits], axis=0)
                x = mm(sel, h_refs[j, 0:rows, :], NN)
                gs = mm(sel, g_refs[j], NN)
                for half in range(2):
                    ex = 2 * i + half
                    count = round16(jnp.minimum(cnt_ref[j * EXPERTS + ex], TILE))
                    part = slice(half * TILE, (half + 1) * TILE)
                    store_rows(off_ref[j * EXPERTS + ex], count, hits[half], x[part], gs[part], gates[pl.ds(ex, 1), :])
                return 0

            lax.fori_loop(0, EXPERTS // 2, two, 0)

            def rare(ex, _, j=j):
                def more(tile, _):
                    hit = match(j, ex, tile)
                    sel = pick(hit)
                    count = round16(jnp.minimum(cnt_ref[j * EXPERTS + ex] - tile * TILE, TILE))
                    store_rows(
                        off_ref[j * EXPERTS + ex] + tile * TILE,
                        count,
                        hit,
                        mm(sel, h_refs[j, 0:rows, :], NN),
                        mm(sel, g_refs[j], NN),
                        gates[pl.ds(ex, 1), :],
                    )
                    return 0

                return lax.fori_loop(1, (cnt_ref[j * EXPERTS + ex] + (TILE - 1)) // TILE, more, 0)

            lax.fori_loop(0, EXPERTS, rare, 0)

    gacc[...] = jnp.zeros_like(gacc)

    def tile_step(m, _):
        at = pl.ds(pl.multiple_of(base_ref[e] + m * ROWS, 16), ROWS)
        x = xbuf[at, :]
        gs = gbuf[at, :].astype(F32)
        gate = wide(cbuf[at, :])
        u = mm(x, w_ref[:, 0:ff], NN)
        up = mm(x, w_ref[:, ff : 2 * ff], NN)
        sig = jax.nn.sigmoid(u)
        silu = u * sig
        act = (silu * up).astype(BF16)
        f = mm(act, w_ref[:, 2 * ff : 3 * ff], NT)
        cbuf[at, :] = jnp.broadcast_to(jnp.sum(gs * f, axis=1, keepdims=True), (ROWS, 128))
        gbuf[at, :] = (f * gate).astype(BF16)
        df = (gs * gate).astype(BF16)
        dact = mm(df, w_ref[:, 2 * ff : 3 * ff], NN)
        dup = (dact * silu).astype(BF16)
        du = (dact * up * sig * (1.0 + u * (1.0 - sig))).astype(BF16)
        xbuf[at, :] = (mm(du, w_ref[:, 0:ff], NT) + mm(dup, w_ref[:, ff : 2 * ff], NT)).astype(BF16)
        gacc[:, 0:ff] += mm(x, du, TN)
        gacc[:, ff : 2 * ff] += mm(x, dup, TN)
        gacc[:, 2 * ff : 3 * ff] += mm(df, act, TN)
        return 0

    lax.fori_loop(0, nt_ref[e], tile_step, 0)
    gw_ref[...] = gacc[...].astype(BF16)

    @pl.when(e == EXPERTS - 1)
    def _scatter():
        for j in range(chunks):
            def take(ex, _, j=j):
                at = pl.ds(pl.multiple_of(off_ref[j * EXPERTS + ex], 16), TILE)
                to = pl.ds(pl.multiple_of(ex * TILE, 16), TILE)
                hit = match(j, ex, 0)
                onehot[to, :] = pick(hit)
                fbuf[to, :] = gbuf[at, :]
                dbuf[to, :] = xbuf[at, :]
                col = jnp.concatenate([cbuf[at, :]] * (rows // 128), axis=1)
                dgrow[pl.ds(ex, 1), :] = jnp.sum(jnp.where(hit, col, 0.0), axis=0, keepdims=True)
                return 0

            lax.fori_loop(0, EXPERTS, take, 0)
            gacc[0:rows, 0:D] = mm(onehot[...], fbuf[...], TN)
            gacc[0:rows, D : 2 * D] = mm(onehot[...], dbuf[...], TN)

            def rare(ex, _, j=j):
                def more(tile, _):
                    at = pl.ds(pl.multiple_of(off_ref[j * EXPERTS + ex] + tile * TILE, 16), TILE)
                    hit = match(j, ex, tile)
                    sel = pick(hit)
                    gacc[0:rows, 0:D] += mm(sel, gbuf[at, :], TN)
                    gacc[0:rows, D : 2 * D] += mm(sel, xbuf[at, :], TN)
                    col = jnp.concatenate([cbuf[at, :]] * (rows // 128), axis=1)
                    dgrow[pl.ds(ex, 1), :] += jnp.sum(jnp.where(hit, col, 0.0), axis=0, keepdims=True)
                    return 0

                return lax.fori_loop(1, (cnt_ref[j * EXPERTS + ex] + (TILE - 1)) // TILE, more, 0)

            lax.fori_loop(0, EXPERTS, rare, 0)
            o_refs[j] = gacc[0:rows, 0:D].astype(BF16)
            d_refs[j, 0:rows, :] = gacc[0:rows, D : 2 * D].astype(BF16)
            total = dgrow[...]
            high = total.astype(BF16).astype(F32)
            both = jnp.concatenate([high, total - high], axis=0)
            d_refs[j, rows : rows + SPARE, :] = jnp.concatenate(
                [both, jnp.zeros((SPARE, D - rows), F32)], axis=1
            ).astype(BF16)


def experts_call(counts, hs, gs, slots, weights, ff):
    chunks, rows = gs.shape[:2]
    width = 3 * ff
    most = (rows + 15 * chunks + ROWS - 1) // ROWS * ROWS * EXPERTS + ROWS
    whole = lambda shape: pl.BlockSpec(shape, lambda e: (0,) * len(shape), pipeline_mode=pl.Buffered(1))
    return pl.pallas_call(
        functools.partial(experts_body, ff, chunks),
        name="experts",
        grid=(EXPERTS,),
        in_specs=[smem(), whole(hs.shape), whole(gs.shape), whole(slots.shape), pl.BlockSpec((D, width), lambda e: (0, e))],
        out_specs=[whole(gs.shape), whole(hs.shape), pl.BlockSpec((D, width), lambda e: (0, e))],
        out_shape=[
            jax.ShapeDtypeStruct(gs.shape, BF16),
            jax.ShapeDtypeStruct(hs.shape, BF16),
            jax.ShapeDtypeStruct((D, EXPERTS * width), BF16),
        ],
        scratch_shapes=[
            pltpu.VMEM((most, D), BF16),
            pltpu.VMEM((most, D), BF16),
            pltpu.VMEM((most, 128), F32),
            pltpu.VMEM((EXPERTS * TILE, rows), BF16),
            pltpu.VMEM((EXPERTS * TILE, D), BF16),
            pltpu.VMEM((EXPERTS * TILE, D), BF16),
            pltpu.VMEM((D, width), F32),
            pltpu.VMEM((SPARE, rows), F32),
            pltpu.VMEM((EXPERTS, rows), F32),
            pltpu.SMEM((chunks * EXPERTS,), I32),
            pltpu.SMEM((EXPERTS,), I32),
            pltpu.SMEM((EXPERTS,), I32),
        ],
        compiler_params=pltpu.CompilerParams(
            dimension_semantics=("arbitrary",), vmem_limit_bytes=VMEM_CAP
        ),
    )(counts, hs, gs, slots, weights)


def rope_tables(lengths, first, count):
    finish = jnp.sum(jnp.where(jnp.arange(lengths.shape[0])[:, None] <= jnp.arange(lengths.shape[0])[None, :], lengths[:, None], 0), axis=0)
    begins = finish - lengths
    rows = first + jnp.arange(count, dtype=I32)
    opening = jnp.max(jnp.where(begins[None, :] <= rows[:, None], begins[None, :], 0), axis=1)
    place = rows - opening
    half = HEAD_DIM // 2
    rates = jnp.exp(jnp.arange(half, dtype=F32) * (-2.0 * math.log(10000.0) / HEAD_DIM))
    angles = place.astype(F32)[:, None] * rates[None, :]
    cos, sin = jnp.cos(angles), jnp.sin(angles)
    return place, jnp.concatenate([cos] * 4, axis=1), jnp.concatenate([-sin, sin] * 2, axis=1)


def body(tokens, cotangent, deal, lengths, routes, gate_residual, w_qkv, w_out, w_gate_up, w_down,
         norm_gain_attn, norm_gain_moe, w_router, w_const, v_const):
    rows = tokens.shape[0]
    n_dp, n_t = lax.axis_size("dp"), lax.axis_size("tensor")
    t = lax.axis_index("tensor")
    ff = w_down.shape[2]
    d_here = w_qkv.shape[0]

    def swap(v, j):
        return lax.ppermute(v, "tensor", [(i, i ^ j) for i in range(n_t)])

    def place_in(parts):
        stacked = jnp.stack(parts)
        return jnp.stack([lax.dynamic_index_in_dim(stacked, t ^ i, 0, keepdims=False) for i in range(n_t)], axis=2)

    attn_shard = jnp.concatenate([w_qkv, w_out[:, None, :]], axis=1)
    attn_shard = place_in([attn_shard] + [swap(attn_shard, j) for j in range(1, n_t)]).reshape(d_here, 4 * D)
    w_attn = lax.all_gather(attn_shard, "dp", axis=0, tiled=True)
    ff_shard = jnp.concatenate([w_gate_up.reshape(d_here, EXPERTS, 2 * ff), w_down], axis=2)
    w_ff = lax.all_gather(ff_shard.reshape(d_here, EXPERTS * 3 * ff), "dp", axis=0, tiled=True)

    routes_t = routes.reshape(n_t, rows, 2).transpose(0, 2, 1)
    row, ext = (rows, D), (3 * rows, D)
    every, every_packed = (n_t, rows, D), (n_t, rows + SPARE, D)
    xs, gs, pos, slots, counts = call(
        functools.partial(deal_body, n_dp),
        "deal",
        [(row, BF16), (row, BF16), ((1, rows), I32), ((n_t, EXPERTS, rows), I32), ((n_t, EXPERTS, 128), I32)],
        [deal.reshape(1, rows), tokens, cotangent, routes_t],
    )
    counts = counts[:, :, 0].reshape(n_t * EXPERTS)
    x0 = lax.all_to_all(xs, "dp", split_axis=0, concat_axis=0, tiled=True)
    g0 = lax.all_to_all(gs, "dp", split_axis=0, concat_axis=0, tiled=True)

    place, cos, sin = rope_tables(lengths[0], (t - 2) * rows, 3 * rows)
    start = (LONGEST + jnp.arange(rows, dtype=I32) - place[2 * rows :]).reshape(1, rows)
    gain_attn, gain_moe = norm_gain_attn.reshape(1, D), norm_gain_moe.reshape(1, D)
    window = LONGEST + 256
    res_t = jnp.concatenate([gate_residual.T, jnp.zeros((4, rows), F32)], axis=0)
    wrc = jnp.concatenate([w_router.T, w_const.transpose(0, 2, 1).reshape(4, D)], axis=0)
    v8 = jnp.concatenate([v_const, jnp.zeros((6, D), F32)], axis=0)
    dma = lambda *shape: pltpu.SemaphoreType.DMA(shape)
    x1, x2, h, q, k, v, o, lse, xm, hp_all, g_all, gt, xl, dhl, sm, gv = call(
        functools.partial(forward_body, n_t),
        "forward",
        [(row, BF16), (row, BF16), (ext, BF16), (row, BF16), (ext, BF16), (ext, BF16), (row, BF16), ((SPARE, rows), F32),
         (row, F32), (every_packed, BF16), (every, BF16), ((8, rows), F32), (row, F32), (row, F32), ((SPARE, rows), F32), ((8, D), F32)],
        [x0, g0, w_attn, gain_attn, gain_moe, cos, sin, start, res_t, wrc, routes_t, v8],
        scratch=[pltpu.VMEM((window, 256), F32), dma(2), dma(2)] + [dma(3)] * 8,
        meet=0,
    )

    out_all, back_all, gw_ff = experts_call(counts, hp_all, g_all, slots, w_ff, ff)
    ff_sum = lax.psum_scatter(gw_ff, "dp", scatter_dimension=0, tiled=True)
    h2 = lax.dynamic_index_in_dim(hp_all, t, 0, keepdims=False)[0:rows]

    dx, da, dres, small, dq, dk, dv, result = call(
        functools.partial(backward_body, n_t),
        "backward",
        [(row, F32), (row, BF16), ((SPARE, rows), F32), ((SPARE + 8, D), F32), (row, BF16), (ext, BF16), (ext, BF16), (row, BF16)],
        [back_all, out_all, dhl, gt, sm, routes_t, wrc, xm, gain_moe, g0, h2, w_attn, o, gv, q, k, v, lse, start, cos, sin, xl],
        scratch=[pltpu.VMEM((rows // 256, window, 256), F32), pltpu.VMEM((3 * rows, 128), F32), pltpu.VMEM((3 * rows, 128), F32),
                 pltpu.VMEM((rows + SPARE, D), F32), pltpu.VMEM(row, BF16), pltpu.VMEM((SPARE, rows), F32)]
        + [pltpu.VMEM((n_t - 1, rows + SPARE, D), BF16)] * 2 + [pltpu.VMEM((n_t - 1, rows, D), BF16)] * 2
        + [dma(n_t - 1, 2)] * 4 + [dma(n_t - 1, 1)] * 4,
        meet=1,
    )
    back_out = lax.all_to_all(result, "dp", split_axis=0, concat_axis=0, tiled=True)
    gw_attn, gain_part, d_start = call(
        functools.partial(grads_body, n_t),
        "grads",
        [((D, 4 * D), BF16), ((8, D), F32), (row, BF16)],
        [x0, x1, x2, h, dq, dk, dv, da, o, w_attn, dx, gain_attn],
        scratch=[pltpu.VMEM(row, F32)] + [pltpu.VMEM(row, BF16)] * 4 + [dma(2), dma(2)],
        meet=2,
    )
    back_grad = lax.all_to_all(d_start, "dp", split_axis=0, concat_axis=0, tiled=True)
    output, grad_tokens = call(restore_body, "restore", [(row, BF16)] * 2, [pos, back_out, back_grad])

    def total(v):
        for axis, count in (("tensor", n_t), ("dp", n_dp)):
            bit = 1
            while bit < count:
                v = v + lax.ppermute(v, axis, [(i, i ^ bit) for i in range(count)])
                bit *= 2
        return v

    small_all = total(small)
    gain_all = total(gain_part[0:1])[0]
    attn_sum = lax.psum_scatter(gw_attn, "dp", scatter_dimension=0, tiled=True).reshape(d_here, 4, n_t, D // n_t)

    def share(j):
        return lax.dynamic_index_in_dim(attn_sum, t ^ j, 2, keepdims=False)

    attn_own = share(0).astype(F32)
    for j in range(1, n_t):
        attn_own = attn_own + swap(share(j), j).astype(F32)
    ff_own = ff_sum.reshape(d_here, EXPERTS, 3 * ff).astype(F32)
    return (
        output,
        grad_tokens,
        dres[0:12].T,
        attn_own[:, 0:3],
        attn_own[:, 3],
        ff_own[:, :, 0 : 2 * ff].reshape(d_here, EXPERTS, 2, ff),
        ff_own[:, :, 2 * ff :],
        gain_all,
        small_all[SPARE + 2],
        small_all[0:12].T,
        small_all[12:16].reshape(2, 2, D).transpose(0, 2, 1),
        small_all[SPARE : SPARE + 2],
    )


def solution(mesh):
    both, every = P(("dp", "tensor"), None), P()
    weights = (P("dp", None, "tensor"), P("dp", "tensor"), P("dp", None, None, "tensor"), P("dp", None, "tensor"))
    return jax.shard_map(
        body,
        mesh=mesh,
        in_specs=(both, both, P(("dp", "tensor")), P("dp", None), P("dp", None), both, *weights) + (every,) * 5,
        out_specs=(both, both, both, *weights) + (every,) * 5,
        check_vma=False,
    )
```

```python
import functools
import math

import jax
import jax.numpy as jnp
from jax import lax
from jax.experimental import pallas as pl
from jax.experimental.pallas import tpu as pltpu
from jax.sharding import PartitionSpec as P

D = 768
HEAD_DIM = 64
HEADS = 12
EXPERTS = 8
LONGEST = 1024
EPSILON = 1e-6
MASKED = -1e30
F32, BF16, I32 = jnp.float32, jnp.bfloat16, jnp.int32
NN = (((1,), (0,)), ((), ()))
NT = (((1,), (1,)), ((), ()))
TN = (((0,), (0,)), ((), ()))
SCORE_SCALE = HEAD_DIM**-0.5
LOG2E = 1.4426950408889634
TILE = 160
ROWS = 256
SPARE = 16
VMEM_CAP = 66_000_000


def mm(a, b, dims):
    return lax.dot_general(a, b, dims, preferred_element_type=F32)


def iota(shape, axis):
    return lax.broadcasted_iota(I32, shape, axis)


def pick(cond):
    return jnp.where(cond, 1.0, 0.0).astype(BF16)


def split2(v):
    high = v.astype(BF16)
    return high, (v - high.astype(F32)).astype(BF16)


def split3(v):
    high = v.astype(BF16)
    rest = v - high.astype(F32)
    mid = rest.astype(BF16)
    return high, mid, (rest - mid.astype(F32)).astype(BF16)


def vmem():
    return pl.BlockSpec(memory_space=pltpu.VMEM)


def smem():
    return pl.BlockSpec(memory_space=pltpu.SMEM)


def call(body, name, outs, operands, scalars=0, scratch=(), meet=None):
    return pl.pallas_call(
        body,
        name=name,
        out_shape=[jax.ShapeDtypeStruct(*o) for o in outs],
        in_specs=[smem()] * scalars + [vmem()] * (len(operands) - scalars),
        out_specs=[vmem()] * len(outs),
        scratch_shapes=list(scratch),
        compiler_params=pltpu.CompilerParams(
            vmem_limit_bytes=VMEM_CAP, collective_id=meet, has_side_effects=meet is not None
        ),
    )(*operands)


def deal_body(n_dp, deal_ref, tok_ref, cot_ref, routes_ref, xs_ref, gs_ref, pos_ref, slot_ref, cnt_ref):
    rows = tok_ref.shape[0]
    first, second = iota((rows, rows), 0), iota((rows, rows), 1)
    before = pick(first < second)
    deal = deal_ref[...]
    hit = iota((n_dp, rows), 0) == deal
    rank = mm(pick(hit), before, NN)
    rank = jnp.sum(jnp.where(hit, rank, 0.0), axis=0, keepdims=True).astype(I32)
    pos = deal * (rows // n_dp) + rank
    pos_ref[...] = pos
    place = pick(first == pos)
    xs_ref[...] = mm(place, tok_ref[...], NN).astype(BF16)
    gs_ref[...] = mm(place, cot_ref[...], NN).astype(BF16)
    expert = iota((EXPERTS, rows), 0)
    for j in range(routes_ref.shape[0]):
        route = routes_ref[j]
        named = (expert == route[0:1]) | (expert == route[1:2])
        ahead = mm(pick(named), before, NN).astype(I32)
        slot_ref[j] = jnp.where(named, ahead, -1)
        total = jnp.sum(jnp.where(named, 1.0, 0.0), axis=1, keepdims=True).astype(I32)
        cnt_ref[j] = jnp.broadcast_to(total, (EXPERTS, 128))


def restore_body(pos_ref, a_ref, b_ref, oa_ref, ob_ref):
    rows = a_ref.shape[0]
    place = pick(iota((rows, rows), 0) == pos_ref[...])
    oa_ref[...] = mm(place, a_ref[...], TN).astype(BF16)
    ob_ref[...] = mm(place, b_ref[...], TN).astype(BF16)


class Line:
    def __init__(self, size):
        self.size = size
        self.place = lax.axis_index("tensor")
        self.sent = {k: [] for k in range(size)}

    def each(self, body):
        for k in range(self.size):
            pl.when(self.place == k)(functools.partial(body, k))

    def enter(self):
        sem = pltpu.get_barrier_semaphore()

        def greet(k):
            near = [n for n in (k - 1, k + 1) if 0 <= n < self.size]
            for n in near:
                pl.semaphore_signal(sem, 1, device_id={"tensor": self.place + (n - k)}, device_id_type=pl.DeviceIdType.MESH)
            pl.semaphore_wait(sem, len(near))

        self.each(greet)

    def copy(self, hop, src, dst, sems):
        return pltpu.make_async_remote_copy(
            src_ref=src,
            dst_ref=dst,
            send_sem=sems[0],
            recv_sem=sems[1],
            device_id={"tensor": self.place + hop},
            device_id_type=pl.DeviceIdType.MESH,
        )

    def send(self, k, to, refs):
        self.copy(to - k, *refs()).start()
        self.sent[k].append((to - k, refs))

    def arrived(self, k, dst, sems):
        self.copy((k ^ 1) - k, dst, dst, sems).wait_recv()

    def leave(self):
        def drain(k):
            for hop, refs in self.sent[k]:
                self.copy(hop, *refs()).wait_send()

        self.each(drain)


def sum_events(size, k):
    events = []
    for dest in range(size):
        if dest >= k and dest > 0:
            events.append((0 if k == 0 else size - 1 - dest + k, 1, dest))
        if dest <= k and dest < size - 1:
            events.append((0 if k == size - 1 else dest + size - 1 - k, -1, dest))
    drop = [(t, w, d) for t, w, d in events if (k == 0 and w == 1 and d == 0) or (k == size - 1 and w == -1 and d == k)]
    return sorted((ev for ev in events if ev not in drop), key=lambda ev: (ev[0], ev[1], -ev[1] * ev[2]))


def turn(u):
    low = (iota((1, u.shape[1]), 1) % HEAD_DIM) < HEAD_DIM // 2
    half = HEAD_DIM // 2
    return jnp.where(low, pltpu.roll(u, u.shape[1] - half, 1), pltpu.roll(u, half, 1))


def wide(table):
    return jnp.concatenate([table] * (D // 128), axis=1)


def key_bias(start, block, first_row, base):
    window = LONGEST + block
    key = iota((window, block), 0) + first_row
    row = iota((1, block), 1) + (base + first_row)
    return jnp.where((key >= start) & (key <= row), 0.0, MASKED)


def router_part(route, o_ref, w_ref, x_ref, gain_ref, res_ref, wrc_ref, x1_ref, hp_ref, gt_ref):
    rows = o_ref.shape[0]
    x1 = x_ref[...].astype(F32) + mm(o_ref[...], w_ref[:, 3 * D : 4 * D], NT)
    x1_ref[...] = x1
    h = x1 * lax.rsqrt(jnp.mean(x1 * x1, axis=1, keepdims=True) + EPSILON) * gain_ref[...]
    h = h.astype(BF16)
    hp_ref[0:rows, :] = h
    high, mid, low = split3(wrc_ref[...])
    z = mm(low, h, NT) + mm(mid, h, NT) + mm(high, h, NT) + res_ref[...]
    expert = iota(z.shape, 0)
    named0, named1 = expert == route[0:1], expert == route[1:2]
    c0 = jnp.sum(jnp.where(named0, z, 0.0), axis=0, keepdims=True)
    c1 = jnp.sum(jnp.where(named1, z, 0.0), axis=0, keepdims=True)
    top = jnp.maximum(c0, c1)
    e0, e1 = jnp.exp(c0 - top), jnp.exp(c1 - top)
    g0, g1 = e0 / (e0 + e1), e1 / (e0 + e1)
    table = [g0, g1]
    for j in range(2):
        l0, l1 = z[12 + 2 * j : 13 + 2 * j], z[13 + 2 * j : 14 + 2 * j]
        top = jnp.maximum(l0, l1)
        m0, m1 = jnp.exp(l0 - top), jnp.exp(l1 - top)
        table += [m0 / (m0 + m1), m1 / (m0 + m1)]
    gt_ref[...] = jnp.concatenate(table + [jnp.zeros((2, rows), F32)], axis=0)
    gates = jnp.where(named0, g0, jnp.where(named1, g1, 0.0))
    gates = jnp.where(expert < EXPERTS, gates, 0.0)
    hp_ref[rows : rows + SPARE, :] = jnp.concatenate([gates, jnp.zeros((SPARE, D - rows), F32)], axis=1).astype(BF16)


def local_part(route, x1_ref, hp_ref, g_ref, gt_ref, v_ref, xl_ref, dhl_ref, sm_ref, gv_ref):
    rows = x1_ref.shape[0]
    h, g = hp_ref[0:rows, :], g_ref[...]
    hf, gf = h.astype(F32), g.astype(F32)
    low0 = gt_ref[0:1].astype(BF16).astype(F32)
    low1 = gt_ref[1:2].astype(BF16).astype(F32)

    def weight(e):
        return jnp.where(route[0:1] == e, low0, 0.0) + jnp.where(route[1:2] == e, low1, 0.0)

    copy, first, second = weight(EXPERTS + 1), weight(EXPERTS + 2), weight(EXPERTS + 3)
    m00, m01, m10, m11 = gt_ref[2:3], gt_ref[3:4], gt_ref[4:5], gt_ref[5:6]
    a = copy + first * m00 + second * m10
    b0, b1 = first * m01, second * m11
    table = jnp.concatenate([a, b0, b1, jnp.zeros((125, rows), F32)], axis=0).T
    ac, b0c, b1c = table[:, 0:1], table[:, 1:2], table[:, 2:3]
    v = v_ref[...]
    xl_ref[...] = x1_ref[...] + ac * hf + b0c * v[0:1] + b1c * v[1:2]
    dhl_ref[...] = ac * gf
    ones = jnp.ones((8, D), BF16)
    high, low = split2(hf * gf)
    gh = (mm(ones, high, NT) + mm(ones, low, NT))[0:1]
    vh, vm, vl = split3(v)
    gvs = mm(vl, g, NT) + mm(vm, g, NT) + mm(vh, g, NT)
    gv0, gv1 = gvs[0:1], gvs[1:2]
    zero = jnp.zeros((9, rows), F32)
    dl0 = first * m00 * m01 * (gh - gv0)
    dl1 = second * m10 * m11 * (gh - gv1)
    sm_ref[...] = jnp.concatenate(
        [zero, gh, m00 * gh + m01 * gv0, m10 * gh + m11 * gv1, dl0, -dl0, dl1, -dl1], axis=0
    )
    bh, bm, bl = split3(jnp.concatenate([b0, b1, jnp.zeros((6, rows), F32)], axis=0))
    gv_ref[...] = mm(bl, g, NN) + mm(bm, g, NN) + mm(bh, g, NN)


def forward_body(size, x0_ref, g0_ref, w_ref, gain_ref, gain2_ref, cos_ref, sin_ref, start_ref, res_ref, wrc_ref, routes_ref, v8_ref,
                 x1_ref, x2_ref, h_ref, q_ref, k_ref, v_ref, o_ref, lse_ref, xm_ref, hp_ref, gall_ref, gt_ref, xl_ref,
                 dhl_ref, sm_ref, gv_ref,
                 bias_ref, sx, rx, sgu, rgu, sgd, rgd, shu, rhu, shd, rhd):
    rows = x0_ref.shape[0]
    step = 256
    line = Line(size)
    t = line.place
    last = size - 1
    line.enter()

    def begin(k):
        if k < last:
            line.send(k, k + 1, lambda: (x0_ref, x1_ref, (sx.at[0], rx.at[0])))
        if k > 0:
            line.send(k, k - 1, lambda: (g0_ref, gall_ref.at[k], (sgd.at[0], rgd.at[0])))

    line.each(begin)
    gain = gain_ref[...]

    def project_chunk(c, x_ref):
        def project(i, _):
            at = pl.multiple_of(i * step, step)
            x = x_ref[pl.ds(at, step), :].astype(F32)
            h = x * lax.rsqrt(jnp.mean(x * x, axis=1, keepdims=True) + EPSILON) * gain
            h = h.astype(BF16)
            to = pl.ds(pl.multiple_of(c * rows + i * step, step), step)
            h_ref[to, :] = h
            cos, sin = wide(cos_ref[to, :]), wide(sin_ref[to, :])
            k = mm(h, w_ref[:, D : 2 * D], NN)
            k_ref[to, :] = (k * cos + turn(k) * sin).astype(BF16)
            v_ref[to, :] = mm(h, w_ref[:, 2 * D : 3 * D], NN).astype(BF16)
            if c == 2:
                q = mm(h, w_ref[:, 0:D], NN)
                q_ref[pl.ds(at, step), :] = (q * cos + turn(q) * sin).astype(BF16)
            return 0

        lax.fori_loop(0, rows // step, project, 0)

    project_chunk(2, x0_ref)
    gall_ref[t] = g0_ref[...]

    def second(k):
        if k > 0:
            line.arrived(k, x1_ref, (sx.at[0], rx.at[0]))
        else:
            x1_ref[...] = jnp.zeros_like(x1_ref)
        if 0 < k < last:
            line.send(k, k + 1, lambda: (x1_ref, x2_ref, (sx.at[1], rx.at[1])))
        if k < last:
            line.send(k, k + 1, lambda: (g0_ref, gall_ref.at[k], (sgu.at[0], rgu.at[0])))
            line.arrived(k, gall_ref.at[k + 1], (sgd.at[0], rgd.at[0]))
            if k > 0:
                line.send(k, k - 1, lambda: (gall_ref.at[k + 1], gall_ref.at[k + 1], (sgd.at[1], rgd.at[1])))

    line.each(second)
    project_chunk(1, x1_ref)

    def third(k):
        if k > 1:
            line.arrived(k, x2_ref, (sx.at[1], rx.at[1]))
        else:
            x2_ref[...] = jnp.zeros_like(x2_ref)
        if k + 2 <= last:
            line.arrived(k, gall_ref.at[k + 2], (sgd.at[1], rgd.at[1]))
            if k > 0:
                line.send(k, k - 1, lambda: (gall_ref.at[k + 2], gall_ref.at[k + 2], (sgd.at[2], rgd.at[2])))

    line.each(third)
    project_chunk(0, x2_ref)

    block = step
    window = LONGEST + block
    lane = iota((1, 128), 1) // HEAD_DIM
    for rb in range(rows // block):
        first = rb * block
        bias_ref[...] = key_bias(start_ref[:, first : first + block], block, first, LONGEST)

        def pair(i, _, first=first):
            lanes = pl.ds(pl.multiple_of(i * 128, 128), 128)
            k = k_ref[first : first + window, lanes]
            vt = v_ref[first : first + window, lanes].T
            q = q_ref[first : first + block, lanes]
            parts = []
            for half in range(2):
                qm = jnp.where(lane == half, q, jnp.zeros_like(q))
                s = mm(k, qm, NT) * (SCORE_SCALE * LOG2E) + bias_ref[...]
                top = jnp.max(s, axis=0, keepdims=True)
                p = jnp.exp2(s - top)
                total = jnp.sum(p, axis=0, keepdims=True)
                out = mm(vt[half * HEAD_DIM : (half + 1) * HEAD_DIM], p.astype(BF16), NN)
                parts.append(out * (1.0 / total))
                lse_ref[pl.ds(i * 2 + half, 1), first : first + block] = top + jnp.log2(total)
            o_ref[first : first + block, lanes] = jnp.concatenate(parts, axis=0).T.astype(BF16)
            return 0

        lax.fori_loop(0, HEADS // 2, pair, 0)
        if rb == 0:
            def fourth(k):
                if k > 0:
                    line.arrived(k, gall_ref.at[k - 1], (sgu.at[0], rgu.at[0]))
                    if k < last:
                        line.send(k, k + 1, lambda: (gall_ref.at[k - 1], gall_ref.at[k - 1], (sgu.at[1], rgu.at[1])))

            line.each(fourth)

    route = routes_ref[t]
    router_part(route, o_ref, w_ref, x0_ref, gain2_ref, res_ref, wrc_ref, xm_ref, hp_ref.at[t], gt_ref)

    def fifth(k):
        if k < last:
            line.send(k, k + 1, lambda: (hp_ref.at[k], hp_ref.at[k], (shu.at[0], rhu.at[0])))
        if k > 0:
            line.send(k, k - 1, lambda: (hp_ref.at[k], hp_ref.at[k], (shd.at[0], rhd.at[0])))
        if k > 1:
            line.arrived(k, gall_ref.at[k - 2], (sgu.at[1], rgu.at[1]))
            if k < last:
                line.send(k, k + 1, lambda: (gall_ref.at[k - 2], gall_ref.at[k - 2], (sgu.at[2], rgu.at[2])))

    line.each(fifth)
    local_part(route, xm_ref, hp_ref.at[t], g0_ref, gt_ref, v8_ref, xl_ref, dhl_ref, sm_ref, gv_ref)

    def sixth(k):
        for hop in range(2):
            up, down = k - 1 - hop, k + 1 + hop
            if up >= 0:
                line.arrived(k, hp_ref.at[up], (shu.at[hop], rhu.at[hop]))
                if k < last:
                    line.send(k, k + 1, lambda up=up, hop=hop: (hp_ref.at[up], hp_ref.at[up], (shu.at[hop + 1], rhu.at[hop + 1])))
            if down <= last:
                line.arrived(k, hp_ref.at[down], (shd.at[hop], rhd.at[hop]))
                if k > 0:
                    line.send(k, k - 1, lambda down=down, hop=hop: (hp_ref.at[down], hp_ref.at[down], (shd.at[hop + 1], rhd.at[hop + 1])))
        if k == last:
            line.arrived(k, hp_ref.at[0], (shu.at[2], rhu.at[2]))
            line.arrived(k, gall_ref.at[0], (sgu.at[2], rgu.at[2]))
        if k == 0:
            line.arrived(k, hp_ref.at[last], (shd.at[2], rhd.at[2]))
            line.arrived(k, gall_ref.at[last], (sgd.at[2], rgd.at[2]))

    line.each(sixth)
    line.leave()


def middle_part(route, dh_ref, gt_ref, sm_ref, wrc_ref, x1_ref, gain_ref, g_ref, h2_ref, w_ref, o_ref, gv_ref,
                dx_ref, da_ref, do_ref, delta_ref, dres_ref, small_ref):
    rows = x1_ref.shape[0]
    dgf = dh_ref[rows : rows + SPARE, 0:rows]
    dh = dh_ref[0:rows, :]
    dgate = jnp.concatenate([dgf[0:EXPERTS] + dgf[EXPERTS:], sm_ref[EXPERTS:SPARE]], axis=0)
    expert = iota((SPARE, rows), 0)
    named0, named1 = expert == route[0:1], expert == route[1:2]
    g0, g1 = gt_ref[0:1], gt_ref[1:2]
    d0 = jnp.sum(jnp.where(named0, dgate, 0.0), axis=0, keepdims=True)
    d1 = jnp.sum(jnp.where(named1, dgate, 0.0), axis=0, keepdims=True)
    inner = g0 * d0 + g1 * d1
    dz = jnp.where(named0, g0 * (d0 - inner), jnp.where(named1, g1 * (d1 - inner), 0.0))
    dres_ref[...] = dz
    dz = jnp.where(expert < 12, dz, sm_ref[...])
    zh, zm, zl = split3(dz)
    wh, wm, wl = split3(wrc_ref[...])
    dh = dh + (mm(zh, wl, TN) + mm(zl, wh, TN) + mm(zm, wm, TN) + mm(zh, wm, TN) + mm(zm, wh, TN) + mm(zh, wh, TN))
    h = h2_ref[...]
    small_ref[0:SPARE, :] = mm(zl, h, NN) + mm(zm, h, NN) + mm(zh, h, NN)
    x1 = x1_ref[...]
    r = lax.rsqrt(jnp.mean(x1 * x1, axis=1, keepdims=True) + EPSILON)
    xr = x1 * r
    grad_gain = jnp.sum(dh * xr, axis=0, keepdims=True)
    gv = gv_ref[...]
    small_ref[SPARE : SPARE + 8, :] = jnp.concatenate([gv[0:2], grad_gain, gv[3:8]], axis=0)
    scaled = dh * gain_ref[...]
    dx = g_ref[...].astype(F32) + r * (scaled - xr * jnp.mean(xr * scaled, axis=1, keepdims=True))
    dx_ref[...] = dx
    da = dx.astype(BF16)
    da_ref[...] = da
    do = mm(da, w_ref[:, 3 * D : 4 * D], NN).astype(BF16)
    do_ref[...] = do
    high, low = split2(do.astype(F32) * o_ref[...].astype(F32))
    heads = pick(iota((SPARE, D), 1) // HEAD_DIM == iota((SPARE, D), 0))
    delta_ref[...] = mm(heads, high, NT) + mm(heads, low, NT)


def backward_body(size, back_ref, out_ref, dhl_ref, gt_ref, sm_ref, routes_ref, wrc_ref, xm_ref, gain_ref, g_ref, h2_ref, w_ref,
                  o_ref, gv_ref, q_ref, k_ref, v_ref, lse_ref, start_ref, cos_ref, sin_ref, xl_ref,
                  dx_ref, da_ref, dres_ref, small_ref, dq_ref, dk_ref, dv_ref, y_ref,
                  bias_ref, dkf_ref, dvf_ref, dh_ref, do_ref, delta_ref, bu_ref, bd_ref, fu_ref, fd_ref,
                  sbu, rbu, sbd, rbd, sfu, rfu, sfd, rfd):
    rows = xm_ref.shape[0]
    packed = rows + SPARE
    cut = 272
    pieces = (slice(0, cut), slice(cut, packed))
    line = Line(size)
    t = line.place
    last = size - 1
    line.enter()

    def handle(k, way, dest, part, index, mine_ref, up_ref, down_ref, ups, downs):
        slot = dest - 1 if way == 1 else dest
        first = k == (0 if way == 1 else last)
        mine = mine_ref.at[dest, part]

        def refs():
            held = (up_ref if way == 1 else down_ref).at[slot, part]
            sems = tuple(s.at[slot, index] for s in (ups if way == 1 else downs))
            return mine_ref.at[dest, part] if first else held, held, sems

        _, held, sems = refs()
        if not first:
            line.arrived(k, held, sems)
        if dest != k:
            if not first:
                held[...] = (held[...].astype(F32) + mine[...].astype(F32)).astype(BF16)
            line.send(k, k + way, refs)

    def sum_back(k):
        for _, way, dest in sum_events(size, k):
            for index, part in enumerate(pieces):
                handle(k, way, dest, part, index, back_ref, bu_ref, bd_ref, (sbu, rbu), (sbd, rbd))

    def sum_out(k, now):
        for time, way, dest in sum_events(size, k):
            if time == now:
                handle(k, way, dest, slice(0, rows), 0, out_ref, fu_ref, fd_ref, (sfu, rfu), (sfd, rfd))

    line.each(sum_back)
    line.each(lambda k: sum_out(k, 0))
    dh_ref[...] = back_ref[t].astype(F32)

    @pl.when(t > 0)
    def _():
        dh_ref[...] += bu_ref[t - 1].astype(F32)

    @pl.when(t < last)
    def _():
        dh_ref[...] += bd_ref[t].astype(F32)

    dh_ref[0:rows, :] += dhl_ref[...]
    middle_part(routes_ref[t], dh_ref, gt_ref, sm_ref, wrc_ref, xm_ref, gain_ref, g_ref, h2_ref, w_ref, o_ref, gv_ref,
                dx_ref, da_ref, do_ref, delta_ref, dres_ref, small_ref)
    line.each(lambda k: sum_out(k, 1))

    block = 256
    window = LONGEST + block
    lane = iota((1, 128), 1) // HEAD_DIM
    for rb in range(rows // block):
        first = rb * block
        bias_ref[rb] = key_bias(start_ref[:, first : first + block], block, first, LONGEST)

    def pair(i, _):
        lanes = pl.ds(pl.multiple_of(i * 128, 128), 128)
        for rb in range(rows // block):
            first = rb * block
            k = k_ref[first : first + window, lanes]
            v = v_ref[first : first + window, lanes]
            kt = k.T
            q = q_ref[first : first + block, lanes]
            do = do_ref[first : first + block, lanes]
            dk = jnp.zeros((window, 128), F32)
            dv = jnp.zeros((window, 128), F32)
            parts = []
            for half in range(2):
                qm = jnp.where(lane == half, q, jnp.zeros_like(q))
                dom = jnp.where(lane == half, do, jnp.zeros_like(do))
                head = pl.ds(i * 2 + half, 1)
                s = mm(k, qm, NT) * (SCORE_SCALE * LOG2E) + bias_ref[rb]
                p = jnp.exp2(s - lse_ref[head, first : first + block])
                dp = mm(v, dom, NT)
                ds = (p * (dp - delta_ref[head, first : first + block])).astype(BF16)
                dv = dv + mm(p.astype(BF16), dom, NN)
                dk = dk + mm(ds, qm, NN)
                parts.append(mm(kt[half * HEAD_DIM : (half + 1) * HEAD_DIM], ds, NN))
            dq = jnp.concatenate(parts, axis=0).T * SCORE_SCALE
            at = slice(2 * rows + first, 2 * rows + first + block)
            dq_ref[first : first + block, lanes] = (dq * cos_ref[at, :] - turn(dq) * sin_ref[at, :]).astype(BF16)
            if first == 0:
                dkf_ref[0:window, :] = dk
                dvf_ref[0:window, :] = dv
            else:
                old = window - block
                dkf_ref[first : first + old, :] += dk[0:old]
                dvf_ref[first : first + old, :] += dv[0:old]
                dkf_ref[first + old : first + window, :] = dk[old:]
                dvf_ref[first + old : first + window, :] = dv[old:]
        dk = dkf_ref[...] * SCORE_SCALE
        dk_ref[:, lanes] = (dk * cos_ref[...] - turn(dk) * sin_ref[...]).astype(BF16)
        dv_ref[:, lanes] = dvf_ref[...].astype(BF16)
        return 0

    lax.fori_loop(0, HEADS // 4, pair, 0)
    line.each(lambda k: sum_out(k, 2))
    lax.fori_loop(HEADS // 4, HEADS // 2, pair, 0)
    line.each(lambda k: sum_out(k, 3))
    xl_ref[...] += out_ref[t].astype(F32)

    @pl.when(t > 0)
    def _():
        xl_ref[...] += fu_ref[t - 1].astype(F32)

    @pl.when(t < last)
    def _():
        xl_ref[...] += fd_ref[t].astype(F32)

    y_ref[...] = xl_ref[...].astype(BF16)
    line.leave()


def grads_body(size, x0_ref, x1_ref, x2_ref, h_ref, dq_ref, dk_ref, dv_ref, da_ref, o_ref, w_ref, dx_ref, gain_ref,
               gw_ref, gpart_ref, out_ref, d0_ref, d1_ref, d2_ref, ra_ref, rb_ref, sems_s, sems_r):
    rows = x0_ref.shape[0]
    line = Line(size)
    last = size - 1
    block = 256
    line.enter()

    def hidden(c, d_ref):
        def one(i, _):
            at = pl.ds(pl.multiple_of(i * block, block), block)
            to = pl.ds(pl.multiple_of(c * rows + i * block, block), block)
            total = mm(dk_ref[to, :], w_ref[:, D : 2 * D], NT) + mm(dv_ref[to, :], w_ref[:, 2 * D : 3 * D], NT)
            if c == 2:
                total = total + mm(dq_ref[at, :], w_ref[:, 0:D], NT)
            d_ref[at, :] = total.astype(d_ref.dtype)
            return 0

        lax.fori_loop(0, rows // block, one, 0)

    def gain_of(x_ref, d_ref):
        x = x_ref[...].astype(F32)
        r = lax.rsqrt(jnp.mean(x * x, axis=1, keepdims=True) + EPSILON)
        return jnp.sum(d_ref[...].astype(F32) * x * r, axis=0, keepdims=True)

    hidden(0, d2_ref)

    def first(k):
        if k > 1:
            line.send(k, k - 1, lambda: (d2_ref, ra_ref, (sems_s.at[0], sems_r.at[0])))

    line.each(first)
    hidden(1, d1_ref)
    gain = gain_of(x2_ref, d2_ref) + gain_of(x1_ref, d1_ref)
    h = h_ref[...]

    def weight(column, left, right_ref):
        for c in range(D // 256):
            cols = slice(c * 256, (c + 1) * 256)
            gw_ref[:, column * D + c * 256 : column * D + c * 256 + 256] = mm(left, right_ref[:, cols], TN).astype(BF16)

    weight(1, h, dk_ref)

    def second(k):
        if 0 < k < last:
            line.arrived(k, ra_ref, (sems_s.at[0], sems_r.at[0]))
            d1_ref[...] = (d1_ref[...].astype(F32) + ra_ref[...].astype(F32)).astype(BF16)
        if k > 0:
            line.send(k, k - 1, lambda: (d1_ref, rb_ref, (sems_s.at[1], sems_r.at[1])))

    line.each(second)
    hidden(2, d0_ref)
    gpart_ref[...] = jnp.broadcast_to(gain + gain_of(x0_ref, d0_ref), (8, D))
    weight(2, h, dv_ref)
    weight(0, h[2 * rows :], dq_ref)
    weight(3, da_ref[...], o_ref)

    def third(k):
        if k < last:
            line.arrived(k, rb_ref, (sems_s.at[1], sems_r.at[1]))
            d0_ref[...] += rb_ref[...].astype(F32)

    line.each(third)
    x = x0_ref[...].astype(F32)
    r = lax.rsqrt(jnp.mean(x * x, axis=1, keepdims=True) + EPSILON)
    xr = x * r
    scaled = d0_ref[...] * gain_ref[...]
    out_ref[...] = (dx_ref[...] + r * (scaled - xr * jnp.mean(xr * scaled, axis=1, keepdims=True))).astype(BF16)
    line.leave()


def experts_body(ff, chunks, cnt_ref, h_refs, g_refs, slot_ref, w_ref, o_refs, d_refs, gw_ref,
                 xbuf, gbuf, cbuf, onehot, fbuf, dbuf, gacc, gates, dgrow, off_ref, base_ref, nt_ref):
    rows = slot_ref.shape[2]
    e = pl.program_id(0)

    def match(j, expert, tile):
        slots = slot_ref[j, pl.ds(expert, 1), :]
        return (iota((TILE, rows), 0) + tile * TILE) == slots

    def store_rows(at, count, hit, x, gs, gate_row):
        to = pl.ds(pl.multiple_of(at, 16), TILE)
        keep = iota((TILE, 1), 0) < count
        col = jnp.sum(jnp.where(hit, gate_row, 0.0), axis=1, keepdims=True)
        xbuf[to, :] = jnp.where(keep, x, xbuf[to, :].astype(F32)).astype(BF16)
        gbuf[to, :] = jnp.where(keep, gs, gbuf[to, :].astype(F32)).astype(BF16)
        cbuf[to, :] = jnp.where(keep, jnp.broadcast_to(col, (TILE, 128)), cbuf[to, :])

    def round16(n):
        return ((n + 15) // 16) * 16

    @pl.when(e == 0)
    def _gather():
        at = jnp.int32(0)
        for ex in range(EXPERTS):
            base_ref[ex] = at
            here = at
            for j in range(chunks):
                off_ref[j * EXPERTS + ex] = here
                here = here + round16(cnt_ref[j * EXPERTS + ex])
            tiles = (here - at + (ROWS - 1)) // ROWS
            nt_ref[ex] = tiles
            tail = pl.ds(pl.multiple_of(here, 16), ROWS)
            xbuf[tail, :] = jnp.zeros((ROWS, D), BF16)
            gbuf[tail, :] = jnp.zeros((ROWS, D), BF16)
            cbuf[tail, :] = jnp.zeros((ROWS, 128), F32)
            at = at + tiles * ROWS
        for j in range(chunks):
            gates[...] = h_refs[j, rows : rows + SPARE, 0:rows].astype(F32)

            def two(i, _, j=j):
                hits = [match(j, 2 * i + half, 0) for half in range(2)]
                sel = jnp.concatenate([pick(hit) for hit in hits], axis=0)
                x = mm(sel, h_refs[j, 0:rows, :], NN)
                gs = mm(sel, g_refs[j], NN)
                for half in range(2):
                    ex = 2 * i + half
                    count = round16(jnp.minimum(cnt_ref[j * EXPERTS + ex], TILE))
                    part = slice(half * TILE, (half + 1) * TILE)
                    store_rows(off_ref[j * EXPERTS + ex], count, hits[half], x[part], gs[part], gates[pl.ds(ex, 1), :])
                return 0

            lax.fori_loop(0, EXPERTS // 2, two, 0)

            def rare(ex, _, j=j):
                def more(tile, _):
                    hit = match(j, ex, tile)
                    sel = pick(hit)
                    count = round16(jnp.minimum(cnt_ref[j * EXPERTS + ex] - tile * TILE, TILE))
                    store_rows(
                        off_ref[j * EXPERTS + ex] + tile * TILE,
                        count,
                        hit,
                        mm(sel, h_refs[j, 0:rows, :], NN),
                        mm(sel, g_refs[j], NN),
                        gates[pl.ds(ex, 1), :],
                    )
                    return 0

                return lax.fori_loop(1, (cnt_ref[j * EXPERTS + ex] + (TILE - 1)) // TILE, more, 0)

            lax.fori_loop(0, EXPERTS, rare, 0)

    gacc[...] = jnp.zeros_like(gacc)

    def tile_step(m, _):
        at = pl.ds(pl.multiple_of(base_ref[e] + m * ROWS, 16), ROWS)
        x = xbuf[at, :]
        gs = gbuf[at, :].astype(F32)
        gate = wide(cbuf[at, :])
        u = mm(x, w_ref[:, 0:ff], NN)
        up = mm(x, w_ref[:, ff : 2 * ff], NN)
        sig = jax.nn.sigmoid(u)
        silu = u * sig
        act = (silu * up).astype(BF16)
        f = mm(act, w_ref[:, 2 * ff : 3 * ff], NT)
        cbuf[at, :] = jnp.broadcast_to(jnp.sum(gs * f, axis=1, keepdims=True), (ROWS, 128))
        gbuf[at, :] = (f * gate).astype(BF16)
        df = (gs * gate).astype(BF16)
        dact = mm(df, w_ref[:, 2 * ff : 3 * ff], NN)
        dup = (dact * silu).astype(BF16)
        du = (dact * up * sig * (1.0 + u * (1.0 - sig))).astype(BF16)
        xbuf[at, :] = (mm(du, w_ref[:, 0:ff], NT) + mm(dup, w_ref[:, ff : 2 * ff], NT)).astype(BF16)
        gacc[:, 0:ff] += mm(x, du, TN)
        gacc[:, ff : 2 * ff] += mm(x, dup, TN)
        gacc[:, 2 * ff : 3 * ff] += mm(df, act, TN)
        return 0

    lax.fori_loop(0, nt_ref[e], tile_step, 0)
    gw_ref[...] = gacc[...].astype(BF16)

    @pl.when(e == EXPERTS - 1)
    def _scatter():
        for j in range(chunks):
            def take(ex, _, j=j):
                at = pl.ds(pl.multiple_of(off_ref[j * EXPERTS + ex], 16), TILE)
                to = pl.ds(pl.multiple_of(ex * TILE, 16), TILE)
                hit = match(j, ex, 0)
                onehot[to, :] = pick(hit)
                fbuf[to, :] = gbuf[at, :]
                dbuf[to, :] = xbuf[at, :]
                col = jnp.concatenate([cbuf[at, :]] * (rows // 128), axis=1)
                dgrow[pl.ds(ex, 1), :] = jnp.sum(jnp.where(hit, col, 0.0), axis=0, keepdims=True)
                return 0

            lax.fori_loop(0, EXPERTS, take, 0)
            gacc[0:rows, 0:D] = mm(onehot[...], fbuf[...], TN)
            gacc[0:rows, D : 2 * D] = mm(onehot[...], dbuf[...], TN)

            def rare(ex, _, j=j):
                def more(tile, _):
                    at = pl.ds(pl.multiple_of(off_ref[j * EXPERTS + ex] + tile * TILE, 16), TILE)
                    hit = match(j, ex, tile)
                    sel = pick(hit)
                    gacc[0:rows, 0:D] += mm(sel, gbuf[at, :], TN)
                    gacc[0:rows, D : 2 * D] += mm(sel, xbuf[at, :], TN)
                    col = jnp.concatenate([cbuf[at, :]] * (rows // 128), axis=1)
                    dgrow[pl.ds(ex, 1), :] += jnp.sum(jnp.where(hit, col, 0.0), axis=0, keepdims=True)
                    return 0

                return lax.fori_loop(1, (cnt_ref[j * EXPERTS + ex] + (TILE - 1)) // TILE, more, 0)

            lax.fori_loop(0, EXPERTS, rare, 0)
            o_refs[j] = gacc[0:rows, 0:D].astype(BF16)
            d_refs[j, 0:rows, :] = gacc[0:rows, D : 2 * D].astype(BF16)
            total = dgrow[...]
            high = total.astype(BF16).astype(F32)
            both = jnp.concatenate([high, total - high], axis=0)
            d_refs[j, rows : rows + SPARE, :] = jnp.concatenate(
                [both, jnp.zeros((SPARE, D - rows), F32)], axis=1
            ).astype(BF16)


def experts_call(counts, hs, gs, slots, weights, ff):
    chunks, rows = gs.shape[:2]
    width = 3 * ff
    most = (rows + 15 * chunks + ROWS - 1) // ROWS * ROWS * EXPERTS + ROWS
    whole = lambda shape: pl.BlockSpec(shape, lambda e: (0,) * len(shape), pipeline_mode=pl.Buffered(1))
    return pl.pallas_call(
        functools.partial(experts_body, ff, chunks),
        name="experts",
        grid=(EXPERTS,),
        in_specs=[smem(), whole(hs.shape), whole(gs.shape), whole(slots.shape), pl.BlockSpec((D, width), lambda e: (0, e))],
        out_specs=[whole(gs.shape), whole(hs.shape), pl.BlockSpec((D, width), lambda e: (0, e))],
        out_shape=[
            jax.ShapeDtypeStruct(gs.shape, BF16),
            jax.ShapeDtypeStruct(hs.shape, BF16),
            jax.ShapeDtypeStruct((D, EXPERTS * width), BF16),
        ],
        scratch_shapes=[
            pltpu.VMEM((most, D), BF16),
            pltpu.VMEM((most, D), BF16),
            pltpu.VMEM((most, 128), F32),
            pltpu.VMEM((EXPERTS * TILE, rows), BF16),
            pltpu.VMEM((EXPERTS * TILE, D), BF16),
            pltpu.VMEM((EXPERTS * TILE, D), BF16),
            pltpu.VMEM((D, width), F32),
            pltpu.VMEM((SPARE, rows), F32),
            pltpu.VMEM((EXPERTS, rows), F32),
            pltpu.SMEM((chunks * EXPERTS,), I32),
            pltpu.SMEM((EXPERTS,), I32),
            pltpu.SMEM((EXPERTS,), I32),
        ],
        compiler_params=pltpu.CompilerParams(
            dimension_semantics=("arbitrary",), vmem_limit_bytes=VMEM_CAP
        ),
    )(counts, hs, gs, slots, weights)


def rope_tables(lengths, first, count):
    finish = jnp.sum(jnp.where(jnp.arange(lengths.shape[0])[:, None] <= jnp.arange(lengths.shape[0])[None, :], lengths[:, None], 0), axis=0)
    begins = finish - lengths
    rows = first + jnp.arange(count, dtype=I32)
    opening = jnp.max(jnp.where(begins[None, :] <= rows[:, None], begins[None, :], 0), axis=1)
    place = rows - opening
    half = HEAD_DIM // 2
    rates = jnp.exp(jnp.arange(half, dtype=F32) * (-2.0 * math.log(10000.0) / HEAD_DIM))
    angles = place.astype(F32)[:, None] * rates[None, :]
    cos, sin = jnp.cos(angles), jnp.sin(angles)
    return place, jnp.concatenate([cos] * 4, axis=1), jnp.concatenate([-sin, sin] * 2, axis=1)


def body(tokens, cotangent, deal, lengths, routes, gate_residual, w_qkv, w_out, w_gate_up, w_down,
         norm_gain_attn, norm_gain_moe, w_router, w_const, v_const):
    rows = tokens.shape[0]
    n_dp, n_t = lax.axis_size("dp"), lax.axis_size("tensor")
    t = lax.axis_index("tensor")
    ff = w_down.shape[2]
    d_here = w_qkv.shape[0]

    def swap(v, j):
        return lax.ppermute(v, "tensor", [(i, i ^ j) for i in range(n_t)])

    def place_in(parts):
        stacked = jnp.stack(parts)
        return jnp.stack([lax.dynamic_index_in_dim(stacked, t ^ i, 0, keepdims=False) for i in range(n_t)], axis=2)

    attn_shard = jnp.concatenate([w_qkv, w_out[:, None, :]], axis=1)
    attn_shard = place_in([attn_shard] + [swap(attn_shard, j) for j in range(1, n_t)]).reshape(d_here, 4 * D)
    w_attn = lax.all_gather(attn_shard, "dp", axis=0, tiled=True)
    ff_shard = jnp.concatenate([w_gate_up.reshape(d_here, EXPERTS, 2 * ff), w_down], axis=2)
    w_ff = lax.all_gather(ff_shard.reshape(d_here, EXPERTS * 3 * ff), "dp", axis=0, tiled=True)

    routes_t = routes.reshape(n_t, rows, 2).transpose(0, 2, 1)
    row, ext = (rows, D), (3 * rows, D)
    every, every_packed = (n_t, rows, D), (n_t, rows + SPARE, D)
    xs, gs, pos, slots, counts = call(
        functools.partial(deal_body, n_dp),
        "deal",
        [(row, BF16), (row, BF16), ((1, rows), I32), ((n_t, EXPERTS, rows), I32), ((n_t, EXPERTS, 128), I32)],
        [deal.reshape(1, rows), tokens, cotangent, routes_t],
    )
    counts = counts[:, :, 0].reshape(n_t * EXPERTS)
    x0 = lax.all_to_all(xs, "dp", split_axis=0, concat_axis=0, tiled=True)
    g0 = lax.all_to_all(gs, "dp", split_axis=0, concat_axis=0, tiled=True)

    place, cos, sin = rope_tables(lengths[0], (t - 2) * rows, 3 * rows)
    start = (LONGEST + jnp.arange(rows, dtype=I32) - place[2 * rows :]).reshape(1, rows)
    gain_attn, gain_moe = norm_gain_attn.reshape(1, D), norm_gain_moe.reshape(1, D)
    window = LONGEST + 256
    res_t = jnp.concatenate([gate_residual.T, jnp.zeros((4, rows), F32)], axis=0)
    wrc = jnp.concatenate([w_router.T, w_const.transpose(0, 2, 1).reshape(4, D)], axis=0)
    v8 = jnp.concatenate([v_const, jnp.zeros((6, D), F32)], axis=0)
    dma = lambda *shape: pltpu.SemaphoreType.DMA(shape)
    x1, x2, h, q, k, v, o, lse, xm, hp_all, g_all, gt, xl, dhl, sm, gv = call(
        functools.partial(forward_body, n_t),
        "forward",
        [(row, BF16), (row, BF16), (ext, BF16), (row, BF16), (ext, BF16), (ext, BF16), (row, BF16), ((SPARE, rows), F32),
         (row, F32), (every_packed, BF16), (every, BF16), ((8, rows), F32), (row, F32), (row, F32), ((SPARE, rows), F32), ((8, D), F32)],
        [x0, g0, w_attn, gain_attn, gain_moe, cos, sin, start, res_t, wrc, routes_t, v8],
        scratch=[pltpu.VMEM((window, 256), F32), dma(2), dma(2)] + [dma(3)] * 8,
        meet=0,
    )

    out_all, back_all, gw_ff = experts_call(counts, hp_all, g_all, slots, w_ff, ff)
    ff_sum = lax.psum_scatter(gw_ff, "dp", scatter_dimension=0, tiled=True)
    h2 = lax.dynamic_index_in_dim(hp_all, t, 0, keepdims=False)[0:rows]

    dx, da, dres, small, dq, dk, dv, result = call(
        functools.partial(backward_body, n_t),
        "backward",
        [(row, F32), (row, BF16), ((SPARE, rows), F32), ((SPARE + 8, D), F32), (row, BF16), (ext, BF16), (ext, BF16), (row, BF16)],
        [back_all, out_all, dhl, gt, sm, routes_t, wrc, xm, gain_moe, g0, h2, w_attn, o, gv, q, k, v, lse, start, cos, sin, xl],
        scratch=[pltpu.VMEM((rows // 256, window, 256), F32), pltpu.VMEM((3 * rows, 128), F32), pltpu.VMEM((3 * rows, 128), F32),
                 pltpu.VMEM((rows + SPARE, D), F32), pltpu.VMEM(row, BF16), pltpu.VMEM((SPARE, rows), F32)]
        + [pltpu.VMEM((n_t - 1, rows + SPARE, D), BF16)] * 2 + [pltpu.VMEM((n_t - 1, rows, D), BF16)] * 2
        + [dma(n_t - 1, 2)] * 4 + [dma(n_t - 1, 1)] * 4,
        meet=1,
    )
    back_out = lax.all_to_all(result, "dp", split_axis=0, concat_axis=0, tiled=True)
    gw_attn, gain_part, d_start = call(
        functools.partial(grads_body, n_t),
        "grads",
        [((D, 4 * D), BF16), ((8, D), F32), (row, BF16)],
        [x0, x1, x2, h, dq, dk, dv, da, o, w_attn, dx, gain_attn],
        scratch=[pltpu.VMEM(row, F32)] + [pltpu.VMEM(row, BF16)] * 4 + [dma(2), dma(2)],
        meet=2,
    )
    back_grad = lax.all_to_all(d_start, "dp", split_axis=0, concat_axis=0, tiled=True)
    output, grad_tokens = call(restore_body, "restore", [(row, BF16)] * 2, [pos, back_out, back_grad])

    def total(v):
        for axis, count in (("tensor", n_t), ("dp", n_dp)):
            bit = 1
            while bit < count:
                v = v + lax.ppermute(v, axis, [(i, i ^ bit) for i in range(count)])
                bit *= 2
        return v

    small_all = total(jnp.concatenate([small, gain_part], axis=0))
    gain_all = small_all[SPARE + 8]
    gw_attn, ff_sum = lax.optimization_barrier((gw_attn, ff_sum))
    attn_sum = lax.psum_scatter(gw_attn, "dp", scatter_dimension=0, tiled=True).reshape(d_here, 4, n_t, D // n_t)

    def share(j):
        return lax.dynamic_index_in_dim(attn_sum, t ^ j, 2, keepdims=False)

    attn_own = share(0).astype(F32)
    for j in range(1, n_t):
        attn_own = attn_own + swap(share(j), j).astype(F32)
    ff_own = ff_sum.reshape(d_here, EXPERTS, 3 * ff).astype(F32)
    return (
        output,
        grad_tokens,
        dres[0:12].T,
        attn_own[:, 0:3],
        attn_own[:, 3],
        ff_own[:, :, 0 : 2 * ff].reshape(d_here, EXPERTS, 2, ff),
        ff_own[:, :, 2 * ff :],
        gain_all,
        small_all[SPARE + 2],
        small_all[0:12].T,
        small_all[12:16].reshape(2, 2, D).transpose(0, 2, 1),
        small_all[SPARE : SPARE + 2],
    )


def solution(mesh):
    both, every = P(("dp", "tensor"), None), P()
    weights = (P("dp", None, "tensor"), P("dp", "tensor"), P("dp", None, None, "tensor"), P("dp", None, "tensor"))
    return jax.shard_map(
        body,
        mesh=mesh,
        in_specs=(both, both, P(("dp", "tensor")), P("dp", None), P("dp", None), both, *weights) + (every,) * 5,
        out_specs=(both, both, both, *weights) + (every,) * 5,
        check_vma=False,
    )
```

```python
import functools
import math

import jax
import jax.numpy as jnp
from jax import lax
from jax.experimental import pallas as pl
from jax.experimental.pallas import tpu as pltpu
from jax.sharding import PartitionSpec as P

D = 768
HEAD_DIM = 64
HEADS = 12
EXPERTS = 8
LONGEST = 1024
EPSILON = 1e-6
MASKED = -1e30
F32, BF16, I32 = jnp.float32, jnp.bfloat16, jnp.int32
NN = (((1,), (0,)), ((), ()))
NT = (((1,), (1,)), ((), ()))
TN = (((0,), (0,)), ((), ()))
SCORE_SCALE = HEAD_DIM**-0.5
LOG2E = 1.4426950408889634
TILE = 160
ROWS = 256
SPARE = 16
VMEM_CAP = 66_000_000


def mm(a, b, dims):
    return lax.dot_general(a, b, dims, preferred_element_type=F32)


def iota(shape, axis):
    return lax.broadcasted_iota(I32, shape, axis)


def pick(cond):
    return jnp.where(cond, 1.0, 0.0).astype(BF16)


def split2(v):
    high = v.astype(BF16)
    return high, (v - high.astype(F32)).astype(BF16)


def split3(v):
    high = v.astype(BF16)
    rest = v - high.astype(F32)
    mid = rest.astype(BF16)
    return high, mid, (rest - mid.astype(F32)).astype(BF16)


def vmem():
    return pl.BlockSpec(memory_space=pltpu.VMEM)


def smem():
    return pl.BlockSpec(memory_space=pltpu.SMEM)


def call(body, name, outs, operands, scalars=0, scratch=(), meet=None):
    return pl.pallas_call(
        body,
        name=name,
        out_shape=[jax.ShapeDtypeStruct(*o) for o in outs],
        in_specs=[smem()] * scalars + [vmem()] * (len(operands) - scalars),
        out_specs=[vmem()] * len(outs),
        scratch_shapes=list(scratch),
        compiler_params=pltpu.CompilerParams(
            vmem_limit_bytes=VMEM_CAP, collective_id=meet, has_side_effects=meet is not None
        ),
    )(*operands)


def deal_body(n_dp, deal_ref, tok_ref, cot_ref, routes_ref, xs_ref, gs_ref, pos_ref, slot_ref, cnt_ref):
    rows = tok_ref.shape[0]
    first, second = iota((rows, rows), 0), iota((rows, rows), 1)
    before = pick(first < second)
    deal = deal_ref[...]
    hit = iota((n_dp, rows), 0) == deal
    rank = mm(pick(hit), before, NN)
    rank = jnp.sum(jnp.where(hit, rank, 0.0), axis=0, keepdims=True).astype(I32)
    pos = deal * (rows // n_dp) + rank
    pos_ref[...] = pos
    place = pick(first == pos)
    xs_ref[...] = mm(place, tok_ref[...], NN).astype(BF16)
    gs_ref[...] = mm(place, cot_ref[...], NN).astype(BF16)
    expert = iota((EXPERTS, rows), 0)
    for j in range(routes_ref.shape[0]):
        route = routes_ref[j]
        named = (expert == route[0:1]) | (expert == route[1:2])
        ahead = mm(pick(named), before, NN).astype(I32)
        slot_ref[j] = jnp.where(named, ahead, -1)
        total = jnp.sum(jnp.where(named, 1.0, 0.0), axis=1, keepdims=True).astype(I32)
        cnt_ref[j] = jnp.broadcast_to(total, (EXPERTS, 128))


def restore_body(pos_ref, a_ref, b_ref, oa_ref, ob_ref):
    rows = a_ref.shape[0]
    place = pick(iota((rows, rows), 0) == pos_ref[...])
    oa_ref[...] = mm(place, a_ref[...], TN).astype(BF16)
    ob_ref[...] = mm(place, b_ref[...], TN).astype(BF16)


class Line:
    def __init__(self, size):
        self.size = size
        self.place = lax.axis_index("tensor")
        self.sent = {k: [] for k in range(size)}

    def each(self, body):
        for k in range(self.size):
            pl.when(self.place == k)(functools.partial(body, k))

    def enter(self):
        sem = pltpu.get_barrier_semaphore()

        def greet(k):
            near = [n for n in (k - 1, k + 1) if 0 <= n < self.size]
            for n in near:
                pl.semaphore_signal(sem, 1, device_id={"tensor": self.place + (n - k)}, device_id_type=pl.DeviceIdType.MESH)
            pl.semaphore_wait(sem, len(near))

        self.each(greet)

    def copy(self, hop, src, dst, sems):
        return pltpu.make_async_remote_copy(
            src_ref=src,
            dst_ref=dst,
            send_sem=sems[0],
            recv_sem=sems[1],
            device_id={"tensor": self.place + hop},
            device_id_type=pl.DeviceIdType.MESH,
        )

    def send(self, k, to, refs):
        self.copy(to - k, *refs()).start()
        self.sent[k].append((to - k, refs))

    def arrived(self, k, dst, sems):
        self.copy((k ^ 1) - k, dst, dst, sems).wait_recv()

    def leave(self):
        def drain(k):
            for hop, refs in self.sent[k]:
                self.copy(hop, *refs()).wait_send()

        self.each(drain)


def sum_events(size, k):
    events = []
    for dest in range(size):
        if dest >= k and dest > 0:
            events.append((0 if k == 0 else size - 1 - dest + k, 1, dest))
        if dest <= k and dest < size - 1:
            events.append((0 if k == size - 1 else dest + size - 1 - k, -1, dest))
    drop = [(t, w, d) for t, w, d in events if (k == 0 and w == 1 and d == 0) or (k == size - 1 and w == -1 and d == k)]
    return sorted((ev for ev in events if ev not in drop), key=lambda ev: (ev[0], ev[1], -ev[1] * ev[2]))


def turn(u):
    low = (iota((1, u.shape[1]), 1) % HEAD_DIM) < HEAD_DIM // 2
    half = HEAD_DIM // 2
    return jnp.where(low, pltpu.roll(u, u.shape[1] - half, 1), pltpu.roll(u, half, 1))


def wide(table):
    return jnp.concatenate([table] * (D // 128), axis=1)


def key_bias(start, block, first_row, base):
    window = LONGEST + block
    key = iota((window, block), 0) + first_row
    row = iota((1, block), 1) + (base + first_row)
    return jnp.where((key >= start) & (key <= row), 0.0, MASKED)


def router_part(route, o_ref, w_ref, x_ref, gain_ref, res_ref, wrc_ref, x1_ref, hp_ref, gt_ref):
    rows = o_ref.shape[0]
    x1 = x_ref[...].astype(F32) + mm(o_ref[...], w_ref[:, 3 * D : 4 * D], NT)
    x1_ref[...] = x1
    h = x1 * lax.rsqrt(jnp.mean(x1 * x1, axis=1, keepdims=True) + EPSILON) * gain_ref[...]
    h = h.astype(BF16)
    hp_ref[0:rows, :] = h
    high, mid, low = split3(wrc_ref[...])
    z = mm(low, h, NT) + mm(mid, h, NT) + mm(high, h, NT) + res_ref[...]
    expert = iota(z.shape, 0)
    named0, named1 = expert == route[0:1], expert == route[1:2]
    c0 = jnp.sum(jnp.where(named0, z, 0.0), axis=0, keepdims=True)
    c1 = jnp.sum(jnp.where(named1, z, 0.0), axis=0, keepdims=True)
    top = jnp.maximum(c0, c1)
    e0, e1 = jnp.exp(c0 - top), jnp.exp(c1 - top)
    g0, g1 = e0 / (e0 + e1), e1 / (e0 + e1)
    table = [g0, g1]
    for j in range(2):
        l0, l1 = z[12 + 2 * j : 13 + 2 * j], z[13 + 2 * j : 14 + 2 * j]
        top = jnp.maximum(l0, l1)
        m0, m1 = jnp.exp(l0 - top), jnp.exp(l1 - top)
        table += [m0 / (m0 + m1), m1 / (m0 + m1)]
    gt_ref[...] = jnp.concatenate(table + [jnp.zeros((2, rows), F32)], axis=0)
    gates = jnp.where(named0, g0, jnp.where(named1, g1, 0.0))
    gates = jnp.where(expert < EXPERTS, gates, 0.0)
    hp_ref[rows : rows + SPARE, :] = jnp.concatenate([gates, jnp.zeros((SPARE, D - rows), F32)], axis=1).astype(BF16)


def local_part(route, x1_ref, hp_ref, g_ref, gt_ref, v_ref, xl_ref, dhl_ref, sm_ref, gv_ref):
    rows = x1_ref.shape[0]
    h, g = hp_ref[0:rows, :], g_ref[...]
    hf, gf = h.astype(F32), g.astype(F32)
    low0 = gt_ref[0:1].astype(BF16).astype(F32)
    low1 = gt_ref[1:2].astype(BF16).astype(F32)

    def weight(e):
        return jnp.where(route[0:1] == e, low0, 0.0) + jnp.where(route[1:2] == e, low1, 0.0)

    copy, first, second = weight(EXPERTS + 1), weight(EXPERTS + 2), weight(EXPERTS + 3)
    m00, m01, m10, m11 = gt_ref[2:3], gt_ref[3:4], gt_ref[4:5], gt_ref[5:6]
    a = copy + first * m00 + second * m10
    b0, b1 = first * m01, second * m11
    table = jnp.concatenate([a, b0, b1, jnp.zeros((125, rows), F32)], axis=0).T
    ac, b0c, b1c = table[:, 0:1], table[:, 1:2], table[:, 2:3]
    v = v_ref[...]
    xl_ref[...] = x1_ref[...] + ac * hf + b0c * v[0:1] + b1c * v[1:2]
    dhl_ref[...] = ac * gf
    ones = jnp.ones((8, D), BF16)
    high, low = split2(hf * gf)
    gh = (mm(ones, high, NT) + mm(ones, low, NT))[0:1]
    vh, vm, vl = split3(v)
    gvs = mm(vl, g, NT) + mm(vm, g, NT) + mm(vh, g, NT)
    gv0, gv1 = gvs[0:1], gvs[1:2]
    zero = jnp.zeros((9, rows), F32)
    dl0 = first * m00 * m01 * (gh - gv0)
    dl1 = second * m10 * m11 * (gh - gv1)
    sm_ref[...] = jnp.concatenate(
        [zero, gh, m00 * gh + m01 * gv0, m10 * gh + m11 * gv1, dl0, -dl0, dl1, -dl1], axis=0
    )
    bh, bm, bl = split3(jnp.concatenate([b0, b1, jnp.zeros((6, rows), F32)], axis=0))
    gv_ref[...] = mm(bl, g, NN) + mm(bm, g, NN) + mm(bh, g, NN)


def forward_body(size, x0_ref, g0_ref, w_ref, gain_ref, gain2_ref, cos_ref, sin_ref, start_ref, res_ref, wrc_ref, routes_ref, v8_ref,
                 x1_ref, x2_ref, h_ref, q_ref, k_ref, v_ref, o_ref, lse_ref, xm_ref, hp_ref, gall_ref, gt_ref, xl_ref,
                 dhl_ref, sm_ref, gv_ref,
                 bias_ref, sx, rx, sgu, rgu, sgd, rgd, shu, rhu, shd, rhd):
    rows = x0_ref.shape[0]
    step = 256
    line = Line(size)
    t = line.place
    last = size - 1
    line.enter()

    def begin(k):
        if k < last:
            line.send(k, k + 1, lambda: (x0_ref, x1_ref, (sx.at[0], rx.at[0])))
        if k > 0:
            line.send(k, k - 1, lambda: (g0_ref, gall_ref.at[k], (sgd.at[0], rgd.at[0])))

    line.each(begin)
    gain = gain_ref[...]

    def project_chunk(c, x_ref):
        def project(i, _):
            at = pl.multiple_of(i * step, step)
            x = x_ref[pl.ds(at, step), :].astype(F32)
            h = x * lax.rsqrt(jnp.mean(x * x, axis=1, keepdims=True) + EPSILON) * gain
            h = h.astype(BF16)
            to = pl.ds(pl.multiple_of(c * rows + i * step, step), step)
            h_ref[to, :] = h
            cos, sin = wide(cos_ref[to, :]), wide(sin_ref[to, :])
            k = mm(h, w_ref[:, D : 2 * D], NN)
            k_ref[to, :] = (k * cos + turn(k) * sin).astype(BF16)
            v_ref[to, :] = mm(h, w_ref[:, 2 * D : 3 * D], NN).astype(BF16)
            if c == 2:
                q = mm(h, w_ref[:, 0:D], NN)
                q_ref[pl.ds(at, step), :] = (q * cos + turn(q) * sin).astype(BF16)
            return 0

        lax.fori_loop(0, rows // step, project, 0)

    project_chunk(2, x0_ref)
    gall_ref[t] = g0_ref[...]

    def second(k):
        if k > 0:
            line.arrived(k, x1_ref, (sx.at[0], rx.at[0]))
        else:
            x1_ref[...] = jnp.zeros_like(x1_ref)
        if 0 < k < last:
            line.send(k, k + 1, lambda: (x1_ref, x2_ref, (sx.at[1], rx.at[1])))
        if k < last:
            line.send(k, k + 1, lambda: (g0_ref, gall_ref.at[k], (sgu.at[0], rgu.at[0])))
            line.arrived(k, gall_ref.at[k + 1], (sgd.at[0], rgd.at[0]))
            if k > 0:
                line.send(k, k - 1, lambda: (gall_ref.at[k + 1], gall_ref.at[k + 1], (sgd.at[1], rgd.at[1])))

    line.each(second)
    project_chunk(1, x1_ref)

    def third(k):
        if k > 1:
            line.arrived(k, x2_ref, (sx.at[1], rx.at[1]))
        else:
            x2_ref[...] = jnp.zeros_like(x2_ref)
        if k + 2 <= last:
            line.arrived(k, gall_ref.at[k + 2], (sgd.at[1], rgd.at[1]))
            if k > 0:
                line.send(k, k - 1, lambda: (gall_ref.at[k + 2], gall_ref.at[k + 2], (sgd.at[2], rgd.at[2])))

    line.each(third)
    project_chunk(0, x2_ref)

    block = step
    window = LONGEST + block
    lane = iota((1, 128), 1) // HEAD_DIM
    for rb in range(rows // block):
        first = rb * block
        bias_ref[...] = key_bias(start_ref[:, first : first + block], block, first, LONGEST)

        def pair(i, _, first=first):
            lanes = pl.ds(pl.multiple_of(i * 128, 128), 128)
            k = k_ref[first : first + window, lanes]
            vt = v_ref[first : first + window, lanes].T
            q = q_ref[first : first + block, lanes]
            parts = []
            for half in range(2):
                qm = jnp.where(lane == half, q, jnp.zeros_like(q))
                s = mm(k, qm, NT) * (SCORE_SCALE * LOG2E) + bias_ref[...]
                top = jnp.max(s, axis=0, keepdims=True)
                p = jnp.exp2(s - top)
                total = jnp.sum(p, axis=0, keepdims=True)
                out = mm(vt[half * HEAD_DIM : (half + 1) * HEAD_DIM], p.astype(BF16), NN)
                parts.append(out * (1.0 / total))
                lse_ref[pl.ds(i * 2 + half, 1), first : first + block] = top + jnp.log2(total)
            o_ref[first : first + block, lanes] = jnp.concatenate(parts, axis=0).T.astype(BF16)
            return 0

        lax.fori_loop(0, HEADS // 2, pair, 0)
        if rb == 0:
            def fourth(k):
                if k > 0:
                    line.arrived(k, gall_ref.at[k - 1], (sgu.at[0], rgu.at[0]))
                    if k < last:
                        line.send(k, k + 1, lambda: (gall_ref.at[k - 1], gall_ref.at[k - 1], (sgu.at[1], rgu.at[1])))

            line.each(fourth)

    route = routes_ref[t]
    router_part(route, o_ref, w_ref, x0_ref, gain2_ref, res_ref, wrc_ref, xm_ref, hp_ref.at[t], gt_ref)

    def fifth(k):
        if k < last:
            line.send(k, k + 1, lambda: (hp_ref.at[k], hp_ref.at[k], (shu.at[0], rhu.at[0])))
        if k > 0:
            line.send(k, k - 1, lambda: (hp_ref.at[k], hp_ref.at[k], (shd.at[0], rhd.at[0])))
        if k > 1:
            line.arrived(k, gall_ref.at[k - 2], (sgu.at[1], rgu.at[1]))
            if k < last:
                line.send(k, k + 1, lambda: (gall_ref.at[k - 2], gall_ref.at[k - 2], (sgu.at[2], rgu.at[2])))

    line.each(fifth)
    local_part(route, xm_ref, hp_ref.at[t], g0_ref, gt_ref, v8_ref, xl_ref, dhl_ref, sm_ref, gv_ref)

    def sixth(k):
        for hop in range(2):
            up, down = k - 1 - hop, k + 1 + hop
            if up >= 0:
                line.arrived(k, hp_ref.at[up], (shu.at[hop], rhu.at[hop]))
                if k < last:
                    line.send(k, k + 1, lambda up=up, hop=hop: (hp_ref.at[up], hp_ref.at[up], (shu.at[hop + 1], rhu.at[hop + 1])))
            if down <= last:
                line.arrived(k, hp_ref.at[down], (shd.at[hop], rhd.at[hop]))
                if k > 0:
                    line.send(k, k - 1, lambda down=down, hop=hop: (hp_ref.at[down], hp_ref.at[down], (shd.at[hop + 1], rhd.at[hop + 1])))
        if k == last:
            line.arrived(k, hp_ref.at[0], (shu.at[2], rhu.at[2]))
            line.arrived(k, gall_ref.at[0], (sgu.at[2], rgu.at[2]))
        if k == 0:
            line.arrived(k, hp_ref.at[last], (shd.at[2], rhd.at[2]))
            line.arrived(k, gall_ref.at[last], (sgd.at[2], rgd.at[2]))

    line.each(sixth)
    line.leave()


def middle_part(route, dh_ref, gt_ref, sm_ref, wrc_ref, x1_ref, gain_ref, g_ref, h2_ref, w_ref, o_ref, gv_ref,
                dx_ref, da_ref, do_ref, delta_ref, dres_ref, small_ref):
    rows = x1_ref.shape[0]
    dgf = dh_ref[rows : rows + SPARE, 0:rows]
    dh = dh_ref[0:rows, :]
    dgate = jnp.concatenate([dgf[0:EXPERTS] + dgf[EXPERTS:], sm_ref[EXPERTS:SPARE]], axis=0)
    expert = iota((SPARE, rows), 0)
    named0, named1 = expert == route[0:1], expert == route[1:2]
    g0, g1 = gt_ref[0:1], gt_ref[1:2]
    d0 = jnp.sum(jnp.where(named0, dgate, 0.0), axis=0, keepdims=True)
    d1 = jnp.sum(jnp.where(named1, dgate, 0.0), axis=0, keepdims=True)
    inner = g0 * d0 + g1 * d1
    dz = jnp.where(named0, g0 * (d0 - inner), jnp.where(named1, g1 * (d1 - inner), 0.0))
    dres_ref[...] = dz
    dz = jnp.where(expert < 12, dz, sm_ref[...])
    zh, zm, zl = split3(dz)
    wh, wm, wl = split3(wrc_ref[...])
    dh = dh + (mm(zh, wl, TN) + mm(zl, wh, TN) + mm(zm, wm, TN) + mm(zh, wm, TN) + mm(zm, wh, TN) + mm(zh, wh, TN))
    h = h2_ref[...]
    small_ref[0:SPARE, :] = mm(zl, h, NN) + mm(zm, h, NN) + mm(zh, h, NN)
    x1 = x1_ref[...]
    r = lax.rsqrt(jnp.mean(x1 * x1, axis=1, keepdims=True) + EPSILON)
    xr = x1 * r
    grad_gain = jnp.sum(dh * xr, axis=0, keepdims=True)
    gv = gv_ref[...]
    small_ref[SPARE : SPARE + 8, :] = jnp.concatenate([gv[0:2], grad_gain, gv[3:8]], axis=0)
    scaled = dh * gain_ref[...]
    dx = g_ref[...].astype(F32) + r * (scaled - xr * jnp.mean(xr * scaled, axis=1, keepdims=True))
    dx_ref[...] = dx
    da = dx.astype(BF16)
    da_ref[...] = da
    do = mm(da, w_ref[:, 3 * D : 4 * D], NN).astype(BF16)
    do_ref[...] = do
    high, low = split2(do.astype(F32) * o_ref[...].astype(F32))
    heads = pick(iota((SPARE, D), 1) // HEAD_DIM == iota((SPARE, D), 0))
    delta_ref[...] = mm(heads, high, NT) + mm(heads, low, NT)


def backward_body(size, back_ref, out_ref, dhl_ref, gt_ref, sm_ref, routes_ref, wrc_ref, xm_ref, gain_ref, g_ref, h2_ref, w_ref,
                  o_ref, gv_ref, q_ref, k_ref, v_ref, lse_ref, start_ref, cos_ref, sin_ref, xl_ref,
                  dx_ref, da_ref, dres_ref, small_ref, dq_ref, dk_ref, dv_ref, y_ref,
                  bias_ref, dkf_ref, dvf_ref, dh_ref, do_ref, delta_ref, bu_ref, bd_ref, fu_ref, fd_ref,
                  sbu, rbu, sbd, rbd, sfu, rfu, sfd, rfd):
    rows = xm_ref.shape[0]
    packed = rows + SPARE
    cut = 272
    pieces = (slice(0, cut), slice(cut, packed))
    line = Line(size)
    t = line.place
    last = size - 1
    line.enter()

    def handle(k, way, dest, part, index, mine_ref, up_ref, down_ref, ups, downs):
        slot = dest - 1 if way == 1 else dest
        first = k == (0 if way == 1 else last)
        mine = mine_ref.at[dest, part]

        def refs():
            held = (up_ref if way == 1 else down_ref).at[slot, part]
            sems = tuple(s.at[slot, index] for s in (ups if way == 1 else downs))
            return mine_ref.at[dest, part] if first else held, held, sems

        _, held, sems = refs()
        if not first:
            line.arrived(k, held, sems)
        if dest != k:
            if not first:
                held[...] = (held[...].astype(F32) + mine[...].astype(F32)).astype(BF16)
            line.send(k, k + way, refs)

    def sum_back(k):
        for _, way, dest in sum_events(size, k):
            for index, part in enumerate(pieces):
                handle(k, way, dest, part, index, back_ref, bu_ref, bd_ref, (sbu, rbu), (sbd, rbd))

    def sum_out(k, now):
        for time, way, dest in sum_events(size, k):
            if time == now:
                handle(k, way, dest, slice(0, rows), 0, out_ref, fu_ref, fd_ref, (sfu, rfu), (sfd, rfd))

    line.each(sum_back)
    line.each(lambda k: sum_out(k, 0))
    dh_ref[...] = back_ref[t].astype(F32)

    @pl.when(t > 0)
    def _():
        dh_ref[...] += bu_ref[t - 1].astype(F32)

    @pl.when(t < last)
    def _():
        dh_ref[...] += bd_ref[t].astype(F32)

    dh_ref[0:rows, :] += dhl_ref[...]
    middle_part(routes_ref[t], dh_ref, gt_ref, sm_ref, wrc_ref, xm_ref, gain_ref, g_ref, h2_ref, w_ref, o_ref, gv_ref,
                dx_ref, da_ref, do_ref, delta_ref, dres_ref, small_ref)
    line.each(lambda k: sum_out(k, 1))

    block = 256
    window = LONGEST + block
    lane = iota((1, 128), 1) // HEAD_DIM
    for rb in range(rows // block):
        first = rb * block
        bias_ref[rb] = key_bias(start_ref[:, first : first + block], block, first, LONGEST)

    def pair(i, _):
        lanes = pl.ds(pl.multiple_of(i * 128, 128), 128)
        for rb in range(rows // block):
            first = rb * block
            k = k_ref[first : first + window, lanes]
            v = v_ref[first : first + window, lanes]
            kt = k.T
            q = q_ref[first : first + block, lanes]
            do = do_ref[first : first + block, lanes]
            dk = jnp.zeros((window, 128), F32)
            dv = jnp.zeros((window, 128), F32)
            parts = []
            for half in range(2):
                qm = jnp.where(lane == half, q, jnp.zeros_like(q))
                dom = jnp.where(lane == half, do, jnp.zeros_like(do))
                head = pl.ds(i * 2 + half, 1)
                s = mm(k, qm, NT) * (SCORE_SCALE * LOG2E) + bias_ref[rb]
                p = jnp.exp2(s - lse_ref[head, first : first + block])
                dp = mm(v, dom, NT)
                ds = (p * (dp - delta_ref[head, first : first + block])).astype(BF16)
                dv = dv + mm(p.astype(BF16), dom, NN)
                dk = dk + mm(ds, qm, NN)
                parts.append(mm(kt[half * HEAD_DIM : (half + 1) * HEAD_DIM], ds, NN))
            dq = jnp.concatenate(parts, axis=0).T * SCORE_SCALE
            at = slice(2 * rows + first, 2 * rows + first + block)
            dq_ref[first : first + block, lanes] = (dq * cos_ref[at, :] - turn(dq) * sin_ref[at, :]).astype(BF16)
            if first == 0:
                dkf_ref[0:window, :] = dk
                dvf_ref[0:window, :] = dv
            else:
                old = window - block
                dkf_ref[first : first + old, :] += dk[0:old]
                dvf_ref[first : first + old, :] += dv[0:old]
                dkf_ref[first + old : first + window, :] = dk[old:]
                dvf_ref[first + old : first + window, :] = dv[old:]
        dk = dkf_ref[...] * SCORE_SCALE
        dk_ref[:, lanes] = (dk * cos_ref[...] - turn(dk) * sin_ref[...]).astype(BF16)
        dv_ref[:, lanes] = dvf_ref[...].astype(BF16)
        return 0

    lax.fori_loop(0, HEADS // 4, pair, 0)
    line.each(lambda k: sum_out(k, 2))
    lax.fori_loop(HEADS // 4, HEADS // 2, pair, 0)
    line.each(lambda k: sum_out(k, 3))
    xl_ref[...] += out_ref[t].astype(F32)

    @pl.when(t > 0)
    def _():
        xl_ref[...] += fu_ref[t - 1].astype(F32)

    @pl.when(t < last)
    def _():
        xl_ref[...] += fd_ref[t].astype(F32)

    y_ref[...] = xl_ref[...].astype(BF16)
    line.leave()


def grads_body(size, x0_ref, x1_ref, x2_ref, h_ref, dq_ref, dk_ref, dv_ref, da_ref, o_ref, w_ref, dx_ref, gain_ref,
               gw_ref, gpart_ref, out_ref, d0_ref, d1_ref, d2_ref, ra_ref, rb_ref, sems_s, sems_r):
    rows = x0_ref.shape[0]
    line = Line(size)
    last = size - 1
    block = 256
    line.enter()

    def hidden(c, d_ref):
        def one(i, _):
            at = pl.ds(pl.multiple_of(i * block, block), block)
            to = pl.ds(pl.multiple_of(c * rows + i * block, block), block)
            total = mm(dk_ref[to, :], w_ref[:, D : 2 * D], NT) + mm(dv_ref[to, :], w_ref[:, 2 * D : 3 * D], NT)
            if c == 2:
                total = total + mm(dq_ref[at, :], w_ref[:, 0:D], NT)
            d_ref[at, :] = total.astype(d_ref.dtype)
            return 0

        lax.fori_loop(0, rows // block, one, 0)

    def gain_of(x_ref, d_ref):
        x = x_ref[...].astype(F32)
        r = lax.rsqrt(jnp.mean(x * x, axis=1, keepdims=True) + EPSILON)
        return jnp.sum(d_ref[...].astype(F32) * x * r, axis=0, keepdims=True)

    hidden(0, d2_ref)

    def first(k):
        if k > 1:
            line.send(k, k - 1, lambda: (d2_ref, ra_ref, (sems_s.at[0], sems_r.at[0])))

    line.each(first)
    hidden(1, d1_ref)
    gain = gain_of(x2_ref, d2_ref) + gain_of(x1_ref, d1_ref)
    h = h_ref[...]

    def weight(column, left, right_ref):
        for c in range(D // 256):
            cols = slice(c * 256, (c + 1) * 256)
            gw_ref[:, column * D + c * 256 : column * D + c * 256 + 256] = mm(left, right_ref[:, cols], TN).astype(BF16)

    weight(1, h, dk_ref)

    def second(k):
        if 0 < k < last:
            line.arrived(k, ra_ref, (sems_s.at[0], sems_r.at[0]))
            d1_ref[...] = (d1_ref[...].astype(F32) + ra_ref[...].astype(F32)).astype(BF16)
        if k > 0:
            line.send(k, k - 1, lambda: (d1_ref, rb_ref, (sems_s.at[1], sems_r.at[1])))

    line.each(second)
    hidden(2, d0_ref)
    gpart_ref[...] = jnp.broadcast_to(gain + gain_of(x0_ref, d0_ref), (8, D))
    weight(2, h, dv_ref)
    weight(0, h[2 * rows :], dq_ref)
    weight(3, da_ref[...], o_ref)

    def third(k):
        if k < last:
            line.arrived(k, rb_ref, (sems_s.at[1], sems_r.at[1]))
            d0_ref[...] += rb_ref[...].astype(F32)

    line.each(third)
    x = x0_ref[...].astype(F32)
    r = lax.rsqrt(jnp.mean(x * x, axis=1, keepdims=True) + EPSILON)
    xr = x * r
    scaled = d0_ref[...] * gain_ref[...]
    out_ref[...] = (dx_ref[...] + r * (scaled - xr * jnp.mean(xr * scaled, axis=1, keepdims=True))).astype(BF16)
    line.leave()


class Peers:
    def __init__(self):
        self.d, self.t = lax.axis_index("dp"), lax.axis_index("tensor")
        self.sent = []

    def enter(self, targets):
        sem = pltpu.get_barrier_semaphore()
        for where in targets:
            pl.semaphore_signal(sem, 1, device_id=where, device_id_type=pl.DeviceIdType.MESH)
        pl.semaphore_wait(sem, len(targets))

    def copy(self, where, src, dst, sems):
        return pltpu.make_async_remote_copy(
            src_ref=src,
            dst_ref=dst,
            send_sem=sems[0],
            recv_sem=sems[1],
            device_id=where,
            device_id_type=pl.DeviceIdType.MESH,
        )

    def send(self, where, src, dst, sems):
        copy = self.copy(where, src, dst, sems)
        copy.start()
        self.sent.append(copy)

    def leave(self):
        for copy in self.sent:
            copy.wait_send()


def flip(index, bit):
    return index + bit * (1 - 2 * ((index // bit) % 2))


def finish_body(n_dp, size, x0_ref, x1_ref, x2_ref, h_ref, dq_ref, dk_ref, dv_ref, da_ref, o_ref, w_ref, dx_ref, gain_ref,
                y_ref, small_ref, pos_ref,
                yo_ref, go_ref, gw_ref, sum_ref,
                d0_ref, d1_ref, d2_ref, ra_ref, rb_ref, out_ref, yr_ref, gr_ref, part_ref, r1_ref, r2_ref, r3_ref,
                zs_ref, zr_ref, cur_ref, got_ref,
                sems_s, sems_r, sy, ry, sg, rg, s1, r1, s2, r2, s3, r3, sz, rz, sb, rb):
    rows = x0_ref.shape[0]
    share = rows // n_dp
    line = Line(size)
    last = size - 1
    block = 256
    net = Peers()
    d, t = net.d, net.t
    place = pick(iota((rows, rows), 0) == pos_ref[...])
    around = [(j, lax.rem(d + j, n_dp), lax.rem(d + n_dp - j, n_dp)) for j in range(1, n_dp)]
    along = [(j, lax.rem(t + j, size), lax.rem(t + size - j, size)) for j in range(1, size)]
    net.enter([{"dp": to} for _, to, _ in around] + [{"tensor": to} for _, to, _ in along])

    def scatter(src_ref, dst_ref, sems):
        for j, to, _ in around:
            net.send({"dp": to}, src_ref.at[to], dst_ref.at[d], (sems[0].at[j - 1], sems[1].at[j - 1]))
        dst_ref[d] = src_ref[d]

    def gathered(dst_ref, sems):
        for j, _, source in around:
            held = dst_ref.at[source]
            net.copy({"dp": source}, held, held, (sems[0].at[j - 1], sems[1].at[j - 1])).wait_recv()

    scatter(y_ref, yr_ref, (sy, ry))

    def hidden(c, d_ref):
        def one(i, _):
            at = pl.ds(pl.multiple_of(i * block, block), block)
            to = pl.ds(pl.multiple_of(c * rows + i * block, block), block)
            total = mm(dk_ref[to, :], w_ref[:, D : 2 * D], NT) + mm(dv_ref[to, :], w_ref[:, 2 * D : 3 * D], NT)
            if c == 2:
                total = total + mm(dq_ref[at, :], w_ref[:, 0:D], NT)
            d_ref[at, :] = total.astype(d_ref.dtype)
            return 0

        lax.fori_loop(0, rows // block, one, 0)

    def gain_of(x_ref, d_ref):
        x = x_ref[...].astype(F32)
        r = lax.rsqrt(jnp.mean(x * x, axis=1, keepdims=True) + EPSILON)
        return jnp.sum(d_ref[...].astype(F32) * x * r, axis=0, keepdims=True)

    core, x, y = lax.rem(d, 2), lax.rem(d // 2, 2), d // 4
    there = ({"dp": flip(d, 2)}, {"dp": flip(d, 4)})
    deep = D // n_dp

    def weight(u, left, right_ref):
        for c in range(D // 256):
            cols = slice(c * 256, (c + 1) * 256)
            value = mm(left, right_ref[:, cols], TN).astype(BF16)
            part_ref[u, :, :, cols] = value.reshape(n_dp, deep, 256)
        for j in range(4):
            net.send({"dp": flip(d, 1)}, part_ref.at[u, 2 * j + 1 - core], r1_ref.at[u, j], (s1.at[u, j], r1.at[u, j]))

    def add(u, j, arrived):
        spot = 2 * j + core
        part_ref[u, spot] = (part_ref[u, spot].astype(F32) + arrived[...].astype(F32)).astype(BF16)

    def chips(u):
        if u % 2 == 0:
            first = (there[0], [2 * i + 1 - x for i in range(2)], [2 * i + x for i in range(2)])
            return first, (there[1], 2 * (1 - y) + x)
        first = (there[1], [2 * (1 - y) + i for i in range(2)], [2 * y + i for i in range(2)])
        return first, (there[0], 2 * y + 1 - x)

    def halve(u):
        for j in range(4):
            held = r1_ref.at[u, j]
            net.copy({"dp": flip(d, 1)}, held, held, (s1.at[u, j], r1.at[u, j])).wait_recv()
            add(u, j, held)
        where, theirs, _ = chips(u)[0]
        for i in range(2):
            net.send(where, part_ref.at[u, 2 * theirs[i] + core], r2_ref.at[u, i], (s2.at[u, i], r2.at[u, i]))

    def quarter(u):
        (where, _, mine), (after, spot) = chips(u)
        for i in range(2):
            held = r2_ref.at[u, i]
            net.copy(where, held, held, (s2.at[u, i], r2.at[u, i])).wait_recv()
            add(u, mine[i], held)
        net.send(after, part_ref.at[u, 2 * spot + core], r3_ref.at[u], (s3.at[u], r3.at[u]))

    def own(u):
        after = chips(u)[1][0]
        held = r3_ref.at[u]
        net.copy(after, held, held, (s3.at[u], r3.at[u])).wait_recv()
        value = part_ref[u, d].astype(F32) + held[...].astype(F32)
        wide_share = D // size
        for p in range(size):
            zs_ref[u, p] = value[:, p * wide_share : (p + 1) * wide_share].astype(BF16)
        for j, to, _ in along:
            net.send({"tensor": to}, zs_ref.at[u, to], zr_ref.at[u, j - 1], (sz.at[u, j - 1], rz.at[u, j - 1]))

    def whole(u):
        total = zs_ref[u, t].astype(F32)
        for j, _, source in along:
            held = zr_ref.at[u, j - 1]
            net.copy({"tensor": source}, held, held, (sz.at[u, j - 1], rz.at[u, j - 1])).wait_recv()
            total = total + held[...].astype(F32)
        gw_ref[u] = total

    steps = [("tensor", bit) for bit in (1, 2, 4, 8) if bit < size] + [("dp", bit) for bit in (1, 2, 4, 8) if bit < n_dp]

    def small_out(i):
        axis, bit = steps[i]
        mine = t if axis == "tensor" else d
        net.send({axis: flip(mine, bit)}, cur_ref.at[i], got_ref.at[i], (sb.at[i], rb.at[i]))

    def small_in(i):
        axis, bit = steps[i]
        mine = t if axis == "tensor" else d
        held = got_ref.at[i]
        net.copy({axis: flip(mine, bit)}, held, held, (sb.at[i], rb.at[i])).wait_recv()
        total = cur_ref[i] + held[...]
        if i + 1 < len(steps):
            cur_ref[i + 1] = total
            small_out(i + 1)
        else:
            sum_ref[...] = total

    hidden(0, d2_ref)

    def first(k):
        if k > 1:
            line.send(k, k - 1, lambda: (d2_ref, ra_ref, (sems_s.at[0], sems_r.at[0])))

    line.each(first)
    h = h_ref[...]
    weight(0, h, dk_ref)
    hidden(1, d1_ref)
    gain = gain_of(x2_ref, d2_ref) + gain_of(x1_ref, d1_ref)

    def second(k):
        if 0 < k < last:
            line.arrived(k, ra_ref, (sems_s.at[0], sems_r.at[0]))
            d1_ref[...] = (d1_ref[...].astype(F32) + ra_ref[...].astype(F32)).astype(BF16)
        if k > 0:
            line.send(k, k - 1, lambda: (d1_ref, rb_ref, (sems_s.at[1], sems_r.at[1])))

    line.each(second)
    weight(1, h, dv_ref)
    halve(0)
    hidden(2, d0_ref)
    gain = gain + gain_of(x0_ref, d0_ref)
    rest = small_ref.shape[0]
    cur_ref[0, 0:rest, :] = small_ref[...]
    cur_ref[0, rest : rest + 8, :] = jnp.broadcast_to(gain, (8, D))
    small_out(0)
    weight(2, h[2 * rows :], dq_ref)
    halve(1)
    quarter(0)
    small_in(0)
    weight(3, da_ref[...], o_ref)
    halve(2)
    quarter(1)
    own(0)
    small_in(1)
    gathered(yr_ref, (sy, ry))
    yo_ref[...] = mm(place, yr_ref[...].reshape(rows, D), TN).astype(BF16)

    def third(k):
        if k < last:
            line.arrived(k, rb_ref, (sems_s.at[1], sems_r.at[1]))
            d0_ref[...] += rb_ref[...].astype(F32)

    line.each(third)
    xv = x0_ref[...].astype(F32)
    r = lax.rsqrt(jnp.mean(xv * xv, axis=1, keepdims=True) + EPSILON)
    xr = xv * r
    scaled = d0_ref[...] * gain_ref[...]
    value = dx_ref[...] + r * (scaled - xr * jnp.mean(xr * scaled, axis=1, keepdims=True))
    out_ref[...] = value.astype(BF16).reshape(n_dp, share, D)
    scatter(out_ref, gr_ref, (sg, rg))
    halve(3)
    quarter(2)
    own(1)
    small_in(2)
    quarter(3)
    own(2)
    small_in(3)
    own(3)
    for i in range(4, len(steps)):
        small_in(i)
    gathered(gr_ref, (sg, rg))
    go_ref[...] = mm(place, gr_ref[...].reshape(rows, D), TN).astype(BF16)
    for u in range(4):
        whole(u)
    line.leave()
    net.leave()


def experts_body(ff, chunks, cnt_ref, h_refs, g_refs, slot_ref, w_ref, o_refs, d_refs, gw_ref,
                 xbuf, gbuf, cbuf, onehot, fbuf, dbuf, gacc, gates, dgrow, off_ref, base_ref, nt_ref):
    rows = slot_ref.shape[2]
    e = pl.program_id(0)

    def match(j, expert, tile):
        slots = slot_ref[j, pl.ds(expert, 1), :]
        return (iota((TILE, rows), 0) + tile * TILE) == slots

    def store_rows(at, count, hit, x, gs, gate_row):
        to = pl.ds(pl.multiple_of(at, 16), TILE)
        keep = iota((TILE, 1), 0) < count
        col = jnp.sum(jnp.where(hit, gate_row, 0.0), axis=1, keepdims=True)
        xbuf[to, :] = jnp.where(keep, x, xbuf[to, :].astype(F32)).astype(BF16)
        gbuf[to, :] = jnp.where(keep, gs, gbuf[to, :].astype(F32)).astype(BF16)
        cbuf[to, :] = jnp.where(keep, jnp.broadcast_to(col, (TILE, 128)), cbuf[to, :])

    def round16(n):
        return ((n + 15) // 16) * 16

    @pl.when(e == 0)
    def _gather():
        at = jnp.int32(0)
        for ex in range(EXPERTS):
            base_ref[ex] = at
            here = at
            for j in range(chunks):
                off_ref[j * EXPERTS + ex] = here
                here = here + round16(cnt_ref[j * EXPERTS + ex])
            tiles = (here - at + (ROWS - 1)) // ROWS
            nt_ref[ex] = tiles
            tail = pl.ds(pl.multiple_of(here, 16), ROWS)
            xbuf[tail, :] = jnp.zeros((ROWS, D), BF16)
            gbuf[tail, :] = jnp.zeros((ROWS, D), BF16)
            cbuf[tail, :] = jnp.zeros((ROWS, 128), F32)
            at = at + tiles * ROWS
        for j in range(chunks):
            gates[...] = h_refs[j, rows : rows + SPARE, 0:rows].astype(F32)

            def two(i, _, j=j):
                hits = [match(j, 2 * i + half, 0) for half in range(2)]
                sel = jnp.concatenate([pick(hit) for hit in hits], axis=0)
                x = mm(sel, h_refs[j, 0:rows, :], NN)
                gs = mm(sel, g_refs[j], NN)
                for half in range(2):
                    ex = 2 * i + half
                    count = round16(jnp.minimum(cnt_ref[j * EXPERTS + ex], TILE))
                    part = slice(half * TILE, (half + 1) * TILE)
                    store_rows(off_ref[j * EXPERTS + ex], count, hits[half], x[part], gs[part], gates[pl.ds(ex, 1), :])
                return 0

            lax.fori_loop(0, EXPERTS // 2, two, 0)

            def rare(ex, _, j=j):
                def more(tile, _):
                    hit = match(j, ex, tile)
                    sel = pick(hit)
                    count = round16(jnp.minimum(cnt_ref[j * EXPERTS + ex] - tile * TILE, TILE))
                    store_rows(
                        off_ref[j * EXPERTS + ex] + tile * TILE,
                        count,
                        hit,
                        mm(sel, h_refs[j, 0:rows, :], NN),
                        mm(sel, g_refs[j], NN),
                        gates[pl.ds(ex, 1), :],
                    )
                    return 0

                return lax.fori_loop(1, (cnt_ref[j * EXPERTS + ex] + (TILE - 1)) // TILE, more, 0)

            lax.fori_loop(0, EXPERTS, rare, 0)

    gacc[...] = jnp.zeros_like(gacc)

    def tile_step(m, _):
        at = pl.ds(pl.multiple_of(base_ref[e] + m * ROWS, 16), ROWS)
        x = xbuf[at, :]
        gs = gbuf[at, :].astype(F32)
        gate = wide(cbuf[at, :])
        u = mm(x, w_ref[:, 0:ff], NN)
        up = mm(x, w_ref[:, ff : 2 * ff], NN)
        sig = jax.nn.sigmoid(u)
        silu = u * sig
        act = (silu * up).astype(BF16)
        f = mm(act, w_ref[:, 2 * ff : 3 * ff], NT)
        cbuf[at, :] = jnp.broadcast_to(jnp.sum(gs * f, axis=1, keepdims=True), (ROWS, 128))
        gbuf[at, :] = (f * gate).astype(BF16)
        df = (gs * gate).astype(BF16)
        dact = mm(df, w_ref[:, 2 * ff : 3 * ff], NN)
        dup = (dact * silu).astype(BF16)
        du = (dact * up * sig * (1.0 + u * (1.0 - sig))).astype(BF16)
        xbuf[at, :] = (mm(du, w_ref[:, 0:ff], NT) + mm(dup, w_ref[:, ff : 2 * ff], NT)).astype(BF16)
        gacc[:, 0:ff] += mm(x, du, TN)
        gacc[:, ff : 2 * ff] += mm(x, dup, TN)
        gacc[:, 2 * ff : 3 * ff] += mm(df, act, TN)
        return 0

    lax.fori_loop(0, nt_ref[e], tile_step, 0)
    gw_ref[...] = gacc[...].astype(BF16)

    @pl.when(e == EXPERTS - 1)
    def _scatter():
        for j in range(chunks):
            def take(ex, _, j=j):
                at = pl.ds(pl.multiple_of(off_ref[j * EXPERTS + ex], 16), TILE)
                to = pl.ds(pl.multiple_of(ex * TILE, 16), TILE)
                hit = match(j, ex, 0)
                onehot[to, :] = pick(hit)
                fbuf[to, :] = gbuf[at, :]
                dbuf[to, :] = xbuf[at, :]
                col = jnp.concatenate([cbuf[at, :]] * (rows // 128), axis=1)
                dgrow[pl.ds(ex, 1), :] = jnp.sum(jnp.where(hit, col, 0.0), axis=0, keepdims=True)
                return 0

            lax.fori_loop(0, EXPERTS, take, 0)
            gacc[0:rows, 0:D] = mm(onehot[...], fbuf[...], TN)
            gacc[0:rows, D : 2 * D] = mm(onehot[...], dbuf[...], TN)

            def rare(ex, _, j=j):
                def more(tile, _):
                    at = pl.ds(pl.multiple_of(off_ref[j * EXPERTS + ex] + tile * TILE, 16), TILE)
                    hit = match(j, ex, tile)
                    sel = pick(hit)
                    gacc[0:rows, 0:D] += mm(sel, gbuf[at, :], TN)
                    gacc[0:rows, D : 2 * D] += mm(sel, xbuf[at, :], TN)
                    col = jnp.concatenate([cbuf[at, :]] * (rows // 128), axis=1)
                    dgrow[pl.ds(ex, 1), :] += jnp.sum(jnp.where(hit, col, 0.0), axis=0, keepdims=True)
                    return 0

                return lax.fori_loop(1, (cnt_ref[j * EXPERTS + ex] + (TILE - 1)) // TILE, more, 0)

            lax.fori_loop(0, EXPERTS, rare, 0)
            o_refs[j] = gacc[0:rows, 0:D].astype(BF16)
            d_refs[j, 0:rows, :] = gacc[0:rows, D : 2 * D].astype(BF16)
            total = dgrow[...]
            high = total.astype(BF16).astype(F32)
            both = jnp.concatenate([high, total - high], axis=0)
            d_refs[j, rows : rows + SPARE, :] = jnp.concatenate(
                [both, jnp.zeros((SPARE, D - rows), F32)], axis=1
            ).astype(BF16)


def experts_call(counts, hs, gs, slots, weights, ff):
    chunks, rows = gs.shape[:2]
    width = 3 * ff
    most = (rows + 15 * chunks + ROWS - 1) // ROWS * ROWS * EXPERTS + ROWS
    whole = lambda shape: pl.BlockSpec(shape, lambda e: (0,) * len(shape), pipeline_mode=pl.Buffered(1))
    return pl.pallas_call(
        functools.partial(experts_body, ff, chunks),
        name="experts",
        grid=(EXPERTS,),
        in_specs=[smem(), whole(hs.shape), whole(gs.shape), whole(slots.shape), pl.BlockSpec((D, width), lambda e: (0, e))],
        out_specs=[whole(gs.shape), whole(hs.shape), pl.BlockSpec((D, width), lambda e: (0, e))],
        out_shape=[
            jax.ShapeDtypeStruct(gs.shape, BF16),
            jax.ShapeDtypeStruct(hs.shape, BF16),
            jax.ShapeDtypeStruct((D, EXPERTS * width), BF16),
        ],
        scratch_shapes=[
            pltpu.VMEM((most, D), BF16),
            pltpu.VMEM((most, D), BF16),
            pltpu.VMEM((most, 128), F32),
            pltpu.VMEM((EXPERTS * TILE, rows), BF16),
            pltpu.VMEM((EXPERTS * TILE, D), BF16),
            pltpu.VMEM((EXPERTS * TILE, D), BF16),
            pltpu.VMEM((D, width), F32),
            pltpu.VMEM((SPARE, rows), F32),
            pltpu.VMEM((EXPERTS, rows), F32),
            pltpu.SMEM((chunks * EXPERTS,), I32),
            pltpu.SMEM((EXPERTS,), I32),
            pltpu.SMEM((EXPERTS,), I32),
        ],
        compiler_params=pltpu.CompilerParams(
            dimension_semantics=("arbitrary",), vmem_limit_bytes=VMEM_CAP
        ),
    )(counts, hs, gs, slots, weights)


def rope_tables(lengths, first, count):
    finish = jnp.sum(jnp.where(jnp.arange(lengths.shape[0])[:, None] <= jnp.arange(lengths.shape[0])[None, :], lengths[:, None], 0), axis=0)
    begins = finish - lengths
    rows = first + jnp.arange(count, dtype=I32)
    opening = jnp.max(jnp.where(begins[None, :] <= rows[:, None], begins[None, :], 0), axis=1)
    place = rows - opening
    half = HEAD_DIM // 2
    rates = jnp.exp(jnp.arange(half, dtype=F32) * (-2.0 * math.log(10000.0) / HEAD_DIM))
    angles = place.astype(F32)[:, None] * rates[None, :]
    cos, sin = jnp.cos(angles), jnp.sin(angles)
    return place, jnp.concatenate([cos] * 4, axis=1), jnp.concatenate([-sin, sin] * 2, axis=1)


def body(tokens, cotangent, deal, lengths, routes, gate_residual, w_qkv, w_out, w_gate_up, w_down,
         norm_gain_attn, norm_gain_moe, w_router, w_const, v_const):
    rows = tokens.shape[0]
    n_dp, n_t = lax.axis_size("dp"), lax.axis_size("tensor")
    t = lax.axis_index("tensor")
    ff = w_down.shape[2]
    d_here = w_qkv.shape[0]

    def swap(v, j):
        return lax.ppermute(v, "tensor", [(i, i ^ j) for i in range(n_t)])

    def place_in(parts):
        stacked = jnp.stack(parts)
        return jnp.stack([lax.dynamic_index_in_dim(stacked, t ^ i, 0, keepdims=False) for i in range(n_t)], axis=2)

    attn_shard = jnp.concatenate([w_qkv, w_out[:, None, :]], axis=1)
    attn_shard = place_in([attn_shard] + [swap(attn_shard, j) for j in range(1, n_t)]).reshape(d_here, 4 * D)
    w_attn = lax.all_gather(attn_shard, "dp", axis=0, tiled=True)
    ff_shard = jnp.concatenate([w_gate_up.reshape(d_here, EXPERTS, 2 * ff), w_down], axis=2)
    w_ff = lax.all_gather(ff_shard.reshape(d_here, EXPERTS * 3 * ff), "dp", axis=0, tiled=True)

    routes_t = routes.reshape(n_t, rows, 2).transpose(0, 2, 1)
    row, ext = (rows, D), (3 * rows, D)
    every, every_packed = (n_t, rows, D), (n_t, rows + SPARE, D)
    xs, gs, pos, slots, counts = call(
        functools.partial(deal_body, n_dp),
        "deal",
        [(row, BF16), (row, BF16), ((1, rows), I32), ((n_t, EXPERTS, rows), I32), ((n_t, EXPERTS, 128), I32)],
        [deal.reshape(1, rows), tokens, cotangent, routes_t],
    )
    counts = counts[:, :, 0].reshape(n_t * EXPERTS)
    x0 = lax.all_to_all(xs, "dp", split_axis=0, concat_axis=0, tiled=True)
    g0 = lax.all_to_all(gs, "dp", split_axis=0, concat_axis=0, tiled=True)

    place, cos, sin = rope_tables(lengths[0], (t - 2) * rows, 3 * rows)
    start = (LONGEST + jnp.arange(rows, dtype=I32) - place[2 * rows :]).reshape(1, rows)
    gain_attn, gain_moe = norm_gain_attn.reshape(1, D), norm_gain_moe.reshape(1, D)
    window = LONGEST + 256
    res_t = jnp.concatenate([gate_residual.T, jnp.zeros((4, rows), F32)], axis=0)
    wrc = jnp.concatenate([w_router.T, w_const.transpose(0, 2, 1).reshape(4, D)], axis=0)
    v8 = jnp.concatenate([v_const, jnp.zeros((6, D), F32)], axis=0)
    dma = lambda *shape: pltpu.SemaphoreType.DMA(shape)
    x1, x2, h, q, k, v, o, lse, xm, hp_all, g_all, gt, xl, dhl, sm, gv = call(
        functools.partial(forward_body, n_t),
        "forward",
        [(row, BF16), (row, BF16), (ext, BF16), (row, BF16), (ext, BF16), (ext, BF16), (row, BF16), ((SPARE, rows), F32),
         (row, F32), (every_packed, BF16), (every, BF16), ((8, rows), F32), (row, F32), (row, F32), ((SPARE, rows), F32), ((8, D), F32)],
        [x0, g0, w_attn, gain_attn, gain_moe, cos, sin, start, res_t, wrc, routes_t, v8],
        scratch=[pltpu.VMEM((window, 256), F32), dma(2), dma(2)] + [dma(3)] * 8,
        meet=0,
    )

    out_all, back_all, gw_ff = experts_call(counts, hp_all, g_all, slots, w_ff, ff)
    ff_sum = lax.psum_scatter(gw_ff, "dp", scatter_dimension=0, tiled=True)
    h2 = lax.dynamic_index_in_dim(hp_all, t, 0, keepdims=False)[0:rows]

    dx, da, dres, small, dq, dk, dv, result = call(
        functools.partial(backward_body, n_t),
        "backward",
        [(row, F32), (row, BF16), ((SPARE, rows), F32), ((SPARE + 8, D), F32), (row, BF16), (ext, BF16), (ext, BF16), (row, BF16)],
        [back_all, out_all, dhl, gt, sm, routes_t, wrc, xm, gain_moe, g0, h2, w_attn, o, gv, q, k, v, lse, start, cos, sin, xl],
        scratch=[pltpu.VMEM((rows // 256, window, 256), F32), pltpu.VMEM((3 * rows, 128), F32), pltpu.VMEM((3 * rows, 128), F32),
                 pltpu.VMEM((rows + SPARE, D), F32), pltpu.VMEM(row, BF16), pltpu.VMEM((SPARE, rows), F32)]
        + [pltpu.VMEM((n_t - 1, rows + SPARE, D), BF16)] * 2 + [pltpu.VMEM((n_t - 1, rows, D), BF16)] * 2
        + [dma(n_t - 1, 2)] * 4 + [dma(n_t - 1, 1)] * 4,
        meet=1,
    )
    if n_dp == 8 and d_here % 16 == 0 and rows % 128 == 0:
        units, share = 4, rows // n_dp
        piece = (d_here, D)
        hops = 3 + (n_t - 1).bit_length()
        output, grad_tokens, attn_parts, small_all = call(
            functools.partial(finish_body, n_dp, n_t),
            "finish",
            [(row, BF16), (row, BF16), ((units, d_here, D // n_t), F32), ((SPARE + 16, D), F32)],
            [x0, x1, x2, h, dq, dk, dv, da, o, w_attn, dx, gain_attn, result.reshape(n_dp, share, D), small, pos],
            scratch=[pltpu.VMEM(row, F32)] + [pltpu.VMEM(row, BF16)] * 4 + [pltpu.VMEM((n_dp, share, D), BF16)] * 3
            + [pltpu.VMEM((units, n_dp) + piece, BF16), pltpu.VMEM((units, 4) + piece, BF16), pltpu.VMEM((units, 2) + piece, BF16),
               pltpu.VMEM((units,) + piece, BF16), pltpu.VMEM((units, n_t, d_here, D // n_t), BF16),
               pltpu.VMEM((units, n_t - 1, d_here, D // n_t), BF16)]
            + [pltpu.VMEM((hops, SPARE + 16, D), F32)] * 2
            + [dma(2)] * 2 + [dma(n_dp - 1)] * 4 + [dma(units, 4)] * 2 + [dma(units, 2)] * 2 + [dma(units)] * 2
            + [dma(units, n_t - 1)] * 2 + [dma(hops)] * 2,
            meet=2,
        )
        gain_all = small_all[SPARE + 8]
        attn_own = jnp.stack([attn_parts[2], attn_parts[0], attn_parts[1], attn_parts[3]], axis=1)
    else:
        back_out = lax.all_to_all(result, "dp", split_axis=0, concat_axis=0, tiled=True)
        gw_attn, gain_part, d_start = call(
            functools.partial(grads_body, n_t),
            "grads",
            [((D, 4 * D), BF16), ((8, D), F32), (row, BF16)],
            [x0, x1, x2, h, dq, dk, dv, da, o, w_attn, dx, gain_attn],
            scratch=[pltpu.VMEM(row, F32)] + [pltpu.VMEM(row, BF16)] * 4 + [dma(2), dma(2)],
            meet=2,
        )
        back_grad = lax.all_to_all(d_start, "dp", split_axis=0, concat_axis=0, tiled=True)
        output, grad_tokens = call(restore_body, "restore", [(row, BF16)] * 2, [pos, back_out, back_grad])

        def total(v):
            for axis, count in (("tensor", n_t), ("dp", n_dp)):
                bit = 1
                while bit < count:
                    v = v + lax.ppermute(v, axis, [(i, i ^ bit) for i in range(count)])
                    bit *= 2
            return v

        small_all = total(jnp.concatenate([small, gain_part], axis=0))
        gain_all = small_all[SPARE + 8]
        gw_attn, ff_sum = lax.optimization_barrier((gw_attn, ff_sum))
        attn_sum = lax.psum_scatter(gw_attn, "dp", scatter_dimension=0, tiled=True).reshape(d_here, 4, n_t, D // n_t)

        def share(j):
            return lax.dynamic_index_in_dim(attn_sum, t ^ j, 2, keepdims=False)

        attn_own = share(0).astype(F32)
        for j in range(1, n_t):
            attn_own = attn_own + swap(share(j), j).astype(F32)
    ff_own = ff_sum.reshape(d_here, EXPERTS, 3 * ff).astype(F32)
    return (
        output,
        grad_tokens,
        dres[0:12].T,
        attn_own[:, 0:3],
        attn_own[:, 3],
        ff_own[:, :, 0 : 2 * ff].reshape(d_here, EXPERTS, 2, ff),
        ff_own[:, :, 2 * ff :],
        gain_all,
        small_all[SPARE + 2],
        small_all[0:12].T,
        small_all[12:16].reshape(2, 2, D).transpose(0, 2, 1),
        small_all[SPARE : SPARE + 2],
    )


def solution(mesh):
    both, every = P(("dp", "tensor"), None), P()
    weights = (P("dp", None, "tensor"), P("dp", "tensor"), P("dp", None, None, "tensor"), P("dp", None, "tensor"))
    return jax.shard_map(
        body,
        mesh=mesh,
        in_specs=(both, both, P(("dp", "tensor")), P("dp", None), P("dp", None), both, *weights) + (every,) * 5,
        out_specs=(both, both, both, *weights) + (every,) * 5,
        check_vma=False,
    )
```

```python
import functools
import math

import jax
import jax.numpy as jnp
from jax import lax
from jax.experimental import pallas as pl
from jax.experimental.pallas import tpu as pltpu
from jax.sharding import PartitionSpec as P

D = 768
HEAD_DIM = 64
HEADS = 12
EXPERTS = 8
LONGEST = 1024
EPSILON = 1e-6
MASKED = -1e30
F32, BF16, I32 = jnp.float32, jnp.bfloat16, jnp.int32
NN = (((1,), (0,)), ((), ()))
NT = (((1,), (1,)), ((), ()))
TN = (((0,), (0,)), ((), ()))
SCORE_SCALE = HEAD_DIM**-0.5
LOG2E = 1.4426950408889634
TILE = 160
ROWS = 192
SPARE = 16
VMEM_CAP = 66_000_000


def mm(a, b, dims):
    return lax.dot_general(a, b, dims, preferred_element_type=F32)


def iota(shape, axis):
    return lax.broadcasted_iota(I32, shape, axis)


def pick(cond):
    return jnp.where(cond, 1.0, 0.0).astype(BF16)


def split2(v):
    high = v.astype(BF16)
    return high, (v - high.astype(F32)).astype(BF16)


def split3(v):
    high = v.astype(BF16)
    rest = v - high.astype(F32)
    mid = rest.astype(BF16)
    return high, mid, (rest - mid.astype(F32)).astype(BF16)


def vmem():
    return pl.BlockSpec(memory_space=pltpu.VMEM)


def smem():
    return pl.BlockSpec(memory_space=pltpu.SMEM)


def call(body, name, outs, operands, scalars=0, scratch=(), meet=None):
    return pl.pallas_call(
        body,
        name=name,
        out_shape=[jax.ShapeDtypeStruct(*o) for o in outs],
        in_specs=[smem()] * scalars + [vmem()] * (len(operands) - scalars),
        out_specs=[vmem()] * len(outs),
        scratch_shapes=list(scratch),
        compiler_params=pltpu.CompilerParams(
            vmem_limit_bytes=VMEM_CAP, collective_id=meet, has_side_effects=meet is not None
        ),
    )(*operands)


def deal_body(n_dp, deal_ref, tok_ref, cot_ref, routes_ref, xs_ref, gs_ref, pos_ref, slot_ref, cnt_ref):
    rows = tok_ref.shape[0]
    first, second = iota((rows, rows), 0), iota((rows, rows), 1)
    before = pick(first < second)
    deal = deal_ref[...]
    hit = iota((n_dp, rows), 0) == deal
    rank = mm(pick(hit), before, NN)
    rank = jnp.sum(jnp.where(hit, rank, 0.0), axis=0, keepdims=True).astype(I32)
    pos = deal * (rows // n_dp) + rank
    pos_ref[...] = pos
    place = pick(first == pos)
    xs_ref[...] = mm(place, tok_ref[...], NN).astype(BF16)
    gs_ref[...] = mm(place, cot_ref[...], NN).astype(BF16)
    expert = iota((EXPERTS, rows), 0)
    for j in range(routes_ref.shape[0]):
        route = routes_ref[j]
        named = (expert == route[0:1]) | (expert == route[1:2])
        ahead = mm(pick(named), before, NN).astype(I32)
        slot_ref[j] = jnp.where(named, ahead, -1)
        total = jnp.sum(jnp.where(named, 1.0, 0.0), axis=1, keepdims=True).astype(I32)
        cnt_ref[j] = jnp.broadcast_to(total, (EXPERTS, 128))


def restore_body(pos_ref, a_ref, b_ref, oa_ref, ob_ref):
    rows = a_ref.shape[0]
    place = pick(iota((rows, rows), 0) == pos_ref[...])
    oa_ref[...] = mm(place, a_ref[...], TN).astype(BF16)
    ob_ref[...] = mm(place, b_ref[...], TN).astype(BF16)


class Line:
    def __init__(self, size):
        self.size = size
        self.place = lax.axis_index("tensor")
        self.sent = {k: [] for k in range(size)}

    def each(self, body):
        for k in range(self.size):
            pl.when(self.place == k)(functools.partial(body, k))

    def enter(self):
        sem = pltpu.get_barrier_semaphore()

        def greet(k):
            near = [n for n in (k - 1, k + 1) if 0 <= n < self.size]
            for n in near:
                pl.semaphore_signal(sem, 1, device_id={"tensor": self.place + (n - k)}, device_id_type=pl.DeviceIdType.MESH)
            pl.semaphore_wait(sem, len(near))

        self.each(greet)

    def copy(self, hop, src, dst, sems):
        return pltpu.make_async_remote_copy(
            src_ref=src,
            dst_ref=dst,
            send_sem=sems[0],
            recv_sem=sems[1],
            device_id={"tensor": self.place + hop},
            device_id_type=pl.DeviceIdType.MESH,
        )

    def send(self, k, to, refs):
        self.copy(to - k, *refs()).start()
        self.sent[k].append((to - k, refs))

    def arrived(self, k, dst, sems):
        self.copy((k ^ 1) - k, dst, dst, sems).wait_recv()

    def leave(self):
        def drain(k):
            for hop, refs in self.sent[k]:
                self.copy(hop, *refs()).wait_send()

        self.each(drain)


def sum_events(size, k):
    events = []
    for dest in range(size):
        if dest >= k and dest > 0:
            events.append((0 if k == 0 else size - 1 - dest + k, 1, dest))
        if dest <= k and dest < size - 1:
            events.append((0 if k == size - 1 else dest + size - 1 - k, -1, dest))
    drop = [(t, w, d) for t, w, d in events if (k == 0 and w == 1 and d == 0) or (k == size - 1 and w == -1 and d == k)]
    return sorted((ev for ev in events if ev not in drop), key=lambda ev: (ev[0], ev[1], -ev[1] * ev[2]))


def turn(u):
    low = (iota((1, u.shape[1]), 1) % HEAD_DIM) < HEAD_DIM // 2
    half = HEAD_DIM // 2
    return jnp.where(low, pltpu.roll(u, u.shape[1] - half, 1), pltpu.roll(u, half, 1))


def wide(table):
    return jnp.concatenate([table] * (D // 128), axis=1)


def key_bias(start, block, first_row, base):
    window = LONGEST + block
    key = iota((window, block), 0) + first_row
    row = iota((1, block), 1) + (base + first_row)
    return jnp.where((key >= start) & (key <= row), 0.0, MASKED)


def router_part(route, o_ref, w_ref, x_ref, gain_ref, res_ref, wrc_ref, x1_ref, hp_ref, gt_ref):
    rows = o_ref.shape[0]
    x1 = x_ref[...].astype(F32) + mm(o_ref[...], w_ref[:, 3 * D : 4 * D], NT)
    x1_ref[...] = x1
    h = x1 * lax.rsqrt(jnp.mean(x1 * x1, axis=1, keepdims=True) + EPSILON) * gain_ref[...]
    h = h.astype(BF16)
    hp_ref[0:rows, :] = h
    high, mid, low = split3(wrc_ref[...])
    z = mm(low, h, NT) + mm(mid, h, NT) + mm(high, h, NT) + res_ref[...]
    expert = iota(z.shape, 0)
    named0, named1 = expert == route[0:1], expert == route[1:2]
    c0 = jnp.sum(jnp.where(named0, z, 0.0), axis=0, keepdims=True)
    c1 = jnp.sum(jnp.where(named1, z, 0.0), axis=0, keepdims=True)
    top = jnp.maximum(c0, c1)
    e0, e1 = jnp.exp(c0 - top), jnp.exp(c1 - top)
    g0, g1 = e0 / (e0 + e1), e1 / (e0 + e1)
    table = [g0, g1]
    for j in range(2):
        l0, l1 = z[12 + 2 * j : 13 + 2 * j], z[13 + 2 * j : 14 + 2 * j]
        top = jnp.maximum(l0, l1)
        m0, m1 = jnp.exp(l0 - top), jnp.exp(l1 - top)
        table += [m0 / (m0 + m1), m1 / (m0 + m1)]
    gt_ref[...] = jnp.concatenate(table + [jnp.zeros((2, rows), F32)], axis=0)
    gates = jnp.where(named0, g0, jnp.where(named1, g1, 0.0))
    gates = jnp.where(expert < EXPERTS, gates, 0.0)
    hp_ref[rows : rows + SPARE, :] = jnp.concatenate([gates, jnp.zeros((SPARE, D - rows), F32)], axis=1).astype(BF16)


def local_part(route, x1_ref, hp_ref, g_ref, gt_ref, v_ref, xl_ref, dhl_ref, sm_ref, gv_ref):
    rows = x1_ref.shape[0]
    h, g = hp_ref[0:rows, :], g_ref[...]
    hf, gf = h.astype(F32), g.astype(F32)
    low0 = gt_ref[0:1].astype(BF16).astype(F32)
    low1 = gt_ref[1:2].astype(BF16).astype(F32)

    def weight(e):
        return jnp.where(route[0:1] == e, low0, 0.0) + jnp.where(route[1:2] == e, low1, 0.0)

    copy, first, second = weight(EXPERTS + 1), weight(EXPERTS + 2), weight(EXPERTS + 3)
    m00, m01, m10, m11 = gt_ref[2:3], gt_ref[3:4], gt_ref[4:5], gt_ref[5:6]
    a = copy + first * m00 + second * m10
    b0, b1 = first * m01, second * m11
    table = jnp.concatenate([a, b0, b1, jnp.zeros((125, rows), F32)], axis=0).T
    ac, b0c, b1c = table[:, 0:1], table[:, 1:2], table[:, 2:3]
    v = v_ref[...]
    xl_ref[...] = x1_ref[...] + ac * hf + b0c * v[0:1] + b1c * v[1:2]
    dhl_ref[...] = ac * gf
    ones = jnp.ones((8, D), BF16)
    high, low = split2(hf * gf)
    gh = (mm(ones, high, NT) + mm(ones, low, NT))[0:1]
    vh, vm, vl = split3(v)
    gvs = mm(vl, g, NT) + mm(vm, g, NT) + mm(vh, g, NT)
    gv0, gv1 = gvs[0:1], gvs[1:2]
    zero = jnp.zeros((9, rows), F32)
    dl0 = first * m00 * m01 * (gh - gv0)
    dl1 = second * m10 * m11 * (gh - gv1)
    sm_ref[...] = jnp.concatenate(
        [zero, gh, m00 * gh + m01 * gv0, m10 * gh + m11 * gv1, dl0, -dl0, dl1, -dl1], axis=0
    )
    bh, bm, bl = split3(jnp.concatenate([b0, b1, jnp.zeros((6, rows), F32)], axis=0))
    gv_ref[...] = mm(bl, g, NN) + mm(bm, g, NN) + mm(bh, g, NN)


def forward_body(size, x0_ref, g0_ref, w_ref, gain_ref, gain2_ref, cos_ref, sin_ref, start_ref, res_ref, wrc_ref, routes_ref, v8_ref,
                 x1_ref, x2_ref, h_ref, q_ref, k_ref, v_ref, o_ref, lse_ref, xm_ref, hp_ref, gall_ref, gt_ref, xl_ref,
                 dhl_ref, sm_ref, gv_ref,
                 bias_ref, sx, rx, sgu, rgu, sgd, rgd, shu, rhu, shd, rhd):
    rows = x0_ref.shape[0]
    step = 256
    line = Line(size)
    t = line.place
    last = size - 1
    line.enter()

    def begin(k):
        if k < last:
            line.send(k, k + 1, lambda: (x0_ref, x1_ref, (sx.at[0], rx.at[0])))
        if k > 0:
            line.send(k, k - 1, lambda: (g0_ref, gall_ref.at[k], (sgd.at[0], rgd.at[0])))

    line.each(begin)
    gain = gain_ref[...]

    def project_chunk(c, x_ref):
        def project(i, _):
            at = pl.multiple_of(i * step, step)
            x = x_ref[pl.ds(at, step), :].astype(F32)
            h = x * lax.rsqrt(jnp.mean(x * x, axis=1, keepdims=True) + EPSILON) * gain
            h = h.astype(BF16)
            to = pl.ds(pl.multiple_of(c * rows + i * step, step), step)
            h_ref[to, :] = h
            cos, sin = wide(cos_ref[to, :]), wide(sin_ref[to, :])
            k = mm(h, w_ref[:, D : 2 * D], NN)
            k_ref[to, :] = (k * cos + turn(k) * sin).astype(BF16)
            v_ref[to, :] = mm(h, w_ref[:, 2 * D : 3 * D], NN).astype(BF16)
            if c == 2:
                q = mm(h, w_ref[:, 0:D], NN)
                q_ref[pl.ds(at, step), :] = (q * cos + turn(q) * sin).astype(BF16)
            return 0

        lax.fori_loop(0, rows // step, project, 0)

    project_chunk(2, x0_ref)
    gall_ref[t] = g0_ref[...]

    def second(k):
        if k > 0:
            line.arrived(k, x1_ref, (sx.at[0], rx.at[0]))
        else:
            x1_ref[...] = jnp.zeros_like(x1_ref)
        if 0 < k < last:
            line.send(k, k + 1, lambda: (x1_ref, x2_ref, (sx.at[1], rx.at[1])))
        if k < last:
            line.send(k, k + 1, lambda: (g0_ref, gall_ref.at[k], (sgu.at[0], rgu.at[0])))
            line.arrived(k, gall_ref.at[k + 1], (sgd.at[0], rgd.at[0]))
            if k > 0:
                line.send(k, k - 1, lambda: (gall_ref.at[k + 1], gall_ref.at[k + 1], (sgd.at[1], rgd.at[1])))

    line.each(second)
    project_chunk(1, x1_ref)

    def third(k):
        if k > 1:
            line.arrived(k, x2_ref, (sx.at[1], rx.at[1]))
        else:
            x2_ref[...] = jnp.zeros_like(x2_ref)
        if k + 2 <= last:
            line.arrived(k, gall_ref.at[k + 2], (sgd.at[1], rgd.at[1]))
            if k > 0:
                line.send(k, k - 1, lambda: (gall_ref.at[k + 2], gall_ref.at[k + 2], (sgd.at[2], rgd.at[2])))

    line.each(third)
    project_chunk(0, x2_ref)

    block = step
    window = LONGEST + block
    lane = iota((1, 128), 1) // HEAD_DIM
    for rb in range(rows // block):
        first = rb * block
        bias_ref[...] = key_bias(start_ref[:, first : first + block], block, first, LONGEST)

        def pair(i, _, first=first):
            lanes = pl.ds(pl.multiple_of(i * 128, 128), 128)
            k = k_ref[first : first + window, lanes]
            vt = v_ref[first : first + window, lanes].T
            q = q_ref[first : first + block, lanes]
            parts = []
            for half in range(2):
                qm = jnp.where(lane == half, q, jnp.zeros_like(q))
                s = mm(k, qm, NT) * (SCORE_SCALE * LOG2E) + bias_ref[...]
                top = jnp.max(s, axis=0, keepdims=True)
                p = jnp.exp2(s - top)
                total = jnp.sum(p, axis=0, keepdims=True)
                out = mm(vt[half * HEAD_DIM : (half + 1) * HEAD_DIM], p.astype(BF16), NN)
                parts.append(out * (1.0 / total))
                lse_ref[pl.ds(i * 2 + half, 1), first : first + block] = top + jnp.log2(total)
            o_ref[first : first + block, lanes] = jnp.concatenate(parts, axis=0).T.astype(BF16)
            return 0

        lax.fori_loop(0, HEADS // 2, pair, 0)
        if rb == 0:
            def fourth(k):
                if k > 0:
                    line.arrived(k, gall_ref.at[k - 1], (sgu.at[0], rgu.at[0]))
                    if k < last:
                        line.send(k, k + 1, lambda: (gall_ref.at[k - 1], gall_ref.at[k - 1], (sgu.at[1], rgu.at[1])))

            line.each(fourth)

    route = routes_ref[t]
    router_part(route, o_ref, w_ref, x0_ref, gain2_ref, res_ref, wrc_ref, xm_ref, hp_ref.at[t], gt_ref)

    def fifth(k):
        if k < last:
            line.send(k, k + 1, lambda: (hp_ref.at[k], hp_ref.at[k], (shu.at[0], rhu.at[0])))
        if k > 0:
            line.send(k, k - 1, lambda: (hp_ref.at[k], hp_ref.at[k], (shd.at[0], rhd.at[0])))
        if k > 1:
            line.arrived(k, gall_ref.at[k - 2], (sgu.at[1], rgu.at[1]))
            if k < last:
                line.send(k, k + 1, lambda: (gall_ref.at[k - 2], gall_ref.at[k - 2], (sgu.at[2], rgu.at[2])))

    line.each(fifth)
    local_part(route, xm_ref, hp_ref.at[t], g0_ref, gt_ref, v8_ref, xl_ref, dhl_ref, sm_ref, gv_ref)

    def sixth(k):
        for hop in range(2):
            up, down = k - 1 - hop, k + 1 + hop
            if up >= 0:
                line.arrived(k, hp_ref.at[up], (shu.at[hop], rhu.at[hop]))
                if k < last:
                    line.send(k, k + 1, lambda up=up, hop=hop: (hp_ref.at[up], hp_ref.at[up], (shu.at[hop + 1], rhu.at[hop + 1])))
            if down <= last:
                line.arrived(k, hp_ref.at[down], (shd.at[hop], rhd.at[hop]))
                if k > 0:
                    line.send(k, k - 1, lambda down=down, hop=hop: (hp_ref.at[down], hp_ref.at[down], (shd.at[hop + 1], rhd.at[hop + 1])))
        if k == last:
            line.arrived(k, hp_ref.at[0], (shu.at[2], rhu.at[2]))
            line.arrived(k, gall_ref.at[0], (sgu.at[2], rgu.at[2]))
        if k == 0:
            line.arrived(k, hp_ref.at[last], (shd.at[2], rhd.at[2]))
            line.arrived(k, gall_ref.at[last], (sgd.at[2], rgd.at[2]))

    line.each(sixth)
    line.leave()


def middle_part(route, dh_ref, gt_ref, sm_ref, wrc_ref, x1_ref, gain_ref, g_ref, h2_ref, w_ref, o_ref, gv_ref,
                dx_ref, da_ref, do_ref, delta_ref, dres_ref, small_ref):
    rows = x1_ref.shape[0]
    dgf = dh_ref[rows : rows + SPARE, 0:rows]
    dh = dh_ref[0:rows, :]
    dgate = jnp.concatenate([dgf[0:EXPERTS] + dgf[EXPERTS:], sm_ref[EXPERTS:SPARE]], axis=0)
    expert = iota((SPARE, rows), 0)
    named0, named1 = expert == route[0:1], expert == route[1:2]
    g0, g1 = gt_ref[0:1], gt_ref[1:2]
    d0 = jnp.sum(jnp.where(named0, dgate, 0.0), axis=0, keepdims=True)
    d1 = jnp.sum(jnp.where(named1, dgate, 0.0), axis=0, keepdims=True)
    inner = g0 * d0 + g1 * d1
    dz = jnp.where(named0, g0 * (d0 - inner), jnp.where(named1, g1 * (d1 - inner), 0.0))
    dres_ref[...] = dz
    dz = jnp.where(expert < 12, dz, sm_ref[...])
    zh, zm, zl = split3(dz)
    wh, wm, wl = split3(wrc_ref[...])
    dh = dh + (mm(zh, wl, TN) + mm(zl, wh, TN) + mm(zm, wm, TN) + mm(zh, wm, TN) + mm(zm, wh, TN) + mm(zh, wh, TN))
    h = h2_ref[...]
    small_ref[0:SPARE, :] = mm(zl, h, NN) + mm(zm, h, NN) + mm(zh, h, NN)
    x1 = x1_ref[...]
    r = lax.rsqrt(jnp.mean(x1 * x1, axis=1, keepdims=True) + EPSILON)
    xr = x1 * r
    grad_gain = jnp.sum(dh * xr, axis=0, keepdims=True)
    gv = gv_ref[...]
    small_ref[SPARE : SPARE + 8, :] = jnp.concatenate([gv[0:2], grad_gain, gv[3:8]], axis=0)
    scaled = dh * gain_ref[...]
    dx = g_ref[...].astype(F32) + r * (scaled - xr * jnp.mean(xr * scaled, axis=1, keepdims=True))
    dx_ref[...] = dx
    da = dx.astype(BF16)
    da_ref[...] = da
    do = mm(da, w_ref[:, 3 * D : 4 * D], NN).astype(BF16)
    do_ref[...] = do
    high, low = split2(do.astype(F32) * o_ref[...].astype(F32))
    heads = pick(iota((SPARE, D), 1) // HEAD_DIM == iota((SPARE, D), 0))
    delta_ref[...] = mm(heads, high, NT) + mm(heads, low, NT)


def backward_body(size, back_ref, out_ref, dhl_ref, gt_ref, sm_ref, routes_ref, wrc_ref, xm_ref, gain_ref, g_ref, h2_ref, w_ref,
                  o_ref, gv_ref, q_ref, k_ref, v_ref, lse_ref, start_ref, cos_ref, sin_ref, xl_ref,
                  dx_ref, da_ref, dres_ref, small_ref, dq_ref, dk_ref, dv_ref, y_ref,
                  bias_ref, dkf_ref, dvf_ref, dh_ref, do_ref, delta_ref, bu_ref, bd_ref, fu_ref, fd_ref,
                  sbu, rbu, sbd, rbd, sfu, rfu, sfd, rfd):
    rows = xm_ref.shape[0]
    packed = rows + SPARE
    cut = 272
    pieces = (slice(0, cut), slice(cut, packed))
    line = Line(size)
    t = line.place
    last = size - 1
    line.enter()

    def handle(k, way, dest, part, index, mine_ref, up_ref, down_ref, ups, downs):
        slot = dest - 1 if way == 1 else dest
        first = k == (0 if way == 1 else last)
        mine = mine_ref.at[dest, part]

        def refs():
            held = (up_ref if way == 1 else down_ref).at[slot, part]
            sems = tuple(s.at[slot, index] for s in (ups if way == 1 else downs))
            return mine_ref.at[dest, part] if first else held, held, sems

        _, held, sems = refs()
        if not first:
            line.arrived(k, held, sems)
        if dest != k:
            if not first:
                held[...] = (held[...].astype(F32) + mine[...].astype(F32)).astype(BF16)
            line.send(k, k + way, refs)

    def sum_back(k):
        for _, way, dest in sum_events(size, k):
            for index, part in enumerate(pieces):
                handle(k, way, dest, part, index, back_ref, bu_ref, bd_ref, (sbu, rbu), (sbd, rbd))

    def sum_out(k, now):
        for time, way, dest in sum_events(size, k):
            if time == now:
                handle(k, way, dest, slice(0, rows), 0, out_ref, fu_ref, fd_ref, (sfu, rfu), (sfd, rfd))

    line.each(sum_back)
    line.each(lambda k: sum_out(k, 0))
    dh_ref[...] = back_ref[t].astype(F32)

    @pl.when(t > 0)
    def _():
        dh_ref[...] += bu_ref[t - 1].astype(F32)

    @pl.when(t < last)
    def _():
        dh_ref[...] += bd_ref[t].astype(F32)

    dh_ref[0:rows, :] += dhl_ref[...]
    middle_part(routes_ref[t], dh_ref, gt_ref, sm_ref, wrc_ref, xm_ref, gain_ref, g_ref, h2_ref, w_ref, o_ref, gv_ref,
                dx_ref, da_ref, do_ref, delta_ref, dres_ref, small_ref)
    line.each(lambda k: sum_out(k, 1))

    block = 256
    window = LONGEST + block
    lane = iota((1, 128), 1) // HEAD_DIM
    for rb in range(rows // block):
        first = rb * block
        bias_ref[rb] = key_bias(start_ref[:, first : first + block], block, first, LONGEST)

    def pair(i, _):
        lanes = pl.ds(pl.multiple_of(i * 128, 128), 128)
        for rb in range(rows // block):
            first = rb * block
            k = k_ref[first : first + window, lanes]
            v = v_ref[first : first + window, lanes]
            kt = k.T
            q = q_ref[first : first + block, lanes]
            do = do_ref[first : first + block, lanes]
            dk = jnp.zeros((window, 128), F32)
            dv = jnp.zeros((window, 128), F32)
            parts = []
            for half in range(2):
                qm = jnp.where(lane == half, q, jnp.zeros_like(q))
                dom = jnp.where(lane == half, do, jnp.zeros_like(do))
                head = pl.ds(i * 2 + half, 1)
                s = mm(k, qm, NT) * (SCORE_SCALE * LOG2E) + bias_ref[rb]
                p = jnp.exp2(s - lse_ref[head, first : first + block])
                dp = mm(v, dom, NT)
                ds = (p * (dp - delta_ref[head, first : first + block])).astype(BF16)
                dv = dv + mm(p.astype(BF16), dom, NN)
                dk = dk + mm(ds, qm, NN)
                parts.append(mm(kt[half * HEAD_DIM : (half + 1) * HEAD_DIM], ds, NN))
            dq = jnp.concatenate(parts, axis=0).T * SCORE_SCALE
            at = slice(2 * rows + first, 2 * rows + first + block)
            dq_ref[first : first + block, lanes] = (dq * cos_ref[at, :] - turn(dq) * sin_ref[at, :]).astype(BF16)
            if first == 0:
                dkf_ref[0:window, :] = dk
                dvf_ref[0:window, :] = dv
            else:
                old = window - block
                dkf_ref[first : first + old, :] += dk[0:old]
                dvf_ref[first : first + old, :] += dv[0:old]
                dkf_ref[first + old : first + window, :] = dk[old:]
                dvf_ref[first + old : first + window, :] = dv[old:]
        dk = dkf_ref[...] * SCORE_SCALE
        dk_ref[:, lanes] = (dk * cos_ref[...] - turn(dk) * sin_ref[...]).astype(BF16)
        dv_ref[:, lanes] = dvf_ref[...].astype(BF16)
        return 0

    lax.fori_loop(0, HEADS // 4, pair, 0)
    line.each(lambda k: sum_out(k, 2))
    lax.fori_loop(HEADS // 4, HEADS // 2, pair, 0)
    line.each(lambda k: sum_out(k, 3))
    xl_ref[...] += out_ref[t].astype(F32)

    @pl.when(t > 0)
    def _():
        xl_ref[...] += fu_ref[t - 1].astype(F32)

    @pl.when(t < last)
    def _():
        xl_ref[...] += fd_ref[t].astype(F32)

    y_ref[...] = xl_ref[...].astype(BF16)
    line.leave()


def grads_body(size, x0_ref, x1_ref, x2_ref, h_ref, dq_ref, dk_ref, dv_ref, da_ref, o_ref, w_ref, dx_ref, gain_ref,
               gw_ref, gpart_ref, out_ref, d0_ref, d1_ref, d2_ref, ra_ref, rb_ref, sems_s, sems_r):
    rows = x0_ref.shape[0]
    line = Line(size)
    last = size - 1
    block = 256
    line.enter()

    def hidden(c, d_ref):
        def one(i, _):
            at = pl.ds(pl.multiple_of(i * block, block), block)
            to = pl.ds(pl.multiple_of(c * rows + i * block, block), block)
            total = mm(dk_ref[to, :], w_ref[:, D : 2 * D], NT) + mm(dv_ref[to, :], w_ref[:, 2 * D : 3 * D], NT)
            if c == 2:
                total = total + mm(dq_ref[at, :], w_ref[:, 0:D], NT)
            d_ref[at, :] = total.astype(d_ref.dtype)
            return 0

        lax.fori_loop(0, rows // block, one, 0)

    def gain_of(x_ref, d_ref):
        x = x_ref[...].astype(F32)
        r = lax.rsqrt(jnp.mean(x * x, axis=1, keepdims=True) + EPSILON)
        return jnp.sum(d_ref[...].astype(F32) * x * r, axis=0, keepdims=True)

    hidden(0, d2_ref)

    def first(k):
        if k > 1:
            line.send(k, k - 1, lambda: (d2_ref, ra_ref, (sems_s.at[0], sems_r.at[0])))

    line.each(first)
    hidden(1, d1_ref)
    gain = gain_of(x2_ref, d2_ref) + gain_of(x1_ref, d1_ref)
    h = h_ref[...]

    def weight(column, left, right_ref):
        for c in range(D // 256):
            cols = slice(c * 256, (c + 1) * 256)
            gw_ref[:, column * D + c * 256 : column * D + c * 256 + 256] = mm(left, right_ref[:, cols], TN).astype(BF16)

    weight(1, h, dk_ref)

    def second(k):
        if 0 < k < last:
            line.arrived(k, ra_ref, (sems_s.at[0], sems_r.at[0]))
            d1_ref[...] = (d1_ref[...].astype(F32) + ra_ref[...].astype(F32)).astype(BF16)
        if k > 0:
            line.send(k, k - 1, lambda: (d1_ref, rb_ref, (sems_s.at[1], sems_r.at[1])))

    line.each(second)
    hidden(2, d0_ref)
    gpart_ref[...] = jnp.broadcast_to(gain + gain_of(x0_ref, d0_ref), (8, D))
    weight(2, h, dv_ref)
    weight(0, h[2 * rows :], dq_ref)
    weight(3, da_ref[...], o_ref)

    def third(k):
        if k < last:
            line.arrived(k, rb_ref, (sems_s.at[1], sems_r.at[1]))
            d0_ref[...] += rb_ref[...].astype(F32)

    line.each(third)
    x = x0_ref[...].astype(F32)
    r = lax.rsqrt(jnp.mean(x * x, axis=1, keepdims=True) + EPSILON)
    xr = x * r
    scaled = d0_ref[...] * gain_ref[...]
    out_ref[...] = (dx_ref[...] + r * (scaled - xr * jnp.mean(xr * scaled, axis=1, keepdims=True))).astype(BF16)
    line.leave()


class Peers:
    def __init__(self):
        self.d, self.t = lax.axis_index("dp"), lax.axis_index("tensor")
        self.sent = []

    def enter(self, targets):
        sem = pltpu.get_barrier_semaphore()
        for where in targets:
            pl.semaphore_signal(sem, 1, device_id=where, device_id_type=pl.DeviceIdType.MESH)
        pl.semaphore_wait(sem, len(targets))

    def copy(self, where, src, dst, sems):
        return pltpu.make_async_remote_copy(
            src_ref=src,
            dst_ref=dst,
            send_sem=sems[0],
            recv_sem=sems[1],
            device_id=where,
            device_id_type=pl.DeviceIdType.MESH,
        )

    def send(self, where, src, dst, sems):
        copy = self.copy(where, src, dst, sems)
        copy.start()
        self.sent.append(copy)

    def leave(self):
        for copy in self.sent:
            copy.wait_send()


def flip(index, bit):
    return index + bit * (1 - 2 * ((index // bit) % 2))


def finish_body(n_dp, size, x0_ref, x1_ref, x2_ref, h_ref, dq_ref, dk_ref, dv_ref, da_ref, o_ref, w_ref, dx_ref, gain_ref,
                y_ref, small_ref, pos_ref,
                yo_ref, go_ref, gw_ref, sum_ref,
                d0_ref, d1_ref, d2_ref, ra_ref, rb_ref, out_ref, yr_ref, gr_ref, part_ref, r1_ref, r2_ref, r3_ref,
                zs_ref, zr_ref, cur_ref, got_ref,
                sems_s, sems_r, sy, ry, sg, rg, s1, r1, s2, r2, s3, r3, sz, rz, sb, rb):
    rows = x0_ref.shape[0]
    share = rows // n_dp
    line = Line(size)
    last = size - 1
    block = 256
    net = Peers()
    d, t = net.d, net.t
    place = pick(iota((rows, rows), 0) == pos_ref[...])
    around = [(j, lax.rem(d + j, n_dp), lax.rem(d + n_dp - j, n_dp)) for j in range(1, n_dp)]
    along = [(j, lax.rem(t + j, size), lax.rem(t + size - j, size)) for j in range(1, size)]
    net.enter([{"dp": to} for _, to, _ in around] + [{"tensor": to} for _, to, _ in along])

    def scatter(src_ref, dst_ref, sems):
        for j, to, _ in around:
            net.send({"dp": to}, src_ref.at[to], dst_ref.at[d], (sems[0].at[j - 1], sems[1].at[j - 1]))
        dst_ref[d] = src_ref[d]

    def gathered(dst_ref, sems):
        for j, _, source in around:
            held = dst_ref.at[source]
            net.copy({"dp": source}, held, held, (sems[0].at[j - 1], sems[1].at[j - 1])).wait_recv()

    scatter(y_ref, yr_ref, (sy, ry))

    def hidden(c, d_ref):
        def one(i, _):
            at = pl.ds(pl.multiple_of(i * block, block), block)
            to = pl.ds(pl.multiple_of(c * rows + i * block, block), block)
            total = mm(dk_ref[to, :], w_ref[:, D : 2 * D], NT) + mm(dv_ref[to, :], w_ref[:, 2 * D : 3 * D], NT)
            if c == 2:
                total = total + mm(dq_ref[at, :], w_ref[:, 0:D], NT)
            d_ref[at, :] = total.astype(d_ref.dtype)
            return 0

        lax.fori_loop(0, rows // block, one, 0)

    def gain_of(x_ref, d_ref):
        x = x_ref[...].astype(F32)
        r = lax.rsqrt(jnp.mean(x * x, axis=1, keepdims=True) + EPSILON)
        return jnp.sum(d_ref[...].astype(F32) * x * r, axis=0, keepdims=True)

    core, x, y = lax.rem(d, 2), lax.rem(d // 2, 2), d // 4
    there = ({"dp": flip(d, 2)}, {"dp": flip(d, 4)})
    deep = D // n_dp

    def weight(u, left, right_ref):
        for c in range(D // 256):
            cols = slice(c * 256, (c + 1) * 256)
            value = mm(left, right_ref[:, cols], TN).astype(BF16)
            part_ref[u, :, :, cols] = value.reshape(n_dp, deep, 256)
        for j in range(4):
            net.send({"dp": flip(d, 1)}, part_ref.at[u, 2 * j + 1 - core], r1_ref.at[u, j], (s1.at[u, j], r1.at[u, j]))

    def add(u, j, arrived):
        spot = 2 * j + core
        part_ref[u, spot] = (part_ref[u, spot].astype(F32) + arrived[...].astype(F32)).astype(BF16)

    def chips(u):
        if u % 2 == 0:
            first = (there[0], [2 * i + 1 - x for i in range(2)], [2 * i + x for i in range(2)])
            return first, (there[1], 2 * (1 - y) + x)
        first = (there[1], [2 * (1 - y) + i for i in range(2)], [2 * y + i for i in range(2)])
        return first, (there[0], 2 * y + 1 - x)

    def halve(u):
        for j in range(4):
            held = r1_ref.at[u, j]
            net.copy({"dp": flip(d, 1)}, held, held, (s1.at[u, j], r1.at[u, j])).wait_recv()
            add(u, j, held)
        where, theirs, _ = chips(u)[0]
        for i in range(2):
            net.send(where, part_ref.at[u, 2 * theirs[i] + core], r2_ref.at[u, i], (s2.at[u, i], r2.at[u, i]))

    def quarter(u):
        (where, _, mine), (after, spot) = chips(u)
        for i in range(2):
            held = r2_ref.at[u, i]
            net.copy(where, held, held, (s2.at[u, i], r2.at[u, i])).wait_recv()
            add(u, mine[i], held)
        net.send(after, part_ref.at[u, 2 * spot + core], r3_ref.at[u], (s3.at[u], r3.at[u]))

    def own(u):
        after = chips(u)[1][0]
        held = r3_ref.at[u]
        net.copy(after, held, held, (s3.at[u], r3.at[u])).wait_recv()
        value = part_ref[u, d].astype(F32) + held[...].astype(F32)
        wide_share = D // size
        for p in range(size):
            zs_ref[u, p] = value[:, p * wide_share : (p + 1) * wide_share].astype(BF16)
        for j, to, _ in along:
            net.send({"tensor": to}, zs_ref.at[u, to], zr_ref.at[u, j - 1], (sz.at[u, j - 1], rz.at[u, j - 1]))

    def whole(u):
        total = zs_ref[u, t].astype(F32)
        for j, _, source in along:
            held = zr_ref.at[u, j - 1]
            net.copy({"tensor": source}, held, held, (sz.at[u, j - 1], rz.at[u, j - 1])).wait_recv()
            total = total + held[...].astype(F32)
        gw_ref[u] = total

    steps = [("dp", bit) for bit in (1, 2, 4, 8) if bit < n_dp] + [("tensor", bit) for bit in (1, 2, 4, 8) if bit < size]

    def small_out(i):
        axis, bit = steps[i]
        mine = t if axis == "tensor" else d
        net.send({axis: flip(mine, bit)}, cur_ref.at[i], got_ref.at[i], (sb.at[i], rb.at[i]))

    def small_in(i):
        axis, bit = steps[i]
        mine = t if axis == "tensor" else d
        held = got_ref.at[i]
        net.copy({axis: flip(mine, bit)}, held, held, (sb.at[i], rb.at[i])).wait_recv()
        total = cur_ref[i] + held[...]
        if i + 1 < len(steps):
            cur_ref[i + 1] = total
            small_out(i + 1)
        else:
            sum_ref[...] = total

    hidden(0, d2_ref)

    def first(k):
        if k > 1:
            line.send(k, k - 1, lambda: (d2_ref, ra_ref, (sems_s.at[0], sems_r.at[0])))

    line.each(first)
    hidden(1, d1_ref)

    def second(k):
        if k == last:
            line.send(k, k - 1, lambda: (d1_ref, rb_ref, (sems_s.at[1], sems_r.at[1])))

    line.each(second)
    h = h_ref[...]
    weight(0, h, dk_ref)
    gain = gain_of(x2_ref, d2_ref) + gain_of(x1_ref, d1_ref)
    weight(1, h, dv_ref)
    halve(0)
    hidden(2, d0_ref)
    gain = gain + gain_of(x0_ref, d0_ref)
    rest = small_ref.shape[0]
    cur_ref[0, 0:rest, :] = small_ref[...]
    cur_ref[0, rest : rest + 8, :] = jnp.broadcast_to(gain, (8, D))
    small_out(0)
    halve(1)

    def third(k):
        if 0 < k < last:
            line.arrived(k, ra_ref, (sems_s.at[0], sems_r.at[0]))
            d1_ref[...] = (d1_ref[...].astype(F32) + ra_ref[...].astype(F32)).astype(BF16)
            line.send(k, k - 1, lambda: (d1_ref, rb_ref, (sems_s.at[1], sems_r.at[1])))

    line.each(third)
    weight(2, h[2 * rows :], dq_ref)
    small_in(0)
    weight(3, da_ref[...], o_ref)
    quarter(0)
    quarter(1)
    halve(2)
    small_in(1)
    halve(3)
    own(0)
    own(1)
    gathered(yr_ref, (sy, ry))
    yo_ref[...] = mm(place, yr_ref[...].reshape(rows, D), TN).astype(BF16)
    quarter(2)
    quarter(3)
    small_in(2)
    own(2)
    own(3)

    def fourth(k):
        if k < last:
            line.arrived(k, rb_ref, (sems_s.at[1], sems_r.at[1]))
            d0_ref[...] += rb_ref[...].astype(F32)

    line.each(fourth)
    xv = x0_ref[...].astype(F32)
    r = lax.rsqrt(jnp.mean(xv * xv, axis=1, keepdims=True) + EPSILON)
    xr = xv * r
    scaled = d0_ref[...] * gain_ref[...]
    value = dx_ref[...] + r * (scaled - xr * jnp.mean(xr * scaled, axis=1, keepdims=True))
    out_ref[...] = value.astype(BF16).reshape(n_dp, share, D)
    scatter(out_ref, gr_ref, (sg, rg))
    for i in range(3, len(steps)):
        small_in(i)
    for u in range(4):
        whole(u)
    gathered(gr_ref, (sg, rg))
    go_ref[...] = mm(place, gr_ref[...].reshape(rows, D), TN).astype(BF16)
    line.leave()
    net.leave()


def experts_body(ff, chunks, cnt_ref, h_refs, g_refs, slot_ref, w_ref, o_refs, d_refs, gw_ref,
                 xbuf, gbuf, cbuf, onehot, fbuf, dbuf, gacc, gates, dgrow, off_ref, base_ref, nt_ref):
    rows = slot_ref.shape[2]
    e = pl.program_id(0)

    def match(j, expert, tile):
        slots = slot_ref[j, pl.ds(expert, 1), :]
        return (iota((TILE, rows), 0) + tile * TILE) == slots

    def store_rows(at, count, hit, x, gs, gate_row):
        to = pl.ds(pl.multiple_of(at, 16), TILE)
        keep = iota((TILE, 1), 0) < count
        col = jnp.sum(jnp.where(hit, gate_row, 0.0), axis=1, keepdims=True)
        xbuf[to, :] = jnp.where(keep, x, xbuf[to, :].astype(F32)).astype(BF16)
        gbuf[to, :] = jnp.where(keep, gs, gbuf[to, :].astype(F32)).astype(BF16)
        cbuf[to, :] = jnp.where(keep, jnp.broadcast_to(col, (TILE, 128)), cbuf[to, :])

    def round16(n):
        return ((n + 15) // 16) * 16

    @pl.when(e == 0)
    def _gather():
        at = jnp.int32(0)
        for ex in range(EXPERTS):
            base_ref[ex] = at
            here = at
            for j in range(chunks):
                off_ref[j * EXPERTS + ex] = here
                here = here + round16(cnt_ref[j * EXPERTS + ex])
            tiles = (here - at + (ROWS - 1)) // ROWS
            nt_ref[ex] = tiles
            tail = pl.ds(pl.multiple_of(here, 16), ROWS)
            xbuf[tail, :] = jnp.zeros((ROWS, D), BF16)
            gbuf[tail, :] = jnp.zeros((ROWS, D), BF16)
            cbuf[tail, :] = jnp.zeros((ROWS, 128), F32)
            at = at + tiles * ROWS
        for j in range(chunks):
            gates[...] = h_refs[j, rows : rows + SPARE, 0:rows].astype(F32)

            def two(i, _, j=j):
                hits = [match(j, 2 * i + half, 0) for half in range(2)]
                sel = jnp.concatenate([pick(hit) for hit in hits], axis=0)
                x = mm(sel, h_refs[j, 0:rows, :], NN)
                gs = mm(sel, g_refs[j], NN)
                for half in range(2):
                    ex = 2 * i + half
                    count = round16(jnp.minimum(cnt_ref[j * EXPERTS + ex], TILE))
                    part = slice(half * TILE, (half + 1) * TILE)
                    store_rows(off_ref[j * EXPERTS + ex], count, hits[half], x[part], gs[part], gates[pl.ds(ex, 1), :])
                return 0

            lax.fori_loop(0, EXPERTS // 2, two, 0)

            def rare(ex, _, j=j):
                def more(tile, _):
                    hit = match(j, ex, tile)
                    sel = pick(hit)
                    count = round16(jnp.minimum(cnt_ref[j * EXPERTS + ex] - tile * TILE, TILE))
                    store_rows(
                        off_ref[j * EXPERTS + ex] + tile * TILE,
                        count,
                        hit,
                        mm(sel, h_refs[j, 0:rows, :], NN),
                        mm(sel, g_refs[j], NN),
                        gates[pl.ds(ex, 1), :],
                    )
                    return 0

                return lax.fori_loop(1, (cnt_ref[j * EXPERTS + ex] + (TILE - 1)) // TILE, more, 0)

            lax.fori_loop(0, EXPERTS, rare, 0)

    gacc[...] = jnp.zeros_like(gacc)

    def tile_step(m, _):
        at = pl.ds(pl.multiple_of(base_ref[e] + m * ROWS, 16), ROWS)
        x = xbuf[at, :]
        gs = gbuf[at, :].astype(F32)
        gate = wide(cbuf[at, :])
        u = mm(x, w_ref[:, 0:ff], NN)
        up = mm(x, w_ref[:, ff : 2 * ff], NN)
        sig = jax.nn.sigmoid(u)
        silu = u * sig
        act = (silu * up).astype(BF16)
        f = mm(act, w_ref[:, 2 * ff : 3 * ff], NT)
        cbuf[at, :] = jnp.broadcast_to(jnp.sum(gs * f, axis=1, keepdims=True), (ROWS, 128))
        gbuf[at, :] = (f * gate).astype(BF16)
        df = (gs * gate).astype(BF16)
        dact = mm(df, w_ref[:, 2 * ff : 3 * ff], NN)
        dup = (dact * silu).astype(BF16)
        du = (dact * up * sig * (1.0 + u * (1.0 - sig))).astype(BF16)
        xbuf[at, :] = (mm(du, w_ref[:, 0:ff], NT) + mm(dup, w_ref[:, ff : 2 * ff], NT)).astype(BF16)
        gacc[:, 0:ff] += mm(x, du, TN)
        gacc[:, ff : 2 * ff] += mm(x, dup, TN)
        gacc[:, 2 * ff : 3 * ff] += mm(df, act, TN)
        return 0

    lax.fori_loop(0, nt_ref[e], tile_step, 0)
    gw_ref[...] = gacc[...].astype(BF16)

    @pl.when(e == EXPERTS - 1)
    def _scatter():
        for j in range(chunks):
            def take(ex, _, j=j):
                at = pl.ds(pl.multiple_of(off_ref[j * EXPERTS + ex], 16), TILE)
                to = pl.ds(pl.multiple_of(ex * TILE, 16), TILE)
                hit = match(j, ex, 0)
                onehot[to, :] = pick(hit)
                fbuf[to, :] = gbuf[at, :]
                dbuf[to, :] = xbuf[at, :]
                col = jnp.concatenate([cbuf[at, :]] * (rows // 128), axis=1)
                dgrow[pl.ds(ex, 1), :] = jnp.sum(jnp.where(hit, col, 0.0), axis=0, keepdims=True)
                return 0

            lax.fori_loop(0, EXPERTS, take, 0)
            gacc[0:rows, 0:D] = mm(onehot[...], fbuf[...], TN)
            gacc[0:rows, D : 2 * D] = mm(onehot[...], dbuf[...], TN)

            def rare(ex, _, j=j):
                def more(tile, _):
                    at = pl.ds(pl.multiple_of(off_ref[j * EXPERTS + ex] + tile * TILE, 16), TILE)
                    hit = match(j, ex, tile)
                    sel = pick(hit)
                    gacc[0:rows, 0:D] += mm(sel, gbuf[at, :], TN)
                    gacc[0:rows, D : 2 * D] += mm(sel, xbuf[at, :], TN)
                    col = jnp.concatenate([cbuf[at, :]] * (rows // 128), axis=1)
                    dgrow[pl.ds(ex, 1), :] += jnp.sum(jnp.where(hit, col, 0.0), axis=0, keepdims=True)
                    return 0

                return lax.fori_loop(1, (cnt_ref[j * EXPERTS + ex] + (TILE - 1)) // TILE, more, 0)

            lax.fori_loop(0, EXPERTS, rare, 0)
            o_refs[j] = gacc[0:rows, 0:D].astype(BF16)
            d_refs[j, 0:rows, :] = gacc[0:rows, D : 2 * D].astype(BF16)
            total = dgrow[...]
            high = total.astype(BF16).astype(F32)
            both = jnp.concatenate([high, total - high], axis=0)
            d_refs[j, rows : rows + SPARE, :] = jnp.concatenate(
                [both, jnp.zeros((SPARE, D - rows), F32)], axis=1
            ).astype(BF16)


def experts_call(counts, hs, gs, slots, weights, ff):
    chunks, rows = gs.shape[:2]
    width = 3 * ff
    most = (rows + 15 * chunks + ROWS - 1) // ROWS * ROWS * EXPERTS + ROWS
    whole = lambda shape: pl.BlockSpec(shape, lambda e: (0,) * len(shape), pipeline_mode=pl.Buffered(1))
    return pl.pallas_call(
        functools.partial(experts_body, ff, chunks),
        name="experts",
        grid=(EXPERTS,),
        in_specs=[smem(), whole(hs.shape), whole(gs.shape), whole(slots.shape), pl.BlockSpec((D, width), lambda e: (0, e))],
        out_specs=[whole(gs.shape), whole(hs.shape), pl.BlockSpec((D, width), lambda e: (0, e))],
        out_shape=[
            jax.ShapeDtypeStruct(gs.shape, BF16),
            jax.ShapeDtypeStruct(hs.shape, BF16),
            jax.ShapeDtypeStruct((D, EXPERTS * width), BF16),
        ],
        scratch_shapes=[
            pltpu.VMEM((most, D), BF16),
            pltpu.VMEM((most, D), BF16),
            pltpu.VMEM((most, 128), F32),
            pltpu.VMEM((EXPERTS * TILE, rows), BF16),
            pltpu.VMEM((EXPERTS * TILE, D), BF16),
            pltpu.VMEM((EXPERTS * TILE, D), BF16),
            pltpu.VMEM((D, width), F32),
            pltpu.VMEM((SPARE, rows), F32),
            pltpu.VMEM((EXPERTS, rows), F32),
            pltpu.SMEM((chunks * EXPERTS,), I32),
            pltpu.SMEM((EXPERTS,), I32),
            pltpu.SMEM((EXPERTS,), I32),
        ],
        compiler_params=pltpu.CompilerParams(
            dimension_semantics=("arbitrary",), vmem_limit_bytes=VMEM_CAP
        ),
    )(counts, hs, gs, slots, weights)


def rope_tables(lengths, first, count):
    finish = jnp.sum(jnp.where(jnp.arange(lengths.shape[0])[:, None] <= jnp.arange(lengths.shape[0])[None, :], lengths[:, None], 0), axis=0)
    begins = finish - lengths
    rows = first + jnp.arange(count, dtype=I32)
    opening = jnp.max(jnp.where(begins[None, :] <= rows[:, None], begins[None, :], 0), axis=1)
    place = rows - opening
    half = HEAD_DIM // 2
    rates = jnp.exp(jnp.arange(half, dtype=F32) * (-2.0 * math.log(10000.0) / HEAD_DIM))
    angles = place.astype(F32)[:, None] * rates[None, :]
    cos, sin = jnp.cos(angles), jnp.sin(angles)
    return place, jnp.concatenate([cos] * 4, axis=1), jnp.concatenate([-sin, sin] * 2, axis=1)


def body(tokens, cotangent, deal, lengths, routes, gate_residual, w_qkv, w_out, w_gate_up, w_down,
         norm_gain_attn, norm_gain_moe, w_router, w_const, v_const):
    rows = tokens.shape[0]
    n_dp, n_t = lax.axis_size("dp"), lax.axis_size("tensor")
    t = lax.axis_index("tensor")
    ff = w_down.shape[2]
    d_here = w_qkv.shape[0]

    def swap(v, j):
        return lax.ppermute(v, "tensor", [(i, i ^ j) for i in range(n_t)])

    def place_in(parts):
        stacked = jnp.stack(parts)
        return jnp.stack([lax.dynamic_index_in_dim(stacked, t ^ i, 0, keepdims=False) for i in range(n_t)], axis=2)

    attn_shard = jnp.concatenate([w_qkv, w_out[:, None, :]], axis=1)
    attn_shard = place_in([attn_shard] + [swap(attn_shard, j) for j in range(1, n_t)]).reshape(d_here, 4 * D)
    w_attn = lax.all_gather(attn_shard, "dp", axis=0, tiled=True)
    ff_shard = jnp.concatenate([w_gate_up.reshape(d_here, EXPERTS, 2 * ff), w_down], axis=2)
    w_ff = lax.all_gather(ff_shard.reshape(d_here, EXPERTS * 3 * ff), "dp", axis=0, tiled=True)

    routes_t = routes.reshape(n_t, rows, 2).transpose(0, 2, 1)
    row, ext = (rows, D), (3 * rows, D)
    every, every_packed = (n_t, rows, D), (n_t, rows + SPARE, D)
    xs, gs, pos, slots, counts = call(
        functools.partial(deal_body, n_dp),
        "deal",
        [(row, BF16), (row, BF16), ((1, rows), I32), ((n_t, EXPERTS, rows), I32), ((n_t, EXPERTS, 128), I32)],
        [deal.reshape(1, rows), tokens, cotangent, routes_t],
    )
    counts = counts[:, :, 0].reshape(n_t * EXPERTS)
    x0 = lax.all_to_all(xs, "dp", split_axis=0, concat_axis=0, tiled=True)
    g0 = lax.all_to_all(gs, "dp", split_axis=0, concat_axis=0, tiled=True)

    place, cos, sin = rope_tables(lengths[0], (t - 2) * rows, 3 * rows)
    start = (LONGEST + jnp.arange(rows, dtype=I32) - place[2 * rows :]).reshape(1, rows)
    gain_attn, gain_moe = norm_gain_attn.reshape(1, D), norm_gain_moe.reshape(1, D)
    window = LONGEST + 256
    res_t = jnp.concatenate([gate_residual.T, jnp.zeros((4, rows), F32)], axis=0)
    wrc = jnp.concatenate([w_router.T, w_const.transpose(0, 2, 1).reshape(4, D)], axis=0)
    v8 = jnp.concatenate([v_const, jnp.zeros((6, D), F32)], axis=0)
    dma = lambda *shape: pltpu.SemaphoreType.DMA(shape)
    x1, x2, h, q, k, v, o, lse, xm, hp_all, g_all, gt, xl, dhl, sm, gv = call(
        functools.partial(forward_body, n_t),
        "forward",
        [(row, BF16), (row, BF16), (ext, BF16), (row, BF16), (ext, BF16), (ext, BF16), (row, BF16), ((SPARE, rows), F32),
         (row, F32), (every_packed, BF16), (every, BF16), ((8, rows), F32), (row, F32), (row, F32), ((SPARE, rows), F32), ((8, D), F32)],
        [x0, g0, w_attn, gain_attn, gain_moe, cos, sin, start, res_t, wrc, routes_t, v8],
        scratch=[pltpu.VMEM((window, 256), F32), dma(2), dma(2)] + [dma(3)] * 8,
        meet=0,
    )

    out_all, back_all, gw_ff = experts_call(counts, hp_all, g_all, slots, w_ff, ff)
    ff_sum = lax.psum_scatter(gw_ff, "dp", scatter_dimension=0, tiled=True)
    h2 = lax.dynamic_index_in_dim(hp_all, t, 0, keepdims=False)[0:rows]

    dx, da, dres, small, dq, dk, dv, result = call(
        functools.partial(backward_body, n_t),
        "backward",
        [(row, F32), (row, BF16), ((SPARE, rows), F32), ((SPARE + 8, D), F32), (row, BF16), (ext, BF16), (ext, BF16), (row, BF16)],
        [back_all, out_all, dhl, gt, sm, routes_t, wrc, xm, gain_moe, g0, h2, w_attn, o, gv, q, k, v, lse, start, cos, sin, xl],
        scratch=[pltpu.VMEM((rows // 256, window, 256), F32), pltpu.VMEM((3 * rows, 128), F32), pltpu.VMEM((3 * rows, 128), F32),
                 pltpu.VMEM((rows + SPARE, D), F32), pltpu.VMEM(row, BF16), pltpu.VMEM((SPARE, rows), F32)]
        + [pltpu.VMEM((n_t - 1, rows + SPARE, D), BF16)] * 2 + [pltpu.VMEM((n_t - 1, rows, D), BF16)] * 2
        + [dma(n_t - 1, 2)] * 4 + [dma(n_t - 1, 1)] * 4,
        meet=1,
    )
    if n_dp == 8 and d_here % 16 == 0 and rows % 128 == 0:
        units, share = 4, rows // n_dp
        piece = (d_here, D)
        hops = 3 + (n_t - 1).bit_length()
        output, grad_tokens, attn_parts, small_all = call(
            functools.partial(finish_body, n_dp, n_t),
            "finish",
            [(row, BF16), (row, BF16), ((units, d_here, D // n_t), F32), ((SPARE + 16, D), F32)],
            [x0, x1, x2, h, dq, dk, dv, da, o, w_attn, dx, gain_attn, result.reshape(n_dp, share, D), small, pos],
            scratch=[pltpu.VMEM(row, F32)] + [pltpu.VMEM(row, BF16)] * 4 + [pltpu.VMEM((n_dp, share, D), BF16)] * 3
            + [pltpu.VMEM((units, n_dp) + piece, BF16), pltpu.VMEM((units, 4) + piece, BF16), pltpu.VMEM((units, 2) + piece, BF16),
               pltpu.VMEM((units,) + piece, BF16), pltpu.VMEM((units, n_t, d_here, D // n_t), BF16),
               pltpu.VMEM((units, n_t - 1, d_here, D // n_t), BF16)]
            + [pltpu.VMEM((hops, SPARE + 16, D), F32)] * 2
            + [dma(2)] * 2 + [dma(n_dp - 1)] * 4 + [dma(units, 4)] * 2 + [dma(units, 2)] * 2 + [dma(units)] * 2
            + [dma(units, n_t - 1)] * 2 + [dma(hops)] * 2,
            meet=2,
        )
        gain_all = small_all[SPARE + 8]
        attn_own = jnp.stack([attn_parts[2], attn_parts[0], attn_parts[1], attn_parts[3]], axis=1)
    else:
        back_out = lax.all_to_all(result, "dp", split_axis=0, concat_axis=0, tiled=True)
        gw_attn, gain_part, d_start = call(
            functools.partial(grads_body, n_t),
            "grads",
            [((D, 4 * D), BF16), ((8, D), F32), (row, BF16)],
            [x0, x1, x2, h, dq, dk, dv, da, o, w_attn, dx, gain_attn],
            scratch=[pltpu.VMEM(row, F32)] + [pltpu.VMEM(row, BF16)] * 4 + [dma(2), dma(2)],
            meet=2,
        )
        back_grad = lax.all_to_all(d_start, "dp", split_axis=0, concat_axis=0, tiled=True)
        output, grad_tokens = call(restore_body, "restore", [(row, BF16)] * 2, [pos, back_out, back_grad])

        def total(v):
            for axis, count in (("tensor", n_t), ("dp", n_dp)):
                bit = 1
                while bit < count:
                    v = v + lax.ppermute(v, axis, [(i, i ^ bit) for i in range(count)])
                    bit *= 2
            return v

        small_all = total(jnp.concatenate([small, gain_part], axis=0))
        gain_all = small_all[SPARE + 8]
        gw_attn, ff_sum = lax.optimization_barrier((gw_attn, ff_sum))
        attn_sum = lax.psum_scatter(gw_attn, "dp", scatter_dimension=0, tiled=True).reshape(d_here, 4, n_t, D // n_t)

        def share(j):
            return lax.dynamic_index_in_dim(attn_sum, t ^ j, 2, keepdims=False)

        attn_own = share(0).astype(F32)
        for j in range(1, n_t):
            attn_own = attn_own + swap(share(j), j).astype(F32)
    ff_own = ff_sum.reshape(d_here, EXPERTS, 3 * ff).astype(F32)
    return (
        output,
        grad_tokens,
        dres[0:12].T,
        attn_own[:, 0:3],
        attn_own[:, 3],
        ff_own[:, :, 0 : 2 * ff].reshape(d_here, EXPERTS, 2, ff),
        ff_own[:, :, 2 * ff :],
        gain_all,
        small_all[SPARE + 2],
        small_all[0:12].T,
        small_all[12:16].reshape(2, 2, D).transpose(0, 2, 1),
        small_all[SPARE : SPARE + 2],
    )


def solution(mesh):
    both, every = P(("dp", "tensor"), None), P()
    weights = (P("dp", None, "tensor"), P("dp", "tensor"), P("dp", None, None, "tensor"), P("dp", None, "tensor"))
    return jax.shard_map(
        body,
        mesh=mesh,
        in_specs=(both, both, P(("dp", "tensor")), P("dp", None), P("dp", None), both, *weights) + (every,) * 5,
        out_specs=(both, both, both, *weights) + (every,) * 5,
        check_vma=False,
    )
```

```python
import functools
import math

import jax
import jax.numpy as jnp
from jax import lax
from jax.experimental import pallas as pl
from jax.experimental.pallas import tpu as pltpu
from jax.sharding import PartitionSpec as P

D = 768
HEAD_DIM = 64
HEADS = 12
EXPERTS = 8
LONGEST = 1024
EPSILON = 1e-6
MASKED = -1e30
F32, BF16, I32 = jnp.float32, jnp.bfloat16, jnp.int32
NN = (((1,), (0,)), ((), ()))
NT = (((1,), (1,)), ((), ()))
TN = (((0,), (0,)), ((), ()))
SCORE_SCALE = HEAD_DIM**-0.5
LOG2E = 1.4426950408889634
TILE = 160
ROWS = 256
SPARE = 16
VMEM_CAP = 66_000_000


def mm(a, b, dims):
    return lax.dot_general(a, b, dims, preferred_element_type=F32)


def iota(shape, axis):
    return lax.broadcasted_iota(I32, shape, axis)


def pick(cond):
    return jnp.where(cond, 1.0, 0.0).astype(BF16)


def split2(v):
    high = v.astype(BF16)
    return high, (v - high.astype(F32)).astype(BF16)


def split3(v):
    high = v.astype(BF16)
    rest = v - high.astype(F32)
    mid = rest.astype(BF16)
    return high, mid, (rest - mid.astype(F32)).astype(BF16)


def vmem():
    return pl.BlockSpec(memory_space=pltpu.VMEM)


def smem():
    return pl.BlockSpec(memory_space=pltpu.SMEM)


def call(body, name, outs, operands, scalars=0, scratch=(), meet=None):
    return pl.pallas_call(
        body,
        name=name,
        out_shape=[jax.ShapeDtypeStruct(*o) for o in outs],
        in_specs=[smem()] * scalars + [vmem()] * (len(operands) - scalars),
        out_specs=[vmem()] * len(outs),
        scratch_shapes=list(scratch),
        compiler_params=pltpu.CompilerParams(
            vmem_limit_bytes=VMEM_CAP, collective_id=meet, has_side_effects=meet is not None
        ),
    )(*operands)


def deal_body(n_dp, deal_ref, tok_ref, cot_ref, routes_ref, xs_ref, gs_ref, pos_ref, slot_ref, cnt_ref):
    rows = tok_ref.shape[0]
    first, second = iota((rows, rows), 0), iota((rows, rows), 1)
    before = pick(first < second)
    deal = deal_ref[...]
    hit = iota((n_dp, rows), 0) == deal
    rank = mm(pick(hit), before, NN)
    rank = jnp.sum(jnp.where(hit, rank, 0.0), axis=0, keepdims=True).astype(I32)
    pos = deal * (rows // n_dp) + rank
    pos_ref[...] = pos
    place = pick(first == pos)
    xs_ref[...] = mm(place, tok_ref[...], NN).astype(BF16)
    gs_ref[...] = mm(place, cot_ref[...], NN).astype(BF16)
    expert = iota((EXPERTS, rows), 0)
    for j in range(routes_ref.shape[0]):
        route = routes_ref[j]
        named = (expert == route[0:1]) | (expert == route[1:2])
        ahead = mm(pick(named), before, NN).astype(I32)
        slot_ref[j] = jnp.where(named, ahead, -1)
        total = jnp.sum(jnp.where(named, 1.0, 0.0), axis=1, keepdims=True).astype(I32)
        cnt_ref[j] = jnp.broadcast_to(total, (EXPERTS, 128))


def restore_body(pos_ref, a_ref, b_ref, oa_ref, ob_ref):
    rows = a_ref.shape[0]
    place = pick(iota((rows, rows), 0) == pos_ref[...])
    oa_ref[...] = mm(place, a_ref[...], TN).astype(BF16)
    ob_ref[...] = mm(place, b_ref[...], TN).astype(BF16)


class Line:
    def __init__(self, size):
        self.size = size
        self.place = lax.axis_index("tensor")
        self.sent = {k: [] for k in range(size)}

    def each(self, body):
        for k in range(self.size):
            pl.when(self.place == k)(functools.partial(body, k))

    def enter(self):
        sem = pltpu.get_barrier_semaphore()

        def greet(k):
            near = [n for n in (k - 1, k + 1) if 0 <= n < self.size]
            for n in near:
                pl.semaphore_signal(sem, 1, device_id={"tensor": self.place + (n - k)}, device_id_type=pl.DeviceIdType.MESH)
            pl.semaphore_wait(sem, len(near))

        self.each(greet)

    def copy(self, hop, src, dst, sems):
        return pltpu.make_async_remote_copy(
            src_ref=src,
            dst_ref=dst,
            send_sem=sems[0],
            recv_sem=sems[1],
            device_id={"tensor": self.place + hop},
            device_id_type=pl.DeviceIdType.MESH,
        )

    def send(self, k, to, refs):
        self.copy(to - k, *refs()).start()
        self.sent[k].append((to - k, refs))

    def arrived(self, k, dst, sems):
        self.copy((k ^ 1) - k, dst, dst, sems).wait_recv()

    def leave(self):
        def drain(k):
            for hop, refs in self.sent[k]:
                self.copy(hop, *refs()).wait_send()

        self.each(drain)


class Peers:
    def __init__(self):
        self.d, self.t = lax.axis_index("dp"), lax.axis_index("tensor")
        self.sent = []

    def enter(self, targets):
        sem = pltpu.get_barrier_semaphore()
        for where in targets:
            pl.semaphore_signal(sem, 1, device_id=where, device_id_type=pl.DeviceIdType.MESH)
        pl.semaphore_wait(sem, len(targets))

    def copy(self, where, src, dst, sems):
        return pltpu.make_async_remote_copy(
            src_ref=src,
            dst_ref=dst,
            send_sem=sems[0],
            recv_sem=sems[1],
            device_id=where,
            device_id_type=pl.DeviceIdType.MESH,
        )

    def send(self, where, src, dst, sems):
        copy = self.copy(where, src, dst, sems)
        copy.start()
        self.sent.append(copy)

    def leave(self):
        for copy in self.sent:
            copy.wait_send()


def flip(index, bit):
    return index + bit * (1 - 2 * ((index // bit) % 2))


def around(index, count):
    return [(j, lax.rem(index + j, count), lax.rem(index + count - j, count)) for j in range(1, count)]


class Rows:
    def __init__(self, ref):
        self.ref = ref

    def __getitem__(self, at):
        columns = slice(None) if at is Ellipsis else at[1]
        value = self.ref[:, :, columns]
        return value.reshape(value.shape[0] * value.shape[1], value.shape[2])


def sum_events(size, k):
    events = []
    for dest in range(size):
        if dest >= k and dest > 0:
            events.append((0 if k == 0 else size - 1 - dest + k, 1, dest))
        if dest <= k and dest < size - 1:
            events.append((0 if k == size - 1 else dest + size - 1 - k, -1, dest))
    drop = [(t, w, d) for t, w, d in events if (k == 0 and w == 1 and d == 0) or (k == size - 1 and w == -1 and d == k)]
    return sorted((ev for ev in events if ev not in drop), key=lambda ev: (ev[0], ev[1], -ev[1] * ev[2]))


def turn(u):
    low = (iota((1, u.shape[1]), 1) % HEAD_DIM) < HEAD_DIM // 2
    half = HEAD_DIM // 2
    return jnp.where(low, pltpu.roll(u, u.shape[1] - half, 1), pltpu.roll(u, half, 1))


def wide(table):
    return jnp.concatenate([table] * (D // 128), axis=1)


def key_bias(start, block, first_row, base):
    window = LONGEST + block
    key = iota((window, block), 0) + first_row
    row = iota((1, block), 1) + (base + first_row)
    return jnp.where((key >= start) & (key <= row), 0.0, MASKED)


def router_part(route, o_ref, w_ref, x_ref, gain_ref, res_ref, wrc_ref, x1_ref, hp_ref, gt_ref):
    rows = o_ref.shape[0]
    x1 = x_ref[...].astype(F32) + mm(o_ref[...], w_ref[:, 3 * D : 4 * D], NT)
    x1_ref[...] = x1
    h = x1 * lax.rsqrt(jnp.mean(x1 * x1, axis=1, keepdims=True) + EPSILON) * gain_ref[...]
    h = h.astype(BF16)
    hp_ref[0:rows, :] = h
    high, mid, low = split3(wrc_ref[...])
    z = mm(low, h, NT) + mm(mid, h, NT) + mm(high, h, NT) + res_ref[...]
    expert = iota(z.shape, 0)
    named0, named1 = expert == route[0:1], expert == route[1:2]
    c0 = jnp.sum(jnp.where(named0, z, 0.0), axis=0, keepdims=True)
    c1 = jnp.sum(jnp.where(named1, z, 0.0), axis=0, keepdims=True)
    top = jnp.maximum(c0, c1)
    e0, e1 = jnp.exp(c0 - top), jnp.exp(c1 - top)
    g0, g1 = e0 / (e0 + e1), e1 / (e0 + e1)
    table = [g0, g1]
    for j in range(2):
        l0, l1 = z[12 + 2 * j : 13 + 2 * j], z[13 + 2 * j : 14 + 2 * j]
        top = jnp.maximum(l0, l1)
        m0, m1 = jnp.exp(l0 - top), jnp.exp(l1 - top)
        table += [m0 / (m0 + m1), m1 / (m0 + m1)]
    gt_ref[...] = jnp.concatenate(table + [jnp.zeros((2, rows), F32)], axis=0)
    gates = jnp.where(named0, g0, jnp.where(named1, g1, 0.0))
    gates = jnp.where(expert < EXPERTS, gates, 0.0)
    hp_ref[rows : rows + SPARE, :] = jnp.concatenate([gates, jnp.zeros((SPARE, D - rows), F32)], axis=1).astype(BF16)


def local_part(route, x1_ref, hp_ref, g_ref, gt_ref, v_ref, xl_ref, dhl_ref, sm_ref, gv_ref):
    rows = x1_ref.shape[0]
    h, g = hp_ref[0:rows, :], g_ref[...]
    hf, gf = h.astype(F32), g.astype(F32)
    low0 = gt_ref[0:1].astype(BF16).astype(F32)
    low1 = gt_ref[1:2].astype(BF16).astype(F32)

    def weight(e):
        return jnp.where(route[0:1] == e, low0, 0.0) + jnp.where(route[1:2] == e, low1, 0.0)

    copy, first, second = weight(EXPERTS + 1), weight(EXPERTS + 2), weight(EXPERTS + 3)
    m00, m01, m10, m11 = gt_ref[2:3], gt_ref[3:4], gt_ref[4:5], gt_ref[5:6]
    a = copy + first * m00 + second * m10
    b0, b1 = first * m01, second * m11
    table = jnp.concatenate([a, b0, b1, jnp.zeros((125, rows), F32)], axis=0).T
    ac, b0c, b1c = table[:, 0:1], table[:, 1:2], table[:, 2:3]
    v = v_ref[...]
    xl_ref[...] = x1_ref[...] + ac * hf + b0c * v[0:1] + b1c * v[1:2]
    dhl_ref[...] = ac * gf
    ones = jnp.ones((8, D), BF16)
    high, low = split2(hf * gf)
    gh = (mm(ones, high, NT) + mm(ones, low, NT))[0:1]
    vh, vm, vl = split3(v)
    gvs = mm(vl, g, NT) + mm(vm, g, NT) + mm(vh, g, NT)
    gv0, gv1 = gvs[0:1], gvs[1:2]
    zero = jnp.zeros((9, rows), F32)
    dl0 = first * m00 * m01 * (gh - gv0)
    dl1 = second * m10 * m11 * (gh - gv1)
    sm_ref[...] = jnp.concatenate(
        [zero, gh, m00 * gh + m01 * gv0, m10 * gh + m11 * gv1, dl0, -dl0, dl1, -dl1], axis=0
    )
    bh, bm, bl = split3(jnp.concatenate([b0, b1, jnp.zeros((6, rows), F32)], axis=0))
    gv_ref[...] = mm(bl, g, NN) + mm(bm, g, NN) + mm(bh, g, NN)


def forward_body(n_dp, size, *refs):
    fast = n_dp > 1
    first_refs, (gain_ref, gain2_ref, cos_ref, sin_ref, start_ref, res_ref, wrc_ref, routes_ref, v8_ref) = refs[:3], refs[3:12]
    refs = refs[12:]
    if fast:
        xs_ref, gs_ref, ws_ref = first_refs
        (x0_ref, g0_ref, w3_ref), refs = refs[:3], refs[3:]
    else:
        x0_ref, g0_ref, w3_ref = first_refs
    (x1_ref, x2_ref, h_ref, q_ref, k_ref, v_ref, o_ref, lse_ref, xm_ref, hp_ref, gall_ref, gt_ref, xl_ref,
     dhl_ref, sm_ref, gv_ref, bias_ref, sx, rx, sgu, rgu, sgd, rgd, shu, rhu, shd, rhd) = refs[:27]
    rows = x0_ref.shape[0] * x0_ref.shape[1]
    step = 256
    line = Line(size)
    t = line.place
    last = size - 1
    w_ref, x_own, g_own = Rows(w3_ref), Rows(x0_ref), Rows(g0_ref)

    def begin(k):
        if k < last:
            line.send(k, k + 1, lambda: (x0_ref, x1_ref, (sx.at[0], rx.at[0])))

    def begin_down(k):
        if k > 0:
            line.send(k, k - 1, lambda: (g0_ref, gall_ref.at[k], (sgd.at[0], rgd.at[0])))

    def second(k):
        if k > 0:
            line.arrived(k, x1_ref, (sx.at[0], rx.at[0]))
        else:
            x1_ref[...] = jnp.zeros_like(x1_ref)
        if 0 < k < last:
            line.send(k, k + 1, lambda: (x1_ref, x2_ref, (sx.at[1], rx.at[1])))
        if k < last:
            line.send(k, k + 1, lambda: (g0_ref, gall_ref.at[k], (sgu.at[0], rgu.at[0])))
            line.arrived(k, gall_ref.at[k + 1], (sgd.at[0], rgd.at[0]))
            if k > 0:
                line.send(k, k - 1, lambda: (gall_ref.at[k + 1], gall_ref.at[k + 1], (sgd.at[1], rgd.at[1])))

    if fast:
        wz_ref, sz, rz, sa, ra, sb, rb_, s1, r1, s2, r2, s3, r3 = refs[27:]
        net = Peers()
        d = net.d
        along, about = around(t, size), around(d, n_dp)
        net.enter([{"dp": to} for _, to, _ in about] + [{"tensor": to} for _, to, _ in along])
        for j, to, _ in along:
            net.send({"tensor": to}, ws_ref, wz_ref.at[t], (sz.at[j - 1], rz.at[j - 1]))
        for src_ref, dst_ref, ss, rr in ((xs_ref, x0_ref, sa, ra), (gs_ref, g0_ref, sb, rb_)):
            for j, to, _ in about:
                net.send({"dp": to}, src_ref.at[to], dst_ref.at[d], (ss.at[j - 1], rr.at[j - 1]))
            dst_ref[d] = src_ref[d]
        wz_ref[t] = ws_ref[...]

        def gathered(dst_ref, ss, rr):
            for j, _, source in about:
                held = dst_ref.at[source]
                net.copy({"dp": source}, held, held, (ss.at[j - 1], rr.at[j - 1])).wait_recv()

        gathered(x0_ref, sa, ra)
        line.each(begin)
        for j, _, source in along:
            held = wz_ref.at[source]
            net.copy({"tensor": source}, held, held, (sz.at[j - 1], rz.at[j - 1])).wait_recv()
        for c in range(4):
            w3_ref[d, :, c * D : (c + 1) * D] = jnp.concatenate([wz_ref[p, c] for p in range(size)], axis=1)
        pair, across = flip(d, 1), (flip(d, 2), flip(d, 4))
        halves = (slice(0, 2 * D), slice(2 * D, 4 * D))

        def pass_on(way, spot, half, sems):
            net.send({"dp": way}, w3_ref.at[spot, :, halves[half]], w3_ref.at[spot, :, halves[half]], sems)

        def passed(way, spot, half, sems):
            held = w3_ref.at[spot, :, halves[half]]
            net.copy({"dp": way}, held, held, sems).wait_recv()

        for half in range(2):
            pass_on(across[half], d, half, (s1.at[half], r1.at[half]))
        gathered(g0_ref, sb, rb_)
        line.each(begin_down)
        gall_ref[t] = g0_ref[...]
        for half in range(2):
            near, far = across[half], across[1 - half]
            passed(near, near, half, (s1.at[half], r1.at[half]))
            for i, spot in enumerate((d, near)):
                pass_on(far, spot, half, (s2.at[half, i], r2.at[half, i]))
        line.each(second)
        beyond = flip(across[0], 4)
        for half in range(2):
            near, far = across[half], across[1 - half]
            for i, spot in enumerate((far, beyond)):
                passed(far, spot, half, (s2.at[half, i], r2.at[half, i]))
        core = lax.rem(d, 2)
        for i in range(n_dp // 2):
            spot = 2 * i + core
            net.send({"dp": pair}, w3_ref.at[spot], w3_ref.at[spot], (s3.at[i], r3.at[i]))
        for i in range(n_dp // 2):
            held = w3_ref.at[2 * i + 1 - core]
            net.copy({"dp": pair}, held, held, (s3.at[i], r3.at[i])).wait_recv()
    else:
        line.enter()
        line.each(begin)
        line.each(begin_down)
    gain = gain_ref[...]

    def part(x_ref, i):
        share = x_ref.shape[1]
        if share == rows:
            return x_ref[0, pl.ds(pl.multiple_of(i * step, step), step), :]
        return x_ref[pl.ds(i * (step // share), step // share)].reshape(step, D)

    def project_chunk(c, x_ref):
        def project(i, _):
            at = pl.multiple_of(i * step, step)
            x = part(x_ref, i).astype(F32)
            h = x * lax.rsqrt(jnp.mean(x * x, axis=1, keepdims=True) + EPSILON) * gain
            h = h.astype(BF16)
            to = pl.ds(pl.multiple_of(c * rows + i * step, step), step)
            h_ref[to, :] = h
            cos, sin = wide(cos_ref[to, :]), wide(sin_ref[to, :])
            k = mm(h, w_ref[:, D : 2 * D], NN)
            k_ref[to, :] = (k * cos + turn(k) * sin).astype(BF16)
            v_ref[to, :] = mm(h, w_ref[:, 2 * D : 3 * D], NN).astype(BF16)
            if c == 2:
                q = mm(h, w_ref[:, 0:D], NN)
                q_ref[pl.ds(at, step), :] = (q * cos + turn(q) * sin).astype(BF16)
            return 0

        lax.fori_loop(0, rows // step, project, 0)

    project_chunk(2, x0_ref)
    if not fast:
        gall_ref[t] = g0_ref[...]
        line.each(second)
    project_chunk(1, x1_ref)

    def third(k):
        if k > 1:
            line.arrived(k, x2_ref, (sx.at[1], rx.at[1]))
        else:
            x2_ref[...] = jnp.zeros_like(x2_ref)
        if k + 2 <= last:
            line.arrived(k, gall_ref.at[k + 2], (sgd.at[1], rgd.at[1]))
            if k > 0:
                line.send(k, k - 1, lambda: (gall_ref.at[k + 2], gall_ref.at[k + 2], (sgd.at[2], rgd.at[2])))

    line.each(third)
    project_chunk(0, x2_ref)

    block = step
    window = LONGEST + block
    lane = iota((1, 128), 1) // HEAD_DIM
    for rb in range(rows // block):
        first = rb * block
        bias_ref[...] = key_bias(start_ref[:, first : first + block], block, first, LONGEST)

        def pair(i, _, first=first):
            lanes = pl.ds(pl.multiple_of(i * 128, 128), 128)
            k = k_ref[first : first + window, lanes]
            vt = v_ref[first : first + window, lanes].T
            q = q_ref[first : first + block, lanes]
            parts = []
            for half in range(2):
                qm = jnp.where(lane == half, q, jnp.zeros_like(q))
                s = mm(k, qm, NT) * (SCORE_SCALE * LOG2E) + bias_ref[...]
                top = jnp.max(s, axis=0, keepdims=True)
                p = jnp.exp2(s - top)
                total = jnp.sum(p, axis=0, keepdims=True)
                out = mm(vt[half * HEAD_DIM : (half + 1) * HEAD_DIM], p.astype(BF16), NN)
                parts.append(out * (1.0 / total))
                lse_ref[pl.ds(i * 2 + half, 1), first : first + block] = top + jnp.log2(total)
            o_ref[first : first + block, lanes] = jnp.concatenate(parts, axis=0).T.astype(BF16)
            return 0

        lax.fori_loop(0, HEADS // 2, pair, 0)
        if rb == 0:
            def fourth(k):
                if k > 0:
                    line.arrived(k, gall_ref.at[k - 1], (sgu.at[0], rgu.at[0]))
                    if k < last:
                        line.send(k, k + 1, lambda: (gall_ref.at[k - 1], gall_ref.at[k - 1], (sgu.at[1], rgu.at[1])))

            line.each(fourth)

    route = routes_ref[t]
    router_part(route, o_ref, w_ref, x_own, gain2_ref, res_ref, wrc_ref, xm_ref, hp_ref.at[t], gt_ref)

    def fifth(k):
        if k < last:
            line.send(k, k + 1, lambda: (hp_ref.at[k], hp_ref.at[k], (shu.at[0], rhu.at[0])))
        if k > 0:
            line.send(k, k - 1, lambda: (hp_ref.at[k], hp_ref.at[k], (shd.at[0], rhd.at[0])))
        if k > 1:
            line.arrived(k, gall_ref.at[k - 2], (sgu.at[1], rgu.at[1]))
            if k < last:
                line.send(k, k + 1, lambda: (gall_ref.at[k - 2], gall_ref.at[k - 2], (sgu.at[2], rgu.at[2])))

    line.each(fifth)
    local_part(route, xm_ref, hp_ref.at[t], g_own, gt_ref, v8_ref, xl_ref, dhl_ref, sm_ref, gv_ref)

    def sixth(k):
        for hop in range(2):
            up, down = k - 1 - hop, k + 1 + hop
            if up >= 0:
                line.arrived(k, hp_ref.at[up], (shu.at[hop], rhu.at[hop]))
                if k < last:
                    line.send(k, k + 1, lambda up=up, hop=hop: (hp_ref.at[up], hp_ref.at[up], (shu.at[hop + 1], rhu.at[hop + 1])))
            if down <= last:
                line.arrived(k, hp_ref.at[down], (shd.at[hop], rhd.at[hop]))
                if k > 0:
                    line.send(k, k - 1, lambda down=down, hop=hop: (hp_ref.at[down], hp_ref.at[down], (shd.at[hop + 1], rhd.at[hop + 1])))
        if k == last:
            line.arrived(k, hp_ref.at[0], (shu.at[2], rhu.at[2]))
            line.arrived(k, gall_ref.at[0], (sgu.at[2], rgu.at[2]))
        if k == 0:
            line.arrived(k, hp_ref.at[last], (shd.at[2], rhd.at[2]))
            line.arrived(k, gall_ref.at[last], (sgd.at[2], rgd.at[2]))

    line.each(sixth)
    line.leave()
    if fast:
        net.leave()


def middle_part(route, dh_ref, gt_ref, sm_ref, wrc_ref, x1_ref, gain_ref, g_ref, h2_ref, w_ref, o_ref, gv_ref,
                dx_ref, da_ref, do_ref, delta_ref, dres_ref, small_ref):
    rows = x1_ref.shape[0]
    dgf = dh_ref[rows : rows + SPARE, 0:rows]
    dh = dh_ref[0:rows, :]
    dgate = jnp.concatenate([dgf[0:EXPERTS] + dgf[EXPERTS:], sm_ref[EXPERTS:SPARE]], axis=0)
    expert = iota((SPARE, rows), 0)
    named0, named1 = expert == route[0:1], expert == route[1:2]
    g0, g1 = gt_ref[0:1], gt_ref[1:2]
    d0 = jnp.sum(jnp.where(named0, dgate, 0.0), axis=0, keepdims=True)
    d1 = jnp.sum(jnp.where(named1, dgate, 0.0), axis=0, keepdims=True)
    inner = g0 * d0 + g1 * d1
    dz = jnp.where(named0, g0 * (d0 - inner), jnp.where(named1, g1 * (d1 - inner), 0.0))
    dres_ref[...] = dz
    dz = jnp.where(expert < 12, dz, sm_ref[...])
    zh, zm, zl = split3(dz)
    wh, wm, wl = split3(wrc_ref[...])
    dh = dh + (mm(zh, wl, TN) + mm(zl, wh, TN) + mm(zm, wm, TN) + mm(zh, wm, TN) + mm(zm, wh, TN) + mm(zh, wh, TN))
    h = h2_ref[...]
    small_ref[0:SPARE, :] = mm(zl, h, NN) + mm(zm, h, NN) + mm(zh, h, NN)
    x1 = x1_ref[...]
    r = lax.rsqrt(jnp.mean(x1 * x1, axis=1, keepdims=True) + EPSILON)
    xr = x1 * r
    grad_gain = jnp.sum(dh * xr, axis=0, keepdims=True)
    gv = gv_ref[...]
    small_ref[SPARE : SPARE + 8, :] = jnp.concatenate([gv[0:2], grad_gain, gv[3:8]], axis=0)
    scaled = dh * gain_ref[...]
    dx = g_ref[...].astype(F32) + r * (scaled - xr * jnp.mean(xr * scaled, axis=1, keepdims=True))
    dx_ref[...] = dx
    da = dx.astype(BF16)
    da_ref[...] = da
    do = mm(da, w_ref[:, 3 * D : 4 * D], NN).astype(BF16)
    do_ref[...] = do
    high, low = split2(do.astype(F32) * o_ref[...].astype(F32))
    heads = pick(iota((SPARE, D), 1) // HEAD_DIM == iota((SPARE, D), 0))
    delta_ref[...] = mm(heads, high, NT) + mm(heads, low, NT)


def backward_body(size, back_ref, out_ref, dhl_ref, gt_ref, sm_ref, routes_ref, wrc_ref, xm_ref, gain_ref, g_ref, h2_ref, w_ref,
                  o_ref, gv_ref, q_ref, k_ref, v_ref, lse_ref, start_ref, cos_ref, sin_ref, xl_ref,
                  dx_ref, da_ref, dres_ref, small_ref, dq_ref, dk_ref, dv_ref, y_ref,
                  bias_ref, dkf_ref, dvf_ref, dh_ref, do_ref, delta_ref, bu_ref, bd_ref, fu_ref, fd_ref,
                  sbu, rbu, sbd, rbd, sfu, rfu, sfd, rfd):
    rows = xm_ref.shape[0]
    packed = rows + SPARE
    cut = 272
    pieces = (slice(0, cut), slice(cut, packed))
    line = Line(size)
    t = line.place
    last = size - 1
    line.enter()

    def handle(k, way, dest, part, index, mine_ref, up_ref, down_ref, ups, downs):
        slot = dest - 1 if way == 1 else dest
        first = k == (0 if way == 1 else last)
        mine = mine_ref.at[dest, part]

        def refs():
            held = (up_ref if way == 1 else down_ref).at[slot, part]
            sems = tuple(s.at[slot, index] for s in (ups if way == 1 else downs))
            return mine_ref.at[dest, part] if first else held, held, sems

        _, held, sems = refs()
        if not first:
            line.arrived(k, held, sems)
        if dest != k:
            if not first:
                held[...] = (held[...].astype(F32) + mine[...].astype(F32)).astype(BF16)
            line.send(k, k + way, refs)

    def sum_back(k):
        for _, way, dest in sum_events(size, k):
            for index, part in enumerate(pieces):
                handle(k, way, dest, part, index, back_ref, bu_ref, bd_ref, (sbu, rbu), (sbd, rbd))

    def sum_out(k, now):
        for time, way, dest in sum_events(size, k):
            if time == now:
                handle(k, way, dest, slice(0, rows), 0, out_ref, fu_ref, fd_ref, (sfu, rfu), (sfd, rfd))

    line.each(sum_back)
    line.each(lambda k: sum_out(k, 0))
    dh_ref[...] = back_ref[t].astype(F32)

    @pl.when(t > 0)
    def _():
        dh_ref[...] += bu_ref[t - 1].astype(F32)

    @pl.when(t < last)
    def _():
        dh_ref[...] += bd_ref[t].astype(F32)

    dh_ref[0:rows, :] += dhl_ref[...]
    middle_part(routes_ref[t], dh_ref, gt_ref, sm_ref, wrc_ref, xm_ref, gain_ref, g_ref, h2_ref, w_ref, o_ref, gv_ref,
                dx_ref, da_ref, do_ref, delta_ref, dres_ref, small_ref)
    line.each(lambda k: sum_out(k, 1))

    block = 256
    window = LONGEST + block
    lane = iota((1, 128), 1) // HEAD_DIM
    for rb in range(rows // block):
        first = rb * block
        bias_ref[rb] = key_bias(start_ref[:, first : first + block], block, first, LONGEST)

    def pair(i, _):
        lanes = pl.ds(pl.multiple_of(i * 128, 128), 128)
        for rb in range(rows // block):
            first = rb * block
            k = k_ref[first : first + window, lanes]
            v = v_ref[first : first + window, lanes]
            kt = k.T
            q = q_ref[first : first + block, lanes]
            do = do_ref[first : first + block, lanes]
            dk = jnp.zeros((window, 128), F32)
            dv = jnp.zeros((window, 128), F32)
            parts = []
            for half in range(2):
                qm = jnp.where(lane == half, q, jnp.zeros_like(q))
                dom = jnp.where(lane == half, do, jnp.zeros_like(do))
                head = pl.ds(i * 2 + half, 1)
                s = mm(k, qm, NT) * (SCORE_SCALE * LOG2E) + bias_ref[rb]
                p = jnp.exp2(s - lse_ref[head, first : first + block])
                dp = mm(v, dom, NT)
                ds = (p * (dp - delta_ref[head, first : first + block])).astype(BF16)
                dv = dv + mm(p.astype(BF16), dom, NN)
                dk = dk + mm(ds, qm, NN)
                parts.append(mm(kt[half * HEAD_DIM : (half + 1) * HEAD_DIM], ds, NN))
            dq = jnp.concatenate(parts, axis=0).T * SCORE_SCALE
            at = slice(2 * rows + first, 2 * rows + first + block)
            dq_ref[first : first + block, lanes] = (dq * cos_ref[at, :] - turn(dq) * sin_ref[at, :]).astype(BF16)
            if first == 0:
                dkf_ref[0:window, :] = dk
                dvf_ref[0:window, :] = dv
            else:
                old = window - block
                dkf_ref[first : first + old, :] += dk[0:old]
                dvf_ref[first : first + old, :] += dv[0:old]
                dkf_ref[first + old : first + window, :] = dk[old:]
                dvf_ref[first + old : first + window, :] = dv[old:]
        dk = dkf_ref[...] * SCORE_SCALE
        dk_ref[:, lanes] = (dk * cos_ref[...] - turn(dk) * sin_ref[...]).astype(BF16)
        dv_ref[:, lanes] = dvf_ref[...].astype(BF16)
        return 0

    lax.fori_loop(0, HEADS // 4, pair, 0)
    line.each(lambda k: sum_out(k, 2))
    lax.fori_loop(HEADS // 4, HEADS // 2, pair, 0)
    line.each(lambda k: sum_out(k, 3))
    xl_ref[...] += out_ref[t].astype(F32)

    @pl.when(t > 0)
    def _():
        xl_ref[...] += fu_ref[t - 1].astype(F32)

    @pl.when(t < last)
    def _():
        xl_ref[...] += fd_ref[t].astype(F32)

    y_ref[...] = xl_ref[...].astype(BF16)
    line.leave()


def grads_body(size, x0_ref, x1_ref, x2_ref, h_ref, dq_ref, dk_ref, dv_ref, da_ref, o_ref, w_ref, dx_ref, gain_ref,
               gw_ref, gpart_ref, out_ref, d0_ref, d1_ref, d2_ref, ra_ref, rb_ref, sems_s, sems_r):
    rows = x0_ref.shape[0]
    line = Line(size)
    last = size - 1
    block = 256
    line.enter()

    def hidden(c, d_ref):
        def one(i, _):
            at = pl.ds(pl.multiple_of(i * block, block), block)
            to = pl.ds(pl.multiple_of(c * rows + i * block, block), block)
            total = mm(dk_ref[to, :], w_ref[:, D : 2 * D], NT) + mm(dv_ref[to, :], w_ref[:, 2 * D : 3 * D], NT)
            if c == 2:
                total = total + mm(dq_ref[at, :], w_ref[:, 0:D], NT)
            d_ref[at, :] = total.astype(d_ref.dtype)
            return 0

        lax.fori_loop(0, rows // block, one, 0)

    def gain_of(x_ref, d_ref):
        x = x_ref[...].astype(F32)
        r = lax.rsqrt(jnp.mean(x * x, axis=1, keepdims=True) + EPSILON)
        return jnp.sum(d_ref[...].astype(F32) * x * r, axis=0, keepdims=True)

    hidden(0, d2_ref)

    def first(k):
        if k > 1:
            line.send(k, k - 1, lambda: (d2_ref, ra_ref, (sems_s.at[0], sems_r.at[0])))

    line.each(first)
    hidden(1, d1_ref)
    gain = gain_of(x2_ref, d2_ref) + gain_of(x1_ref, d1_ref)
    h = h_ref[...]

    def weight(column, left, right_ref):
        for c in range(D // 256):
            cols = slice(c * 256, (c + 1) * 256)
            gw_ref[:, column * D + c * 256 : column * D + c * 256 + 256] = mm(left, right_ref[:, cols], TN).astype(BF16)

    weight(1, h, dk_ref)

    def second(k):
        if 0 < k < last:
            line.arrived(k, ra_ref, (sems_s.at[0], sems_r.at[0]))
            d1_ref[...] = (d1_ref[...].astype(F32) + ra_ref[...].astype(F32)).astype(BF16)
        if k > 0:
            line.send(k, k - 1, lambda: (d1_ref, rb_ref, (sems_s.at[1], sems_r.at[1])))

    line.each(second)
    hidden(2, d0_ref)
    gpart_ref[...] = jnp.broadcast_to(gain + gain_of(x0_ref, d0_ref), (8, D))
    weight(2, h, dv_ref)
    weight(0, h[2 * rows :], dq_ref)
    weight(3, da_ref[...], o_ref)

    def third(k):
        if k < last:
            line.arrived(k, rb_ref, (sems_s.at[1], sems_r.at[1]))
            d0_ref[...] += rb_ref[...].astype(F32)

    line.each(third)
    x = x0_ref[...].astype(F32)
    r = lax.rsqrt(jnp.mean(x * x, axis=1, keepdims=True) + EPSILON)
    xr = x * r
    scaled = d0_ref[...] * gain_ref[...]
    out_ref[...] = (dx_ref[...] + r * (scaled - xr * jnp.mean(xr * scaled, axis=1, keepdims=True))).astype(BF16)
    line.leave()


def finish_body(n_dp, size, x0_ref, x1_ref, x2_ref, h_ref, dq_ref, dk_ref, dv_ref, da_ref, o_ref, w_ref, dx_ref, gain_ref,
                y_ref, small_ref, pos_ref,
                yo_ref, go_ref, gw_ref, sum_ref,
                d0_ref, d1_ref, d2_ref, ra_ref, rb_ref, out_ref, yr_ref, gr_ref, part_ref, r1_ref, r2_ref, r3_ref,
                zs_ref, zr_ref, cur_ref, got_ref,
                sems_s, sems_r, sy, ry, sg, rg, s1, r1, s2, r2, s3, r3, sz, rz, sb, rb):
    rows = x0_ref.shape[0]
    share = rows // n_dp
    line = Line(size)
    last = size - 1
    block = 256
    net = Peers()
    d, t = net.d, net.t
    place = pick(iota((rows, rows), 0) == pos_ref[...])
    about, along = around(d, n_dp), around(t, size)
    net.enter([{"dp": to} for _, to, _ in about] + [{"tensor": to} for _, to, _ in along])

    def scatter(src_ref, dst_ref, sems):
        for j, to, _ in about:
            net.send({"dp": to}, src_ref.at[to], dst_ref.at[d], (sems[0].at[j - 1], sems[1].at[j - 1]))
        dst_ref[d] = src_ref[d]

    def gathered(dst_ref, sems):
        for j, _, source in about:
            held = dst_ref.at[source]
            net.copy({"dp": source}, held, held, (sems[0].at[j - 1], sems[1].at[j - 1])).wait_recv()

    scatter(y_ref, yr_ref, (sy, ry))

    def hidden(c, d_ref):
        def one(i, _):
            at = pl.ds(pl.multiple_of(i * block, block), block)
            to = pl.ds(pl.multiple_of(c * rows + i * block, block), block)
            total = mm(dk_ref[to, :], w_ref[:, D : 2 * D], NT) + mm(dv_ref[to, :], w_ref[:, 2 * D : 3 * D], NT)
            if c == 2:
                total = total + mm(dq_ref[at, :], w_ref[:, 0:D], NT)
            d_ref[at, :] = total.astype(d_ref.dtype)
            return 0

        lax.fori_loop(0, rows // block, one, 0)

    def gain_of(x_ref, d_ref):
        x = x_ref[...].astype(F32)
        r = lax.rsqrt(jnp.mean(x * x, axis=1, keepdims=True) + EPSILON)
        return jnp.sum(d_ref[...].astype(F32) * x * r, axis=0, keepdims=True)

    core, x, y = lax.rem(d, 2), lax.rem(d // 2, 2), d // 4
    there = ({"dp": flip(d, 2)}, {"dp": flip(d, 4)})
    deep = D // n_dp

    def weight(u, left, right_ref):
        for c in range(D // 256):
            cols = slice(c * 256, (c + 1) * 256)
            value = mm(left, right_ref[:, cols], TN).astype(BF16)
            part_ref[u, :, :, cols] = value.reshape(n_dp, deep, 256)
        for j in range(4):
            net.send({"dp": flip(d, 1)}, part_ref.at[u, 2 * j + 1 - core], r1_ref.at[u, j], (s1.at[u, j], r1.at[u, j]))

    def add(u, j, arrived):
        spot = 2 * j + core
        part_ref[u, spot] = (part_ref[u, spot].astype(F32) + arrived[...].astype(F32)).astype(BF16)

    def chips(u):
        if u % 2 == 0:
            first = (there[0], [2 * i + 1 - x for i in range(2)], [2 * i + x for i in range(2)])
            return first, (there[1], 2 * (1 - y) + x)
        first = (there[1], [2 * (1 - y) + i for i in range(2)], [2 * y + i for i in range(2)])
        return first, (there[0], 2 * y + 1 - x)

    def halve(u):
        for j in range(4):
            held = r1_ref.at[u, j]
            net.copy({"dp": flip(d, 1)}, held, held, (s1.at[u, j], r1.at[u, j])).wait_recv()
            add(u, j, held)
        where, theirs, _ = chips(u)[0]
        for i in range(2):
            net.send(where, part_ref.at[u, 2 * theirs[i] + core], r2_ref.at[u, i], (s2.at[u, i], r2.at[u, i]))

    def quarter(u):
        (where, _, mine), (after, spot) = chips(u)
        for i in range(2):
            held = r2_ref.at[u, i]
            net.copy(where, held, held, (s2.at[u, i], r2.at[u, i])).wait_recv()
            add(u, mine[i], held)
        net.send(after, part_ref.at[u, 2 * spot + core], r3_ref.at[u], (s3.at[u], r3.at[u]))

    def own(u):
        after = chips(u)[1][0]
        held = r3_ref.at[u]
        net.copy(after, held, held, (s3.at[u], r3.at[u])).wait_recv()
        value = part_ref[u, d].astype(F32) + held[...].astype(F32)
        wide_share = D // size
        for p in range(size):
            zs_ref[u, p] = value[:, p * wide_share : (p + 1) * wide_share].astype(BF16)
        for j, to, _ in along:
            net.send({"tensor": to}, zs_ref.at[u, to], zr_ref.at[u, j - 1], (sz.at[u, j - 1], rz.at[u, j - 1]))

    def whole(u):
        total = zs_ref[u, t].astype(F32)
        for j, _, source in along:
            held = zr_ref.at[u, j - 1]
            net.copy({"tensor": source}, held, held, (sz.at[u, j - 1], rz.at[u, j - 1])).wait_recv()
            total = total + held[...].astype(F32)
        gw_ref[u] = total

    steps = [("dp", bit) for bit in (1, 2, 4, 8) if bit < n_dp] + [("tensor", bit) for bit in (1, 2, 4, 8) if bit < size]

    def small_out(i):
        axis, bit = steps[i]
        mine = t if axis == "tensor" else d
        net.send({axis: flip(mine, bit)}, cur_ref.at[i], got_ref.at[i], (sb.at[i], rb.at[i]))

    def small_in(i):
        axis, bit = steps[i]
        mine = t if axis == "tensor" else d
        held = got_ref.at[i]
        net.copy({axis: flip(mine, bit)}, held, held, (sb.at[i], rb.at[i])).wait_recv()
        total = cur_ref[i] + held[...]
        if i + 1 < len(steps):
            cur_ref[i + 1] = total
            small_out(i + 1)
        else:
            sum_ref[...] = total

    hidden(0, d2_ref)

    def first(k):
        if k > 1:
            line.send(k, k - 1, lambda: (d2_ref, ra_ref, (sems_s.at[0], sems_r.at[0])))

    line.each(first)
    hidden(1, d1_ref)

    def second(k):
        if k == last:
            line.send(k, k - 1, lambda: (d1_ref, rb_ref, (sems_s.at[1], sems_r.at[1])))

    line.each(second)
    h = h_ref[...]
    weight(0, h, dk_ref)
    gain = gain_of(x2_ref, d2_ref) + gain_of(x1_ref, d1_ref)
    weight(1, h, dv_ref)
    halve(0)
    hidden(2, d0_ref)
    gain = gain + gain_of(x0_ref, d0_ref)
    rest = small_ref.shape[0]
    cur_ref[0, 0:rest, :] = small_ref[...]
    cur_ref[0, rest : rest + 8, :] = jnp.broadcast_to(gain, (8, D))
    small_out(0)
    halve(1)

    def third(k):
        if 0 < k < last:
            line.arrived(k, ra_ref, (sems_s.at[0], sems_r.at[0]))
            d1_ref[...] = (d1_ref[...].astype(F32) + ra_ref[...].astype(F32)).astype(BF16)
            line.send(k, k - 1, lambda: (d1_ref, rb_ref, (sems_s.at[1], sems_r.at[1])))

    line.each(third)
    weight(2, h[2 * rows :], dq_ref)
    small_in(0)
    weight(3, da_ref[...], o_ref)
    quarter(0)
    quarter(1)
    halve(2)
    small_in(1)
    halve(3)
    own(0)
    own(1)
    gathered(yr_ref, (sy, ry))
    yo_ref[...] = mm(place, yr_ref[...].reshape(rows, D), TN).astype(BF16)
    quarter(2)
    quarter(3)
    small_in(2)
    own(2)
    own(3)

    def fourth(k):
        if k < last:
            line.arrived(k, rb_ref, (sems_s.at[1], sems_r.at[1]))
            d0_ref[...] += rb_ref[...].astype(F32)

    line.each(fourth)
    xv = x0_ref[...].astype(F32)
    r = lax.rsqrt(jnp.mean(xv * xv, axis=1, keepdims=True) + EPSILON)
    xr = xv * r
    scaled = d0_ref[...] * gain_ref[...]
    value = dx_ref[...] + r * (scaled - xr * jnp.mean(xr * scaled, axis=1, keepdims=True))
    out_ref[...] = value.astype(BF16).reshape(n_dp, share, D)
    scatter(out_ref, gr_ref, (sg, rg))
    for i in range(3, len(steps)):
        small_in(i)
    for u in range(4):
        whole(u)
    gathered(gr_ref, (sg, rg))
    go_ref[...] = mm(place, gr_ref[...].reshape(rows, D), TN).astype(BF16)
    line.leave()
    net.leave()


def experts_body(ff, chunks, cnt_ref, h_refs, g_refs, slot_ref, w_ref, o_refs, d_refs, gw_ref,
                 xbuf, gbuf, cbuf, onehot, fbuf, dbuf, gacc, gates, dgrow, off_ref, base_ref, nt_ref):
    rows = slot_ref.shape[2]
    e = pl.program_id(0)

    def match(j, expert, tile):
        slots = slot_ref[j, pl.ds(expert, 1), :]
        return (iota((TILE, rows), 0) + tile * TILE) == slots

    def store_rows(at, count, hit, x, gs, gate_row):
        to = pl.ds(pl.multiple_of(at, 16), TILE)
        keep = iota((TILE, 1), 0) < count
        col = jnp.sum(jnp.where(hit, gate_row, 0.0), axis=1, keepdims=True)
        xbuf[to, :] = jnp.where(keep, x, xbuf[to, :].astype(F32)).astype(BF16)
        gbuf[to, :] = jnp.where(keep, gs, gbuf[to, :].astype(F32)).astype(BF16)
        cbuf[to, :] = jnp.where(keep, jnp.broadcast_to(col, (TILE, 128)), cbuf[to, :])

    def round16(n):
        return ((n + 15) // 16) * 16

    @pl.when(e == 0)
    def _gather():
        at = jnp.int32(0)
        for ex in range(EXPERTS):
            base_ref[ex] = at
            here = at
            for j in range(chunks):
                off_ref[j * EXPERTS + ex] = here
                here = here + round16(cnt_ref[j * EXPERTS + ex])
            tiles = (here - at + (ROWS - 1)) // ROWS
            nt_ref[ex] = tiles
            tail = pl.ds(pl.multiple_of(here, 16), ROWS)
            xbuf[tail, :] = jnp.zeros((ROWS, D), BF16)
            gbuf[tail, :] = jnp.zeros((ROWS, D), BF16)
            cbuf[tail, :] = jnp.zeros((ROWS, 128), F32)
            at = at + tiles * ROWS
        for j in range(chunks):
            gates[...] = h_refs[j, rows : rows + SPARE, 0:rows].astype(F32)

            def two(i, _, j=j):
                hits = [match(j, 2 * i + half, 0) for half in range(2)]
                sel = jnp.concatenate([pick(hit) for hit in hits], axis=0)
                x = mm(sel, h_refs[j, 0:rows, :], NN)
                gs = mm(sel, g_refs[j], NN)
                for half in range(2):
                    ex = 2 * i + half
                    count = round16(jnp.minimum(cnt_ref[j * EXPERTS + ex], TILE))
                    part = slice(half * TILE, (half + 1) * TILE)
                    store_rows(off_ref[j * EXPERTS + ex], count, hits[half], x[part], gs[part], gates[pl.ds(ex, 1), :])
                return 0

            lax.fori_loop(0, EXPERTS // 2, two, 0)

            def rare(ex, _, j=j):
                def more(tile, _):
                    hit = match(j, ex, tile)
                    sel = pick(hit)
                    count = round16(jnp.minimum(cnt_ref[j * EXPERTS + ex] - tile * TILE, TILE))
                    store_rows(
                        off_ref[j * EXPERTS + ex] + tile * TILE,
                        count,
                        hit,
                        mm(sel, h_refs[j, 0:rows, :], NN),
                        mm(sel, g_refs[j], NN),
                        gates[pl.ds(ex, 1), :],
                    )
                    return 0

                return lax.fori_loop(1, (cnt_ref[j * EXPERTS + ex] + (TILE - 1)) // TILE, more, 0)

            lax.fori_loop(0, EXPERTS, rare, 0)

    gacc[...] = jnp.zeros_like(gacc)

    def tile_step(m, _):
        at = pl.ds(pl.multiple_of(base_ref[e] + m * ROWS, 16), ROWS)
        x = xbuf[at, :]
        gs = gbuf[at, :].astype(F32)
        gate = wide(cbuf[at, :])
        u = mm(x, w_ref[:, 0:ff], NN)
        up = mm(x, w_ref[:, ff : 2 * ff], NN)
        sig = jax.nn.sigmoid(u)
        silu = u * sig
        act = (silu * up).astype(BF16)
        f = mm(act, w_ref[:, 2 * ff : 3 * ff], NT)
        cbuf[at, :] = jnp.broadcast_to(jnp.sum(gs * f, axis=1, keepdims=True), (ROWS, 128))
        gbuf[at, :] = (f * gate).astype(BF16)
        df = (gs * gate).astype(BF16)
        dact = mm(df, w_ref[:, 2 * ff : 3 * ff], NN)
        dup = (dact * silu).astype(BF16)
        du = (dact * up * sig * (1.0 + u * (1.0 - sig))).astype(BF16)
        xbuf[at, :] = (mm(du, w_ref[:, 0:ff], NT) + mm(dup, w_ref[:, ff : 2 * ff], NT)).astype(BF16)
        gacc[:, 0:ff] += mm(x, du, TN)
        gacc[:, ff : 2 * ff] += mm(x, dup, TN)
        gacc[:, 2 * ff : 3 * ff] += mm(df, act, TN)
        return 0

    lax.fori_loop(0, nt_ref[e], tile_step, 0)
    gw_ref[...] = gacc[...].astype(BF16)

    @pl.when(e == EXPERTS - 1)
    def _scatter():
        for j in range(chunks):
            def take(ex, _, j=j):
                at = pl.ds(pl.multiple_of(off_ref[j * EXPERTS + ex], 16), TILE)
                to = pl.ds(pl.multiple_of(ex * TILE, 16), TILE)
                hit = match(j, ex, 0)
                onehot[to, :] = pick(hit)
                fbuf[to, :] = gbuf[at, :]
                dbuf[to, :] = xbuf[at, :]
                col = jnp.concatenate([cbuf[at, :]] * (rows // 128), axis=1)
                dgrow[pl.ds(ex, 1), :] = jnp.sum(jnp.where(hit, col, 0.0), axis=0, keepdims=True)
                return 0

            lax.fori_loop(0, EXPERTS, take, 0)
            gacc[0:rows, 0:D] = mm(onehot[...], fbuf[...], TN)
            gacc[0:rows, D : 2 * D] = mm(onehot[...], dbuf[...], TN)

            def rare(ex, _, j=j):
                def more(tile, _):
                    at = pl.ds(pl.multiple_of(off_ref[j * EXPERTS + ex] + tile * TILE, 16), TILE)
                    hit = match(j, ex, tile)
                    sel = pick(hit)
                    gacc[0:rows, 0:D] += mm(sel, gbuf[at, :], TN)
                    gacc[0:rows, D : 2 * D] += mm(sel, xbuf[at, :], TN)
                    col = jnp.concatenate([cbuf[at, :]] * (rows // 128), axis=1)
                    dgrow[pl.ds(ex, 1), :] += jnp.sum(jnp.where(hit, col, 0.0), axis=0, keepdims=True)
                    return 0

                return lax.fori_loop(1, (cnt_ref[j * EXPERTS + ex] + (TILE - 1)) // TILE, more, 0)

            lax.fori_loop(0, EXPERTS, rare, 0)
            o_refs[j] = gacc[0:rows, 0:D].astype(BF16)
            d_refs[j, 0:rows, :] = gacc[0:rows, D : 2 * D].astype(BF16)
            total = dgrow[...]
            high = total.astype(BF16).astype(F32)
            both = jnp.concatenate([high, total - high], axis=0)
            d_refs[j, rows : rows + SPARE, :] = jnp.concatenate(
                [both, jnp.zeros((SPARE, D - rows), F32)], axis=1
            ).astype(BF16)


def experts_call(counts, hs, gs, slots, weights, ff):
    chunks, rows = gs.shape[:2]
    width = 3 * ff
    most = (rows + 15 * chunks + ROWS - 1) // ROWS * ROWS * EXPERTS + ROWS
    whole = lambda shape: pl.BlockSpec(shape, lambda e: (0,) * len(shape), pipeline_mode=pl.Buffered(1))
    return pl.pallas_call(
        functools.partial(experts_body, ff, chunks),
        name="experts",
        grid=(EXPERTS,),
        in_specs=[smem(), whole(hs.shape), whole(gs.shape), whole(slots.shape), pl.BlockSpec((D, width), lambda e: (0, e))],
        out_specs=[whole(gs.shape), whole(hs.shape), pl.BlockSpec((D, width), lambda e: (0, e))],
        out_shape=[
            jax.ShapeDtypeStruct(gs.shape, BF16),
            jax.ShapeDtypeStruct(hs.shape, BF16),
            jax.ShapeDtypeStruct((D, EXPERTS * width), BF16),
        ],
        scratch_shapes=[
            pltpu.VMEM((most, D), BF16),
            pltpu.VMEM((most, D), BF16),
            pltpu.VMEM((most, 128), F32),
            pltpu.VMEM((EXPERTS * TILE, rows), BF16),
            pltpu.VMEM((EXPERTS * TILE, D), BF16),
            pltpu.VMEM((EXPERTS * TILE, D), BF16),
            pltpu.VMEM((D, width), F32),
            pltpu.VMEM((SPARE, rows), F32),
            pltpu.VMEM((EXPERTS, rows), F32),
            pltpu.SMEM((chunks * EXPERTS,), I32),
            pltpu.SMEM((EXPERTS,), I32),
            pltpu.SMEM((EXPERTS,), I32),
        ],
        compiler_params=pltpu.CompilerParams(
            dimension_semantics=("arbitrary",), vmem_limit_bytes=VMEM_CAP
        ),
    )(counts, hs, gs, slots, weights)


def rope_tables(lengths, first, count):
    finish = jnp.sum(jnp.where(jnp.arange(lengths.shape[0])[:, None] <= jnp.arange(lengths.shape[0])[None, :], lengths[:, None], 0), axis=0)
    begins = finish - lengths
    rows = first + jnp.arange(count, dtype=I32)
    opening = jnp.max(jnp.where(begins[None, :] <= rows[:, None], begins[None, :], 0), axis=1)
    place = rows - opening
    half = HEAD_DIM // 2
    rates = jnp.exp(jnp.arange(half, dtype=F32) * (-2.0 * math.log(10000.0) / HEAD_DIM))
    angles = place.astype(F32)[:, None] * rates[None, :]
    cos, sin = jnp.cos(angles), jnp.sin(angles)
    return place, jnp.concatenate([cos] * 4, axis=1), jnp.concatenate([-sin, sin] * 2, axis=1)


def body(tokens, cotangent, deal, lengths, routes, gate_residual, w_qkv, w_out, w_gate_up, w_down,
         norm_gain_attn, norm_gain_moe, w_router, w_const, v_const):
    rows = tokens.shape[0]
    n_dp, n_t = lax.axis_size("dp"), lax.axis_size("tensor")
    t = lax.axis_index("tensor")
    ff = w_down.shape[2]
    d_here = w_qkv.shape[0]

    def swap(v, j):
        return lax.ppermute(v, "tensor", [(i, i ^ j) for i in range(n_t)])

    def place_in(parts):
        stacked = jnp.stack(parts)
        return jnp.stack([lax.dynamic_index_in_dim(stacked, t ^ i, 0, keepdims=False) for i in range(n_t)], axis=2)

    fast = n_dp == 8 and d_here % 16 == 0 and rows % 128 == 0
    attn_shard = jnp.concatenate([w_qkv, w_out[:, None, :]], axis=1)
    if not fast:
        attn_shard = place_in([attn_shard] + [swap(attn_shard, j) for j in range(1, n_t)]).reshape(d_here, 4 * D)
        w_attn = lax.all_gather(attn_shard, "dp", axis=0, tiled=True)
    ff_shard = jnp.concatenate([w_gate_up.reshape(d_here, EXPERTS, 2 * ff), w_down], axis=2)
    w_ff = lax.all_gather(ff_shard.reshape(d_here, EXPERTS * 3 * ff), "dp", axis=0, tiled=True)

    routes_t = routes.reshape(n_t, rows, 2).transpose(0, 2, 1)
    row, ext = (rows, D), (3 * rows, D)
    every, every_packed = (n_t, rows, D), (n_t, rows + SPARE, D)
    xs, gs, pos, slots, counts = call(
        functools.partial(deal_body, n_dp),
        "deal",
        [(row, BF16), (row, BF16), ((1, rows), I32), ((n_t, EXPERTS, rows), I32), ((n_t, EXPERTS, 128), I32)],
        [deal.reshape(1, rows), tokens, cotangent, routes_t],
    )
    counts = counts[:, :, 0].reshape(n_t * EXPERTS)
    share = rows // n_dp
    if fast:
        parts = (n_dp, share, D)
        opening = [xs.reshape(parts), gs.reshape(parts), attn_shard.transpose(1, 0, 2)]
        opened = [(parts, BF16), (parts, BF16), ((n_dp, d_here, 4 * D), BF16)]
    else:
        parts = (1, rows, D)
        x0 = lax.all_to_all(xs, "dp", split_axis=0, concat_axis=0, tiled=True)
        g0 = lax.all_to_all(gs, "dp", split_axis=0, concat_axis=0, tiled=True)
        opening, opened = [x0.reshape(parts), g0.reshape(parts), w_attn.reshape(1, D, 4 * D)], []

    place, cos, sin = rope_tables(lengths[0], (t - 2) * rows, 3 * rows)
    start = (LONGEST + jnp.arange(rows, dtype=I32) - place[2 * rows :]).reshape(1, rows)
    gain_attn, gain_moe = norm_gain_attn.reshape(1, D), norm_gain_moe.reshape(1, D)
    window = LONGEST + 256
    res_t = jnp.concatenate([gate_residual.T, jnp.zeros((4, rows), F32)], axis=0)
    wrc = jnp.concatenate([w_router.T, w_const.transpose(0, 2, 1).reshape(4, D)], axis=0)
    v8 = jnp.concatenate([v_const, jnp.zeros((6, D), F32)], axis=0)
    dma = lambda *shape: pltpu.SemaphoreType.DMA(shape)
    scratch = [pltpu.VMEM((window, 256), F32), dma(2), dma(2)] + [dma(3)] * 8
    if fast:
        scratch += [pltpu.VMEM((n_t, 4, d_here, D // n_t), BF16)] + [dma(n_t - 1)] * 2 + [dma(n_dp - 1)] * 4
        scratch += [dma(2)] * 2 + [dma(2, 2)] * 2 + [dma(n_dp // 2)] * 2
    results = call(
        functools.partial(forward_body, n_dp if fast else 1, n_t),
        "forward",
        opened
        + [(parts, BF16), (parts, BF16), (ext, BF16), (row, BF16), (ext, BF16), (ext, BF16), (row, BF16), ((SPARE, rows), F32),
           (row, F32), (every_packed, BF16), ((n_t,) + parts, BF16), ((8, rows), F32), (row, F32), (row, F32), ((SPARE, rows), F32),
           ((8, D), F32)],
        opening + [gain_attn, gain_moe, cos, sin, start, res_t, wrc, routes_t, v8],
        scratch=scratch,
        meet=0,
    )
    if fast:
        x0, g0, w_attn = results[0].reshape(row), results[1].reshape(row), results[2].reshape(D, 4 * D)
        results = results[3:]
    x1, x2, h, q, k, v, o, lse, xm, hp_all, g_all, gt, xl, dhl, sm, gv = results
    x1, x2, g_all = x1.reshape(row), x2.reshape(row), g_all.reshape(every)

    out_all, back_all, gw_ff = experts_call(counts, hp_all, g_all, slots, w_ff, ff)
    ff_sum = lax.psum_scatter(gw_ff, "dp", scatter_dimension=0, tiled=True)
    h2 = lax.dynamic_index_in_dim(hp_all, t, 0, keepdims=False)[0:rows]

    dx, da, dres, small, dq, dk, dv, result = call(
        functools.partial(backward_body, n_t),
        "backward",
        [(row, F32), (row, BF16), ((SPARE, rows), F32), ((SPARE + 8, D), F32), (row, BF16), (ext, BF16), (ext, BF16), (row, BF16)],
        [back_all, out_all, dhl, gt, sm, routes_t, wrc, xm, gain_moe, g0, h2, w_attn, o, gv, q, k, v, lse, start, cos, sin, xl],
        scratch=[pltpu.VMEM((rows // 256, window, 256), F32), pltpu.VMEM((3 * rows, 128), F32), pltpu.VMEM((3 * rows, 128), F32),
                 pltpu.VMEM((rows + SPARE, D), F32), pltpu.VMEM(row, BF16), pltpu.VMEM((SPARE, rows), F32)]
        + [pltpu.VMEM((n_t - 1, rows + SPARE, D), BF16)] * 2 + [pltpu.VMEM((n_t - 1, rows, D), BF16)] * 2
        + [dma(n_t - 1, 2)] * 4 + [dma(n_t - 1, 1)] * 4,
        meet=1,
    )
    if fast:
        units = 4
        piece = (d_here, D)
        hops = 3 + (n_t - 1).bit_length()
        output, grad_tokens, attn_parts, small_all = call(
            functools.partial(finish_body, n_dp, n_t),
            "finish",
            [(row, BF16), (row, BF16), ((units, d_here, D // n_t), F32), ((SPARE + 16, D), F32)],
            [x0, x1, x2, h, dq, dk, dv, da, o, w_attn, dx, gain_attn, result.reshape(n_dp, share, D), small, pos],
            scratch=[pltpu.VMEM(row, F32)] + [pltpu.VMEM(row, BF16)] * 4 + [pltpu.VMEM((n_dp, share, D), BF16)] * 3
            + [pltpu.VMEM((units, n_dp) + piece, BF16), pltpu.VMEM((units, 4) + piece, BF16), pltpu.VMEM((units, 2) + piece, BF16),
               pltpu.VMEM((units,) + piece, BF16), pltpu.VMEM((units, n_t, d_here, D // n_t), BF16),
               pltpu.VMEM((units, n_t - 1, d_here, D // n_t), BF16)]
            + [pltpu.VMEM((hops, SPARE + 16, D), F32)] * 2
            + [dma(2)] * 2 + [dma(n_dp - 1)] * 4 + [dma(units, 4)] * 2 + [dma(units, 2)] * 2 + [dma(units)] * 2
            + [dma(units, n_t - 1)] * 2 + [dma(hops)] * 2,
            meet=2,
        )
        gain_all = small_all[SPARE + 8]
        attn_own = jnp.stack([attn_parts[2], attn_parts[0], attn_parts[1], attn_parts[3]], axis=1)
    else:
        back_out = lax.all_to_all(result, "dp", split_axis=0, concat_axis=0, tiled=True)
        gw_attn, gain_part, d_start = call(
            functools.partial(grads_body, n_t),
            "grads",
            [((D, 4 * D), BF16), ((8, D), F32), (row, BF16)],
            [x0, x1, x2, h, dq, dk, dv, da, o, w_attn, dx, gain_attn],
            scratch=[pltpu.VMEM(row, F32)] + [pltpu.VMEM(row, BF16)] * 4 + [dma(2), dma(2)],
            meet=2,
        )
        back_grad = lax.all_to_all(d_start, "dp", split_axis=0, concat_axis=0, tiled=True)
        output, grad_tokens = call(restore_body, "restore", [(row, BF16)] * 2, [pos, back_out, back_grad])

        def total(v):
            for axis, count in (("tensor", n_t), ("dp", n_dp)):
                bit = 1
                while bit < count:
                    v = v + lax.ppermute(v, axis, [(i, i ^ bit) for i in range(count)])
                    bit *= 2
            return v

        small_all = total(jnp.concatenate([small, gain_part], axis=0))
        gain_all = small_all[SPARE + 8]
        gw_attn, ff_sum = lax.optimization_barrier((gw_attn, ff_sum))
        attn_sum = lax.psum_scatter(gw_attn, "dp", scatter_dimension=0, tiled=True).reshape(d_here, 4, n_t, D // n_t)

        def share(j):
            return lax.dynamic_index_in_dim(attn_sum, t ^ j, 2, keepdims=False)

        attn_own = share(0).astype(F32)
        for j in range(1, n_t):
            attn_own = attn_own + swap(share(j), j).astype(F32)
    ff_own = ff_sum.reshape(d_here, EXPERTS, 3 * ff).astype(F32)
    return (
        output,
        grad_tokens,
        dres[0:12].T,
        attn_own[:, 0:3],
        attn_own[:, 3],
        ff_own[:, :, 0 : 2 * ff].reshape(d_here, EXPERTS, 2, ff),
        ff_own[:, :, 2 * ff :],
        gain_all,
        small_all[SPARE + 2],
        small_all[0:12].T,
        small_all[12:16].reshape(2, 2, D).transpose(0, 2, 1),
        small_all[SPARE : SPARE + 2],
    )


def solution(mesh):
    both, every = P(("dp", "tensor"), None), P()
    weights = (P("dp", None, "tensor"), P("dp", "tensor"), P("dp", None, None, "tensor"), P("dp", None, "tensor"))
    return jax.shard_map(
        body,
        mesh=mesh,
        in_specs=(both, both, P(("dp", "tensor")), P("dp", None), P("dp", None), both, *weights) + (every,) * 5,
        out_specs=(both, both, both, *weights) + (every,) * 5,
        check_vma=False,
    )
```

```python
import functools

import jax
import jax.numpy as jnp
import numpy as np
from jax import lax
from jax.experimental import pallas as pl
from jax.experimental.pallas import tpu as pltpu
from jax.sharding import PartitionSpec as P

D = 768
HEAD_DIM = 64
HEADS = 12
EXPERTS = 8
LONGEST = 1024
EPSILON = 1e-6
MASKED = -1e30
F32, BF16, I32 = jnp.float32, jnp.bfloat16, jnp.int32
NN = (((1,), (0,)), ((), ()))
NT = (((1,), (1,)), ((), ()))
TN = (((0,), (0,)), ((), ()))
SCORE_SCALE = HEAD_DIM**-0.5
LOG2E = 1.4426950408889634
TILE = 160
ROWS = 256
SPARE = 16
VMEM_CAP = 66_000_000


def mm(a, b, dims):
    return lax.dot_general(a, b, dims, preferred_element_type=F32)


def iota(shape, axis):
    return lax.broadcasted_iota(I32, shape, axis)


def pick(cond):
    return jnp.where(cond, 1.0, 0.0).astype(BF16)


def split2(v):
    high = v.astype(BF16)
    return high, (v - high.astype(F32)).astype(BF16)


def split3(v):
    high = v.astype(BF16)
    rest = v - high.astype(F32)
    mid = rest.astype(BF16)
    return high, mid, (rest - mid.astype(F32)).astype(BF16)


def vmem():
    return pl.BlockSpec(memory_space=pltpu.VMEM)


def smem():
    return pl.BlockSpec(memory_space=pltpu.SMEM)


def call(body, name, outs, operands, scalars=0, scratch=(), meet=None):
    return pl.pallas_call(
        body,
        name=name,
        out_shape=[jax.ShapeDtypeStruct(*o) for o in outs],
        in_specs=[smem()] * scalars + [vmem()] * (len(operands) - scalars),
        out_specs=[vmem()] * len(outs),
        scratch_shapes=list(scratch),
        compiler_params=pltpu.CompilerParams(
            vmem_limit_bytes=VMEM_CAP, collective_id=meet, has_side_effects=meet is not None
        ),
    )(*operands)


def deal_body(n_dp, deal_ref, tok_ref, cot_ref, routes_ref, xs_ref, gs_ref, pos_ref, slot_ref, cnt_ref):
    rows = tok_ref.shape[0]
    first, second = iota((rows, rows), 0), iota((rows, rows), 1)
    before = pick(first < second)
    deal = deal_ref[...]
    hit = iota((n_dp, rows), 0) == deal
    rank = mm(pick(hit), before, NN)
    rank = jnp.sum(jnp.where(hit, rank, 0.0), axis=0, keepdims=True).astype(I32)
    pos = deal * (rows // n_dp) + rank
    pos_ref[...] = pos
    place = pick(first == pos)
    xs_ref[...] = mm(place, tok_ref[...], NN).astype(BF16)
    gs_ref[...] = mm(place, cot_ref[...], NN).astype(BF16)
    expert = iota((EXPERTS, rows), 0)
    for j in range(routes_ref.shape[0]):
        route = routes_ref[j]
        named = (expert == route[0:1]) | (expert == route[1:2])
        ahead = mm(pick(named), before, NN).astype(I32)
        slot_ref[j] = jnp.where(named, ahead, -1)
        total = jnp.sum(jnp.where(named, 1.0, 0.0), axis=1, keepdims=True).astype(I32)
        cnt_ref[j] = jnp.broadcast_to(total, (EXPERTS, 128))


def restore_body(pos_ref, a_ref, b_ref, oa_ref, ob_ref):
    rows = a_ref.shape[0]
    place = pick(iota((rows, rows), 0) == pos_ref[...])
    oa_ref[...] = mm(place, a_ref[...], TN).astype(BF16)
    ob_ref[...] = mm(place, b_ref[...], TN).astype(BF16)


class Line:
    def __init__(self, size):
        self.size = size
        self.place = lax.axis_index("tensor")
        self.sent = {k: [] for k in range(size)}

    def each(self, body):
        for k in range(self.size):
            pl.when(self.place == k)(functools.partial(body, k))

    def enter(self):
        sem = pltpu.get_barrier_semaphore()

        def greet(k):
            near = [n for n in (k - 1, k + 1) if 0 <= n < self.size]
            for n in near:
                pl.semaphore_signal(sem, 1, device_id={"tensor": self.place + (n - k)}, device_id_type=pl.DeviceIdType.MESH)
            pl.semaphore_wait(sem, len(near))

        self.each(greet)

    def copy(self, hop, src, dst, sems):
        return pltpu.make_async_remote_copy(
            src_ref=src,
            dst_ref=dst,
            send_sem=sems[0],
            recv_sem=sems[1],
            device_id={"tensor": self.place + hop},
            device_id_type=pl.DeviceIdType.MESH,
        )

    def send(self, k, to, refs):
        self.copy(to - k, *refs()).start()
        self.sent[k].append((to - k, refs))

    def arrived(self, k, dst, sems):
        self.copy((k ^ 1) - k, dst, dst, sems).wait_recv()

    def leave(self):
        def drain(k):
            for hop, refs in self.sent[k]:
                self.copy(hop, *refs()).wait_send()

        self.each(drain)


class Peers:
    def __init__(self):
        self.d, self.t = lax.axis_index("dp"), lax.axis_index("tensor")
        self.sent = []

    def enter(self, targets):
        sem = pltpu.get_barrier_semaphore()
        for where in targets:
            pl.semaphore_signal(sem, 1, device_id=where, device_id_type=pl.DeviceIdType.MESH)
        pl.semaphore_wait(sem, len(targets))

    def copy(self, where, src, dst, sems):
        return pltpu.make_async_remote_copy(
            src_ref=src,
            dst_ref=dst,
            send_sem=sems[0],
            recv_sem=sems[1],
            device_id=where,
            device_id_type=pl.DeviceIdType.MESH,
        )

    def send(self, where, src, dst, sems):
        copy = self.copy(where, src, dst, sems)
        copy.start()
        self.sent.append(copy)

    def leave(self):
        for copy in self.sent:
            copy.wait_send()


def flip(index, bit):
    return index + bit * (1 - 2 * ((index // bit) % 2))


def around(index, count):
    return [(j, lax.rem(index + j, count), lax.rem(index + count - j, count)) for j in range(1, count)]


class Rows:
    def __init__(self, ref):
        self.ref = ref

    def __getitem__(self, at):
        columns = slice(None) if at is Ellipsis else at[1]
        value = self.ref[:, :, columns]
        return value.reshape(value.shape[0] * value.shape[1], value.shape[2])


def sum_events(size, k):
    events = []
    for dest in range(size):
        if dest >= k and dest > 0:
            events.append((0 if k == 0 else size - 1 - dest + k, 1, dest))
        if dest <= k and dest < size - 1:
            events.append((0 if k == size - 1 else dest + size - 1 - k, -1, dest))
    drop = [(t, w, d) for t, w, d in events if (k == 0 and w == 1 and d == 0) or (k == size - 1 and w == -1 and d == k)]
    return sorted((ev for ev in events if ev not in drop), key=lambda ev: (ev[0], ev[1], -ev[1] * ev[2]))


def turn(u):
    low = (iota((1, u.shape[1]), 1) % HEAD_DIM) < HEAD_DIM // 2
    half = HEAD_DIM // 2
    return jnp.where(low, pltpu.roll(u, u.shape[1] - half, 1), pltpu.roll(u, half, 1))


def wide(table):
    return jnp.concatenate([table] * (D // 128), axis=1)


def key_bias(start, block, first_row, base):
    window = LONGEST + block
    key = iota((window, block), 0) + first_row
    row = iota((1, block), 1) + (base + first_row)
    return jnp.where((key >= start) & (key <= row), 0.0, MASKED)


def router_part(route, o_ref, w_ref, x_ref, gain_ref, res_ref, wrc_ref, x1_ref, hp_ref, gt_ref):
    rows = o_ref.shape[0]
    x1 = x_ref[...].astype(F32) + mm(o_ref[...], w_ref[:, 3 * D : 4 * D], NT)
    x1_ref[...] = x1
    h = x1 * lax.rsqrt(jnp.mean(x1 * x1, axis=1, keepdims=True) + EPSILON) * gain_ref[...]
    h = h.astype(BF16)
    hp_ref[0:rows, :] = h
    high, mid, low = split3(wrc_ref[...])
    z = mm(low, h, NT) + mm(mid, h, NT) + mm(high, h, NT) + res_ref[...]
    expert = iota(z.shape, 0)
    named0, named1 = expert == route[0:1], expert == route[1:2]
    c0 = jnp.sum(jnp.where(named0, z, 0.0), axis=0, keepdims=True)
    c1 = jnp.sum(jnp.where(named1, z, 0.0), axis=0, keepdims=True)
    top = jnp.maximum(c0, c1)
    e0, e1 = jnp.exp(c0 - top), jnp.exp(c1 - top)
    g0, g1 = e0 / (e0 + e1), e1 / (e0 + e1)
    table = [g0, g1]
    for j in range(2):
        l0, l1 = z[12 + 2 * j : 13 + 2 * j], z[13 + 2 * j : 14 + 2 * j]
        top = jnp.maximum(l0, l1)
        m0, m1 = jnp.exp(l0 - top), jnp.exp(l1 - top)
        table += [m0 / (m0 + m1), m1 / (m0 + m1)]
    gt_ref[...] = jnp.concatenate(table + [jnp.zeros((2, rows), F32)], axis=0)
    gates = jnp.where(named0, g0, jnp.where(named1, g1, 0.0))
    gates = jnp.where(expert < EXPERTS, gates, 0.0)
    hp_ref[rows : rows + SPARE, :] = jnp.concatenate([gates, jnp.zeros((SPARE, D - rows), F32)], axis=1).astype(BF16)


def local_part(route, x1_ref, hp_ref, g_ref, gt_ref, v_ref, xl_ref, dhl_ref, sm_ref, gv_ref):
    rows = x1_ref.shape[0]
    h, g = hp_ref[0:rows, :], g_ref[...]
    hf, gf = h.astype(F32), g.astype(F32)
    low0 = gt_ref[0:1].astype(BF16).astype(F32)
    low1 = gt_ref[1:2].astype(BF16).astype(F32)

    def weight(e):
        return jnp.where(route[0:1] == e, low0, 0.0) + jnp.where(route[1:2] == e, low1, 0.0)

    copy, first, second = weight(EXPERTS + 1), weight(EXPERTS + 2), weight(EXPERTS + 3)
    m00, m01, m10, m11 = gt_ref[2:3], gt_ref[3:4], gt_ref[4:5], gt_ref[5:6]
    a = copy + first * m00 + second * m10
    b0, b1 = first * m01, second * m11
    table = jnp.concatenate([a, b0, b1, jnp.zeros((125, rows), F32)], axis=0).T
    ac, b0c, b1c = table[:, 0:1], table[:, 1:2], table[:, 2:3]
    v = v_ref[...]
    xl_ref[...] = x1_ref[...] + ac * hf + b0c * v[0:1] + b1c * v[1:2]
    dhl_ref[...] = ac * gf
    ones = jnp.ones((8, D), BF16)
    high, low = split2(hf * gf)
    gh = (mm(ones, high, NT) + mm(ones, low, NT))[0:1]
    vh, vm, vl = split3(v)
    gvs = mm(vl, g, NT) + mm(vm, g, NT) + mm(vh, g, NT)
    gv0, gv1 = gvs[0:1], gvs[1:2]
    zero = jnp.zeros((9, rows), F32)
    dl0 = first * m00 * m01 * (gh - gv0)
    dl1 = second * m10 * m11 * (gh - gv1)
    sm_ref[...] = jnp.concatenate(
        [zero, gh, m00 * gh + m01 * gv0, m10 * gh + m11 * gv1, dl0, -dl0, dl1, -dl1], axis=0
    )
    bh, bm, bl = split3(jnp.concatenate([b0, b1, jnp.zeros((6, rows), F32)], axis=0))
    gv_ref[...] = mm(bl, g, NN) + mm(bm, g, NN) + mm(bh, g, NN)


def rope_tables(lengths_ref, rates_ref, t, rows, cos_ref, sin_ref, start_ref):
    begins, total = [], jnp.int32(0)
    for i in range(lengths_ref.shape[0]):
        begins.append(total)
        total = total + lengths_ref[i]

    def opening(row):
        found = jnp.zeros_like(row)
        for begin in begins:
            found = jnp.where(begin <= row, jnp.maximum(found, begin), found)
        return found

    start_ref[...] = LONGEST - t * rows + opening(iota((1, rows), 1) + t * rows)
    sign = jnp.where(iota((1, 128), 1) % HEAD_DIM < HEAD_DIM // 2, -1.0, 1.0)
    step = 128

    def tile(i, _):
        at = pl.multiple_of(i * step, step)
        row = iota((step, 128), 0) + (at + (t - 2) * rows)
        angles = (row - opening(row)).astype(F32) * rates_ref[...]
        cos_ref[pl.ds(at, step), :] = jnp.cos(angles)
        sin_ref[pl.ds(at, step), :] = jnp.sin(angles) * sign
        return 0

    lax.fori_loop(0, cos_ref.shape[0] // step, tile, 0)


def forward_body(n_dp, size, lengths_ref, *refs):
    fast = n_dp > 1
    first_refs, (gain_ref, gain2_ref, rates_ref, res_ref, wrc_ref, routes_ref, v8_ref) = refs[:3], refs[3:10]
    refs = refs[10:]
    if fast:
        xs_ref, gs_ref, ws_ref = first_refs
        (x0_ref, g0_ref, w3_ref), refs = refs[:3], refs[3:]
    else:
        x0_ref, g0_ref, w3_ref = first_refs
    (x1_ref, x2_ref, h_ref, q_ref, k_ref, v_ref, o_ref, lse_ref, xm_ref, hp_ref, gall_ref, gt_ref, xl_ref,
     dhl_ref, sm_ref, gv_ref, cos_ref, sin_ref, start_ref,
     bias_ref, sx, rx, sgu, rgu, sgd, rgd, shu, rhu, shd, rhd) = refs[:30]
    rows = x0_ref.shape[0] * x0_ref.shape[1]
    step = 256
    line = Line(size)
    t = line.place
    last = size - 1
    w_ref, x_own, g_own = Rows(w3_ref), Rows(x0_ref), Rows(g0_ref)

    def begin(k):
        if k < last:
            line.send(k, k + 1, lambda: (x0_ref, x1_ref, (sx.at[0], rx.at[0])))

    def begin_down(k):
        if k > 0:
            line.send(k, k - 1, lambda: (g0_ref, gall_ref.at[k], (sgd.at[0], rgd.at[0])))

    def second(k):
        if k > 0:
            line.arrived(k, x1_ref, (sx.at[0], rx.at[0]))
        else:
            x1_ref[...] = jnp.zeros_like(x1_ref)
        if 0 < k < last:
            line.send(k, k + 1, lambda: (x1_ref, x2_ref, (sx.at[1], rx.at[1])))
        if k < last:
            line.send(k, k + 1, lambda: (g0_ref, gall_ref.at[k], (sgu.at[0], rgu.at[0])))
            line.arrived(k, gall_ref.at[k + 1], (sgd.at[0], rgd.at[0]))
            if k > 0:
                line.send(k, k - 1, lambda: (gall_ref.at[k + 1], gall_ref.at[k + 1], (sgd.at[1], rgd.at[1])))

    if fast:
        wz_ref, sz, rz, sa, ra, sb, rb_, s1, r1, s2, r2, s3, r3 = refs[30:]
        net = Peers()
        d = net.d
        along, about = around(t, size), around(d, n_dp)
        net.enter([{"dp": to} for _, to, _ in about] + [{"tensor": to} for _, to, _ in along])
        for j, to, _ in along:
            net.send({"tensor": to}, ws_ref, wz_ref.at[t], (sz.at[j - 1], rz.at[j - 1]))
        for src_ref, dst_ref, ss, rr in ((xs_ref, x0_ref, sa, ra), (gs_ref, g0_ref, sb, rb_)):
            for j, to, _ in about:
                net.send({"dp": to}, src_ref.at[to], dst_ref.at[d], (ss.at[j - 1], rr.at[j - 1]))
            dst_ref[d] = src_ref[d]
        wz_ref[t] = ws_ref[...]
        rope_tables(lengths_ref, rates_ref, t, rows, cos_ref, sin_ref, start_ref)

        def gathered(dst_ref, ss, rr):
            for j, _, source in about:
                held = dst_ref.at[source]
                net.copy({"dp": source}, held, held, (ss.at[j - 1], rr.at[j - 1])).wait_recv()

        gathered(x0_ref, sa, ra)
        line.each(begin)
        for j, _, source in along:
            held = wz_ref.at[source]
            net.copy({"tensor": source}, held, held, (sz.at[j - 1], rz.at[j - 1])).wait_recv()
        for c in range(4):
            w3_ref[d, :, c * D : (c + 1) * D] = jnp.concatenate([wz_ref[p, c] for p in range(size)], axis=1)
        pair, across = flip(d, 1), (flip(d, 2), flip(d, 4))
        halves = (slice(0, 2 * D), slice(2 * D, 4 * D))

        def pass_on(way, spot, half, sems):
            net.send({"dp": way}, w3_ref.at[spot, :, halves[half]], w3_ref.at[spot, :, halves[half]], sems)

        def passed(way, spot, half, sems):
            held = w3_ref.at[spot, :, halves[half]]
            net.copy({"dp": way}, held, held, sems).wait_recv()

        for half in range(2):
            pass_on(across[half], d, half, (s1.at[half], r1.at[half]))
        gathered(g0_ref, sb, rb_)
        line.each(begin_down)
        gall_ref[t] = g0_ref[...]
        for half in range(2):
            near, far = across[half], across[1 - half]
            passed(near, near, half, (s1.at[half], r1.at[half]))
            for i, spot in enumerate((d, near)):
                pass_on(far, spot, half, (s2.at[half, i], r2.at[half, i]))
        line.each(second)
        beyond = flip(across[0], 4)
        for half in range(2):
            near, far = across[half], across[1 - half]
            for i, spot in enumerate((far, beyond)):
                passed(far, spot, half, (s2.at[half, i], r2.at[half, i]))
        core = lax.rem(d, 2)
        for i in range(n_dp // 2):
            spot = 2 * i + core
            net.send({"dp": pair}, w3_ref.at[spot], w3_ref.at[spot], (s3.at[i], r3.at[i]))
        for i in range(n_dp // 2):
            held = w3_ref.at[2 * i + 1 - core]
            net.copy({"dp": pair}, held, held, (s3.at[i], r3.at[i])).wait_recv()
    else:
        line.enter()
        line.each(begin)
        line.each(begin_down)
        rope_tables(lengths_ref, rates_ref, t, rows, cos_ref, sin_ref, start_ref)
    gain = gain_ref[...]

    def part(x_ref, i):
        share = x_ref.shape[1]
        if share == rows:
            return x_ref[0, pl.ds(pl.multiple_of(i * step, step), step), :]
        return x_ref[pl.ds(i * (step // share), step // share)].reshape(step, D)

    def project_chunk(c, x_ref):
        def project(i, _):
            at = pl.multiple_of(i * step, step)
            x = part(x_ref, i).astype(F32)
            h = x * lax.rsqrt(jnp.mean(x * x, axis=1, keepdims=True) + EPSILON) * gain
            h = h.astype(BF16)
            to = pl.ds(pl.multiple_of(c * rows + i * step, step), step)
            h_ref[to, :] = h
            cos, sin = wide(cos_ref[to, :]), wide(sin_ref[to, :])
            k = mm(h, w_ref[:, D : 2 * D], NN)
            k_ref[to, :] = (k * cos + turn(k) * sin).astype(BF16)
            v_ref[to, :] = mm(h, w_ref[:, 2 * D : 3 * D], NN).astype(BF16)
            if c == 2:
                q = mm(h, w_ref[:, 0:D], NN)
                q_ref[pl.ds(at, step), :] = (q * cos + turn(q) * sin).astype(BF16)
            return 0

        lax.fori_loop(0, rows // step, project, 0)

    project_chunk(2, x0_ref)
    if not fast:
        gall_ref[t] = g0_ref[...]
        line.each(second)
    project_chunk(1, x1_ref)

    def third(k):
        if k > 1:
            line.arrived(k, x2_ref, (sx.at[1], rx.at[1]))
        else:
            x2_ref[...] = jnp.zeros_like(x2_ref)
        if k + 2 <= last:
            line.arrived(k, gall_ref.at[k + 2], (sgd.at[1], rgd.at[1]))
            if k > 0:
                line.send(k, k - 1, lambda: (gall_ref.at[k + 2], gall_ref.at[k + 2], (sgd.at[2], rgd.at[2])))

    line.each(third)
    project_chunk(0, x2_ref)

    block = step
    window = LONGEST + block
    lane = iota((1, 128), 1) // HEAD_DIM
    for rb in range(rows // block):
        first = rb * block
        bias_ref[...] = key_bias(start_ref[:, first : first + block], block, first, LONGEST)

        def pair(i, _, first=first):
            lanes = pl.ds(pl.multiple_of(i * 128, 128), 128)
            k = k_ref[first : first + window, lanes]
            vt = v_ref[first : first + window, lanes].T
            q = q_ref[first : first + block, lanes]
            parts = []
            for half in range(2):
                qm = jnp.where(lane == half, q, jnp.zeros_like(q))
                s = mm(k, qm, NT) * (SCORE_SCALE * LOG2E) + bias_ref[...]
                top = jnp.max(s, axis=0, keepdims=True)
                p = jnp.exp2(s - top)
                total = jnp.sum(p, axis=0, keepdims=True)
                out = mm(vt[half * HEAD_DIM : (half + 1) * HEAD_DIM], p.astype(BF16), NN)
                parts.append(out * (1.0 / total))
                lse_ref[pl.ds(i * 2 + half, 1), first : first + block] = top + jnp.log2(total)
            o_ref[first : first + block, lanes] = jnp.concatenate(parts, axis=0).T.astype(BF16)
            return 0

        lax.fori_loop(0, HEADS // 2, pair, 0)
        if rb == 0:
            def fourth(k):
                if k > 0:
                    line.arrived(k, gall_ref.at[k - 1], (sgu.at[0], rgu.at[0]))
                    if k < last:
                        line.send(k, k + 1, lambda: (gall_ref.at[k - 1], gall_ref.at[k - 1], (sgu.at[1], rgu.at[1])))

            line.each(fourth)

    route = routes_ref[t]
    router_part(route, o_ref, w_ref, x_own, gain2_ref, res_ref, wrc_ref, xm_ref, hp_ref.at[t], gt_ref)

    def fifth(k):
        if k < last:
            line.send(k, k + 1, lambda: (hp_ref.at[k], hp_ref.at[k], (shu.at[0], rhu.at[0])))
        if k > 0:
            line.send(k, k - 1, lambda: (hp_ref.at[k], hp_ref.at[k], (shd.at[0], rhd.at[0])))
        if k > 1:
            line.arrived(k, gall_ref.at[k - 2], (sgu.at[1], rgu.at[1]))
            if k < last:
                line.send(k, k + 1, lambda: (gall_ref.at[k - 2], gall_ref.at[k - 2], (sgu.at[2], rgu.at[2])))

    line.each(fifth)
    local_part(route, xm_ref, hp_ref.at[t], g_own, gt_ref, v8_ref, xl_ref, dhl_ref, sm_ref, gv_ref)

    def sixth(k):
        for hop in range(2):
            up, down = k - 1 - hop, k + 1 + hop
            if up >= 0:
                line.arrived(k, hp_ref.at[up], (shu.at[hop], rhu.at[hop]))
                if k < last:
                    line.send(k, k + 1, lambda up=up, hop=hop: (hp_ref.at[up], hp_ref.at[up], (shu.at[hop + 1], rhu.at[hop + 1])))
            if down <= last:
                line.arrived(k, hp_ref.at[down], (shd.at[hop], rhd.at[hop]))
                if k > 0:
                    line.send(k, k - 1, lambda down=down, hop=hop: (hp_ref.at[down], hp_ref.at[down], (shd.at[hop + 1], rhd.at[hop + 1])))
        if k == last:
            line.arrived(k, hp_ref.at[0], (shu.at[2], rhu.at[2]))
            line.arrived(k, gall_ref.at[0], (sgu.at[2], rgu.at[2]))
        if k == 0:
            line.arrived(k, hp_ref.at[last], (shd.at[2], rhd.at[2]))
            line.arrived(k, gall_ref.at[last], (sgd.at[2], rgd.at[2]))

    line.each(sixth)
    line.leave()
    if fast:
        net.leave()


def middle_part(route, dh_ref, gt_ref, sm_ref, wrc_ref, x1_ref, gain_ref, g_ref, h2_ref, w_ref, o_ref, gv_ref,
                dx_ref, da_ref, do_ref, delta_ref, dres_ref, small_ref):
    rows = x1_ref.shape[0]
    dgf = dh_ref[rows : rows + SPARE, 0:rows]
    dh = dh_ref[0:rows, :]
    dgate = jnp.concatenate([dgf[0:EXPERTS] + dgf[EXPERTS:], sm_ref[EXPERTS:SPARE]], axis=0)
    expert = iota((SPARE, rows), 0)
    named0, named1 = expert == route[0:1], expert == route[1:2]
    g0, g1 = gt_ref[0:1], gt_ref[1:2]
    d0 = jnp.sum(jnp.where(named0, dgate, 0.0), axis=0, keepdims=True)
    d1 = jnp.sum(jnp.where(named1, dgate, 0.0), axis=0, keepdims=True)
    inner = g0 * d0 + g1 * d1
    dz = jnp.where(named0, g0 * (d0 - inner), jnp.where(named1, g1 * (d1 - inner), 0.0))
    dres_ref[...] = dz
    dz = jnp.where(expert < 12, dz, sm_ref[...])
    zh, zm, zl = split3(dz)
    wh, wm, wl = split3(wrc_ref[...])
    dh = dh + (mm(zh, wl, TN) + mm(zl, wh, TN) + mm(zm, wm, TN) + mm(zh, wm, TN) + mm(zm, wh, TN) + mm(zh, wh, TN))
    h = h2_ref[...]
    small_ref[0:SPARE, :] = mm(zl, h, NN) + mm(zm, h, NN) + mm(zh, h, NN)
    x1 = x1_ref[...]
    r = lax.rsqrt(jnp.mean(x1 * x1, axis=1, keepdims=True) + EPSILON)
    xr = x1 * r
    grad_gain = jnp.sum(dh * xr, axis=0, keepdims=True)
    gv = gv_ref[...]
    small_ref[SPARE : SPARE + 8, :] = jnp.concatenate([gv[0:2], grad_gain, gv[3:8]], axis=0)
    scaled = dh * gain_ref[...]
    dx = g_ref[...].astype(F32) + r * (scaled - xr * jnp.mean(xr * scaled, axis=1, keepdims=True))
    dx_ref[...] = dx
    da = dx.astype(BF16)
    da_ref[...] = da
    do = mm(da, w_ref[:, 3 * D : 4 * D], NN).astype(BF16)
    do_ref[...] = do
    high, low = split2(do.astype(F32) * o_ref[...].astype(F32))
    heads = pick(iota((SPARE, D), 1) // HEAD_DIM == iota((SPARE, D), 0))
    delta_ref[...] = mm(heads, high, NT) + mm(heads, low, NT)


def backward_body(size, back_ref, out_ref, dhl_ref, gt_ref, sm_ref, routes_ref, wrc_ref, xm_ref, gain_ref, g_ref, hp_ref, w_ref,
                  o_ref, gv_ref, q_ref, k_ref, v_ref, lse_ref, start_ref, cos_ref, sin_ref, xl_ref,
                  dx_ref, da_ref, dres_ref, small_ref, dq_ref, dk_ref, dv_ref, y_ref,
                  bias_ref, dkf_ref, dvf_ref, dh_ref, do_ref, delta_ref, bu_ref, bd_ref, fu_ref, fd_ref,
                  sbu, rbu, sbd, rbd, sfu, rfu, sfd, rfd):
    rows = xm_ref.shape[0]
    packed = rows + SPARE
    cut = 272
    pieces = (slice(0, cut), slice(cut, packed))
    line = Line(size)
    t = line.place
    last = size - 1
    line.enter()

    def add_rows(held, mine):
        def one(i, _):
            at = pl.ds(pl.multiple_of(i * 16, 16), 16)
            held[at, :] = (held[at, :].astype(F32) + mine[at, :].astype(F32)).astype(BF16)
            return 0

        lax.fori_loop(0, held.shape[0] // 16, one, 0)

    def handle(k, way, dest, part, index, mine_ref, up_ref, down_ref, ups, downs):
        slot = dest - 1 if way == 1 else dest
        first = k == (0 if way == 1 else last)
        mine = mine_ref.at[dest, part]

        def refs():
            held = (up_ref if way == 1 else down_ref).at[slot, part]
            sems = tuple(s.at[slot, index] for s in (ups if way == 1 else downs))
            return mine_ref.at[dest, part] if first else held, held, sems

        _, held, sems = refs()
        if not first:
            line.arrived(k, held, sems)
        if dest != k:
            if not first:
                add_rows(held, mine)
            line.send(k, k + way, refs)

    def sum_back(k, opening):
        for time, way, dest in sum_events(size, k):
            if (time == 0) != opening:
                continue
            for index, part in enumerate(pieces):
                handle(k, way, dest, part, index, back_ref, bu_ref, bd_ref, (sbu, rbu), (sbd, rbd))

    def sum_out(k, now):
        for time, way, dest in sum_events(size, k):
            if time == now:
                handle(k, way, dest, slice(0, rows), 0, out_ref, fu_ref, fd_ref, (sfu, rfu), (sfd, rfd))

    line.each(lambda k: (sum_back(k, True), sum_out(k, 0), None)[2])
    line.each(lambda k: sum_back(k, False))
    dh_ref[...] = back_ref[t].astype(F32)

    @pl.when(t > 0)
    def _():
        dh_ref[...] += bu_ref[t - 1].astype(F32)

    @pl.when(t < last)
    def _():
        dh_ref[...] += bd_ref[t].astype(F32)

    dh_ref[0:rows, :] += dhl_ref[...]
    middle_part(routes_ref[t], dh_ref, gt_ref, sm_ref, wrc_ref, xm_ref, gain_ref, g_ref, hp_ref.at[t, 0:rows], w_ref, o_ref, gv_ref,
                dx_ref, da_ref, do_ref, delta_ref, dres_ref, small_ref)
    line.each(lambda k: sum_out(k, 1))

    block = 256
    window = LONGEST + block
    lane = iota((1, 128), 1) // HEAD_DIM
    for rb in range(rows // block):
        first = rb * block
        bias_ref[rb] = key_bias(start_ref[:, first : first + block], block, first, LONGEST)

    def pair(i, _):
        lanes = pl.ds(pl.multiple_of(i * 128, 128), 128)
        for rb in range(rows // block):
            first = rb * block
            k = k_ref[first : first + window, lanes]
            v = v_ref[first : first + window, lanes]
            kt = k.T
            q = q_ref[first : first + block, lanes]
            do = do_ref[first : first + block, lanes]
            dk = jnp.zeros((window, 128), F32)
            dv = jnp.zeros((window, 128), F32)
            parts = []
            for half in range(2):
                qm = jnp.where(lane == half, q, jnp.zeros_like(q))
                dom = jnp.where(lane == half, do, jnp.zeros_like(do))
                head = pl.ds(i * 2 + half, 1)
                s = mm(k, qm, NT) * (SCORE_SCALE * LOG2E) + bias_ref[rb]
                p = jnp.exp2(s - lse_ref[head, first : first + block])
                dp = mm(v, dom, NT)
                ds = (p * (dp - delta_ref[head, first : first + block])).astype(BF16)
                dv = dv + mm(p.astype(BF16), dom, NN)
                dk = dk + mm(ds, qm, NN)
                parts.append(mm(kt[half * HEAD_DIM : (half + 1) * HEAD_DIM], ds, NN))
            dq = jnp.concatenate(parts, axis=0).T * SCORE_SCALE
            at = slice(2 * rows + first, 2 * rows + first + block)
            dq_ref[first : first + block, lanes] = (dq * cos_ref[at, :] - turn(dq) * sin_ref[at, :]).astype(BF16)
            if first == 0:
                dkf_ref[0:window, :] = dk
                dvf_ref[0:window, :] = dv
            else:
                old = window - block
                dkf_ref[first : first + old, :] += dk[0:old]
                dvf_ref[first : first + old, :] += dv[0:old]
                dkf_ref[first + old : first + window, :] = dk[old:]
                dvf_ref[first + old : first + window, :] = dv[old:]
        dk = dkf_ref[...] * SCORE_SCALE
        dk_ref[:, lanes] = (dk * cos_ref[...] - turn(dk) * sin_ref[...]).astype(BF16)
        dv_ref[:, lanes] = dvf_ref[...].astype(BF16)
        return 0

    lax.fori_loop(0, HEADS // 4, pair, 0)
    line.each(lambda k: sum_out(k, 2))
    lax.fori_loop(HEADS // 4, HEADS // 2, pair, 0)
    line.each(lambda k: sum_out(k, 3))
    xl_ref[...] += out_ref[t].astype(F32)

    @pl.when(t > 0)
    def _():
        xl_ref[...] += fu_ref[t - 1].astype(F32)

    @pl.when(t < last)
    def _():
        xl_ref[...] += fd_ref[t].astype(F32)

    y_ref[...] = xl_ref[...].astype(BF16)
    line.leave()


def grads_body(size, x0_ref, x1_ref, x2_ref, h_ref, dq_ref, dk_ref, dv_ref, da_ref, o_ref, w_ref, dx_ref, gain_ref,
               gw_ref, gpart_ref, out_ref, d0_ref, d1_ref, d2_ref, ra_ref, rb_ref, sems_s, sems_r):
    rows = x0_ref.shape[0]
    line = Line(size)
    last = size - 1
    block = 256
    line.enter()

    def hidden(c, d_ref):
        def one(i, _):
            at = pl.ds(pl.multiple_of(i * block, block), block)
            to = pl.ds(pl.multiple_of(c * rows + i * block, block), block)
            total = mm(dk_ref[to, :], w_ref[:, D : 2 * D], NT) + mm(dv_ref[to, :], w_ref[:, 2 * D : 3 * D], NT)
            if c == 2:
                total = total + mm(dq_ref[at, :], w_ref[:, 0:D], NT)
            d_ref[at, :] = total.astype(d_ref.dtype)
            return 0

        lax.fori_loop(0, rows // block, one, 0)

    def gain_of(x_ref, d_ref):
        x = x_ref[...].astype(F32)
        r = lax.rsqrt(jnp.mean(x * x, axis=1, keepdims=True) + EPSILON)
        return jnp.sum(d_ref[...].astype(F32) * x * r, axis=0, keepdims=True)

    hidden(0, d2_ref)

    def first(k):
        if k > 1:
            line.send(k, k - 1, lambda: (d2_ref, ra_ref, (sems_s.at[0], sems_r.at[0])))

    line.each(first)
    hidden(1, d1_ref)
    gain = gain_of(x2_ref, d2_ref) + gain_of(x1_ref, d1_ref)
    h = h_ref[...]

    def weight(column, left, right_ref):
        for c in range(D // 256):
            cols = slice(c * 256, (c + 1) * 256)
            gw_ref[:, column * D + c * 256 : column * D + c * 256 + 256] = mm(left, right_ref[:, cols], TN).astype(BF16)

    weight(1, h, dk_ref)

    def second(k):
        if 0 < k < last:
            line.arrived(k, ra_ref, (sems_s.at[0], sems_r.at[0]))
            d1_ref[...] = (d1_ref[...].astype(F32) + ra_ref[...].astype(F32)).astype(BF16)
        if k > 0:
            line.send(k, k - 1, lambda: (d1_ref, rb_ref, (sems_s.at[1], sems_r.at[1])))

    line.each(second)
    hidden(2, d0_ref)
    gpart_ref[...] = jnp.broadcast_to(gain + gain_of(x0_ref, d0_ref), (8, D))
    weight(2, h, dv_ref)
    weight(0, h[2 * rows :], dq_ref)
    weight(3, da_ref[...], o_ref)

    def third(k):
        if k < last:
            line.arrived(k, rb_ref, (sems_s.at[1], sems_r.at[1]))
            d0_ref[...] += rb_ref[...].astype(F32)

    line.each(third)
    x = x0_ref[...].astype(F32)
    r = lax.rsqrt(jnp.mean(x * x, axis=1, keepdims=True) + EPSILON)
    xr = x * r
    scaled = d0_ref[...] * gain_ref[...]
    out_ref[...] = (dx_ref[...] + r * (scaled - xr * jnp.mean(xr * scaled, axis=1, keepdims=True))).astype(BF16)
    line.leave()


def finish_body(n_dp, size, x0_ref, x1_ref, x2_ref, h_ref, dq_ref, dk_ref, dv_ref, da_ref, o_ref, w_ref, dx_ref, gain_ref,
                y_ref, small_ref, pos_ref,
                yo_ref, go_ref, gw_ref, sum_ref,
                d0_ref, d1_ref, d2_ref, ra_ref, rb_ref, out_ref, yr_ref, gr_ref, part_ref, r1_ref, r2_ref, r3_ref,
                zs_ref, zr_ref, cur_ref, got_ref,
                sems_s, sems_r, sy, ry, sg, rg, s1, r1, s2, r2, s3, r3, sz, rz, sb, rb):
    rows = x0_ref.shape[0]
    share = rows // n_dp
    line = Line(size)
    last = size - 1
    block = 256
    net = Peers()
    d, t = net.d, net.t
    place = pick(iota((rows, rows), 0) == pos_ref[...])
    about, along = around(d, n_dp), around(t, size)
    net.enter([{"dp": to} for _, to, _ in about] + [{"tensor": to} for _, to, _ in along])

    def scatter(src_ref, dst_ref, sems):
        for j, to, _ in about:
            net.send({"dp": to}, src_ref.at[to], dst_ref.at[d], (sems[0].at[j - 1], sems[1].at[j - 1]))
        dst_ref[d] = src_ref[d]

    def gathered(dst_ref, sems):
        for j, _, source in about:
            held = dst_ref.at[source]
            net.copy({"dp": source}, held, held, (sems[0].at[j - 1], sems[1].at[j - 1])).wait_recv()

    scatter(y_ref, yr_ref, (sy, ry))

    def hidden(c, d_ref):
        def one(i, _):
            at = pl.ds(pl.multiple_of(i * block, block), block)
            to = pl.ds(pl.multiple_of(c * rows + i * block, block), block)
            total = mm(dk_ref[to, :], w_ref[:, D : 2 * D], NT) + mm(dv_ref[to, :], w_ref[:, 2 * D : 3 * D], NT)
            if c == 2:
                total = total + mm(dq_ref[at, :], w_ref[:, 0:D], NT)
            d_ref[at, :] = total.astype(d_ref.dtype)
            return 0

        lax.fori_loop(0, rows // block, one, 0)

    def gain_of(x_ref, d_ref):
        x = x_ref[...].astype(F32)
        r = lax.rsqrt(jnp.mean(x * x, axis=1, keepdims=True) + EPSILON)
        return jnp.sum(d_ref[...].astype(F32) * x * r, axis=0, keepdims=True)

    core, x, y = lax.rem(d, 2), lax.rem(d // 2, 2), d // 4
    there = ({"dp": flip(d, 2)}, {"dp": flip(d, 4)})
    deep = D // n_dp

    def weight(u, left, right_ref):
        for c in range(D // 256):
            cols = slice(c * 256, (c + 1) * 256)
            value = mm(left, right_ref[:, cols], TN).astype(BF16)
            part_ref[u, :, :, cols] = value.reshape(n_dp, deep, 256)
        for j in range(4):
            net.send({"dp": flip(d, 1)}, part_ref.at[u, 2 * j + 1 - core], r1_ref.at[u, j], (s1.at[u, j], r1.at[u, j]))

    def add(u, j, arrived):
        spot = 2 * j + core
        part_ref[u, spot] = (part_ref[u, spot].astype(F32) + arrived[...].astype(F32)).astype(BF16)

    def chips(u):
        if u % 2 == 0:
            first = (there[0], [2 * i + 1 - x for i in range(2)], [2 * i + x for i in range(2)])
            return first, (there[1], 2 * (1 - y) + x)
        first = (there[1], [2 * (1 - y) + i for i in range(2)], [2 * y + i for i in range(2)])
        return first, (there[0], 2 * y + 1 - x)

    def halve(u):
        for j in range(4):
            held = r1_ref.at[u, j]
            net.copy({"dp": flip(d, 1)}, held, held, (s1.at[u, j], r1.at[u, j])).wait_recv()
            add(u, j, held)
        where, theirs, _ = chips(u)[0]
        for i in range(2):
            net.send(where, part_ref.at[u, 2 * theirs[i] + core], r2_ref.at[u, i], (s2.at[u, i], r2.at[u, i]))

    def quarter(u):
        (where, _, mine), (after, spot) = chips(u)
        for i in range(2):
            held = r2_ref.at[u, i]
            net.copy(where, held, held, (s2.at[u, i], r2.at[u, i])).wait_recv()
            add(u, mine[i], held)
        net.send(after, part_ref.at[u, 2 * spot + core], r3_ref.at[u], (s3.at[u], r3.at[u]))

    def own(u):
        after = chips(u)[1][0]
        held = r3_ref.at[u]
        net.copy(after, held, held, (s3.at[u], r3.at[u])).wait_recv()
        value = part_ref[u, d].astype(F32) + held[...].astype(F32)
        wide_share = D // size
        for p in range(size):
            zs_ref[u, p] = value[:, p * wide_share : (p + 1) * wide_share].astype(BF16)
        for j, to, _ in along:
            net.send({"tensor": to}, zs_ref.at[u, to], zr_ref.at[u, j - 1], (sz.at[u, j - 1], rz.at[u, j - 1]))

    def whole(u):
        total = zs_ref[u, t].astype(F32)
        for j, _, source in along:
            held = zr_ref.at[u, j - 1]
            net.copy({"tensor": source}, held, held, (sz.at[u, j - 1], rz.at[u, j - 1])).wait_recv()
            total = total + held[...].astype(F32)
        gw_ref[u] = total

    steps = [("dp", bit) for bit in (1, 2, 4, 8) if bit < n_dp] + [("tensor", bit) for bit in (1, 2, 4, 8) if bit < size]

    def small_out(i):
        axis, bit = steps[i]
        mine = t if axis == "tensor" else d
        net.send({axis: flip(mine, bit)}, cur_ref.at[i], got_ref.at[i], (sb.at[i], rb.at[i]))

    def small_in(i):
        axis, bit = steps[i]
        mine = t if axis == "tensor" else d
        held = got_ref.at[i]
        net.copy({axis: flip(mine, bit)}, held, held, (sb.at[i], rb.at[i])).wait_recv()
        total = cur_ref[i] + held[...]
        if i + 1 < len(steps):
            cur_ref[i + 1] = total
            small_out(i + 1)
        else:
            sum_ref[...] = total

    hidden(0, d2_ref)

    def first(k):
        if k > 1:
            line.send(k, k - 1, lambda: (d2_ref, ra_ref, (sems_s.at[0], sems_r.at[0])))

    line.each(first)
    hidden(1, d1_ref)

    def second(k):
        if k == last:
            line.send(k, k - 1, lambda: (d1_ref, rb_ref, (sems_s.at[1], sems_r.at[1])))

    line.each(second)
    h = h_ref[...]
    weight(0, h, dk_ref)
    gain = gain_of(x2_ref, d2_ref) + gain_of(x1_ref, d1_ref)
    weight(1, h, dv_ref)
    halve(0)
    hidden(2, d0_ref)
    gain = gain + gain_of(x0_ref, d0_ref)
    rest = small_ref.shape[0]
    cur_ref[0, 0:rest, :] = small_ref[...]
    cur_ref[0, rest : rest + 8, :] = jnp.broadcast_to(gain, (8, D))
    small_out(0)
    halve(1)

    def third(k):
        if 0 < k < last:
            line.arrived(k, ra_ref, (sems_s.at[0], sems_r.at[0]))
            d1_ref[...] = (d1_ref[...].astype(F32) + ra_ref[...].astype(F32)).astype(BF16)
            line.send(k, k - 1, lambda: (d1_ref, rb_ref, (sems_s.at[1], sems_r.at[1])))

    line.each(third)
    weight(2, h[2 * rows :], dq_ref)
    small_in(0)
    weight(3, da_ref[...], o_ref)
    quarter(0)
    quarter(1)
    halve(2)
    small_in(1)
    halve(3)
    own(0)
    own(1)
    gathered(yr_ref, (sy, ry))
    yo_ref[...] = mm(place, yr_ref[...].reshape(rows, D), TN).astype(BF16)
    quarter(2)
    quarter(3)
    small_in(2)
    own(2)
    own(3)

    def fourth(k):
        if k < last:
            line.arrived(k, rb_ref, (sems_s.at[1], sems_r.at[1]))
            d0_ref[...] += rb_ref[...].astype(F32)

    line.each(fourth)
    xv = x0_ref[...].astype(F32)
    r = lax.rsqrt(jnp.mean(xv * xv, axis=1, keepdims=True) + EPSILON)
    xr = xv * r
    scaled = d0_ref[...] * gain_ref[...]
    value = dx_ref[...] + r * (scaled - xr * jnp.mean(xr * scaled, axis=1, keepdims=True))
    out_ref[...] = value.astype(BF16).reshape(n_dp, share, D)
    scatter(out_ref, gr_ref, (sg, rg))
    for i in range(3, len(steps)):
        small_in(i)
    for u in range(4):
        whole(u)
    gathered(gr_ref, (sg, rg))
    go_ref[...] = mm(place, gr_ref[...].reshape(rows, D), TN).astype(BF16)
    line.leave()
    net.leave()


def experts_body(ff, chunks, first, part, cnt_ref, h_refs, g_refs, slot_ref, w_ref, *refs):
    before, refs = (refs[:2], refs[2:]) if first else (None, refs)
    o_refs, d_refs, gw_ref = refs[:3]
    (xbuf, gbuf, cbuf, onehot, fbuf, dbuf, gacc, gates, dgrow, off_ref, base_ref, nt_ref) = refs[3:]
    rows = slot_ref.shape[2]
    e = pl.program_id(0)

    def match(j, expert, tile):
        slots = slot_ref[j, pl.ds(first + expert, 1), :]
        return (iota((TILE, rows), 0) + tile * TILE) == slots

    def store_rows(at, count, hit, x, gs, gate_row):
        to = pl.ds(pl.multiple_of(at, 16), TILE)
        keep = iota((TILE, 1), 0) < count
        col = jnp.sum(jnp.where(hit, gate_row, 0.0), axis=1, keepdims=True)
        xbuf[to, :] = jnp.where(keep, x, xbuf[to, :].astype(F32)).astype(BF16)
        gbuf[to, :] = jnp.where(keep, gs, gbuf[to, :].astype(F32)).astype(BF16)
        cbuf[to, :] = jnp.where(keep, jnp.broadcast_to(col, (TILE, 128)), cbuf[to, :])

    def round16(n):
        return ((n + 15) // 16) * 16

    @pl.when(e == 0)
    def _gather():
        at = jnp.int32(0)
        for ex in range(part):
            base_ref[ex] = at
            here = at
            for j in range(chunks):
                off_ref[j * EXPERTS + ex] = here
                here = here + round16(cnt_ref[j * EXPERTS + first + ex])
            tiles = (here - at + (ROWS - 1)) // ROWS
            nt_ref[ex] = tiles
            tail = pl.ds(pl.multiple_of(here, 16), ROWS)
            xbuf[tail, :] = jnp.zeros((ROWS, D), BF16)
            gbuf[tail, :] = jnp.zeros((ROWS, D), BF16)
            cbuf[tail, :] = jnp.zeros((ROWS, 128), F32)
            at = at + tiles * ROWS
        for j in range(chunks):
            gates[...] = h_refs[j, rows : rows + SPARE, 0:rows].astype(F32)

            def two(i, _, j=j):
                hits = [match(j, 2 * i + half, 0) for half in range(2)]
                sel = jnp.concatenate([pick(hit) for hit in hits], axis=0)
                x = mm(sel, h_refs[j, 0:rows, :], NN)
                gs = mm(sel, g_refs[j], NN)
                for half in range(2):
                    ex = 2 * i + half
                    count = round16(jnp.minimum(cnt_ref[j * EXPERTS + first + ex], TILE))
                    span = slice(half * TILE, (half + 1) * TILE)
                    store_rows(off_ref[j * EXPERTS + ex], count, hits[half], x[span], gs[span], gates[pl.ds(first + ex, 1), :])
                return 0

            lax.fori_loop(0, part // 2, two, 0)

            def rare(ex, _, j=j):
                def more(tile, _):
                    hit = match(j, ex, tile)
                    sel = pick(hit)
                    count = round16(jnp.minimum(cnt_ref[j * EXPERTS + first + ex] - tile * TILE, TILE))
                    store_rows(
                        off_ref[j * EXPERTS + ex] + tile * TILE,
                        count,
                        hit,
                        mm(sel, h_refs[j, 0:rows, :], NN),
                        mm(sel, g_refs[j], NN),
                        gates[pl.ds(first + ex, 1), :],
                    )
                    return 0

                return lax.fori_loop(1, (cnt_ref[j * EXPERTS + first + ex] + (TILE - 1)) // TILE, more, 0)

            lax.fori_loop(0, part, rare, 0)

    gacc[...] = jnp.zeros_like(gacc)

    def tile_step(m, _):
        at = pl.ds(pl.multiple_of(base_ref[e] + m * ROWS, 16), ROWS)
        x = xbuf[at, :]
        gs = gbuf[at, :].astype(F32)
        gate = wide(cbuf[at, :])
        u = mm(x, w_ref[:, 0:ff], NN)
        up = mm(x, w_ref[:, ff : 2 * ff], NN)
        sig = jax.nn.sigmoid(u)
        silu = u * sig
        act = (silu * up).astype(BF16)
        f = mm(act, w_ref[:, 2 * ff : 3 * ff], NT)
        cbuf[at, :] = jnp.broadcast_to(jnp.sum(gs * f, axis=1, keepdims=True), (ROWS, 128))
        gbuf[at, :] = (f * gate).astype(BF16)
        df = (gs * gate).astype(BF16)
        dact = mm(df, w_ref[:, 2 * ff : 3 * ff], NN)
        dup = (dact * silu).astype(BF16)
        du = (dact * up * sig * (1.0 + u * (1.0 - sig))).astype(BF16)
        xbuf[at, :] = (mm(du, w_ref[:, 0:ff], NT) + mm(dup, w_ref[:, ff : 2 * ff], NT)).astype(BF16)
        gacc[:, 0:ff] += mm(x, du, TN)
        gacc[:, ff : 2 * ff] += mm(x, dup, TN)
        gacc[:, 2 * ff : 3 * ff] += mm(df, act, TN)
        return 0

    lax.fori_loop(0, nt_ref[e], tile_step, 0)
    gw_ref[...] = gacc[...].astype(BF16)

    @pl.when(e == part - 1)
    def _scatter():
        dgrow[...] = jnp.zeros_like(dgrow)
        for j in range(chunks):
            def take(ex, _, j=j):
                at = pl.ds(pl.multiple_of(off_ref[j * EXPERTS + ex], 16), TILE)
                to = pl.ds(pl.multiple_of(ex * TILE, 16), TILE)
                hit = match(j, ex, 0)
                onehot[to, :] = pick(hit)
                fbuf[to, :] = gbuf[at, :]
                dbuf[to, :] = xbuf[at, :]
                col = jnp.concatenate([cbuf[at, :]] * (rows // 128), axis=1)
                dgrow[pl.ds(first + ex, 1), :] = jnp.sum(jnp.where(hit, col, 0.0), axis=0, keepdims=True)
                return 0

            lax.fori_loop(0, part, take, 0)
            gacc[0:rows, 0:D] = mm(onehot[...], fbuf[...], TN)
            gacc[0:rows, D : 2 * D] = mm(onehot[...], dbuf[...], TN)

            def rare(ex, _, j=j):
                def more(tile, _):
                    at = pl.ds(pl.multiple_of(off_ref[j * EXPERTS + ex] + tile * TILE, 16), TILE)
                    hit = match(j, ex, tile)
                    sel = pick(hit)
                    gacc[0:rows, 0:D] += mm(sel, gbuf[at, :], TN)
                    gacc[0:rows, D : 2 * D] += mm(sel, xbuf[at, :], TN)
                    col = jnp.concatenate([cbuf[at, :]] * (rows // 128), axis=1)
                    dgrow[pl.ds(first + ex, 1), :] += jnp.sum(jnp.where(hit, col, 0.0), axis=0, keepdims=True)
                    return 0

                return lax.fori_loop(1, (cnt_ref[j * EXPERTS + first + ex] + (TILE - 1)) // TILE, more, 0)

            lax.fori_loop(0, part, rare, 0)
            if before:
                gacc[0:rows, 0:D] += before[0][j].astype(F32)
                gacc[0:rows, D : 2 * D] += before[1][j, 0:rows, :].astype(F32)
            o_refs[j] = gacc[0:rows, 0:D].astype(BF16)
            d_refs[j, 0:rows, :] = gacc[0:rows, D : 2 * D].astype(BF16)
            total = dgrow[...]
            high = total.astype(BF16).astype(F32)
            both = jnp.concatenate([high, total - high], axis=0)
            both = jnp.concatenate([both, jnp.zeros((SPARE, D - rows), F32)], axis=1)
            if before:
                both = both + before[1][j, rows : rows + SPARE, :].astype(F32)
            d_refs[j, rows : rows + SPARE, :] = both.astype(BF16)


def experts_call(counts, hs, gs, slots, weights, ff, first, part, before=()):
    chunks, rows = gs.shape[:2]
    width = 3 * ff
    most = (rows + 15 * chunks + ROWS - 1) // ROWS * ROWS * part + ROWS
    whole = lambda shape: pl.BlockSpec(shape, lambda e: (0,) * len(shape), pipeline_mode=pl.Buffered(1))
    return pl.pallas_call(
        functools.partial(experts_body, ff, chunks, first, part),
        name="experts",
        grid=(part,),
        in_specs=[smem(), whole(hs.shape), whole(gs.shape), whole(slots.shape), pl.BlockSpec((D, width), lambda e: (0, first + e))]
        + [whole(b.shape) for b in before],
        out_specs=[whole(gs.shape), whole(hs.shape), pl.BlockSpec((D, width), lambda e: (0, e))],
        out_shape=[
            jax.ShapeDtypeStruct(gs.shape, BF16),
            jax.ShapeDtypeStruct(hs.shape, BF16),
            jax.ShapeDtypeStruct((D, part * width), BF16),
        ],
        scratch_shapes=[
            pltpu.VMEM((most, D), BF16),
            pltpu.VMEM((most, D), BF16),
            pltpu.VMEM((most, 128), F32),
            pltpu.VMEM((part * TILE, rows), BF16),
            pltpu.VMEM((part * TILE, D), BF16),
            pltpu.VMEM((part * TILE, D), BF16),
            pltpu.VMEM((D, width), F32),
            pltpu.VMEM((SPARE, rows), F32),
            pltpu.VMEM((EXPERTS, rows), F32),
            pltpu.SMEM((chunks * EXPERTS,), I32),
            pltpu.SMEM((EXPERTS,), I32),
            pltpu.SMEM((EXPERTS,), I32),
        ],
        compiler_params=pltpu.CompilerParams(
            dimension_semantics=("arbitrary",), vmem_limit_bytes=VMEM_CAP
        ),
    )(counts, hs, gs, slots, weights, *before)


def body(tokens, cotangent, deal, lengths, routes, gate_residual, w_qkv, w_out, w_gate_up, w_down,
         norm_gain_attn, norm_gain_moe, w_router, w_const, v_const):
    rows = tokens.shape[0]
    n_dp, n_t = lax.axis_size("dp"), lax.axis_size("tensor")
    t = lax.axis_index("tensor")
    ff = w_down.shape[2]
    d_here = w_qkv.shape[0]

    def swap(v, j):
        return lax.ppermute(v, "tensor", [(i, i ^ j) for i in range(n_t)])

    def place_in(parts):
        stacked = jnp.stack(parts)
        return jnp.stack([lax.dynamic_index_in_dim(stacked, t ^ i, 0, keepdims=False) for i in range(n_t)], axis=2)

    fast = n_dp == 8 and d_here % 16 == 0 and rows % 128 == 0
    attn_shard = jnp.concatenate([w_qkv, w_out[:, None, :]], axis=1)
    if not fast:
        attn_shard = place_in([attn_shard] + [swap(attn_shard, j) for j in range(1, n_t)]).reshape(d_here, 4 * D)
        w_attn = lax.all_gather(attn_shard, "dp", axis=0, tiled=True)
    ff_shard = jnp.concatenate([w_gate_up.reshape(d_here, EXPERTS, 2 * ff), w_down], axis=2)
    w_ff = lax.all_gather(ff_shard.reshape(d_here, EXPERTS * 3 * ff), "dp", axis=0, tiled=True)

    routes_t = routes.reshape(n_t, rows, 2).transpose(0, 2, 1)
    row, ext = (rows, D), (3 * rows, D)
    every, every_packed = (n_t, rows, D), (n_t, rows + SPARE, D)
    xs, gs, pos, slots, counts = call(
        functools.partial(deal_body, n_dp),
        "deal",
        [(row, BF16), (row, BF16), ((1, rows), I32), ((n_t, EXPERTS, rows), I32), ((n_t, EXPERTS, 128), I32)],
        [deal.reshape(1, rows), tokens, cotangent, routes_t],
    )
    counts = counts[:, :, 0].reshape(n_t * EXPERTS)
    share = rows // n_dp
    if fast:
        parts = (n_dp, share, D)
        opening = [xs.reshape(parts), gs.reshape(parts), attn_shard.transpose(1, 0, 2)]
        opened = [(parts, BF16), (parts, BF16), ((n_dp, d_here, 4 * D), BF16)]
    else:
        parts = (1, rows, D)
        x0 = lax.all_to_all(xs, "dp", split_axis=0, concat_axis=0, tiled=True)
        g0 = lax.all_to_all(gs, "dp", split_axis=0, concat_axis=0, tiled=True)
        opening, opened = [x0.reshape(parts), g0.reshape(parts), w_attn.reshape(1, D, 4 * D)], []

    turns = HEAD_DIM // 2
    rates = jnp.asarray(np.tile(10000.0 ** (np.arange(turns) / -turns), 4).reshape(1, 128), F32)
    gain_attn, gain_moe = norm_gain_attn.reshape(1, D), norm_gain_moe.reshape(1, D)
    window = LONGEST + 256
    res_t = jnp.concatenate([gate_residual.T, jnp.zeros((4, rows), F32)], axis=0)
    wrc = jnp.concatenate([w_router.T, w_const.transpose(0, 2, 1).reshape(4, D)], axis=0)
    v8 = jnp.concatenate([v_const, jnp.zeros((6, D), F32)], axis=0)
    dma = lambda *shape: pltpu.SemaphoreType.DMA(shape)
    scratch = [pltpu.VMEM((window, 256), F32), dma(2), dma(2)] + [dma(3)] * 8
    if fast:
        scratch += [pltpu.VMEM((n_t, 4, d_here, D // n_t), BF16)] + [dma(n_t - 1)] * 2 + [dma(n_dp - 1)] * 4
        scratch += [dma(2)] * 2 + [dma(2, 2)] * 2 + [dma(n_dp // 2)] * 2
    results = call(
        functools.partial(forward_body, n_dp if fast else 1, n_t),
        "forward",
        opened
        + [(parts, BF16), (parts, BF16), (ext, BF16), (row, BF16), (ext, BF16), (ext, BF16), (row, BF16), ((SPARE, rows), F32),
           (row, F32), (every_packed, BF16), ((n_t,) + parts, BF16), ((8, rows), F32), (row, F32), (row, F32), ((SPARE, rows), F32),
           ((8, D), F32), ((3 * rows, 128), F32), ((3 * rows, 128), F32), ((1, rows), I32)],
        [lengths[0]] + opening + [gain_attn, gain_moe, rates, res_t, wrc, routes_t, v8],
        scalars=1,
        scratch=scratch,
        meet=0,
    )
    if fast:
        x0, g0, w_attn = results[0].reshape(row), results[1].reshape(row), results[2].reshape(D, 4 * D)
        results = results[3:]
    x1, x2, h, q, k, v, o, lse, xm, hp_all, g_all, gt, xl, dhl, sm, gv, cos, sin, start = results
    x1, x2, g_all = x1.reshape(row), x2.reshape(row), g_all.reshape(every)

    half = EXPERTS // 2
    early = experts_call(counts, hp_all, g_all, slots, w_ff, ff, 0, half)
    out_all, back_all, gw_ff = experts_call(counts, hp_all, g_all, slots, w_ff, ff, half, half, early[:2])
    ff_sum = [lax.psum_scatter(gw, "dp", scatter_dimension=0, tiled=True) for gw in (early[2], gw_ff)]

    dx, da, dres, small, dq, dk, dv, result = call(
        functools.partial(backward_body, n_t),
        "backward",
        [(row, F32), (row, BF16), ((SPARE, rows), F32), ((SPARE + 8, D), F32), (row, BF16), (ext, BF16), (ext, BF16), (row, BF16)],
        [back_all, out_all, dhl, gt, sm, routes_t, wrc, xm, gain_moe, g0, hp_all, w_attn, o, gv, q, k, v, lse, start, cos, sin, xl],
        scratch=[pltpu.VMEM((rows // 256, window, 256), F32), pltpu.VMEM((3 * rows, 128), F32), pltpu.VMEM((3 * rows, 128), F32),
                 pltpu.VMEM((rows + SPARE, D), F32), pltpu.VMEM(row, BF16), pltpu.VMEM((SPARE, rows), F32)]
        + [pltpu.VMEM((n_t - 1, rows + SPARE, D), BF16)] * 2 + [pltpu.VMEM((n_t - 1, rows, D), BF16)] * 2
        + [dma(n_t - 1, 2)] * 4 + [dma(n_t - 1, 1)] * 4,
        meet=1,
    )
    if fast:
        units = 4
        piece = (d_here, D)
        hops = 3 + (n_t - 1).bit_length()
        output, grad_tokens, attn_parts, small_all = call(
            functools.partial(finish_body, n_dp, n_t),
            "finish",
            [(row, BF16), (row, BF16), ((units, d_here, D // n_t), F32), ((SPARE + 16, D), F32)],
            [x0, x1, x2, h, dq, dk, dv, da, o, w_attn, dx, gain_attn, result.reshape(n_dp, share, D), small, pos],
            scratch=[pltpu.VMEM(row, F32)] + [pltpu.VMEM(row, BF16)] * 4 + [pltpu.VMEM((n_dp, share, D), BF16)] * 3
            + [pltpu.VMEM((units, n_dp) + piece, BF16), pltpu.VMEM((units, 4) + piece, BF16), pltpu.VMEM((units, 2) + piece, BF16),
               pltpu.VMEM((units,) + piece, BF16), pltpu.VMEM((units, n_t, d_here, D // n_t), BF16),
               pltpu.VMEM((units, n_t - 1, d_here, D // n_t), BF16)]
            + [pltpu.VMEM((hops, SPARE + 16, D), F32)] * 2
            + [dma(2)] * 2 + [dma(n_dp - 1)] * 4 + [dma(units, 4)] * 2 + [dma(units, 2)] * 2 + [dma(units)] * 2
            + [dma(units, n_t - 1)] * 2 + [dma(hops)] * 2,
            meet=2,
        )
        gain_all = small_all[SPARE + 8]
        attn_own = jnp.stack([attn_parts[2], attn_parts[0], attn_parts[1], attn_parts[3]], axis=1)
    else:
        back_out = lax.all_to_all(result, "dp", split_axis=0, concat_axis=0, tiled=True)
        gw_attn, gain_part, d_start = call(
            functools.partial(grads_body, n_t),
            "grads",
            [((D, 4 * D), BF16), ((8, D), F32), (row, BF16)],
            [x0, x1, x2, h, dq, dk, dv, da, o, w_attn, dx, gain_attn],
            scratch=[pltpu.VMEM(row, F32)] + [pltpu.VMEM(row, BF16)] * 4 + [dma(2), dma(2)],
            meet=2,
        )
        back_grad = lax.all_to_all(d_start, "dp", split_axis=0, concat_axis=0, tiled=True)
        output, grad_tokens = call(restore_body, "restore", [(row, BF16)] * 2, [pos, back_out, back_grad])

        def total(v):
            for axis, count in (("tensor", n_t), ("dp", n_dp)):
                bit = 1
                while bit < count:
                    v = v + lax.ppermute(v, axis, [(i, i ^ bit) for i in range(count)])
                    bit *= 2
            return v

        small_all = total(jnp.concatenate([small, gain_part], axis=0))
        gain_all = small_all[SPARE + 8]
        gw_attn, ff_sum = lax.optimization_barrier((gw_attn, ff_sum))
        attn_sum = lax.psum_scatter(gw_attn, "dp", scatter_dimension=0, tiled=True).reshape(d_here, 4, n_t, D // n_t)

        def share(j):
            return lax.dynamic_index_in_dim(attn_sum, t ^ j, 2, keepdims=False)

        attn_own = share(0).astype(F32)
        for j in range(1, n_t):
            attn_own = attn_own + swap(share(j), j).astype(F32)
    ff_own = [v.reshape(d_here, half, 3 * ff) for v in ff_sum]
    gate_up, down = (jnp.concatenate([v[:, :, at] for v in ff_own], axis=1).astype(F32) for at in (slice(0, 2 * ff), slice(2 * ff, None)))
    return (
        output,
        grad_tokens,
        dres[0:12].T,
        attn_own[:, 0:3],
        attn_own[:, 3],
        gate_up.reshape(d_here, EXPERTS, 2, ff),
        down,
        gain_all,
        small_all[SPARE + 2],
        small_all[0:12].T,
        small_all[12:16].reshape(2, 2, D).transpose(0, 2, 1),
        small_all[SPARE : SPARE + 2],
    )


def solution(mesh):
    both, every = P(("dp", "tensor"), None), P()
    weights = (P("dp", None, "tensor"), P("dp", "tensor"), P("dp", None, None, "tensor"), P("dp", None, "tensor"))
    return jax.shard_map(
        body,
        mesh=mesh,
        in_specs=(both, both, P(("dp", "tensor")), P("dp", None), P("dp", None), both, *weights) + (every,) * 5,
        out_specs=(both, both, both, *weights) + (every,) * 5,
        check_vma=False,
    )
```

```python
import functools

import jax
import jax.numpy as jnp
import numpy as np
from jax import lax
from jax.experimental import pallas as pl
from jax.experimental.pallas import tpu as pltpu
from jax.sharding import PartitionSpec as P

D = 768
HEAD_DIM = 64
HEADS = 12
EXPERTS = 8
LONGEST = 1024
EPSILON = 1e-6
MASKED = -1e30
F32, BF16, I32 = jnp.float32, jnp.bfloat16, jnp.int32
NN = (((1,), (0,)), ((), ()))
NT = (((1,), (1,)), ((), ()))
TN = (((0,), (0,)), ((), ()))
SCORE_SCALE = HEAD_DIM**-0.5
LOG2E = 1.4426950408889634
TILE = 160
ROWS = 256
SPARE = 16
VMEM_CAP = 66_000_000


def mm(a, b, dims):
    return lax.dot_general(a, b, dims, preferred_element_type=F32)


def iota(shape, axis):
    return lax.broadcasted_iota(I32, shape, axis)


def pick(cond):
    return jnp.where(cond, 1.0, 0.0).astype(BF16)


def split2(v):
    high = v.astype(BF16)
    return high, (v - high.astype(F32)).astype(BF16)


def split3(v):
    high = v.astype(BF16)
    rest = v - high.astype(F32)
    mid = rest.astype(BF16)
    return high, mid, (rest - mid.astype(F32)).astype(BF16)


def vmem():
    return pl.BlockSpec(memory_space=pltpu.VMEM)


def smem():
    return pl.BlockSpec(memory_space=pltpu.SMEM)


def call(body, name, outs, operands, scalars=0, scratch=(), meet=None):
    return pl.pallas_call(
        body,
        name=name,
        out_shape=[jax.ShapeDtypeStruct(*o) for o in outs],
        in_specs=[smem()] * scalars + [vmem()] * (len(operands) - scalars),
        out_specs=[vmem()] * len(outs),
        scratch_shapes=list(scratch),
        compiler_params=pltpu.CompilerParams(
            vmem_limit_bytes=VMEM_CAP, collective_id=meet, has_side_effects=meet is not None
        ),
    )(*operands)


def deal_body(n_dp, deal_ref, tok_ref, cot_ref, routes_ref, xs_ref, gs_ref, pos_ref, slot_ref, cnt_ref):
    rows = tok_ref.shape[0]
    first, second = iota((rows, rows), 0), iota((rows, rows), 1)
    before = pick(first < second)
    deal = deal_ref[...]
    hit = iota((n_dp, rows), 0) == deal
    rank = mm(pick(hit), before, NN)
    rank = jnp.sum(jnp.where(hit, rank, 0.0), axis=0, keepdims=True).astype(I32)
    pos = deal * (rows // n_dp) + rank
    pos_ref[...] = pos
    place = pick(first == pos)
    xs_ref[...] = mm(place, tok_ref[...], NN).astype(BF16)
    gs_ref[...] = mm(place, cot_ref[...], NN).astype(BF16)
    expert = iota((EXPERTS, rows), 0)
    for j in range(routes_ref.shape[0]):
        route = routes_ref[j]
        named = (expert == route[0:1]) | (expert == route[1:2])
        ahead = mm(pick(named), before, NN).astype(I32)
        slot_ref[j] = jnp.where(named, ahead, -1)
        total = jnp.sum(jnp.where(named, 1.0, 0.0), axis=1, keepdims=True).astype(I32)
        cnt_ref[j] = jnp.broadcast_to(total, (EXPERTS, 128))


def restore_body(pos_ref, a_ref, b_ref, oa_ref, ob_ref):
    rows = a_ref.shape[0]
    place = pick(iota((rows, rows), 0) == pos_ref[...])
    oa_ref[...] = mm(place, a_ref[...], TN).astype(BF16)
    ob_ref[...] = mm(place, b_ref[...], TN).astype(BF16)


class Line:
    def __init__(self, size):
        self.size = size
        self.place = lax.axis_index("tensor")
        self.sent = {k: [] for k in range(size)}

    def each(self, body):
        for k in range(self.size):
            pl.when(self.place == k)(functools.partial(body, k))

    def enter(self):
        sem = pltpu.get_barrier_semaphore()

        def greet(k):
            near = [n for n in (k - 1, k + 1) if 0 <= n < self.size]
            for n in near:
                pl.semaphore_signal(sem, 1, device_id={"tensor": self.place + (n - k)}, device_id_type=pl.DeviceIdType.MESH)
            pl.semaphore_wait(sem, len(near))

        self.each(greet)

    def copy(self, hop, src, dst, sems):
        return pltpu.make_async_remote_copy(
            src_ref=src,
            dst_ref=dst,
            send_sem=sems[0],
            recv_sem=sems[1],
            device_id={"tensor": self.place + hop},
            device_id_type=pl.DeviceIdType.MESH,
        )

    def send(self, k, to, refs):
        self.copy(to - k, *refs()).start()
        self.sent[k].append((to - k, refs))

    def arrived(self, k, dst, sems):
        self.copy((k ^ 1) - k, dst, dst, sems).wait_recv()

    def leave(self):
        def drain(k):
            for hop, refs in self.sent[k]:
                self.copy(hop, *refs()).wait_send()

        self.each(drain)


class Peers:
    def __init__(self):
        self.d, self.t = lax.axis_index("dp"), lax.axis_index("tensor")
        self.sent = []

    def enter(self, targets):
        sem = pltpu.get_barrier_semaphore()
        for where in targets:
            pl.semaphore_signal(sem, 1, device_id=where, device_id_type=pl.DeviceIdType.MESH)
        pl.semaphore_wait(sem, len(targets))

    def copy(self, where, src, dst, sems):
        return pltpu.make_async_remote_copy(
            src_ref=src,
            dst_ref=dst,
            send_sem=sems[0],
            recv_sem=sems[1],
            device_id=where,
            device_id_type=pl.DeviceIdType.MESH,
        )

    def send(self, where, src, dst, sems):
        copy = self.copy(where, src, dst, sems)
        copy.start()
        self.sent.append(copy)

    def leave(self):
        for copy in self.sent:
            copy.wait_send()


def flip(index, bit):
    return index + bit * (1 - 2 * ((index // bit) % 2))


def around(index, count):
    return [(j, lax.rem(index + j, count), lax.rem(index + count - j, count)) for j in range(1, count)]


class Rows:
    def __init__(self, ref):
        self.ref = ref

    def __getitem__(self, at):
        columns = slice(None) if at is Ellipsis else at[1]
        value = self.ref[:, :, columns]
        return value.reshape(value.shape[0] * value.shape[1], value.shape[2])


def sum_events(size, k):
    events = []
    for dest in range(size):
        if dest >= k and dest > 0:
            events.append((0 if k == 0 else size - 1 - dest + k, 1, dest))
        if dest <= k and dest < size - 1:
            events.append((0 if k == size - 1 else dest + size - 1 - k, -1, dest))
    drop = [(t, w, d) for t, w, d in events if (k == 0 and w == 1 and d == 0) or (k == size - 1 and w == -1 and d == k)]
    return sorted((ev for ev in events if ev not in drop), key=lambda ev: (ev[0], ev[1], -ev[1] * ev[2]))


def turn(u):
    low = (iota((1, u.shape[1]), 1) % HEAD_DIM) < HEAD_DIM // 2
    half = HEAD_DIM // 2
    return jnp.where(low, pltpu.roll(u, u.shape[1] - half, 1), pltpu.roll(u, half, 1))


def wide(table):
    return jnp.concatenate([table] * (D // 128), axis=1)


def key_bias(start, block, first_row, base):
    window = LONGEST + block
    key = iota((window, block), 0) + first_row
    row = iota((1, block), 1) + (base + first_row)
    return jnp.where((key >= start) & (key <= row), 0.0, MASKED)


def router_part(route, o_ref, w_ref, x_ref, gain_ref, res_ref, wrc_ref, x1_ref, hp_ref, gt_ref):
    rows = o_ref.shape[0]
    x1 = x_ref[...].astype(F32) + mm(o_ref[...], w_ref[:, 3 * D : 4 * D], NT)
    x1_ref[...] = x1
    h = x1 * lax.rsqrt(jnp.mean(x1 * x1, axis=1, keepdims=True) + EPSILON) * gain_ref[...]
    h = h.astype(BF16)
    hp_ref[0:rows, :] = h
    high, mid, low = split3(wrc_ref[...])
    z = mm(low, h, NT) + mm(mid, h, NT) + mm(high, h, NT) + res_ref[...]
    expert = iota(z.shape, 0)
    named0, named1 = expert == route[0:1], expert == route[1:2]
    c0 = jnp.sum(jnp.where(named0, z, 0.0), axis=0, keepdims=True)
    c1 = jnp.sum(jnp.where(named1, z, 0.0), axis=0, keepdims=True)
    top = jnp.maximum(c0, c1)
    e0, e1 = jnp.exp(c0 - top), jnp.exp(c1 - top)
    g0, g1 = e0 / (e0 + e1), e1 / (e0 + e1)
    table = [g0, g1]
    for j in range(2):
        l0, l1 = z[12 + 2 * j : 13 + 2 * j], z[13 + 2 * j : 14 + 2 * j]
        top = jnp.maximum(l0, l1)
        m0, m1 = jnp.exp(l0 - top), jnp.exp(l1 - top)
        table += [m0 / (m0 + m1), m1 / (m0 + m1)]
    gt_ref[...] = jnp.concatenate(table + [jnp.zeros((2, rows), F32)], axis=0)
    gates = jnp.where(named0, g0, jnp.where(named1, g1, 0.0))
    gates = jnp.where(expert < EXPERTS, gates, 0.0)
    hp_ref[rows : rows + SPARE, :] = jnp.concatenate([gates, jnp.zeros((SPARE, D - rows), F32)], axis=1).astype(BF16)


def local_part(route, x1_ref, hp_ref, g_ref, gt_ref, v_ref, xl_ref, dhl_ref, sm_ref, gv_ref):
    rows = x1_ref.shape[0]
    h, g = hp_ref[0:rows, :], g_ref[...]
    hf, gf = h.astype(F32), g.astype(F32)
    low0 = gt_ref[0:1].astype(BF16).astype(F32)
    low1 = gt_ref[1:2].astype(BF16).astype(F32)

    def weight(e):
        return jnp.where(route[0:1] == e, low0, 0.0) + jnp.where(route[1:2] == e, low1, 0.0)

    copy, first, second = weight(EXPERTS + 1), weight(EXPERTS + 2), weight(EXPERTS + 3)
    m00, m01, m10, m11 = gt_ref[2:3], gt_ref[3:4], gt_ref[4:5], gt_ref[5:6]
    a = copy + first * m00 + second * m10
    b0, b1 = first * m01, second * m11
    table = jnp.concatenate([a, b0, b1, jnp.zeros((125, rows), F32)], axis=0).T
    ac, b0c, b1c = table[:, 0:1], table[:, 1:2], table[:, 2:3]
    v = v_ref[...]
    xl_ref[...] = x1_ref[...] + ac * hf + b0c * v[0:1] + b1c * v[1:2]
    dhl_ref[...] = ac * gf
    ones = jnp.ones((8, D), BF16)
    high, low = split2(hf * gf)
    gh = (mm(ones, high, NT) + mm(ones, low, NT))[0:1]
    vh, vm, vl = split3(v)
    gvs = mm(vl, g, NT) + mm(vm, g, NT) + mm(vh, g, NT)
    gv0, gv1 = gvs[0:1], gvs[1:2]
    zero = jnp.zeros((9, rows), F32)
    dl0 = first * m00 * m01 * (gh - gv0)
    dl1 = second * m10 * m11 * (gh - gv1)
    sm_ref[...] = jnp.concatenate(
        [zero, gh, m00 * gh + m01 * gv0, m10 * gh + m11 * gv1, dl0, -dl0, dl1, -dl1], axis=0
    )
    bh, bm, bl = split3(jnp.concatenate([b0, b1, jnp.zeros((6, rows), F32)], axis=0))
    gv_ref[...] = mm(bl, g, NN) + mm(bm, g, NN) + mm(bh, g, NN)


def rope_tables(lengths_ref, rates_ref, t, rows, cos_ref, sin_ref, start_ref):
    begins, total = [], jnp.int32(0)
    for i in range(lengths_ref.shape[0]):
        begins.append(total)
        total = total + lengths_ref[i]

    def opening(row):
        found = jnp.zeros_like(row)
        for begin in begins:
            found = jnp.where(begin <= row, jnp.maximum(found, begin), found)
        return found

    start_ref[...] = LONGEST - t * rows + opening(iota((1, rows), 1) + t * rows)
    sign = jnp.where(iota((1, 128), 1) % HEAD_DIM < HEAD_DIM // 2, -1.0, 1.0)
    step = 128

    def tile(i, _):
        at = pl.multiple_of(i * step, step)
        row = iota((step, 128), 0) + (at + (t - 2) * rows)
        angles = (row - opening(row)).astype(F32) * rates_ref[...]
        cos_ref[pl.ds(at, step), :] = jnp.cos(angles)
        sin_ref[pl.ds(at, step), :] = jnp.sin(angles) * sign
        return 0

    lax.fori_loop(0, cos_ref.shape[0] // step, tile, 0)


def opening_body(n_dp, size, lengths_ref, xs_ref, gs_ref, ws_ref, rates_ref,
                 x0_ref, g0_ref, w3_ref, x1_ref, x2_ref, cos_ref, sin_ref, start_ref,
                 wz_ref, sz, rz, sa, ra, sb, rb, s1, r1, s2, r2, s3, r3, sx, rx):
    rows = x0_ref.shape[0] * x0_ref.shape[1]
    line = Line(size)
    t = line.place
    last = size - 1

    def begin(k):
        if k < last:
            line.send(k, k + 1, lambda: (x0_ref, x1_ref, (sx.at[0], rx.at[0])))

    def second(k):
        if k > 0:
            line.arrived(k, x1_ref, (sx.at[0], rx.at[0]))
        else:
            x1_ref[...] = jnp.zeros_like(x1_ref)
        if 0 < k < last:
            line.send(k, k + 1, lambda: (x1_ref, x2_ref, (sx.at[1], rx.at[1])))

    def third(k):
        if k > 1:
            line.arrived(k, x2_ref, (sx.at[1], rx.at[1]))
        else:
            x2_ref[...] = jnp.zeros_like(x2_ref)

    net = Peers()
    d = net.d
    along, about = around(t, size), around(d, n_dp)
    net.enter([{"dp": to} for _, to, _ in about] + [{"tensor": to} for _, to, _ in along])
    for j, to, _ in along:
        net.send({"tensor": to}, ws_ref, wz_ref.at[t], (sz.at[j - 1], rz.at[j - 1]))
    for src_ref, dst_ref, ss, rr in ((xs_ref, x0_ref, sa, ra), (gs_ref, g0_ref, sb, rb)):
        for j, to, _ in about:
            net.send({"dp": to}, src_ref.at[to], dst_ref.at[d], (ss.at[j - 1], rr.at[j - 1]))
        dst_ref[d] = src_ref[d]
    wz_ref[t] = ws_ref[...]
    rope_tables(lengths_ref, rates_ref, t, rows, cos_ref, sin_ref, start_ref)

    def gathered(dst_ref, ss, rr):
        for j, _, source in about:
            held = dst_ref.at[source]
            net.copy({"dp": source}, held, held, (ss.at[j - 1], rr.at[j - 1])).wait_recv()

    gathered(x0_ref, sa, ra)
    line.each(begin)
    for j, _, source in along:
        held = wz_ref.at[source]
        net.copy({"tensor": source}, held, held, (sz.at[j - 1], rz.at[j - 1])).wait_recv()
    for c in range(4):
        w3_ref[d, :, c * D : (c + 1) * D] = jnp.concatenate([wz_ref[p, c] for p in range(size)], axis=1)
    pair, across = flip(d, 1), (flip(d, 2), flip(d, 4))
    halves = (slice(0, 2 * D), slice(2 * D, 4 * D))

    def pass_on(way, spot, half, sems):
        net.send({"dp": way}, w3_ref.at[spot, :, halves[half]], w3_ref.at[spot, :, halves[half]], sems)

    def passed(way, spot, half, sems):
        held = w3_ref.at[spot, :, halves[half]]
        net.copy({"dp": way}, held, held, sems).wait_recv()

    for half in range(2):
        pass_on(across[half], d, half, (s1.at[half], r1.at[half]))
    for half in range(2):
        near, far = across[half], across[1 - half]
        passed(near, near, half, (s1.at[half], r1.at[half]))
        for i, spot in enumerate((d, near)):
            pass_on(far, spot, half, (s2.at[half, i], r2.at[half, i]))
    line.each(second)
    beyond = flip(across[0], 4)
    for half in range(2):
        near, far = across[half], across[1 - half]
        for i, spot in enumerate((far, beyond)):
            passed(far, spot, half, (s2.at[half, i], r2.at[half, i]))
    core = lax.rem(d, 2)
    for i in range(n_dp // 2):
        spot = 2 * i + core
        net.send({"dp": pair}, w3_ref.at[spot], w3_ref.at[spot], (s3.at[i], r3.at[i]))
    for i in range(n_dp // 2):
        held = w3_ref.at[2 * i + 1 - core]
        net.copy({"dp": pair}, held, held, (s3.at[i], r3.at[i])).wait_recv()
    gathered(g0_ref, sb, rb)
    line.each(third)
    line.leave()
    net.leave()


def forward_body(fast, size, *refs):
    if fast:
        (x0_ref, g0_ref, w3_ref, x1_ref, x2_ref, cos_ref, sin_ref, start_ref), refs = refs[:8], refs[8:]
    else:
        (lengths_ref, rates_ref, x0_ref, g0_ref, w3_ref), refs = refs[:5], refs[5:]
    (gain_ref, gain2_ref, res_ref, wrc_ref, routes_ref, v8_ref), refs = refs[:6], refs[6:]
    if not fast:
        (x1_ref, x2_ref, cos_ref, sin_ref, start_ref), refs = refs[:5], refs[5:]
    (h_ref, q_ref, k_ref, v_ref, o_ref, lse_ref, xm_ref, hp_ref, gall_ref, gt_ref, xl_ref, dhl_ref, sm_ref, gv_ref,
     bias_ref, sx, rx, sgu, rgu, sgd, rgd, shu, rhu, shd, rhd) = refs
    rows = x0_ref.shape[0] * x0_ref.shape[1]
    step = 256
    line = Line(size)
    t = line.place
    last = size - 1
    w_ref, x_own, g_own = Rows(w3_ref), Rows(x0_ref), Rows(g0_ref)

    def begin(k):
        if k < last:
            if not fast:
                line.send(k, k + 1, lambda: (x0_ref, x1_ref, (sx.at[0], rx.at[0])))
            line.send(k, k + 1, lambda: (g0_ref, gall_ref.at[k], (sgu.at[0], rgu.at[0])))
        if k > 0:
            line.send(k, k - 1, lambda: (g0_ref, gall_ref.at[k], (sgd.at[0], rgd.at[0])))

    def first_rows(k):
        if k > 0:
            line.arrived(k, x1_ref, (sx.at[0], rx.at[0]))
        else:
            x1_ref[...] = jnp.zeros_like(x1_ref)
        if 0 < k < last:
            line.send(k, k + 1, lambda: (x1_ref, x2_ref, (sx.at[1], rx.at[1])))

    def second_rows(k):
        if k > 1:
            line.arrived(k, x2_ref, (sx.at[1], rx.at[1]))
        else:
            x2_ref[...] = jnp.zeros_like(x2_ref)

    def hop(k, far):
        up, down = k - far, k + far
        if up >= 0:
            line.arrived(k, gall_ref.at[up], (sgu.at[far - 1], rgu.at[far - 1]))
            if k < last:
                line.send(k, k + 1, lambda: (gall_ref.at[up], gall_ref.at[up], (sgu.at[far], rgu.at[far])))
        if down <= last:
            line.arrived(k, gall_ref.at[down], (sgd.at[far - 1], rgd.at[far - 1]))
            if k > 0:
                line.send(k, k - 1, lambda: (gall_ref.at[down], gall_ref.at[down], (sgd.at[far], rgd.at[far])))

    line.enter()
    line.each(begin)
    gall_ref[t] = g0_ref[...]
    if not fast:
        rope_tables(lengths_ref, rates_ref, t, rows, cos_ref, sin_ref, start_ref)
    gain = gain_ref[...]

    def part(x_ref, i):
        share = x_ref.shape[1]
        if share == rows:
            return x_ref[0, pl.ds(pl.multiple_of(i * step, step), step), :]
        return x_ref[pl.ds(i * (step // share), step // share)].reshape(step, D)

    def project_chunk(c, x_ref):
        def project(i, _):
            at = pl.multiple_of(i * step, step)
            x = part(x_ref, i).astype(F32)
            h = x * lax.rsqrt(jnp.mean(x * x, axis=1, keepdims=True) + EPSILON) * gain
            h = h.astype(BF16)
            to = pl.ds(pl.multiple_of(c * rows + i * step, step), step)
            h_ref[to, :] = h
            cos, sin = wide(cos_ref[to, :]), wide(sin_ref[to, :])
            k = mm(h, w_ref[:, D : 2 * D], NN)
            k_ref[to, :] = (k * cos + turn(k) * sin).astype(BF16)
            v_ref[to, :] = mm(h, w_ref[:, 2 * D : 3 * D], NN).astype(BF16)
            if c == 2:
                q = mm(h, w_ref[:, 0:D], NN)
                q_ref[pl.ds(at, step), :] = (q * cos + turn(q) * sin).astype(BF16)
            return 0

        lax.fori_loop(0, rows // step, project, 0)

    project_chunk(2, x0_ref)
    if not fast:
        line.each(first_rows)
    project_chunk(1, x1_ref)
    if not fast:
        line.each(second_rows)
    project_chunk(0, x2_ref)
    line.each(lambda k: hop(k, 1))

    block = step
    window = LONGEST + block
    lane = iota((1, 128), 1) // HEAD_DIM
    for rb in range(rows // block):
        first = rb * block
        bias_ref[...] = key_bias(start_ref[:, first : first + block], block, first, LONGEST)

        def pair(i, _, first=first):
            lanes = pl.ds(pl.multiple_of(i * 128, 128), 128)
            k = k_ref[first : first + window, lanes]
            vt = v_ref[first : first + window, lanes].T
            q = q_ref[first : first + block, lanes]
            parts = []
            for half in range(2):
                qm = jnp.where(lane == half, q, jnp.zeros_like(q))
                s = mm(k, qm, NT) * (SCORE_SCALE * LOG2E) + bias_ref[...]
                top = jnp.max(s, axis=0, keepdims=True)
                p = jnp.exp2(s - top)
                total = jnp.sum(p, axis=0, keepdims=True)
                out = mm(vt[half * HEAD_DIM : (half + 1) * HEAD_DIM], p.astype(BF16), NN)
                parts.append(out * (1.0 / total))
                lse_ref[pl.ds(i * 2 + half, 1), first : first + block] = top + jnp.log2(total)
            o_ref[first : first + block, lanes] = jnp.concatenate(parts, axis=0).T.astype(BF16)
            return 0

        lax.fori_loop(0, HEADS // 2, pair, 0)
        if rb == 0:
            line.each(lambda k: hop(k, 2))

    route = routes_ref[t]
    router_part(route, o_ref, w_ref, x_own, gain2_ref, res_ref, wrc_ref, xm_ref, hp_ref.at[t], gt_ref)

    def fifth(k):
        if k < last:
            line.send(k, k + 1, lambda: (hp_ref.at[k], hp_ref.at[k], (shu.at[0], rhu.at[0])))
        if k > 0:
            line.send(k, k - 1, lambda: (hp_ref.at[k], hp_ref.at[k], (shd.at[0], rhd.at[0])))

    line.each(fifth)
    local_part(route, xm_ref, hp_ref.at[t], g_own, gt_ref, v8_ref, xl_ref, dhl_ref, sm_ref, gv_ref)

    def sixth(k):
        for hop in range(2):
            up, down = k - 1 - hop, k + 1 + hop
            if up >= 0:
                line.arrived(k, hp_ref.at[up], (shu.at[hop], rhu.at[hop]))
                if k < last:
                    line.send(k, k + 1, lambda up=up, hop=hop: (hp_ref.at[up], hp_ref.at[up], (shu.at[hop + 1], rhu.at[hop + 1])))
            if down <= last:
                line.arrived(k, hp_ref.at[down], (shd.at[hop], rhd.at[hop]))
                if k > 0:
                    line.send(k, k - 1, lambda down=down, hop=hop: (hp_ref.at[down], hp_ref.at[down], (shd.at[hop + 1], rhd.at[hop + 1])))
        if k == last:
            line.arrived(k, hp_ref.at[0], (shu.at[2], rhu.at[2]))
            line.arrived(k, gall_ref.at[0], (sgu.at[2], rgu.at[2]))
        if k == 0:
            line.arrived(k, hp_ref.at[last], (shd.at[2], rhd.at[2]))
            line.arrived(k, gall_ref.at[last], (sgd.at[2], rgd.at[2]))

    line.each(sixth)
    line.leave()


def middle_part(route, dh_ref, gt_ref, sm_ref, wrc_ref, x1_ref, gain_ref, g_ref, h2_ref, w_ref, o_ref, gv_ref,
                dx_ref, da_ref, do_ref, delta_ref, dres_ref, small_ref):
    rows = x1_ref.shape[0]
    dgf = dh_ref[rows : rows + SPARE, 0:rows]
    dh = dh_ref[0:rows, :]
    dgate = jnp.concatenate([dgf[0:EXPERTS] + dgf[EXPERTS:], sm_ref[EXPERTS:SPARE]], axis=0)
    expert = iota((SPARE, rows), 0)
    named0, named1 = expert == route[0:1], expert == route[1:2]
    g0, g1 = gt_ref[0:1], gt_ref[1:2]
    d0 = jnp.sum(jnp.where(named0, dgate, 0.0), axis=0, keepdims=True)
    d1 = jnp.sum(jnp.where(named1, dgate, 0.0), axis=0, keepdims=True)
    inner = g0 * d0 + g1 * d1
    dz = jnp.where(named0, g0 * (d0 - inner), jnp.where(named1, g1 * (d1 - inner), 0.0))
    dres_ref[...] = dz
    dz = jnp.where(expert < 12, dz, sm_ref[...])
    zh, zm, zl = split3(dz)
    wh, wm, wl = split3(wrc_ref[...])
    dh = dh + (mm(zh, wl, TN) + mm(zl, wh, TN) + mm(zm, wm, TN) + mm(zh, wm, TN) + mm(zm, wh, TN) + mm(zh, wh, TN))
    h = h2_ref[...]
    small_ref[0:SPARE, :] = mm(zl, h, NN) + mm(zm, h, NN) + mm(zh, h, NN)
    x1 = x1_ref[...]
    r = lax.rsqrt(jnp.mean(x1 * x1, axis=1, keepdims=True) + EPSILON)
    xr = x1 * r
    grad_gain = jnp.sum(dh * xr, axis=0, keepdims=True)
    gv = gv_ref[...]
    small_ref[SPARE : SPARE + 8, :] = jnp.concatenate([gv[0:2], grad_gain, gv[3:8]], axis=0)
    scaled = dh * gain_ref[...]
    dx = g_ref[...].astype(F32) + r * (scaled - xr * jnp.mean(xr * scaled, axis=1, keepdims=True))
    dx_ref[...] = dx
    da = dx.astype(BF16)
    da_ref[...] = da
    do = mm(da, w_ref[:, 3 * D : 4 * D], NN).astype(BF16)
    do_ref[...] = do
    high, low = split2(do.astype(F32) * o_ref[...].astype(F32))
    heads = pick(iota((SPARE, D), 1) // HEAD_DIM == iota((SPARE, D), 0))
    delta_ref[...] = mm(heads, high, NT) + mm(heads, low, NT)


def backward_body(size, back_ref, out_ref, dhl_ref, gt_ref, sm_ref, routes_ref, wrc_ref, xm_ref, gain_ref, g_ref, hp_ref, w_ref,
                  o_ref, gv_ref, q_ref, k_ref, v_ref, lse_ref, start_ref, cos_ref, sin_ref, xl_ref,
                  dx_ref, da_ref, dres_ref, small_ref, dq_ref, dk_ref, dv_ref, y_ref,
                  bias_ref, dkf_ref, dvf_ref, dh_ref, do_ref, delta_ref, bu_ref, bd_ref, fu_ref, fd_ref,
                  sbu, rbu, sbd, rbd, sfu, rfu, sfd, rfd):
    rows = xm_ref.shape[0]
    packed = rows + SPARE
    cut = 272
    pieces = (slice(0, cut), slice(cut, packed))
    line = Line(size)
    t = line.place
    last = size - 1
    line.enter()

    def add_rows(held, mine):
        def one(i, _):
            at = pl.ds(pl.multiple_of(i * 16, 16), 16)
            held[at, :] = (held[at, :].astype(F32) + mine[at, :].astype(F32)).astype(BF16)
            return 0

        lax.fori_loop(0, held.shape[0] // 16, one, 0)

    def handle(k, way, dest, part, index, mine_ref, up_ref, down_ref, ups, downs):
        slot = dest - 1 if way == 1 else dest
        first = k == (0 if way == 1 else last)
        mine = mine_ref.at[dest, part]

        def refs():
            held = (up_ref if way == 1 else down_ref).at[slot, part]
            sems = tuple(s.at[slot, index] for s in (ups if way == 1 else downs))
            return mine_ref.at[dest, part] if first else held, held, sems

        _, held, sems = refs()
        if not first:
            line.arrived(k, held, sems)
        if dest != k:
            if not first:
                add_rows(held, mine)
            line.send(k, k + way, refs)

    def sum_back(k, opening):
        for time, way, dest in sum_events(size, k):
            if (time == 0) != opening:
                continue
            for index, part in enumerate(pieces):
                handle(k, way, dest, part, index, back_ref, bu_ref, bd_ref, (sbu, rbu), (sbd, rbd))

    def sum_out(k, now):
        for time, way, dest in sum_events(size, k):
            if time == now:
                handle(k, way, dest, slice(0, rows), 0, out_ref, fu_ref, fd_ref, (sfu, rfu), (sfd, rfd))

    line.each(lambda k: (sum_back(k, True), sum_out(k, 0), None)[2])
    line.each(lambda k: sum_back(k, False))
    dh_ref[...] = back_ref[t].astype(F32)

    @pl.when(t > 0)
    def _():
        dh_ref[...] += bu_ref[t - 1].astype(F32)

    @pl.when(t < last)
    def _():
        dh_ref[...] += bd_ref[t].astype(F32)

    dh_ref[0:rows, :] += dhl_ref[...]
    middle_part(routes_ref[t], dh_ref, gt_ref, sm_ref, wrc_ref, xm_ref, gain_ref, g_ref, hp_ref.at[t, 0:rows], w_ref, o_ref, gv_ref,
                dx_ref, da_ref, do_ref, delta_ref, dres_ref, small_ref)
    line.each(lambda k: sum_out(k, 1))

    block = 256
    window = LONGEST + block
    lane = iota((1, 128), 1) // HEAD_DIM
    for rb in range(rows // block):
        first = rb * block
        bias_ref[rb] = key_bias(start_ref[:, first : first + block], block, first, LONGEST)

    def pair(i, _):
        lanes = pl.ds(pl.multiple_of(i * 128, 128), 128)
        for rb in range(rows // block):
            first = rb * block
            k = k_ref[first : first + window, lanes]
            v = v_ref[first : first + window, lanes]
            kt = k.T
            q = q_ref[first : first + block, lanes]
            do = do_ref[first : first + block, lanes]
            dk = jnp.zeros((window, 128), F32)
            dv = jnp.zeros((window, 128), F32)
            parts = []
            for half in range(2):
                qm = jnp.where(lane == half, q, jnp.zeros_like(q))
                dom = jnp.where(lane == half, do, jnp.zeros_like(do))
                head = pl.ds(i * 2 + half, 1)
                s = mm(k, qm, NT) * (SCORE_SCALE * LOG2E) + bias_ref[rb]
                p = jnp.exp2(s - lse_ref[head, first : first + block])
                dp = mm(v, dom, NT)
                ds = (p * (dp - delta_ref[head, first : first + block])).astype(BF16)
                dv = dv + mm(p.astype(BF16), dom, NN)
                dk = dk + mm(ds, qm, NN)
                parts.append(mm(kt[half * HEAD_DIM : (half + 1) * HEAD_DIM], ds, NN))
            dq = jnp.concatenate(parts, axis=0).T * SCORE_SCALE
            at = slice(2 * rows + first, 2 * rows + first + block)
            dq_ref[first : first + block, lanes] = (dq * cos_ref[at, :] - turn(dq) * sin_ref[at, :]).astype(BF16)
            if first == 0:
                dkf_ref[0:window, :] = dk
                dvf_ref[0:window, :] = dv
            else:
                old = window - block
                dkf_ref[first : first + old, :] += dk[0:old]
                dvf_ref[first : first + old, :] += dv[0:old]
                dkf_ref[first + old : first + window, :] = dk[old:]
                dvf_ref[first + old : first + window, :] = dv[old:]
        dk = dkf_ref[...] * SCORE_SCALE
        dk_ref[:, lanes] = (dk * cos_ref[...] - turn(dk) * sin_ref[...]).astype(BF16)
        dv_ref[:, lanes] = dvf_ref[...].astype(BF16)
        return 0

    lax.fori_loop(0, HEADS // 4, pair, 0)
    line.each(lambda k: sum_out(k, 2))
    lax.fori_loop(HEADS // 4, HEADS // 2, pair, 0)
    line.each(lambda k: sum_out(k, 3))
    xl_ref[...] += out_ref[t].astype(F32)

    @pl.when(t > 0)
    def _():
        xl_ref[...] += fu_ref[t - 1].astype(F32)

    @pl.when(t < last)
    def _():
        xl_ref[...] += fd_ref[t].astype(F32)

    y_ref[...] = xl_ref[...].astype(BF16)
    line.leave()


def grads_body(size, x0_ref, x1_ref, x2_ref, h_ref, dq_ref, dk_ref, dv_ref, da_ref, o_ref, w_ref, dx_ref, gain_ref,
               gw_ref, gpart_ref, out_ref, d0_ref, d1_ref, d2_ref, ra_ref, rb_ref, sems_s, sems_r):
    rows = x0_ref.shape[0]
    line = Line(size)
    last = size - 1
    block = 256
    line.enter()

    def hidden(c, d_ref):
        def one(i, _):
            at = pl.ds(pl.multiple_of(i * block, block), block)
            to = pl.ds(pl.multiple_of(c * rows + i * block, block), block)
            total = mm(dk_ref[to, :], w_ref[:, D : 2 * D], NT) + mm(dv_ref[to, :], w_ref[:, 2 * D : 3 * D], NT)
            if c == 2:
                total = total + mm(dq_ref[at, :], w_ref[:, 0:D], NT)
            d_ref[at, :] = total.astype(d_ref.dtype)
            return 0

        lax.fori_loop(0, rows // block, one, 0)

    def gain_of(x_ref, d_ref):
        x = x_ref[...].astype(F32)
        r = lax.rsqrt(jnp.mean(x * x, axis=1, keepdims=True) + EPSILON)
        return jnp.sum(d_ref[...].astype(F32) * x * r, axis=0, keepdims=True)

    hidden(0, d2_ref)

    def first(k):
        if k > 1:
            line.send(k, k - 1, lambda: (d2_ref, ra_ref, (sems_s.at[0], sems_r.at[0])))

    line.each(first)
    hidden(1, d1_ref)
    gain = gain_of(x2_ref, d2_ref) + gain_of(x1_ref, d1_ref)
    h = h_ref[...]

    def weight(column, left, right_ref):
        for c in range(D // 256):
            cols = slice(c * 256, (c + 1) * 256)
            gw_ref[:, column * D + c * 256 : column * D + c * 256 + 256] = mm(left, right_ref[:, cols], TN).astype(BF16)

    weight(1, h, dk_ref)

    def second(k):
        if 0 < k < last:
            line.arrived(k, ra_ref, (sems_s.at[0], sems_r.at[0]))
            d1_ref[...] = (d1_ref[...].astype(F32) + ra_ref[...].astype(F32)).astype(BF16)
        if k > 0:
            line.send(k, k - 1, lambda: (d1_ref, rb_ref, (sems_s.at[1], sems_r.at[1])))

    line.each(second)
    hidden(2, d0_ref)
    gpart_ref[...] = jnp.broadcast_to(gain + gain_of(x0_ref, d0_ref), (8, D))
    weight(2, h, dv_ref)
    weight(0, h[2 * rows :], dq_ref)
    weight(3, da_ref[...], o_ref)

    def third(k):
        if k < last:
            line.arrived(k, rb_ref, (sems_s.at[1], sems_r.at[1]))
            d0_ref[...] += rb_ref[...].astype(F32)

    line.each(third)
    x = x0_ref[...].astype(F32)
    r = lax.rsqrt(jnp.mean(x * x, axis=1, keepdims=True) + EPSILON)
    xr = x * r
    scaled = d0_ref[...] * gain_ref[...]
    out_ref[...] = (dx_ref[...] + r * (scaled - xr * jnp.mean(xr * scaled, axis=1, keepdims=True))).astype(BF16)
    line.leave()


def finish_body(n_dp, size, x0_ref, x1_ref, x2_ref, h_ref, dq_ref, dk_ref, dv_ref, da_ref, o_ref, w_ref, dx_ref, gain_ref,
                y_ref, small_ref, pos_ref,
                yo_ref, go_ref, gw_ref, sum_ref,
                d0_ref, d1_ref, d2_ref, ra_ref, rb_ref, out_ref, yr_ref, gr_ref, part_ref, r1_ref, r2_ref, r3_ref,
                zs_ref, zr_ref, cur_ref, got_ref,
                sems_s, sems_r, sy, ry, sg, rg, s1, r1, s2, r2, s3, r3, sz, rz, sb, rb):
    rows = x0_ref.shape[0]
    share = rows // n_dp
    line = Line(size)
    last = size - 1
    block = 256
    net = Peers()
    d, t = net.d, net.t
    place = pick(iota((rows, rows), 0) == pos_ref[...])
    about, along = around(d, n_dp), around(t, size)
    net.enter([{"dp": to} for _, to, _ in about] + [{"tensor": to} for _, to, _ in along])

    def scatter(src_ref, dst_ref, sems):
        for j, to, _ in about:
            net.send({"dp": to}, src_ref.at[to], dst_ref.at[d], (sems[0].at[j - 1], sems[1].at[j - 1]))
        dst_ref[d] = src_ref[d]

    def gathered(dst_ref, sems):
        for j, _, source in about:
            held = dst_ref.at[source]
            net.copy({"dp": source}, held, held, (sems[0].at[j - 1], sems[1].at[j - 1])).wait_recv()

    scatter(y_ref, yr_ref, (sy, ry))

    def hidden(c, d_ref):
        def one(i, _):
            at = pl.ds(pl.multiple_of(i * block, block), block)
            to = pl.ds(pl.multiple_of(c * rows + i * block, block), block)
            total = mm(dk_ref[to, :], w_ref[:, D : 2 * D], NT) + mm(dv_ref[to, :], w_ref[:, 2 * D : 3 * D], NT)
            if c == 2:
                total = total + mm(dq_ref[at, :], w_ref[:, 0:D], NT)
            d_ref[at, :] = total.astype(d_ref.dtype)
            return 0

        lax.fori_loop(0, rows // block, one, 0)

    def gain_of(x_ref, d_ref):
        x = x_ref[...].astype(F32)
        r = lax.rsqrt(jnp.mean(x * x, axis=1, keepdims=True) + EPSILON)
        return jnp.sum(d_ref[...].astype(F32) * x * r, axis=0, keepdims=True)

    core, x, y = lax.rem(d, 2), lax.rem(d // 2, 2), d // 4
    there = ({"dp": flip(d, 2)}, {"dp": flip(d, 4)})
    deep = D // n_dp

    def weight(u, left, right_ref):
        for c in range(D // 256):
            cols = slice(c * 256, (c + 1) * 256)
            value = mm(left, right_ref[:, cols], TN).astype(BF16)
            part_ref[u, :, :, cols] = value.reshape(n_dp, deep, 256)
        for j in range(4):
            net.send({"dp": flip(d, 1)}, part_ref.at[u, 2 * j + 1 - core], r1_ref.at[u, j], (s1.at[u, j], r1.at[u, j]))

    def add(u, j, arrived):
        spot = 2 * j + core
        part_ref[u, spot] = (part_ref[u, spot].astype(F32) + arrived[...].astype(F32)).astype(BF16)

    def chips(u):
        if u % 2 == 0:
            first = (there[0], [2 * i + 1 - x for i in range(2)], [2 * i + x for i in range(2)])
            return first, (there[1], 2 * (1 - y) + x)
        first = (there[1], [2 * (1 - y) + i for i in range(2)], [2 * y + i for i in range(2)])
        return first, (there[0], 2 * y + 1 - x)

    def halve(u):
        for j in range(4):
            held = r1_ref.at[u, j]
            net.copy({"dp": flip(d, 1)}, held, held, (s1.at[u, j], r1.at[u, j])).wait_recv()
            add(u, j, held)
        where, theirs, _ = chips(u)[0]
        for i in range(2):
            net.send(where, part_ref.at[u, 2 * theirs[i] + core], r2_ref.at[u, i], (s2.at[u, i], r2.at[u, i]))

    def quarter(u):
        (where, _, mine), (after, spot) = chips(u)
        for i in range(2):
            held = r2_ref.at[u, i]
            net.copy(where, held, held, (s2.at[u, i], r2.at[u, i])).wait_recv()
            add(u, mine[i], held)
        net.send(after, part_ref.at[u, 2 * spot + core], r3_ref.at[u], (s3.at[u], r3.at[u]))

    def own(u):
        after = chips(u)[1][0]
        held = r3_ref.at[u]
        net.copy(after, held, held, (s3.at[u], r3.at[u])).wait_recv()
        value = part_ref[u, d].astype(F32) + held[...].astype(F32)
        wide_share = D // size
        for p in range(size):
            zs_ref[u, p] = value[:, p * wide_share : (p + 1) * wide_share].astype(BF16)
        for j, to, _ in along:
            net.send({"tensor": to}, zs_ref.at[u, to], zr_ref.at[u, j - 1], (sz.at[u, j - 1], rz.at[u, j - 1]))

    def whole(u):
        total = zs_ref[u, t].astype(F32)
        for j, _, source in along:
            held = zr_ref.at[u, j - 1]
            net.copy({"tensor": source}, held, held, (sz.at[u, j - 1], rz.at[u, j - 1])).wait_recv()
            total = total + held[...].astype(F32)
        gw_ref[u] = total

    steps = [("dp", bit) for bit in (1, 2, 4, 8) if bit < n_dp] + [("tensor", bit) for bit in (1, 2, 4, 8) if bit < size]

    def small_out(i):
        axis, bit = steps[i]
        mine = t if axis == "tensor" else d
        net.send({axis: flip(mine, bit)}, cur_ref.at[i], got_ref.at[i], (sb.at[i], rb.at[i]))

    def small_in(i):
        axis, bit = steps[i]
        mine = t if axis == "tensor" else d
        held = got_ref.at[i]
        net.copy({axis: flip(mine, bit)}, held, held, (sb.at[i], rb.at[i])).wait_recv()
        total = cur_ref[i] + held[...]
        if i + 1 < len(steps):
            cur_ref[i + 1] = total
            small_out(i + 1)
        else:
            sum_ref[...] = total

    hidden(0, d2_ref)

    def first(k):
        if k > 1:
            line.send(k, k - 1, lambda: (d2_ref, ra_ref, (sems_s.at[0], sems_r.at[0])))

    line.each(first)
    hidden(1, d1_ref)

    def second(k):
        if k == last:
            line.send(k, k - 1, lambda: (d1_ref, rb_ref, (sems_s.at[1], sems_r.at[1])))

    line.each(second)
    h = h_ref[...]
    weight(0, h, dk_ref)
    gain = gain_of(x2_ref, d2_ref) + gain_of(x1_ref, d1_ref)
    weight(1, h, dv_ref)
    halve(0)
    hidden(2, d0_ref)
    gain = gain + gain_of(x0_ref, d0_ref)
    rest = small_ref.shape[0]
    cur_ref[0, 0:rest, :] = small_ref[...]
    cur_ref[0, rest : rest + 8, :] = jnp.broadcast_to(gain, (8, D))
    small_out(0)
    halve(1)

    def third(k):
        if 0 < k < last:
            line.arrived(k, ra_ref, (sems_s.at[0], sems_r.at[0]))
            d1_ref[...] = (d1_ref[...].astype(F32) + ra_ref[...].astype(F32)).astype(BF16)
            line.send(k, k - 1, lambda: (d1_ref, rb_ref, (sems_s.at[1], sems_r.at[1])))

    line.each(third)
    weight(2, h[2 * rows :], dq_ref)
    small_in(0)
    weight(3, da_ref[...], o_ref)
    quarter(0)
    quarter(1)
    halve(2)
    small_in(1)
    halve(3)
    own(0)
    own(1)
    gathered(yr_ref, (sy, ry))
    yo_ref[...] = mm(place, yr_ref[...].reshape(rows, D), TN).astype(BF16)
    quarter(2)
    quarter(3)
    small_in(2)
    own(2)
    own(3)

    def fourth(k):
        if k < last:
            line.arrived(k, rb_ref, (sems_s.at[1], sems_r.at[1]))
            d0_ref[...] += rb_ref[...].astype(F32)

    line.each(fourth)
    xv = x0_ref[...].astype(F32)
    r = lax.rsqrt(jnp.mean(xv * xv, axis=1, keepdims=True) + EPSILON)
    xr = xv * r
    scaled = d0_ref[...] * gain_ref[...]
    value = dx_ref[...] + r * (scaled - xr * jnp.mean(xr * scaled, axis=1, keepdims=True))
    out_ref[...] = value.astype(BF16).reshape(n_dp, share, D)
    scatter(out_ref, gr_ref, (sg, rg))
    for i in range(3, len(steps)):
        small_in(i)
    for u in range(4):
        whole(u)
    gathered(gr_ref, (sg, rg))
    go_ref[...] = mm(place, gr_ref[...].reshape(rows, D), TN).astype(BF16)
    line.leave()
    net.leave()


def experts_body(ff, chunks, cnt_ref, h_refs, g_refs, slot_ref, w_ref, o_refs, d_refs, gw_ref,
                 xbuf, gbuf, cbuf, onehot, fbuf, dbuf, gacc, gates, dgrow, off_ref, base_ref, nt_ref):
    rows = slot_ref.shape[2]
    e = pl.program_id(0)

    def match(j, expert, tile):
        slots = slot_ref[j, pl.ds(expert, 1), :]
        return (iota((TILE, rows), 0) + tile * TILE) == slots

    def store_rows(at, count, hit, x, gs, gate_row):
        to = pl.ds(pl.multiple_of(at, 16), TILE)
        keep = iota((TILE, 1), 0) < count
        col = jnp.sum(jnp.where(hit, gate_row, 0.0), axis=1, keepdims=True)
        xbuf[to, :] = jnp.where(keep, x, xbuf[to, :].astype(F32)).astype(BF16)
        gbuf[to, :] = jnp.where(keep, gs, gbuf[to, :].astype(F32)).astype(BF16)
        cbuf[to, :] = jnp.where(keep, jnp.broadcast_to(col, (TILE, 128)), cbuf[to, :])

    def round16(n):
        return ((n + 15) // 16) * 16

    @pl.when(e == 0)
    def _gather():
        at = jnp.int32(0)
        for ex in range(EXPERTS):
            base_ref[ex] = at
            here = at
            for j in range(chunks):
                off_ref[j * EXPERTS + ex] = here
                here = here + round16(cnt_ref[j * EXPERTS + ex])
            tiles = (here - at + (ROWS - 1)) // ROWS
            nt_ref[ex] = tiles
            tail = pl.ds(pl.multiple_of(here, 16), ROWS)
            xbuf[tail, :] = jnp.zeros((ROWS, D), BF16)
            gbuf[tail, :] = jnp.zeros((ROWS, D), BF16)
            cbuf[tail, :] = jnp.zeros((ROWS, 128), F32)
            at = at + tiles * ROWS
        for j in range(chunks):
            gates[...] = h_refs[j, rows : rows + SPARE, 0:rows].astype(F32)

            def two(i, _, j=j):
                hits = [match(j, 2 * i + half, 0) for half in range(2)]
                sel = jnp.concatenate([pick(hit) for hit in hits], axis=0)
                x = mm(sel, h_refs[j, 0:rows, :], NN)
                gs = mm(sel, g_refs[j], NN)
                for half in range(2):
                    ex = 2 * i + half
                    count = round16(jnp.minimum(cnt_ref[j * EXPERTS + ex], TILE))
                    part = slice(half * TILE, (half + 1) * TILE)
                    store_rows(off_ref[j * EXPERTS + ex], count, hits[half], x[part], gs[part], gates[pl.ds(ex, 1), :])
                return 0

            lax.fori_loop(0, EXPERTS // 2, two, 0)

            def rare(ex, _, j=j):
                def more(tile, _):
                    hit = match(j, ex, tile)
                    sel = pick(hit)
                    count = round16(jnp.minimum(cnt_ref[j * EXPERTS + ex] - tile * TILE, TILE))
                    store_rows(
                        off_ref[j * EXPERTS + ex] + tile * TILE,
                        count,
                        hit,
                        mm(sel, h_refs[j, 0:rows, :], NN),
                        mm(sel, g_refs[j], NN),
                        gates[pl.ds(ex, 1), :],
                    )
                    return 0

                return lax.fori_loop(1, (cnt_ref[j * EXPERTS + ex] + (TILE - 1)) // TILE, more, 0)

            lax.fori_loop(0, EXPERTS, rare, 0)

    gacc[...] = jnp.zeros_like(gacc)

    def tile_step(m, _):
        at = pl.ds(pl.multiple_of(base_ref[e] + m * ROWS, 16), ROWS)
        x = xbuf[at, :]
        gs = gbuf[at, :].astype(F32)
        gate = wide(cbuf[at, :])
        u = mm(x, w_ref[:, 0:ff], NN)
        up = mm(x, w_ref[:, ff : 2 * ff], NN)
        sig = jax.nn.sigmoid(u)
        silu = u * sig
        act = (silu * up).astype(BF16)
        f = mm(act, w_ref[:, 2 * ff : 3 * ff], NT)
        cbuf[at, :] = jnp.broadcast_to(jnp.sum(gs * f, axis=1, keepdims=True), (ROWS, 128))
        gbuf[at, :] = (f * gate).astype(BF16)
        df = (gs * gate).astype(BF16)
        dact = mm(df, w_ref[:, 2 * ff : 3 * ff], NN)
        dup = (dact * silu).astype(BF16)
        du = (dact * up * sig * (1.0 + u * (1.0 - sig))).astype(BF16)
        xbuf[at, :] = (mm(du, w_ref[:, 0:ff], NT) + mm(dup, w_ref[:, ff : 2 * ff], NT)).astype(BF16)
        gacc[:, 0:ff] += mm(x, du, TN)
        gacc[:, ff : 2 * ff] += mm(x, dup, TN)
        gacc[:, 2 * ff : 3 * ff] += mm(df, act, TN)
        return 0

    lax.fori_loop(0, nt_ref[e], tile_step, 0)
    gw_ref[...] = gacc[...].astype(BF16)

    @pl.when(e == EXPERTS - 1)
    def _scatter():
        for j in range(chunks):
            def take(ex, _, j=j):
                at = pl.ds(pl.multiple_of(off_ref[j * EXPERTS + ex], 16), TILE)
                to = pl.ds(pl.multiple_of(ex * TILE, 16), TILE)
                hit = match(j, ex, 0)
                onehot[to, :] = pick(hit)
                fbuf[to, :] = gbuf[at, :]
                dbuf[to, :] = xbuf[at, :]
                col = jnp.concatenate([cbuf[at, :]] * (rows // 128), axis=1)
                dgrow[pl.ds(ex, 1), :] = jnp.sum(jnp.where(hit, col, 0.0), axis=0, keepdims=True)
                return 0

            lax.fori_loop(0, EXPERTS, take, 0)
            gacc[0:rows, 0:D] = mm(onehot[...], fbuf[...], TN)
            gacc[0:rows, D : 2 * D] = mm(onehot[...], dbuf[...], TN)

            def rare(ex, _, j=j):
                def more(tile, _):
                    at = pl.ds(pl.multiple_of(off_ref[j * EXPERTS + ex] + tile * TILE, 16), TILE)
                    hit = match(j, ex, tile)
                    sel = pick(hit)
                    gacc[0:rows, 0:D] += mm(sel, gbuf[at, :], TN)
                    gacc[0:rows, D : 2 * D] += mm(sel, xbuf[at, :], TN)
                    col = jnp.concatenate([cbuf[at, :]] * (rows // 128), axis=1)
                    dgrow[pl.ds(ex, 1), :] += jnp.sum(jnp.where(hit, col, 0.0), axis=0, keepdims=True)
                    return 0

                return lax.fori_loop(1, (cnt_ref[j * EXPERTS + ex] + (TILE - 1)) // TILE, more, 0)

            lax.fori_loop(0, EXPERTS, rare, 0)
            o_refs[j] = gacc[0:rows, 0:D].astype(BF16)
            d_refs[j, 0:rows, :] = gacc[0:rows, D : 2 * D].astype(BF16)
            total = dgrow[...]
            high = total.astype(BF16).astype(F32)
            both = jnp.concatenate([high, total - high], axis=0)
            d_refs[j, rows : rows + SPARE, :] = jnp.concatenate(
                [both, jnp.zeros((SPARE, D - rows), F32)], axis=1
            ).astype(BF16)


def experts_call(counts, hs, gs, slots, weights, ff):
    chunks, rows = gs.shape[:2]
    width = 3 * ff
    most = (rows + 15 * chunks + ROWS - 1) // ROWS * ROWS * EXPERTS + ROWS
    whole = lambda shape: pl.BlockSpec(shape, lambda e: (0,) * len(shape), pipeline_mode=pl.Buffered(1))
    return pl.pallas_call(
        functools.partial(experts_body, ff, chunks),
        name="experts",
        grid=(EXPERTS,),
        in_specs=[smem(), whole(hs.shape), whole(gs.shape), whole(slots.shape), pl.BlockSpec((D, width), lambda e: (0, e))],
        out_specs=[whole(gs.shape), whole(hs.shape), pl.BlockSpec((D, width), lambda e: (0, e))],
        out_shape=[
            jax.ShapeDtypeStruct(gs.shape, BF16),
            jax.ShapeDtypeStruct(hs.shape, BF16),
            jax.ShapeDtypeStruct((D, EXPERTS * width), BF16),
        ],
        scratch_shapes=[
            pltpu.VMEM((most, D), BF16),
            pltpu.VMEM((most, D), BF16),
            pltpu.VMEM((most, 128), F32),
            pltpu.VMEM((EXPERTS * TILE, rows), BF16),
            pltpu.VMEM((EXPERTS * TILE, D), BF16),
            pltpu.VMEM((EXPERTS * TILE, D), BF16),
            pltpu.VMEM((D, width), F32),
            pltpu.VMEM((SPARE, rows), F32),
            pltpu.VMEM((EXPERTS, rows), F32),
            pltpu.SMEM((chunks * EXPERTS,), I32),
            pltpu.SMEM((EXPERTS,), I32),
            pltpu.SMEM((EXPERTS,), I32),
        ],
        compiler_params=pltpu.CompilerParams(
            dimension_semantics=("arbitrary",), vmem_limit_bytes=VMEM_CAP
        ),
    )(counts, hs, gs, slots, weights)


def body(tokens, cotangent, deal, lengths, routes, gate_residual, w_qkv, w_out, w_gate_up, w_down,
         norm_gain_attn, norm_gain_moe, w_router, w_const, v_const):
    rows = tokens.shape[0]
    n_dp, n_t = lax.axis_size("dp"), lax.axis_size("tensor")
    t = lax.axis_index("tensor")
    ff = w_down.shape[2]
    d_here = w_qkv.shape[0]

    def swap(v, j):
        return lax.ppermute(v, "tensor", [(i, i ^ j) for i in range(n_t)])

    def place_in(parts):
        stacked = jnp.stack(parts)
        return jnp.stack([lax.dynamic_index_in_dim(stacked, t ^ i, 0, keepdims=False) for i in range(n_t)], axis=2)

    fast = n_dp == 8 and d_here % 16 == 0 and rows % 128 == 0
    attn_shard = jnp.concatenate([w_qkv, w_out[:, None, :]], axis=1)
    if not fast:
        attn_shard = place_in([attn_shard] + [swap(attn_shard, j) for j in range(1, n_t)]).reshape(d_here, 4 * D)
        w_attn = lax.all_gather(attn_shard, "dp", axis=0, tiled=True)
    ff_shard = jnp.concatenate([w_gate_up.reshape(d_here, EXPERTS, 2 * ff), w_down], axis=2)

    routes_t = routes.reshape(n_t, rows, 2).transpose(0, 2, 1)
    row, ext = (rows, D), (3 * rows, D)
    every, every_packed = (n_t, rows, D), (n_t, rows + SPARE, D)
    xs, gs, pos, slots, counts = call(
        functools.partial(deal_body, n_dp),
        "deal",
        [(row, BF16), (row, BF16), ((1, rows), I32), ((n_t, EXPERTS, rows), I32), ((n_t, EXPERTS, 128), I32)],
        [deal.reshape(1, rows), tokens, cotangent, routes_t],
    )
    counts = counts[:, :, 0].reshape(n_t * EXPERTS)
    share = rows // n_dp
    if fast:
        parts = (n_dp, share, D)
    else:
        parts = (1, rows, D)
        x0 = lax.all_to_all(xs, "dp", split_axis=0, concat_axis=0, tiled=True)
        g0 = lax.all_to_all(gs, "dp", split_axis=0, concat_axis=0, tiled=True)

    half = HEAD_DIM // 2
    rates = jnp.asarray(np.tile(10000.0 ** (np.arange(half) / -half), 4).reshape(1, 128), F32)
    gain_attn, gain_moe = norm_gain_attn.reshape(1, D), norm_gain_moe.reshape(1, D)
    window = LONGEST + 256
    res_t = jnp.concatenate([gate_residual.T, jnp.zeros((4, rows), F32)], axis=0)
    wrc = jnp.concatenate([w_router.T, w_const.transpose(0, 2, 1).reshape(4, D)], axis=0)
    v8 = jnp.concatenate([v_const, jnp.zeros((6, D), F32)], axis=0)
    dma = lambda *shape: pltpu.SemaphoreType.DMA(shape)
    found = [(parts, BF16), (parts, BF16), ((3 * rows, 128), F32), ((3 * rows, 128), F32), ((1, rows), I32)]
    if fast:
        x0, g0, w_attn, x1, x2, cos, sin, start = call(
            functools.partial(opening_body, n_dp, n_t),
            "opening",
            [(parts, BF16), (parts, BF16), ((n_dp, d_here, 4 * D), BF16)] + found,
            [lengths[0], xs.reshape(parts), gs.reshape(parts), attn_shard.transpose(1, 0, 2), rates],
            scalars=1,
            scratch=[pltpu.VMEM((n_t, 4, d_here, D // n_t), BF16)] + [dma(n_t - 1)] * 2 + [dma(n_dp - 1)] * 4
            + [dma(2)] * 2 + [dma(2, 2)] * 2 + [dma(n_dp // 2)] * 2 + [dma(2)] * 2,
            meet=3,
        )
        x0, ff_shard = lax.optimization_barrier((x0, ff_shard))
        given, more = [x0, g0, w_attn, x1, x2, cos, sin, start], []
    else:
        given, more = [lengths[0], rates, x0.reshape(parts), g0.reshape(parts), w_attn.reshape(1, D, 4 * D)], found
    w_ff = lax.all_gather(ff_shard.reshape(d_here, EXPERTS * 3 * ff), "dp", axis=0, tiled=True)
    results = call(
        functools.partial(forward_body, fast, n_t),
        "forward",
        more
        + [(ext, BF16), (row, BF16), (ext, BF16), (ext, BF16), (row, BF16), ((SPARE, rows), F32),
           (row, F32), (every_packed, BF16), ((n_t,) + parts, BF16), ((8, rows), F32), (row, F32), (row, F32), ((SPARE, rows), F32),
           ((8, D), F32)],
        given + [gain_attn, gain_moe, res_t, wrc, routes_t, v8],
        scalars=0 if fast else 1,
        scratch=[pltpu.VMEM((window, 256), F32), dma(2), dma(2)] + [dma(3)] * 8,
        meet=0,
    )
    if fast:
        x0, g0, w_attn = x0.reshape(row), g0.reshape(row), w_attn.reshape(D, 4 * D)
    else:
        x1, x2, cos, sin, start = results[:5]
        results = results[5:]
    h, q, k, v, o, lse, xm, hp_all, g_all, gt, xl, dhl, sm, gv = results
    x1, x2, g_all = x1.reshape(row), x2.reshape(row), g_all.reshape(every)

    out_all, back_all, gw_ff = experts_call(counts, hp_all, g_all, slots, w_ff, ff)
    ff_sum = lax.psum_scatter(gw_ff, "dp", scatter_dimension=0, tiled=True)

    dx, da, dres, small, dq, dk, dv, result = call(
        functools.partial(backward_body, n_t),
        "backward",
        [(row, F32), (row, BF16), ((SPARE, rows), F32), ((SPARE + 8, D), F32), (row, BF16), (ext, BF16), (ext, BF16), (row, BF16)],
        [back_all, out_all, dhl, gt, sm, routes_t, wrc, xm, gain_moe, g0, hp_all, w_attn, o, gv, q, k, v, lse, start, cos, sin, xl],
        scratch=[pltpu.VMEM((rows // 256, window, 256), F32), pltpu.VMEM((3 * rows, 128), F32), pltpu.VMEM((3 * rows, 128), F32),
                 pltpu.VMEM((rows + SPARE, D), F32), pltpu.VMEM(row, BF16), pltpu.VMEM((SPARE, rows), F32)]
        + [pltpu.VMEM((n_t - 1, rows + SPARE, D), BF16)] * 2 + [pltpu.VMEM((n_t - 1, rows, D), BF16)] * 2
        + [dma(n_t - 1, 2)] * 4 + [dma(n_t - 1, 1)] * 4,
        meet=1,
    )
    if fast:
        units = 4
        piece = (d_here, D)
        hops = 3 + (n_t - 1).bit_length()
        output, grad_tokens, attn_parts, small_all = call(
            functools.partial(finish_body, n_dp, n_t),
            "finish",
            [(row, BF16), (row, BF16), ((units, d_here, D // n_t), F32), ((SPARE + 16, D), F32)],
            [x0, x1, x2, h, dq, dk, dv, da, o, w_attn, dx, gain_attn, result.reshape(n_dp, share, D), small, pos],
            scratch=[pltpu.VMEM(row, F32)] + [pltpu.VMEM(row, BF16)] * 4 + [pltpu.VMEM((n_dp, share, D), BF16)] * 3
            + [pltpu.VMEM((units, n_dp) + piece, BF16), pltpu.VMEM((units, 4) + piece, BF16), pltpu.VMEM((units, 2) + piece, BF16),
               pltpu.VMEM((units,) + piece, BF16), pltpu.VMEM((units, n_t, d_here, D // n_t), BF16),
               pltpu.VMEM((units, n_t - 1, d_here, D // n_t), BF16)]
            + [pltpu.VMEM((hops, SPARE + 16, D), F32)] * 2
            + [dma(2)] * 2 + [dma(n_dp - 1)] * 4 + [dma(units, 4)] * 2 + [dma(units, 2)] * 2 + [dma(units)] * 2
            + [dma(units, n_t - 1)] * 2 + [dma(hops)] * 2,
            meet=2,
        )
        gain_all = small_all[SPARE + 8]
        attn_own = jnp.stack([attn_parts[2], attn_parts[0], attn_parts[1], attn_parts[3]], axis=1)
    else:
        back_out = lax.all_to_all(result, "dp", split_axis=0, concat_axis=0, tiled=True)
        gw_attn, gain_part, d_start = call(
            functools.partial(grads_body, n_t),
            "grads",
            [((D, 4 * D), BF16), ((8, D), F32), (row, BF16)],
            [x0, x1, x2, h, dq, dk, dv, da, o, w_attn, dx, gain_attn],
            scratch=[pltpu.VMEM(row, F32)] + [pltpu.VMEM(row, BF16)] * 4 + [dma(2), dma(2)],
            meet=2,
        )
        back_grad = lax.all_to_all(d_start, "dp", split_axis=0, concat_axis=0, tiled=True)
        output, grad_tokens = call(restore_body, "restore", [(row, BF16)] * 2, [pos, back_out, back_grad])

        def total(v):
            for axis, count in (("tensor", n_t), ("dp", n_dp)):
                bit = 1
                while bit < count:
                    v = v + lax.ppermute(v, axis, [(i, i ^ bit) for i in range(count)])
                    bit *= 2
            return v

        small_all = total(jnp.concatenate([small, gain_part], axis=0))
        gain_all = small_all[SPARE + 8]
        gw_attn, ff_sum = lax.optimization_barrier((gw_attn, ff_sum))
        attn_sum = lax.psum_scatter(gw_attn, "dp", scatter_dimension=0, tiled=True).reshape(d_here, 4, n_t, D // n_t)

        def share(j):
            return lax.dynamic_index_in_dim(attn_sum, t ^ j, 2, keepdims=False)

        attn_own = share(0).astype(F32)
        for j in range(1, n_t):
            attn_own = attn_own + swap(share(j), j).astype(F32)
    ff_own = ff_sum.reshape(d_here, EXPERTS, 3 * ff).astype(F32)
    return (
        output,
        grad_tokens,
        dres[0:12].T,
        attn_own[:, 0:3],
        attn_own[:, 3],
        ff_own[:, :, 0 : 2 * ff].reshape(d_here, EXPERTS, 2, ff),
        ff_own[:, :, 2 * ff :],
        gain_all,
        small_all[SPARE + 2],
        small_all[0:12].T,
        small_all[12:16].reshape(2, 2, D).transpose(0, 2, 1),
        small_all[SPARE : SPARE + 2],
    )


def solution(mesh):
    both, every = P(("dp", "tensor"), None), P()
    weights = (P("dp", None, "tensor"), P("dp", "tensor"), P("dp", None, None, "tensor"), P("dp", None, "tensor"))
    return jax.shard_map(
        body,
        mesh=mesh,
        in_specs=(both, both, P(("dp", "tensor")), P("dp", None), P("dp", None), both, *weights) + (every,) * 5,
        out_specs=(both, both, both, *weights) + (every,) * 5,
        check_vma=False,
    )
```

```python
import functools

import jax
import jax.numpy as jnp
import numpy as np
from jax import lax
from jax.experimental import pallas as pl
from jax.experimental.pallas import tpu as pltpu
from jax.sharding import PartitionSpec as P

D = 768
HEAD_DIM = 64
HEADS = 12
EXPERTS = 8
LONGEST = 1024
EPSILON = 1e-6
MASKED = -1e30
F32, BF16, I32 = jnp.float32, jnp.bfloat16, jnp.int32
NN = (((1,), (0,)), ((), ()))
NT = (((1,), (1,)), ((), ()))
TN = (((0,), (0,)), ((), ()))
SCORE_SCALE = HEAD_DIM**-0.5
LOG2E = 1.4426950408889634
TILE = 160
ROWS = 256
SPARE = 16
VMEM_CAP = 66_000_000


def mm(a, b, dims):
    return lax.dot_general(a, b, dims, preferred_element_type=F32)


def iota(shape, axis):
    return lax.broadcasted_iota(I32, shape, axis)


def pick(cond):
    return jnp.where(cond, 1.0, 0.0).astype(BF16)


def split2(v):
    high = v.astype(BF16)
    return high, (v - high.astype(F32)).astype(BF16)


def split3(v):
    high = v.astype(BF16)
    rest = v - high.astype(F32)
    mid = rest.astype(BF16)
    return high, mid, (rest - mid.astype(F32)).astype(BF16)


def vmem():
    return pl.BlockSpec(memory_space=pltpu.VMEM)


def smem():
    return pl.BlockSpec(memory_space=pltpu.SMEM)


def call(body, name, outs, operands, scalars=0, scratch=(), meet=None):
    return pl.pallas_call(
        body,
        name=name,
        out_shape=[jax.ShapeDtypeStruct(*o) for o in outs],
        in_specs=[smem()] * scalars + [vmem()] * (len(operands) - scalars),
        out_specs=[vmem()] * len(outs),
        scratch_shapes=list(scratch),
        compiler_params=pltpu.CompilerParams(
            vmem_limit_bytes=VMEM_CAP, collective_id=meet, has_side_effects=meet is not None
        ),
    )(*operands)


def deal_body(n_dp, deal_ref, tok_ref, cot_ref, routes_ref, xs_ref, gs_ref, pos_ref, slot_ref, cnt_ref):
    rows = tok_ref.shape[0]
    first, second = iota((rows, rows), 0), iota((rows, rows), 1)
    before = pick(first < second)
    deal = deal_ref[...]
    hit = iota((n_dp, rows), 0) == deal
    rank = mm(pick(hit), before, NN)
    rank = jnp.sum(jnp.where(hit, rank, 0.0), axis=0, keepdims=True).astype(I32)
    pos = deal * (rows // n_dp) + rank
    pos_ref[...] = pos
    place = pick(first == pos)
    xs_ref[...] = mm(place, tok_ref[...], NN).astype(BF16)
    gs_ref[...] = mm(place, cot_ref[...], NN).astype(BF16)
    expert = iota((EXPERTS, rows), 0)
    for j in range(routes_ref.shape[0]):
        route = routes_ref[j]
        named = (expert == route[0:1]) | (expert == route[1:2])
        ahead = mm(pick(named), before, NN).astype(I32)
        slot_ref[j] = jnp.where(named, ahead, -1)
        total = jnp.sum(jnp.where(named, 1.0, 0.0), axis=1, keepdims=True).astype(I32)
        cnt_ref[j] = jnp.broadcast_to(total, (EXPERTS, 128))


def restore_body(pos_ref, a_ref, b_ref, oa_ref, ob_ref):
    rows = a_ref.shape[0]
    place = pick(iota((rows, rows), 0) == pos_ref[...])
    oa_ref[...] = mm(place, a_ref[...], TN).astype(BF16)
    ob_ref[...] = mm(place, b_ref[...], TN).astype(BF16)


class Line:
    def __init__(self, size):
        self.size = size
        self.place = lax.axis_index("tensor")
        self.sent = {k: [] for k in range(size)}

    def each(self, body):
        for k in range(self.size):
            pl.when(self.place == k)(functools.partial(body, k))

    def enter(self):
        sem = pltpu.get_barrier_semaphore()

        def greet(k):
            near = [n for n in (k - 1, k + 1) if 0 <= n < self.size]
            for n in near:
                pl.semaphore_signal(sem, 1, device_id={"tensor": self.place + (n - k)}, device_id_type=pl.DeviceIdType.MESH)
            pl.semaphore_wait(sem, len(near))

        self.each(greet)

    def copy(self, hop, src, dst, sems):
        return pltpu.make_async_remote_copy(
            src_ref=src,
            dst_ref=dst,
            send_sem=sems[0],
            recv_sem=sems[1],
            device_id={"tensor": self.place + hop},
            device_id_type=pl.DeviceIdType.MESH,
        )

    def send(self, k, to, refs):
        self.copy(to - k, *refs()).start()
        self.sent[k].append((to - k, refs))

    def arrived(self, k, dst, sems):
        self.copy((k ^ 1) - k, dst, dst, sems).wait_recv()

    def leave(self):
        def drain(k):
            for hop, refs in self.sent[k]:
                self.copy(hop, *refs()).wait_send()

        self.each(drain)


class Peers:
    def __init__(self):
        self.d, self.t = lax.axis_index("dp"), lax.axis_index("tensor")
        self.sent = []

    def enter(self, targets):
        sem = pltpu.get_barrier_semaphore()
        for where in targets:
            pl.semaphore_signal(sem, 1, device_id=where, device_id_type=pl.DeviceIdType.MESH)
        pl.semaphore_wait(sem, len(targets))

    def copy(self, where, src, dst, sems):
        return pltpu.make_async_remote_copy(
            src_ref=src,
            dst_ref=dst,
            send_sem=sems[0],
            recv_sem=sems[1],
            device_id=where,
            device_id_type=pl.DeviceIdType.MESH,
        )

    def send(self, where, src, dst, sems):
        copy = self.copy(where, src, dst, sems)
        copy.start()
        self.sent.append(copy)

    def leave(self):
        for copy in self.sent:
            copy.wait_send()


def flip(index, bit):
    return index + bit * (1 - 2 * ((index // bit) % 2))


def around(index, count):
    return [(j, lax.rem(index + j, count), lax.rem(index + count - j, count)) for j in range(1, count)]


class Rows:
    def __init__(self, ref):
        self.ref = ref

    def __getitem__(self, at):
        columns = slice(None) if at is Ellipsis else at[1]
        value = self.ref[:, :, columns]
        return value.reshape(value.shape[0] * value.shape[1], value.shape[2])


def sum_events(size, k):
    events = []
    for dest in range(size):
        if dest >= k and dest > 0:
            events.append((0 if k == 0 else size - 1 - dest + k, 1, dest))
        if dest <= k and dest < size - 1:
            events.append((0 if k == size - 1 else dest + size - 1 - k, -1, dest))
    drop = [(t, w, d) for t, w, d in events if (k == 0 and w == 1 and d == 0) or (k == size - 1 and w == -1 and d == k)]
    return sorted((ev for ev in events if ev not in drop), key=lambda ev: (ev[0], ev[1], -ev[1] * ev[2]))


def turn(u):
    low = (iota((1, u.shape[1]), 1) % HEAD_DIM) < HEAD_DIM // 2
    half = HEAD_DIM // 2
    return jnp.where(low, pltpu.roll(u, u.shape[1] - half, 1), pltpu.roll(u, half, 1))


def wide(table):
    return jnp.concatenate([table] * (D // 128), axis=1)


def key_bias(start, block, first_row, base):
    window = LONGEST + block
    key = iota((window, block), 0) + first_row
    row = iota((1, block), 1) + (base + first_row)
    return jnp.where((key >= start) & (key <= row), 0.0, MASKED)


def router_part(route, o_ref, w_ref, x_ref, gain_ref, res_ref, wrc_ref, x1_ref, hp_ref, gt_ref):
    rows = o_ref.shape[0]
    x1 = x_ref[...].astype(F32) + mm(o_ref[...], w_ref[:, 3 * D : 4 * D], NT)
    x1_ref[...] = x1
    h = x1 * lax.rsqrt(jnp.mean(x1 * x1, axis=1, keepdims=True) + EPSILON) * gain_ref[...]
    h = h.astype(BF16)
    hp_ref[0:rows, :] = h
    high, mid, low = split3(wrc_ref[...])
    z = mm(low, h, NT) + mm(mid, h, NT) + mm(high, h, NT) + res_ref[...]
    expert = iota(z.shape, 0)
    named0, named1 = expert == route[0:1], expert == route[1:2]
    c0 = jnp.sum(jnp.where(named0, z, 0.0), axis=0, keepdims=True)
    c1 = jnp.sum(jnp.where(named1, z, 0.0), axis=0, keepdims=True)
    top = jnp.maximum(c0, c1)
    e0, e1 = jnp.exp(c0 - top), jnp.exp(c1 - top)
    g0, g1 = e0 / (e0 + e1), e1 / (e0 + e1)
    table = [g0, g1]
    for j in range(2):
        l0, l1 = z[12 + 2 * j : 13 + 2 * j], z[13 + 2 * j : 14 + 2 * j]
        top = jnp.maximum(l0, l1)
        m0, m1 = jnp.exp(l0 - top), jnp.exp(l1 - top)
        table += [m0 / (m0 + m1), m1 / (m0 + m1)]
    gt_ref[...] = jnp.concatenate(table + [jnp.zeros((2, rows), F32)], axis=0)
    gates = jnp.where(named0, g0, jnp.where(named1, g1, 0.0))
    gates = jnp.where(expert < EXPERTS, gates, 0.0)
    hp_ref[rows : rows + SPARE, :] = jnp.concatenate([gates, jnp.zeros((SPARE, D - rows), F32)], axis=1).astype(BF16)


def local_part(route, x1_ref, hp_ref, g_ref, gt_ref, v_ref, xl_ref, dhl_ref, sm_ref, gv_ref):
    rows = x1_ref.shape[0]
    h, g = hp_ref[0:rows, :], g_ref[...]
    hf, gf = h.astype(F32), g.astype(F32)
    low0 = gt_ref[0:1].astype(BF16).astype(F32)
    low1 = gt_ref[1:2].astype(BF16).astype(F32)

    def weight(e):
        return jnp.where(route[0:1] == e, low0, 0.0) + jnp.where(route[1:2] == e, low1, 0.0)

    copy, first, second = weight(EXPERTS + 1), weight(EXPERTS + 2), weight(EXPERTS + 3)
    m00, m01, m10, m11 = gt_ref[2:3], gt_ref[3:4], gt_ref[4:5], gt_ref[5:6]
    a = copy + first * m00 + second * m10
    b0, b1 = first * m01, second * m11
    table = jnp.concatenate([a, b0, b1, jnp.zeros((125, rows), F32)], axis=0).T
    ac, b0c, b1c = table[:, 0:1], table[:, 1:2], table[:, 2:3]
    v = jnp.concatenate([v_ref[...], jnp.zeros((6, D), F32)], axis=0)
    xl_ref[...] = x1_ref[...] + ac * hf + b0c * v[0:1] + b1c * v[1:2]
    dhl_ref[...] = ac * gf
    ones = jnp.ones((8, D), BF16)
    high, low = split2(hf * gf)
    gh = (mm(ones, high, NT) + mm(ones, low, NT))[0:1]
    vh, vm, vl = split3(v)
    gvs = mm(vl, g, NT) + mm(vm, g, NT) + mm(vh, g, NT)
    gv0, gv1 = gvs[0:1], gvs[1:2]
    zero = jnp.zeros((9, rows), F32)
    dl0 = first * m00 * m01 * (gh - gv0)
    dl1 = second * m10 * m11 * (gh - gv1)
    sm_ref[...] = jnp.concatenate(
        [zero, gh, m00 * gh + m01 * gv0, m10 * gh + m11 * gv1, dl0, -dl0, dl1, -dl1], axis=0
    )
    bh, bm, bl = split3(jnp.concatenate([b0, b1, jnp.zeros((6, rows), F32)], axis=0))
    gv_ref[...] = mm(bl, g, NN) + mm(bm, g, NN) + mm(bh, g, NN)


def rope_tables(lengths_ref, rates_ref, t, rows, cos_ref, sin_ref, start_ref):
    begins, total = [], jnp.int32(0)
    for i in range(lengths_ref.shape[0]):
        begins.append(total)
        total = total + lengths_ref[i]

    def opening(row):
        found = jnp.zeros_like(row)
        for begin in begins:
            found = jnp.where(begin <= row, jnp.maximum(found, begin), found)
        return found

    start_ref[...] = LONGEST - t * rows + opening(iota((1, rows), 1) + t * rows)
    sign = jnp.where(iota((1, 128), 1) % HEAD_DIM < HEAD_DIM // 2, -1.0, 1.0)
    step = 128

    def tile(i, _):
        at = pl.multiple_of(i * step, step)
        row = iota((step, 128), 0) + (at + (t - 2) * rows)
        angles = (row - opening(row)).astype(F32) * rates_ref[...]
        cos_ref[pl.ds(at, step), :] = jnp.cos(angles)
        sin_ref[pl.ds(at, step), :] = jnp.sin(angles) * sign
        return 0

    lax.fori_loop(0, cos_ref.shape[0] // step, tile, 0)


def opening_body(n_dp, size, lengths_ref, xs_ref, gs_ref, ws_ref, rates_ref,
                 x0_ref, g0_ref, w3_ref, x1_ref, x2_ref, cos_ref, sin_ref, start_ref,
                 wz_ref, sz, rz, sa, ra, sb, rb, s1, r1, s2, r2, s3, r3, sx, rx):
    rows = x0_ref.shape[0] * x0_ref.shape[1]
    line = Line(size)
    t = line.place
    last = size - 1

    def begin(k):
        if k < last:
            line.send(k, k + 1, lambda: (x0_ref, x1_ref, (sx.at[0], rx.at[0])))

    def second(k):
        if k > 0:
            line.arrived(k, x1_ref, (sx.at[0], rx.at[0]))
        else:
            x1_ref[...] = jnp.zeros_like(x1_ref)
        if 0 < k < last:
            line.send(k, k + 1, lambda: (x1_ref, x2_ref, (sx.at[1], rx.at[1])))

    def third(k):
        if k > 1:
            line.arrived(k, x2_ref, (sx.at[1], rx.at[1]))
        else:
            x2_ref[...] = jnp.zeros_like(x2_ref)

    net = Peers()
    d = net.d
    along, about = around(t, size), around(d, n_dp)
    net.enter([{"dp": to} for _, to, _ in about] + [{"tensor": to} for _, to, _ in along])
    for j, to, _ in along:
        net.send({"tensor": to}, ws_ref, wz_ref.at[t], (sz.at[j - 1], rz.at[j - 1]))
    for src_ref, dst_ref, ss, rr in ((xs_ref, x0_ref, sa, ra), (gs_ref, g0_ref, sb, rb)):
        for j, to, _ in about:
            net.send({"dp": to}, src_ref.at[to], dst_ref.at[d], (ss.at[j - 1], rr.at[j - 1]))
        dst_ref[d] = src_ref[d]
    wz_ref[t] = ws_ref[...]
    rope_tables(lengths_ref, rates_ref, t, rows, cos_ref, sin_ref, start_ref)

    def gathered(dst_ref, ss, rr):
        for j, _, source in about:
            held = dst_ref.at[source]
            net.copy({"dp": source}, held, held, (ss.at[j - 1], rr.at[j - 1])).wait_recv()

    gathered(x0_ref, sa, ra)
    line.each(begin)
    for j, _, source in along:
        held = wz_ref.at[source]
        net.copy({"tensor": source}, held, held, (sz.at[j - 1], rz.at[j - 1])).wait_recv()
    for c in range(4):
        w3_ref[d, :, c * D : (c + 1) * D] = jnp.concatenate([wz_ref[p, c] for p in range(size)], axis=1)
    pair, across = flip(d, 1), (flip(d, 2), flip(d, 4))
    halves = (slice(0, 2 * D), slice(2 * D, 4 * D))

    def pass_on(way, spot, half, sems):
        net.send({"dp": way}, w3_ref.at[spot, :, halves[half]], w3_ref.at[spot, :, halves[half]], sems)

    def passed(way, spot, half, sems):
        held = w3_ref.at[spot, :, halves[half]]
        net.copy({"dp": way}, held, held, sems).wait_recv()

    for half in range(2):
        pass_on(across[half], d, half, (s1.at[half], r1.at[half]))
    for half in range(2):
        near, far = across[half], across[1 - half]
        passed(near, near, half, (s1.at[half], r1.at[half]))
        for i, spot in enumerate((d, near)):
            pass_on(far, spot, half, (s2.at[half, i], r2.at[half, i]))
    line.each(second)
    beyond = flip(across[0], 4)
    for half in range(2):
        near, far = across[half], across[1 - half]
        for i, spot in enumerate((far, beyond)):
            passed(far, spot, half, (s2.at[half, i], r2.at[half, i]))
    core = lax.rem(d, 2)
    for i in range(n_dp // 2):
        spot = 2 * i + core
        net.send({"dp": pair}, w3_ref.at[spot], w3_ref.at[spot], (s3.at[i], r3.at[i]))
    for i in range(n_dp // 2):
        held = w3_ref.at[2 * i + 1 - core]
        net.copy({"dp": pair}, held, held, (s3.at[i], r3.at[i])).wait_recv()
    gathered(g0_ref, sb, rb)
    line.each(third)
    line.leave()
    net.leave()


def forward_body(fast, size, *refs):
    if fast:
        (x0_ref, g0_ref, w3_ref, x1_ref, x2_ref, cos_ref, sin_ref, start_ref), refs = refs[:8], refs[8:]
    else:
        (lengths_ref, rates_ref, x0_ref, g0_ref, w3_ref), refs = refs[:5], refs[5:]
    (gain_ref, gain2_ref, res_ref, wrc_ref, routes_ref, v8_ref), refs = refs[:6], refs[6:]
    if not fast:
        (x1_ref, x2_ref, cos_ref, sin_ref, start_ref), refs = refs[:5], refs[5:]
    (h_ref, q_ref, k_ref, v_ref, o_ref, lse_ref, xm_ref, hp_ref, gall_ref, gt_ref, xl_ref, dhl_ref, sm_ref, gv_ref,
     bias_ref, sx, rx, sgu, rgu, sgd, rgd, shu, rhu, shd, rhd) = refs
    rows = x0_ref.shape[0] * x0_ref.shape[1]
    step = 256
    line = Line(size)
    t = line.place
    last = size - 1
    w_ref, x_own, g_own = Rows(w3_ref), Rows(x0_ref), Rows(g0_ref)

    def begin(k):
        if k < last:
            if not fast:
                line.send(k, k + 1, lambda: (x0_ref, x1_ref, (sx.at[0], rx.at[0])))
            line.send(k, k + 1, lambda: (g0_ref, gall_ref.at[k], (sgu.at[0], rgu.at[0])))
        if k > 0:
            line.send(k, k - 1, lambda: (g0_ref, gall_ref.at[k], (sgd.at[0], rgd.at[0])))

    def first_rows(k):
        if k > 0:
            line.arrived(k, x1_ref, (sx.at[0], rx.at[0]))
        else:
            x1_ref[...] = jnp.zeros_like(x1_ref)
        if 0 < k < last:
            line.send(k, k + 1, lambda: (x1_ref, x2_ref, (sx.at[1], rx.at[1])))

    def second_rows(k):
        if k > 1:
            line.arrived(k, x2_ref, (sx.at[1], rx.at[1]))
        else:
            x2_ref[...] = jnp.zeros_like(x2_ref)

    def hop(k, far):
        up, down = k - far, k + far
        if up >= 0:
            line.arrived(k, gall_ref.at[up], (sgu.at[far - 1], rgu.at[far - 1]))
            if k < last:
                line.send(k, k + 1, lambda: (gall_ref.at[up], gall_ref.at[up], (sgu.at[far], rgu.at[far])))
        if down <= last:
            line.arrived(k, gall_ref.at[down], (sgd.at[far - 1], rgd.at[far - 1]))
            if k > 0:
                line.send(k, k - 1, lambda: (gall_ref.at[down], gall_ref.at[down], (sgd.at[far], rgd.at[far])))

    line.enter()
    line.each(begin)
    gall_ref[t] = g0_ref[...]
    if not fast:
        rope_tables(lengths_ref, rates_ref, t, rows, cos_ref, sin_ref, start_ref)
    gain = gain_ref[...]

    def part(x_ref, i):
        share = x_ref.shape[1]
        if share == rows:
            return x_ref[0, pl.ds(pl.multiple_of(i * step, step), step), :]
        return x_ref[pl.ds(i * (step // share), step // share)].reshape(step, D)

    def project_chunk(c, x_ref):
        def project(i, _):
            at = pl.multiple_of(i * step, step)
            x = part(x_ref, i).astype(F32)
            h = x * lax.rsqrt(jnp.mean(x * x, axis=1, keepdims=True) + EPSILON) * gain
            h = h.astype(BF16)
            to = pl.ds(pl.multiple_of(c * rows + i * step, step), step)
            h_ref[to, :] = h
            cos, sin = wide(cos_ref[to, :]), wide(sin_ref[to, :])
            k = mm(h, w_ref[:, D : 2 * D], NN)
            k_ref[to, :] = (k * cos + turn(k) * sin).astype(BF16)
            v_ref[to, :] = mm(h, w_ref[:, 2 * D : 3 * D], NN).astype(BF16)
            if c == 2:
                q = mm(h, w_ref[:, 0:D], NN)
                q_ref[pl.ds(at, step), :] = (q * cos + turn(q) * sin).astype(BF16)
            return 0

        lax.fori_loop(0, rows // step, project, 0)

    project_chunk(2, x0_ref)
    if not fast:
        line.each(first_rows)
    project_chunk(1, x1_ref)
    if not fast:
        line.each(second_rows)
    project_chunk(0, x2_ref)
    line.each(lambda k: hop(k, 1))

    block = step
    window = LONGEST + block
    lane = iota((1, 128), 1) // HEAD_DIM
    for rb in range(rows // block):
        first = rb * block
        bias_ref[...] = key_bias(start_ref[:, first : first + block], block, first, LONGEST)

        def pair(i, _, first=first):
            lanes = pl.ds(pl.multiple_of(i * 128, 128), 128)
            k = k_ref[first : first + window, lanes]
            vt = v_ref[first : first + window, lanes].T
            q = q_ref[first : first + block, lanes]
            parts = []
            for half in range(2):
                qm = jnp.where(lane == half, q, jnp.zeros_like(q))
                s = mm(k, qm, NT) * (SCORE_SCALE * LOG2E) + bias_ref[...]
                top = jnp.max(s, axis=0, keepdims=True)
                p = jnp.exp2(s - top)
                total = jnp.sum(p, axis=0, keepdims=True)
                out = mm(vt[half * HEAD_DIM : (half + 1) * HEAD_DIM], p.astype(BF16), NN)
                parts.append(out * (1.0 / total))
                lse_ref[pl.ds(i * 2 + half, 1), first : first + block] = top + jnp.log2(total)
            o_ref[first : first + block, lanes] = jnp.concatenate(parts, axis=0).T.astype(BF16)
            return 0

        lax.fori_loop(0, HEADS // 2, pair, 0)
        if rb == 0:
            line.each(lambda k: hop(k, 2))

    route = routes_ref[t]
    router_part(route, o_ref, w_ref, x_own, gain2_ref, res_ref, wrc_ref, xm_ref, hp_ref.at[t], gt_ref)

    def fifth(k):
        if k < last:
            line.send(k, k + 1, lambda: (hp_ref.at[k], hp_ref.at[k], (shu.at[0], rhu.at[0])))
        if k > 0:
            line.send(k, k - 1, lambda: (hp_ref.at[k], hp_ref.at[k], (shd.at[0], rhd.at[0])))

    line.each(fifth)
    local_part(route, xm_ref, hp_ref.at[t], g_own, gt_ref, v8_ref, xl_ref, dhl_ref, sm_ref, gv_ref)

    def sixth(k):
        for hop in range(2):
            up, down = k - 1 - hop, k + 1 + hop
            if up >= 0:
                line.arrived(k, hp_ref.at[up], (shu.at[hop], rhu.at[hop]))
                if k < last:
                    line.send(k, k + 1, lambda up=up, hop=hop: (hp_ref.at[up], hp_ref.at[up], (shu.at[hop + 1], rhu.at[hop + 1])))
            if down <= last:
                line.arrived(k, hp_ref.at[down], (shd.at[hop], rhd.at[hop]))
                if k > 0:
                    line.send(k, k - 1, lambda down=down, hop=hop: (hp_ref.at[down], hp_ref.at[down], (shd.at[hop + 1], rhd.at[hop + 1])))
        if k == last:
            line.arrived(k, hp_ref.at[0], (shu.at[2], rhu.at[2]))
            line.arrived(k, gall_ref.at[0], (sgu.at[2], rgu.at[2]))
        if k == 0:
            line.arrived(k, hp_ref.at[last], (shd.at[2], rhd.at[2]))
            line.arrived(k, gall_ref.at[last], (sgd.at[2], rgd.at[2]))

    line.each(sixth)
    line.leave()


def middle_part(route, dh_ref, gt_ref, sm_ref, wrc_ref, x1_ref, gain_ref, g_ref, h2_ref, w_ref, o_ref, gv_ref,
                dx_ref, da_ref, do_ref, delta_ref, dres_ref, small_ref):
    rows = x1_ref.shape[0]
    dgf = dh_ref[rows : rows + SPARE, 0:rows]
    dh = dh_ref[0:rows, :]
    dgate = jnp.concatenate([dgf[0:EXPERTS] + dgf[EXPERTS:], sm_ref[EXPERTS:SPARE]], axis=0)
    expert = iota((SPARE, rows), 0)
    named0, named1 = expert == route[0:1], expert == route[1:2]
    g0, g1 = gt_ref[0:1], gt_ref[1:2]
    d0 = jnp.sum(jnp.where(named0, dgate, 0.0), axis=0, keepdims=True)
    d1 = jnp.sum(jnp.where(named1, dgate, 0.0), axis=0, keepdims=True)
    inner = g0 * d0 + g1 * d1
    dz = jnp.where(named0, g0 * (d0 - inner), jnp.where(named1, g1 * (d1 - inner), 0.0))
    dres_ref[...] = dz
    dz = jnp.where(expert < 12, dz, sm_ref[...])
    zh, zm, zl = split3(dz)
    wh, wm, wl = split3(wrc_ref[...])
    dh = dh + (mm(zh, wl, TN) + mm(zl, wh, TN) + mm(zm, wm, TN) + mm(zh, wm, TN) + mm(zm, wh, TN) + mm(zh, wh, TN))
    h = h2_ref[...]
    small_ref[0:SPARE, :] = mm(zl, h, NN) + mm(zm, h, NN) + mm(zh, h, NN)
    x1 = x1_ref[...]
    r = lax.rsqrt(jnp.mean(x1 * x1, axis=1, keepdims=True) + EPSILON)
    xr = x1 * r
    grad_gain = jnp.sum(dh * xr, axis=0, keepdims=True)
    gv = gv_ref[...]
    small_ref[SPARE : SPARE + 8, :] = jnp.concatenate([gv[0:2], grad_gain, gv[3:8]], axis=0)
    scaled = dh * gain_ref[...]
    dx = g_ref[...].astype(F32) + r * (scaled - xr * jnp.mean(xr * scaled, axis=1, keepdims=True))
    dx_ref[...] = dx
    da = dx.astype(BF16)
    da_ref[...] = da
    do = mm(da, w_ref[:, 3 * D : 4 * D], NN).astype(BF16)
    do_ref[...] = do
    high, low = split2(do.astype(F32) * o_ref[...].astype(F32))
    heads = pick(iota((SPARE, D), 1) // HEAD_DIM == iota((SPARE, D), 0))
    delta_ref[...] = mm(heads, high, NT) + mm(heads, low, NT)


def backward_body(size, back_ref, out_ref, dhl_ref, gt_ref, sm_ref, routes_ref, wrc_ref, xm_ref, gain_ref, g_ref, hp_ref, w_ref,
                  o_ref, gv_ref, q_ref, k_ref, v_ref, lse_ref, start_ref, cos_ref, sin_ref, xl_ref,
                  dx_ref, da_ref, dres_ref, small_ref, dq_ref, dk_ref, dv_ref, y_ref,
                  bias_ref, dkf_ref, dvf_ref, dh_ref, do_ref, delta_ref, bu_ref, bd_ref, fu_ref, fd_ref,
                  sbu, rbu, sbd, rbd, sfu, rfu, sfd, rfd):
    rows = xm_ref.shape[0]
    packed = rows + SPARE
    cut = 272
    pieces = (slice(0, cut), slice(cut, packed))
    line = Line(size)
    t = line.place
    last = size - 1
    line.enter()

    def add_rows(held, mine):
        def one(i, _):
            at = pl.ds(pl.multiple_of(i * 16, 16), 16)
            held[at, :] = (held[at, :].astype(F32) + mine[at, :].astype(F32)).astype(BF16)
            return 0

        lax.fori_loop(0, held.shape[0] // 16, one, 0)

    def handle(k, way, dest, part, index, mine_ref, up_ref, down_ref, ups, downs):
        slot = dest - 1 if way == 1 else dest
        first = k == (0 if way == 1 else last)
        mine = mine_ref.at[dest, part]

        def refs():
            held = (up_ref if way == 1 else down_ref).at[slot, part]
            sems = tuple(s.at[slot, index] for s in (ups if way == 1 else downs))
            return mine_ref.at[dest, part] if first else held, held, sems

        _, held, sems = refs()
        if not first:
            line.arrived(k, held, sems)
        if dest != k:
            if not first:
                add_rows(held, mine)
            line.send(k, k + way, refs)

    def sum_back(k, opening):
        for time, way, dest in sum_events(size, k):
            if (time == 0) != opening:
                continue
            for index, part in enumerate(pieces):
                handle(k, way, dest, part, index, back_ref, bu_ref, bd_ref, (sbu, rbu), (sbd, rbd))

    def sum_out(k, now):
        for time, way, dest in sum_events(size, k):
            if time == now:
                handle(k, way, dest, slice(0, rows), 0, out_ref, fu_ref, fd_ref, (sfu, rfu), (sfd, rfd))

    line.each(lambda k: (sum_back(k, True), sum_out(k, 0), None)[2])
    line.each(lambda k: sum_back(k, False))
    dh_ref[...] = back_ref[t].astype(F32)

    @pl.when(t > 0)
    def _():
        dh_ref[...] += bu_ref[t - 1].astype(F32)

    @pl.when(t < last)
    def _():
        dh_ref[...] += bd_ref[t].astype(F32)

    dh_ref[0:rows, :] += dhl_ref[...]
    middle_part(routes_ref[t], dh_ref, gt_ref, sm_ref, wrc_ref, xm_ref, gain_ref, g_ref, hp_ref.at[t, 0:rows], w_ref, o_ref, gv_ref,
                dx_ref, da_ref, do_ref, delta_ref, dres_ref, small_ref)
    line.each(lambda k: sum_out(k, 1))

    block = 256
    window = LONGEST + block
    lane = iota((1, 128), 1) // HEAD_DIM
    for rb in range(rows // block):
        first = rb * block
        bias_ref[rb] = key_bias(start_ref[:, first : first + block], block, first, LONGEST)

    def pair(i, _):
        lanes = pl.ds(pl.multiple_of(i * 128, 128), 128)
        for rb in range(rows // block):
            first = rb * block
            k = k_ref[first : first + window, lanes]
            v = v_ref[first : first + window, lanes]
            kt = k.T
            q = q_ref[first : first + block, lanes]
            do = do_ref[first : first + block, lanes]
            dk = jnp.zeros((window, 128), F32)
            dv = jnp.zeros((window, 128), F32)
            parts = []
            for half in range(2):
                qm = jnp.where(lane == half, q, jnp.zeros_like(q))
                dom = jnp.where(lane == half, do, jnp.zeros_like(do))
                head = pl.ds(i * 2 + half, 1)
                s = mm(k, qm, NT) * (SCORE_SCALE * LOG2E) + bias_ref[rb]
                p = jnp.exp2(s - lse_ref[head, first : first + block])
                dp = mm(v, dom, NT)
                ds = (p * (dp - delta_ref[head, first : first + block])).astype(BF16)
                dv = dv + mm(p.astype(BF16), dom, NN)
                dk = dk + mm(ds, qm, NN)
                parts.append(mm(kt[half * HEAD_DIM : (half + 1) * HEAD_DIM], ds, NN))
            dq = jnp.concatenate(parts, axis=0).T * SCORE_SCALE
            at = slice(2 * rows + first, 2 * rows + first + block)
            dq_ref[first : first + block, lanes] = (dq * cos_ref[at, :] - turn(dq) * sin_ref[at, :]).astype(BF16)
            if first == 0:
                dkf_ref[0:window, :] = dk
                dvf_ref[0:window, :] = dv
            else:
                old = window - block
                dkf_ref[first : first + old, :] += dk[0:old]
                dvf_ref[first : first + old, :] += dv[0:old]
                dkf_ref[first + old : first + window, :] = dk[old:]
                dvf_ref[first + old : first + window, :] = dv[old:]
        dk = dkf_ref[...] * SCORE_SCALE
        dk_ref[:, lanes] = (dk * cos_ref[...] - turn(dk) * sin_ref[...]).astype(BF16)
        dv_ref[:, lanes] = dvf_ref[...].astype(BF16)
        return 0

    lax.fori_loop(0, HEADS // 4, pair, 0)
    line.each(lambda k: sum_out(k, 2))
    lax.fori_loop(HEADS // 4, HEADS // 2, pair, 0)
    line.each(lambda k: sum_out(k, 3))
    xl_ref[...] += out_ref[t].astype(F32)

    @pl.when(t > 0)
    def _():
        xl_ref[...] += fu_ref[t - 1].astype(F32)

    @pl.when(t < last)
    def _():
        xl_ref[...] += fd_ref[t].astype(F32)

    y_ref[...] = xl_ref[...].astype(BF16)
    line.leave()


def grads_body(size, x0_ref, x1_ref, x2_ref, h_ref, dq_ref, dk_ref, dv_ref, da_ref, o_ref, w_ref, dx_ref, gain_ref,
               gw_ref, gpart_ref, out_ref, d0_ref, d1_ref, d2_ref, ra_ref, rb_ref, sems_s, sems_r):
    rows = x0_ref.shape[0]
    line = Line(size)
    last = size - 1
    block = 256
    line.enter()

    def hidden(c, d_ref):
        def one(i, _):
            at = pl.ds(pl.multiple_of(i * block, block), block)
            to = pl.ds(pl.multiple_of(c * rows + i * block, block), block)
            total = mm(dk_ref[to, :], w_ref[:, D : 2 * D], NT) + mm(dv_ref[to, :], w_ref[:, 2 * D : 3 * D], NT)
            if c == 2:
                total = total + mm(dq_ref[at, :], w_ref[:, 0:D], NT)
            d_ref[at, :] = total.astype(d_ref.dtype)
            return 0

        lax.fori_loop(0, rows // block, one, 0)

    def gain_of(x_ref, d_ref):
        x = x_ref[...].astype(F32)
        r = lax.rsqrt(jnp.mean(x * x, axis=1, keepdims=True) + EPSILON)
        return jnp.sum(d_ref[...].astype(F32) * x * r, axis=0, keepdims=True)

    hidden(0, d2_ref)

    def first(k):
        if k > 1:
            line.send(k, k - 1, lambda: (d2_ref, ra_ref, (sems_s.at[0], sems_r.at[0])))

    line.each(first)
    hidden(1, d1_ref)
    gain = gain_of(x2_ref, d2_ref) + gain_of(x1_ref, d1_ref)
    h = h_ref[...]

    def weight(column, left, right_ref):
        for c in range(D // 256):
            cols = slice(c * 256, (c + 1) * 256)
            gw_ref[:, column * D + c * 256 : column * D + c * 256 + 256] = mm(left, right_ref[:, cols], TN).astype(BF16)

    weight(1, h, dk_ref)

    def second(k):
        if 0 < k < last:
            line.arrived(k, ra_ref, (sems_s.at[0], sems_r.at[0]))
            d1_ref[...] = (d1_ref[...].astype(F32) + ra_ref[...].astype(F32)).astype(BF16)
        if k > 0:
            line.send(k, k - 1, lambda: (d1_ref, rb_ref, (sems_s.at[1], sems_r.at[1])))

    line.each(second)
    hidden(2, d0_ref)
    gpart_ref[...] = jnp.broadcast_to(gain + gain_of(x0_ref, d0_ref), (8, D))
    weight(2, h, dv_ref)
    weight(0, h[2 * rows :], dq_ref)
    weight(3, da_ref[...], o_ref)

    def third(k):
        if k < last:
            line.arrived(k, rb_ref, (sems_s.at[1], sems_r.at[1]))
            d0_ref[...] += rb_ref[...].astype(F32)

    line.each(third)
    x = x0_ref[...].astype(F32)
    r = lax.rsqrt(jnp.mean(x * x, axis=1, keepdims=True) + EPSILON)
    xr = x * r
    scaled = d0_ref[...] * gain_ref[...]
    out_ref[...] = (dx_ref[...] + r * (scaled - xr * jnp.mean(xr * scaled, axis=1, keepdims=True))).astype(BF16)
    line.leave()


def finish_body(n_dp, size, x0_ref, x1_ref, x2_ref, h_ref, dq_ref, dk_ref, dv_ref, da_ref, o_ref, w_ref, dx_ref, gain_ref,
                y_ref, small_ref,
                yr_ref, gr_ref, gw_ref, sum_ref,
                d0_ref, d1_ref, d2_ref, ra_ref, rb_ref, out_ref, part_ref, r1_ref, r2_ref, r3_ref,
                zs_ref, zr_ref, cur_ref, got_ref,
                sems_s, sems_r, sy, ry, sg, rg, s1, r1, s2, r2, s3, r3, sz, rz, sb, rb):
    rows = x0_ref.shape[0]
    share = rows // n_dp
    line = Line(size)
    last = size - 1
    block = 256
    net = Peers()
    d, t = net.d, net.t
    about, along = around(d, n_dp), around(t, size)
    net.enter([{"dp": to} for _, to, _ in about] + [{"tensor": to} for _, to, _ in along])

    def scatter(src_ref, dst_ref, sems):
        for j, to, _ in about:
            net.send({"dp": to}, src_ref.at[to], dst_ref.at[d], (sems[0].at[j - 1], sems[1].at[j - 1]))
        dst_ref[d] = src_ref[d]

    def gathered(dst_ref, sems):
        for j, _, source in about:
            held = dst_ref.at[source]
            net.copy({"dp": source}, held, held, (sems[0].at[j - 1], sems[1].at[j - 1])).wait_recv()

    scatter(y_ref, yr_ref, (sy, ry))

    def hidden(c, d_ref):
        def one(i, _):
            at = pl.ds(pl.multiple_of(i * block, block), block)
            to = pl.ds(pl.multiple_of(c * rows + i * block, block), block)
            total = mm(dk_ref[to, :], w_ref[:, D : 2 * D], NT) + mm(dv_ref[to, :], w_ref[:, 2 * D : 3 * D], NT)
            if c == 2:
                total = total + mm(dq_ref[at, :], w_ref[:, 0:D], NT)
            d_ref[at, :] = total.astype(d_ref.dtype)
            return 0

        lax.fori_loop(0, rows // block, one, 0)

    def gain_of(x_ref, d_ref):
        x = x_ref[...].astype(F32)
        r = lax.rsqrt(jnp.mean(x * x, axis=1, keepdims=True) + EPSILON)
        return jnp.sum(d_ref[...].astype(F32) * x * r, axis=0, keepdims=True)

    core, x, y = lax.rem(d, 2), lax.rem(d // 2, 2), d // 4
    there = ({"dp": flip(d, 2)}, {"dp": flip(d, 4)})
    deep = D // n_dp

    def weight(u, left, right_ref):
        for c in range(D // 256):
            cols = slice(c * 256, (c + 1) * 256)
            value = mm(left, right_ref[:, cols], TN).astype(BF16)
            part_ref[u, :, :, cols] = value.reshape(n_dp, deep, 256)
        for j in range(4):
            net.send({"dp": flip(d, 1)}, part_ref.at[u, 2 * j + 1 - core], r1_ref.at[u, j], (s1.at[u, j], r1.at[u, j]))

    def add(u, j, arrived):
        spot = 2 * j + core
        part_ref[u, spot] = (part_ref[u, spot].astype(F32) + arrived[...].astype(F32)).astype(BF16)

    def chips(u):
        if u % 2 == 0:
            first = (there[0], [2 * i + 1 - x for i in range(2)], [2 * i + x for i in range(2)])
            return first, (there[1], 2 * (1 - y) + x)
        first = (there[1], [2 * (1 - y) + i for i in range(2)], [2 * y + i for i in range(2)])
        return first, (there[0], 2 * y + 1 - x)

    def halve(u):
        for j in range(4):
            held = r1_ref.at[u, j]
            net.copy({"dp": flip(d, 1)}, held, held, (s1.at[u, j], r1.at[u, j])).wait_recv()
            add(u, j, held)
        where, theirs, _ = chips(u)[0]
        for i in range(2):
            net.send(where, part_ref.at[u, 2 * theirs[i] + core], r2_ref.at[u, i], (s2.at[u, i], r2.at[u, i]))

    def quarter(u):
        (where, _, mine), (after, spot) = chips(u)
        for i in range(2):
            held = r2_ref.at[u, i]
            net.copy(where, held, held, (s2.at[u, i], r2.at[u, i])).wait_recv()
            add(u, mine[i], held)
        net.send(after, part_ref.at[u, 2 * spot + core], r3_ref.at[u], (s3.at[u], r3.at[u]))

    def own(u):
        after = chips(u)[1][0]
        held = r3_ref.at[u]
        net.copy(after, held, held, (s3.at[u], r3.at[u])).wait_recv()
        value = part_ref[u, d].astype(F32) + held[...].astype(F32)
        wide_share = D // size
        for p in range(size):
            zs_ref[u, p] = value[:, p * wide_share : (p + 1) * wide_share].astype(BF16)
        for j, to, _ in along:
            net.send({"tensor": to}, zs_ref.at[u, to], zr_ref.at[u, j - 1], (sz.at[u, j - 1], rz.at[u, j - 1]))

    def whole(u):
        total = zs_ref[u, t].astype(F32)
        for j, _, source in along:
            held = zr_ref.at[u, j - 1]
            net.copy({"tensor": source}, held, held, (sz.at[u, j - 1], rz.at[u, j - 1])).wait_recv()
            total = total + held[...].astype(F32)
        gw_ref[u] = total

    steps = [("dp", bit) for bit in (1, 2, 4, 8) if bit < n_dp] + [("tensor", bit) for bit in (1, 2, 4, 8) if bit < size]

    def small_out(i):
        axis, bit = steps[i]
        mine = t if axis == "tensor" else d
        net.send({axis: flip(mine, bit)}, cur_ref.at[i], got_ref.at[i], (sb.at[i], rb.at[i]))

    def small_in(i):
        axis, bit = steps[i]
        mine = t if axis == "tensor" else d
        held = got_ref.at[i]
        net.copy({axis: flip(mine, bit)}, held, held, (sb.at[i], rb.at[i])).wait_recv()
        total = cur_ref[i] + held[...]
        if i + 1 < len(steps):
            cur_ref[i + 1] = total
            small_out(i + 1)
        else:
            sum_ref[...] = total

    hidden(0, d2_ref)

    def first(k):
        if k > 1:
            line.send(k, k - 1, lambda: (d2_ref, ra_ref, (sems_s.at[0], sems_r.at[0])))

    line.each(first)
    hidden(1, d1_ref)

    def second(k):
        if k == last:
            line.send(k, k - 1, lambda: (d1_ref, rb_ref, (sems_s.at[1], sems_r.at[1])))

    line.each(second)
    h = h_ref[...]
    weight(0, h, dk_ref)
    gain = gain_of(x2_ref, d2_ref) + gain_of(x1_ref, d1_ref)
    weight(1, h, dv_ref)
    halve(0)
    hidden(2, d0_ref)
    gain = gain + gain_of(x0_ref, d0_ref)
    rest = small_ref.shape[0]
    cur_ref[0, 0:rest, :] = small_ref[...]
    cur_ref[0, rest : rest + 8, :] = jnp.broadcast_to(gain, (8, D))
    small_out(0)
    halve(1)

    def third(k):
        if 0 < k < last:
            line.arrived(k, ra_ref, (sems_s.at[0], sems_r.at[0]))
            d1_ref[...] = (d1_ref[...].astype(F32) + ra_ref[...].astype(F32)).astype(BF16)
            line.send(k, k - 1, lambda: (d1_ref, rb_ref, (sems_s.at[1], sems_r.at[1])))

    line.each(third)
    weight(2, h[2 * rows :], dq_ref)
    small_in(0)
    weight(3, da_ref[...], o_ref)
    quarter(0)
    quarter(1)
    halve(2)
    small_in(1)
    halve(3)
    own(0)
    own(1)
    gathered(yr_ref, (sy, ry))
    quarter(2)
    quarter(3)
    small_in(2)
    own(2)
    own(3)

    def fourth(k):
        if k < last:
            line.arrived(k, rb_ref, (sems_s.at[1], sems_r.at[1]))
            d0_ref[...] += rb_ref[...].astype(F32)

    line.each(fourth)
    xv = x0_ref[...].astype(F32)
    r = lax.rsqrt(jnp.mean(xv * xv, axis=1, keepdims=True) + EPSILON)
    xr = xv * r
    scaled = d0_ref[...] * gain_ref[...]
    value = dx_ref[...] + r * (scaled - xr * jnp.mean(xr * scaled, axis=1, keepdims=True))
    out_ref[...] = value.astype(BF16).reshape(n_dp, share, D)
    scatter(out_ref, gr_ref, (sg, rg))
    for i in range(3, len(steps)):
        small_in(i)
    for u in range(4):
        whole(u)
    gathered(gr_ref, (sg, rg))
    line.leave()
    net.leave()


def experts_body(ff, chunks, cnt_ref, h_refs, g_refs, slot_ref, w_ref, o_refs, d_refs, gw_ref,
                 xbuf, gbuf, cbuf, onehot, fbuf, dbuf, gacc, gates, dgrow, off_ref, base_ref, nt_ref):
    rows = slot_ref.shape[2]
    e = pl.program_id(0)

    def match(j, expert, tile):
        slots = slot_ref[j, pl.ds(expert, 1), :]
        return (iota((TILE, rows), 0) + tile * TILE) == slots

    def store_rows(at, count, hit, x, gs, gate_row):
        to = pl.ds(pl.multiple_of(at, 16), TILE)
        keep = iota((TILE, 1), 0) < count
        col = jnp.sum(jnp.where(hit, gate_row, 0.0), axis=1, keepdims=True)
        xbuf[to, :] = jnp.where(keep, x, xbuf[to, :].astype(F32)).astype(BF16)
        gbuf[to, :] = jnp.where(keep, gs, gbuf[to, :].astype(F32)).astype(BF16)
        cbuf[to, :] = jnp.where(keep, jnp.broadcast_to(col, (TILE, 128)), cbuf[to, :])

    def round16(n):
        return ((n + 15) // 16) * 16

    @pl.when(e == 0)
    def _gather():
        at = jnp.int32(0)
        for ex in range(EXPERTS):
            base_ref[ex] = at
            here = at
            for j in range(chunks):
                off_ref[j * EXPERTS + ex] = here
                here = here + round16(cnt_ref[j * EXPERTS + ex])
            tiles = (here - at + (ROWS - 1)) // ROWS
            nt_ref[ex] = tiles
            tail = pl.ds(pl.multiple_of(here, 16), ROWS)
            xbuf[tail, :] = jnp.zeros((ROWS, D), BF16)
            gbuf[tail, :] = jnp.zeros((ROWS, D), BF16)
            cbuf[tail, :] = jnp.zeros((ROWS, 128), F32)
            at = at + tiles * ROWS
        for j in range(chunks):
            gates[...] = h_refs[j, rows : rows + SPARE, 0:rows].astype(F32)

            def two(i, _, j=j):
                hits = [match(j, 2 * i + half, 0) for half in range(2)]
                sel = jnp.concatenate([pick(hit) for hit in hits], axis=0)
                x = mm(sel, h_refs[j, 0:rows, :], NN)
                gs = mm(sel, g_refs[j], NN)
                for half in range(2):
                    ex = 2 * i + half
                    count = round16(jnp.minimum(cnt_ref[j * EXPERTS + ex], TILE))
                    part = slice(half * TILE, (half + 1) * TILE)
                    store_rows(off_ref[j * EXPERTS + ex], count, hits[half], x[part], gs[part], gates[pl.ds(ex, 1), :])
                return 0

            lax.fori_loop(0, EXPERTS // 2, two, 0)

            def rare(ex, _, j=j):
                def more(tile, _):
                    hit = match(j, ex, tile)
                    sel = pick(hit)
                    count = round16(jnp.minimum(cnt_ref[j * EXPERTS + ex] - tile * TILE, TILE))
                    store_rows(
                        off_ref[j * EXPERTS + ex] + tile * TILE,
                        count,
                        hit,
                        mm(sel, h_refs[j, 0:rows, :], NN),
                        mm(sel, g_refs[j], NN),
                        gates[pl.ds(ex, 1), :],
                    )
                    return 0

                return lax.fori_loop(1, (cnt_ref[j * EXPERTS + ex] + (TILE - 1)) // TILE, more, 0)

            lax.fori_loop(0, EXPERTS, rare, 0)

    gacc[...] = jnp.zeros_like(gacc)

    def tile_step(m, _):
        at = pl.ds(pl.multiple_of(base_ref[e] + m * ROWS, 16), ROWS)
        x = xbuf[at, :]
        gs = gbuf[at, :].astype(F32)
        gate = wide(cbuf[at, :])
        u = mm(x, w_ref[:, 0:ff], NN)
        up = mm(x, w_ref[:, ff : 2 * ff], NN)
        sig = jax.nn.sigmoid(u)
        silu = u * sig
        act = (silu * up).astype(BF16)
        f = mm(act, w_ref[:, 2 * ff : 3 * ff], NT)
        cbuf[at, :] = jnp.broadcast_to(jnp.sum(gs * f, axis=1, keepdims=True), (ROWS, 128))
        gbuf[at, :] = (f * gate).astype(BF16)
        df = (gs * gate).astype(BF16)
        dact = mm(df, w_ref[:, 2 * ff : 3 * ff], NN)
        dup = (dact * silu).astype(BF16)
        du = (dact * up * sig * (1.0 + u * (1.0 - sig))).astype(BF16)
        xbuf[at, :] = (mm(du, w_ref[:, 0:ff], NT) + mm(dup, w_ref[:, ff : 2 * ff], NT)).astype(BF16)
        gacc[:, 0:ff] += mm(x, du, TN)
        gacc[:, ff : 2 * ff] += mm(x, dup, TN)
        gacc[:, 2 * ff : 3 * ff] += mm(df, act, TN)
        return 0

    lax.fori_loop(0, nt_ref[e], tile_step, 0)
    gw_ref[...] = gacc[...].astype(BF16)

    @pl.when(e == EXPERTS - 1)
    def _scatter():
        for j in range(chunks):
            def take(ex, _, j=j):
                at = pl.ds(pl.multiple_of(off_ref[j * EXPERTS + ex], 16), TILE)
                to = pl.ds(pl.multiple_of(ex * TILE, 16), TILE)
                hit = match(j, ex, 0)
                onehot[to, :] = pick(hit)
                fbuf[to, :] = gbuf[at, :]
                dbuf[to, :] = xbuf[at, :]
                col = jnp.concatenate([cbuf[at, :]] * (rows // 128), axis=1)
                dgrow[pl.ds(ex, 1), :] = jnp.sum(jnp.where(hit, col, 0.0), axis=0, keepdims=True)
                return 0

            lax.fori_loop(0, EXPERTS, take, 0)
            gacc[0:rows, 0:D] = mm(onehot[...], fbuf[...], TN)
            gacc[0:rows, D : 2 * D] = mm(onehot[...], dbuf[...], TN)

            def rare(ex, _, j=j):
                def more(tile, _):
                    at = pl.ds(pl.multiple_of(off_ref[j * EXPERTS + ex] + tile * TILE, 16), TILE)
                    hit = match(j, ex, tile)
                    sel = pick(hit)
                    gacc[0:rows, 0:D] += mm(sel, gbuf[at, :], TN)
                    gacc[0:rows, D : 2 * D] += mm(sel, xbuf[at, :], TN)
                    col = jnp.concatenate([cbuf[at, :]] * (rows // 128), axis=1)
                    dgrow[pl.ds(ex, 1), :] += jnp.sum(jnp.where(hit, col, 0.0), axis=0, keepdims=True)
                    return 0

                return lax.fori_loop(1, (cnt_ref[j * EXPERTS + ex] + (TILE - 1)) // TILE, more, 0)

            lax.fori_loop(0, EXPERTS, rare, 0)
            o_refs[j] = gacc[0:rows, 0:D].astype(BF16)
            d_refs[j, 0:rows, :] = gacc[0:rows, D : 2 * D].astype(BF16)
            total = dgrow[...]
            high = total.astype(BF16).astype(F32)
            both = jnp.concatenate([high, total - high], axis=0)
            d_refs[j, rows : rows + SPARE, :] = jnp.concatenate(
                [both, jnp.zeros((SPARE, D - rows), F32)], axis=1
            ).astype(BF16)


def experts_call(counts, hs, gs, slots, weights, ff):
    chunks, rows = gs.shape[:2]
    width = 3 * ff
    most = (rows + 15 * chunks + ROWS - 1) // ROWS * ROWS * EXPERTS + ROWS
    whole = lambda shape: pl.BlockSpec(shape, lambda e: (0,) * len(shape), pipeline_mode=pl.Buffered(1))
    return pl.pallas_call(
        functools.partial(experts_body, ff, chunks),
        name="experts",
        grid=(EXPERTS,),
        in_specs=[smem(), whole(hs.shape), whole(gs.shape), whole(slots.shape), pl.BlockSpec((D, width), lambda e: (0, e))],
        out_specs=[whole(gs.shape), whole(hs.shape), pl.BlockSpec((D, width), lambda e: (0, e))],
        out_shape=[
            jax.ShapeDtypeStruct(gs.shape, BF16),
            jax.ShapeDtypeStruct(hs.shape, BF16),
            jax.ShapeDtypeStruct((D, EXPERTS * width), BF16),
        ],
        scratch_shapes=[
            pltpu.VMEM((most, D), BF16),
            pltpu.VMEM((most, D), BF16),
            pltpu.VMEM((most, 128), F32),
            pltpu.VMEM((EXPERTS * TILE, rows), BF16),
            pltpu.VMEM((EXPERTS * TILE, D), BF16),
            pltpu.VMEM((EXPERTS * TILE, D), BF16),
            pltpu.VMEM((D, width), F32),
            pltpu.VMEM((SPARE, rows), F32),
            pltpu.VMEM((EXPERTS, rows), F32),
            pltpu.SMEM((chunks * EXPERTS,), I32),
            pltpu.SMEM((EXPERTS,), I32),
            pltpu.SMEM((EXPERTS,), I32),
        ],
        compiler_params=pltpu.CompilerParams(
            dimension_semantics=("arbitrary",), vmem_limit_bytes=VMEM_CAP
        ),
    )(counts, hs, gs, slots, weights)


def body(tokens, cotangent, deal, lengths, routes, gate_residual, w_qkv, w_out, w_gate_up, w_down,
         norm_gain_attn, norm_gain_moe, w_router, w_const, v_const):
    rows = tokens.shape[0]
    n_dp, n_t = lax.axis_size("dp"), lax.axis_size("tensor")
    t = lax.axis_index("tensor")
    ff = w_down.shape[2]
    d_here = w_qkv.shape[0]

    def swap(v, j):
        return lax.ppermute(v, "tensor", [(i, i ^ j) for i in range(n_t)])

    def place_in(parts):
        stacked = jnp.stack(parts)
        return jnp.stack([lax.dynamic_index_in_dim(stacked, t ^ i, 0, keepdims=False) for i in range(n_t)], axis=2)

    fast = n_dp == 8 and d_here % 16 == 0 and rows % 128 == 0
    attn_shard = jnp.concatenate([w_qkv, w_out[:, None, :]], axis=1)
    if not fast:
        attn_shard = place_in([attn_shard] + [swap(attn_shard, j) for j in range(1, n_t)]).reshape(d_here, 4 * D)
        w_attn = lax.all_gather(attn_shard, "dp", axis=0, tiled=True)
    ff_shard = jnp.concatenate([w_gate_up.reshape(d_here, EXPERTS, 2 * ff), w_down], axis=2)

    routes_t = routes.reshape(n_t, rows, 2).transpose(0, 2, 1)
    row, ext = (rows, D), (3 * rows, D)
    every, every_packed = (n_t, rows, D), (n_t, rows + SPARE, D)
    xs, gs, pos, slots, counts = call(
        functools.partial(deal_body, n_dp),
        "deal",
        [(row, BF16), (row, BF16), ((1, rows), I32), ((n_t, EXPERTS, rows), I32), ((n_t, EXPERTS, 128), I32)],
        [deal.reshape(1, rows), tokens, cotangent, routes_t],
    )
    counts = counts[:, :, 0].reshape(n_t * EXPERTS)
    share = rows // n_dp
    if fast:
        parts = (n_dp, share, D)
    else:
        parts = (1, rows, D)
        x0 = lax.all_to_all(xs, "dp", split_axis=0, concat_axis=0, tiled=True)
        g0 = lax.all_to_all(gs, "dp", split_axis=0, concat_axis=0, tiled=True)

    half = HEAD_DIM // 2
    rates = jnp.asarray(np.tile(10000.0 ** (np.arange(half) / -half), 4).reshape(1, 128), F32)
    gain_attn, gain_moe = norm_gain_attn.reshape(1, D), norm_gain_moe.reshape(1, D)
    window = LONGEST + 256
    res_t = jnp.concatenate([gate_residual.T, jnp.zeros((4, rows), F32)], axis=0)
    wrc = jnp.concatenate([w_router.T, w_const.transpose(0, 2, 1).reshape(4, D)], axis=0)
    dma = lambda *shape: pltpu.SemaphoreType.DMA(shape)
    found = [(parts, BF16), (parts, BF16), ((3 * rows, 128), F32), ((3 * rows, 128), F32), ((1, rows), I32)]
    if fast:
        x0, g0, w_attn, x1, x2, cos, sin, start = call(
            functools.partial(opening_body, n_dp, n_t),
            "opening",
            [(parts, BF16), (parts, BF16), ((n_dp, d_here, 4 * D), BF16)] + found,
            [lengths[0], xs.reshape(parts), gs.reshape(parts), attn_shard.transpose(1, 0, 2), rates],
            scalars=1,
            scratch=[pltpu.VMEM((n_t, 4, d_here, D // n_t), BF16)] + [dma(n_t - 1)] * 2 + [dma(n_dp - 1)] * 4
            + [dma(2)] * 2 + [dma(2, 2)] * 2 + [dma(n_dp // 2)] * 2 + [dma(2)] * 2,
            meet=3,
        )
        ff_shard = ff_shard.reshape(d_here, EXPERTS * 3 * ff)
        x0, ff_shard = lax.optimization_barrier((x0, ff_shard))
        given, more = [x0, g0, w_attn, x1, x2, cos, sin, start], []
    else:
        given, more = [lengths[0], rates, x0.reshape(parts), g0.reshape(parts), w_attn.reshape(1, D, 4 * D)], found
    w_ff = lax.all_gather(ff_shard.reshape(d_here, EXPERTS * 3 * ff), "dp", axis=0, tiled=True)
    results = call(
        functools.partial(forward_body, fast, n_t),
        "forward",
        more
        + [(ext, BF16), (row, BF16), (ext, BF16), (ext, BF16), (row, BF16), ((SPARE, rows), F32),
           (row, F32), (every_packed, BF16), ((n_t,) + parts, BF16), ((8, rows), F32), (row, F32), (row, F32), ((SPARE, rows), F32),
           ((8, D), F32)],
        given + [gain_attn, gain_moe, res_t, wrc, routes_t, v_const],
        scalars=0 if fast else 1,
        scratch=[pltpu.VMEM((window, 256), F32), dma(2), dma(2)] + [dma(3)] * 8,
        meet=0,
    )
    if fast:
        x0, g0, w_attn = x0.reshape(row), g0.reshape(row), w_attn.reshape(D, 4 * D)
    else:
        x1, x2, cos, sin, start = results[:5]
        results = results[5:]
    h, q, k, v, o, lse, xm, hp_all, g_all, gt, xl, dhl, sm, gv = results
    x1, x2, g_all = x1.reshape(row), x2.reshape(row), g_all.reshape(every)

    out_all, back_all, gw_ff = experts_call(counts, hp_all, g_all, slots, w_ff, ff)
    ff_sum = lax.psum_scatter(gw_ff, "dp", scatter_dimension=0, tiled=True)

    dx, da, dres, small, dq, dk, dv, result = call(
        functools.partial(backward_body, n_t),
        "backward",
        [(row, F32), (row, BF16), ((SPARE, rows), F32), ((SPARE + 8, D), F32), (row, BF16), (ext, BF16), (ext, BF16), (row, BF16)],
        [back_all, out_all, dhl, gt, sm, routes_t, wrc, xm, gain_moe, g0, hp_all, w_attn, o, gv, q, k, v, lse, start, cos, sin, xl],
        scratch=[pltpu.VMEM((rows // 256, window, 256), F32), pltpu.VMEM((3 * rows, 128), F32), pltpu.VMEM((3 * rows, 128), F32),
                 pltpu.VMEM((rows + SPARE, D), F32), pltpu.VMEM(row, BF16), pltpu.VMEM((SPARE, rows), F32)]
        + [pltpu.VMEM((n_t - 1, rows + SPARE, D), BF16)] * 2 + [pltpu.VMEM((n_t - 1, rows, D), BF16)] * 2
        + [dma(n_t - 1, 2)] * 4 + [dma(n_t - 1, 1)] * 4,
        meet=1,
    )
    if fast:
        units = 4
        piece = (d_here, D)
        hops = 3 + (n_t - 1).bit_length()
        back_out, back_grad, attn_parts, small_all = call(
            functools.partial(finish_body, n_dp, n_t),
            "finish",
            [(parts, BF16), (parts, BF16), ((units, d_here, D // n_t), F32), ((SPARE + 16, D), F32)],
            [x0, x1, x2, h, dq, dk, dv, da, o, w_attn, dx, gain_attn, result.reshape(n_dp, share, D), small],
            scratch=[pltpu.VMEM(row, F32)] + [pltpu.VMEM(row, BF16)] * 4 + [pltpu.VMEM((n_dp, share, D), BF16)]
            + [pltpu.VMEM((units, n_dp) + piece, BF16), pltpu.VMEM((units, 4) + piece, BF16), pltpu.VMEM((units, 2) + piece, BF16),
               pltpu.VMEM((units,) + piece, BF16), pltpu.VMEM((units, n_t, d_here, D // n_t), BF16),
               pltpu.VMEM((units, n_t - 1, d_here, D // n_t), BF16)]
            + [pltpu.VMEM((hops, SPARE + 16, D), F32)] * 2
            + [dma(2)] * 2 + [dma(n_dp - 1)] * 4 + [dma(units, 4)] * 2 + [dma(units, 2)] * 2 + [dma(units)] * 2
            + [dma(units, n_t - 1)] * 2 + [dma(hops)] * 2,
            meet=2,
        )
        gain_all = small_all[SPARE + 8]
        attn_own = jnp.stack([attn_parts[2], attn_parts[0], attn_parts[1], attn_parts[3]], axis=1)
    else:
        back_out = lax.all_to_all(result, "dp", split_axis=0, concat_axis=0, tiled=True)
        gw_attn, gain_part, d_start = call(
            functools.partial(grads_body, n_t),
            "grads",
            [((D, 4 * D), BF16), ((8, D), F32), (row, BF16)],
            [x0, x1, x2, h, dq, dk, dv, da, o, w_attn, dx, gain_attn],
            scratch=[pltpu.VMEM(row, F32)] + [pltpu.VMEM(row, BF16)] * 4 + [dma(2), dma(2)],
            meet=2,
        )
        back_grad = lax.all_to_all(d_start, "dp", split_axis=0, concat_axis=0, tiled=True)

        def total(v):
            for axis, count in (("tensor", n_t), ("dp", n_dp)):
                bit = 1
                while bit < count:
                    v = v + lax.ppermute(v, axis, [(i, i ^ bit) for i in range(count)])
                    bit *= 2
            return v

        small_all = total(jnp.concatenate([small, gain_part], axis=0))
        gain_all = small_all[SPARE + 8]
        gw_attn, ff_sum = lax.optimization_barrier((gw_attn, ff_sum))
        attn_sum = lax.psum_scatter(gw_attn, "dp", scatter_dimension=0, tiled=True).reshape(d_here, 4, n_t, D // n_t)

        def share(j):
            return lax.dynamic_index_in_dim(attn_sum, t ^ j, 2, keepdims=False)

        attn_own = share(0).astype(F32)
        for j in range(1, n_t):
            attn_own = attn_own + swap(share(j), j).astype(F32)
    output, grad_tokens = call(restore_body, "restore", [(row, BF16)] * 2, [pos, back_out.reshape(row), back_grad.reshape(row)])
    ff_own = ff_sum.reshape(d_here, EXPERTS, 3 * ff).astype(F32)
    return (
        output,
        grad_tokens,
        dres[0:12].T,
        attn_own[:, 0:3],
        attn_own[:, 3],
        ff_own[:, :, 0 : 2 * ff].reshape(d_here, EXPERTS, 2, ff),
        ff_own[:, :, 2 * ff :],
        gain_all,
        small_all[SPARE + 2],
        small_all[0:12].T,
        small_all[12:16].reshape(2, 2, D).transpose(0, 2, 1),
        small_all[SPARE : SPARE + 2],
    )


def solution(mesh):
    both, every = P(("dp", "tensor"), None), P()
    weights = (P("dp", None, "tensor"), P("dp", "tensor"), P("dp", None, None, "tensor"), P("dp", None, "tensor"))
    return jax.shard_map(
        body,
        mesh=mesh,
        in_specs=(both, both, P(("dp", "tensor")), P("dp", None), P("dp", None), both, *weights) + (every,) * 5,
        out_specs=(both, both, both, *weights) + (every,) * 5,
        check_vma=False,
    )
```
